32 devices in a mesh: fsdp: 8 (over z, x), ctx: 2 (over y), tp: 2 (over core).
Axes of the slice: x: 2, y: 2, z: 4, core: 2. Of those that a mesh axis runs over, the one named last changes fastest.
Arguments:
- hidden_in: bfloat16 [4096, 2048], P(('fsdp', 'ctx', 'tp')), may hold values from -6 to 6
- cotangent: bfloat16 [4096, 2048], P(('fsdp', 'ctx', 'tp')), may hold values from -6 to 6
- segments: int32 [4096], P('fsdp'), may hold values from 0 to 31, never falling along the last dimension, each value on 1 to 512 neighbouring positions
- w_query: bfloat16 [2048, 2048], P(('fsdp', 'ctx'), 'tp'), may hold values from -0.125 to 0.125
- key_projection_weight: bfloat16 [2048, 1024], P(('fsdp', 'ctx'), 'tp'), may hold values from -0.125 to 0.125
- value_projection_weight: bfloat16 [2048, 1024], P(('fsdp', 'ctx'), 'tp'), may hold values from -0.125 to 0.125
- w_out: bfloat16 [2048, 2048], P('tp', ('fsdp', 'ctx')), may hold values from -0.5 to 0.5
- w_gate: bfloat16 [2048, 6144], P('fsdp', ('ctx', 'tp')), may hold values from -0.125 to 0.125
- w_up: bfloat16 [2048, 6144], P('fsdp', ('ctx', 'tp')), may hold values from -0.125 to 0.125
- w_down: bfloat16 [6144, 2048], P(('ctx', 'tp'), 'fsdp'), may hold values from -0.078125 to 0.078125
- gain_attn: float32 [2048], replicated, may hold values from 0.5 to 1.5
- gain_mlp: float32 [2048], replicated, may hold values from 0.5 to 1.5
- gain_query: float32 [128], replicated, may hold values from 0.6 to 1.6
- key_norm_gain: float32 [128], replicated, may hold values from 0.6 to 1.6
Outputs:
- hidden_out: float32 [4096, 2048], P(('fsdp', 'ctx', 'tp'))
- grad_input: float32 [4096, 2048], P(('fsdp', 'ctx', 'tp'))
- grad_w_query: float32 [2048, 2048], P(('fsdp', 'ctx'), 'tp')
- grad_w_key: float32 [2048, 1024], P(('fsdp', 'ctx'), 'tp')
- grad_w_value: float32 [2048, 1024], P(('fsdp', 'ctx'), 'tp')
- grad_w_out: float32 [2048, 2048], P('tp', ('fsdp', 'ctx'))
- grad_w_gate: float32 [2048, 6144], P('fsdp', ('ctx', 'tp'))
- grad_w_up: float32 [2048, 6144], P('fsdp', ('ctx', 'tp'))
- grad_w_down: float32 [6144, 2048], P(('ctx', 'tp'), 'fsdp')
- grad_gain_attn: float32 [2048], replicated
- grad_gain_mlp: float32 [2048], replicated
- grad_gain_query: float32 [128], replicated
- grad_gain_key: float32 [128], replicated
The draws below stay inside these ranges and needn't reach their ends.
Inputs may be any that keep to these rules, and one draw needn't show every extreme that they name: `segments`: segment numbers never fall along the tokens, and every number up to the largest names a run of 1 to 512 tokens.
All inputs are finite; a program needn't handle non-finite values.
Results may differ from the reference program's by a relative error of at most 0.014.
Values may be sent and summed in bfloat16 or wider, within the bound.
A program may use at most 256 MiB of HBM per device.

```python
import math
import jax
import jax.numpy as jnp
import numpy as np
from jax import lax

MODEL_WIDTH = 2048
QUERY_HEAD_COUNT = 16
KEY_VALUE_HEADS = 8
HEAD_SIZE = 128
FF = 6144
L = 512
TOKENS = 4096


def gain_values(key):
    return jax.random.uniform(key, (HEAD_SIZE,), jnp.float32, 0.6, 1.6)


def draw_gain_query(key, part):
    return gain_values(jax.random.fold_in(key, 11))


def draw_key_norm_gain(key, part):
    return gain_values(jax.random.fold_in(key, 23))


def spiked(values, own_key, source, target, shards_of, factor):
    owner, partner = [(jnp.arange(values.shape[axis_at]) // (values.shape[axis_at] // shards_of)).reshape([-1 if axis == axis_at else 1 for axis in range(values.ndim)]) for axis_at in (source, target)]
    chosen = jax.random.permutation(own_key, shards_of)[partner]
    strong = (owner == chosen) | (owner == (partner + shards_of // 2) % shards_of)
    return jnp.where(strong, factor * values, values)


def levels(rng, dims, cuts, smallest, largest):
    level, own = 1.0, jax.random.fold_in(rng, 6)
    for axis_at, shards_of in cuts:
        steps = jnp.exp(jax.random.uniform(jax.random.fold_in(own, axis_at), (shards_of,), jnp.float32, smallest / len(cuts), largest / len(cuts)))
        level = level * jnp.repeat(steps, dims[axis_at] // shards_of).reshape([-1 if axis == axis_at else 1 for axis in range(len(dims))])
    return level


def length_profile(amount, total, most, lean):
    portions = [(1 << 20) // math.isqrt(grade ** lean) + 1 for grade in range(2, amount + 1)]
    surplus, counts = total - most - (amount - 1), [1] * (amount - 1)
    while surplus > 0:
        free = [i for i in range(amount - 1) if counts[i] < most]
        pool, remaining = sum([portions[i] for i in free]), surplus
        for i in free:
            extra = min(most - counts[i], max(1, remaining * portions[i] // pool), surplus)
            counts[i] = counts[i] + extra
            surplus = surplus - extra
    return np.array([most] + counts)


def ragged(stream_key, number_of, total, most, slope):
    if number_of == 2:
        one = jax.random.randint(stream_key, (), max(1, total - most), min(most, total - 1) + 1)
        return jnp.stack([one, total - one])
    lengths = jnp.asarray(length_profile(number_of, total, most, slope), jnp.int32)
    twos = (number_of - 1) // 2
    source_of, taker = lengths[1:1 + 2 * twos:2], lengths[2:2 + 2 * twos:2]
    slack = jnp.minimum(source_of - 1, most - taker)
    moved = jax.random.randint(jax.random.fold_in(stream_key, 1), (twos,), 0, 1 << 20) % (slack + 1)
    lengths = lengths.at[1:1 + 2 * twos:2].set(source_of - moved).at[2:2 + 2 * twos:2].set(taker + moved)
    return lengths[jax.random.permutation(jax.random.fold_in(stream_key, 2), number_of)]


def gaussian(key, extent, scale, most, cuts=(), kind=jnp.bfloat16):
    values = scale * jax.random.normal(key, extent, jnp.float32)
    if cuts:
        values = values * levels(key, extent, cuts, -0.22, 0.18)
    return jnp.clip(values, -most, most).astype(kind)


def heavy_noise(key, extent, deviation, most, split, heavy, held_as=jnp.bfloat16):
    array = deviation * jax.random.normal(key, extent, jnp.float32)
    if split:
        array = array * levels(key, extent, split, -0.22, 0.18)
    return jnp.clip(spiked(array, jax.random.fold_in(key, 3), *heavy), -most, most).astype(held_as)


def setup_inputs(seed: int = 0) -> dict:
    keys = jax.random.split(jax.random.key(seed), 15)
    return {
        "hidden_in": heavy_noise(keys[0], (TOKENS, MODEL_WIDTH), 1.0, 6.0, ((0, 32),), (0, 1, 32, 2.75)),
        "cotangent": heavy_noise(keys[1], (TOKENS, MODEL_WIDTH), 1.0, 6.0, ((0, 32),), (0, 1, 32, 2.75)),
        "segments": jnp.searchsorted(jnp.cumsum(ragged(keys[2], TOKENS // (L // 4), TOKENS, L, 2)), jnp.arange(TOKENS), side="right").astype(jnp.int32),
        "w_query": gaussian(keys[3], (MODEL_WIDTH, QUERY_HEAD_COUNT * HEAD_SIZE), MODEL_WIDTH ** -0.5, 0.125, ((0, 16), (1, 2))),
        "key_projection_weight": gaussian(keys[4], (MODEL_WIDTH, KEY_VALUE_HEADS * HEAD_SIZE), MODEL_WIDTH ** -0.5, 0.125, ((0, 16), (1, 2))),
        "value_projection_weight": gaussian(keys[5], (MODEL_WIDTH, KEY_VALUE_HEADS * HEAD_SIZE), MODEL_WIDTH ** -0.5, 0.125, ((0, 16), (1, 2))),
        "w_out": gaussian(keys[6], (QUERY_HEAD_COUNT * HEAD_SIZE, MODEL_WIDTH), (QUERY_HEAD_COUNT * HEAD_SIZE // 16) ** -0.5, 0.5, ((0, 2), (1, 16))),
        "w_gate": gaussian(keys[7], (MODEL_WIDTH, FF), MODEL_WIDTH ** -0.5, 0.125, ((0, 8), (1, 4))),
        "w_up": gaussian(keys[8], (MODEL_WIDTH, FF), MODEL_WIDTH ** -0.5, 0.125, ((0, 8), (1, 4))),
        "w_down": gaussian(keys[9], (FF, MODEL_WIDTH), FF ** -0.5, 0.078125, ((0, 4), (1, 8))),
        "gain_attn": jnp.clip(1.0 + 0.1 * jax.random.normal(keys[10], (MODEL_WIDTH,), jnp.float32), 0.5, 1.5),
        "gain_mlp": jnp.clip(1.0 + 0.1 * jax.random.normal(keys[11], (MODEL_WIDTH,), jnp.float32), 0.5, 1.5),
        "gain_query": draw_gain_query(jax.random.fold_in(keys[14], 71), 0),
        "key_norm_gain": draw_key_norm_gain(jax.random.fold_in(keys[14], 71), 0),
    }


EPS = 1e-06
THETA = 1000000.0

def rounded_weights(values_in):
    return lax.optimization_barrier(values_in.astype(jnp.bfloat16)).astype(jnp.float32)

def norm_moments(hidden):
    row_scale = lax.rsqrt(lax.optimization_barrier(jnp.mean(hidden * hidden, axis=-1, keepdims=True)) + EPS)
    return (hidden * row_scale, row_scale)

def norm_backward_step(grad_norm, unit_rows, row_scale, gain):
    scaled = grad_norm * gain
    return row_scale * (scaled - unit_rows * lax.optimization_barrier(jnp.mean(scaled * unit_rows, axis=-1, keepdims=True)))

def positions_of(segments):
    count = segments.shape[0]
    token_index = jnp.arange(count, dtype=jnp.int32)
    starts_here = jnp.concatenate([jnp.ones((1,), dtype=bool), segments[1:] != segments[:-1]])
    seg_start = lax.cummax(jnp.where(starts_here, token_index, jnp.zeros_like(token_index)), axis=0)
    return token_index - seg_start

def rotary_tables(positions):
    half_dim = HEAD_SIZE // 2
    freqs = THETA ** (-2.0 * jnp.arange(half_dim, dtype=jnp.float32) / HEAD_SIZE)
    angles = positions.astype(jnp.float32)[:, None] * freqs[None, :]
    return (jnp.cos(angles)[:, None, :], jnp.sin(angles)[:, None, :])

def rotate(values_in, cosine, sine):
    half_dim = values_in.shape[-1] // 2
    first_half = values_in[..., :half_dim]
    second_half = values_in[..., half_dim:]
    return jnp.concatenate([first_half * cosine - second_half * sine, second_half * cosine + first_half * sine], axis=-1)

def rotate_back(grads_in, cosine, sine):
    half_dim = grads_in.shape[-1] // 2
    first_half = grads_in[..., :half_dim]
    second_half = grads_in[..., half_dim:]
    return jnp.concatenate([first_half * cosine + second_half * sine, second_half * cosine - first_half * sine], axis=-1)

def one_sequence(hidden_in, cotangent, segments, w_query, key_projection_weight, value_projection_weight, w_out, w_gate, w_up, w_down, gain_attn, gain_mlp, gain_query, key_norm_gain):
    packed_length = hidden_in.shape[0]
    query_group_width = QUERY_HEAD_COUNT // KEY_VALUE_HEADS
    score_scale = HEAD_SIZE ** (-0.5)
    residual_in = hidden_in.astype(jnp.float32)
    unit_one, scale_one = norm_moments(residual_in)
    normed_one = (unit_one * gain_attn).astype(jnp.bfloat16)
    query_flat = jnp.dot(normed_one, w_query, preferred_element_type=jnp.float32)
    flattened_key = jnp.dot(normed_one, key_projection_weight, preferred_element_type=jnp.float32)
    flattened_value = jnp.dot(normed_one, value_projection_weight, preferred_element_type=jnp.float32)
    unit_q, scale_q = norm_moments(rounded_weights(query_flat).reshape(packed_length, QUERY_HEAD_COUNT, HEAD_SIZE))
    unit_key_rows, key_norm_scale = norm_moments(rounded_weights(flattened_key).reshape(packed_length, KEY_VALUE_HEADS, HEAD_SIZE))
    cosine, sine = rotary_tables(positions_of(segments))
    rotated_query = rounded_weights(rotate(unit_q * gain_query, cosine, sine))
    key_rot = rounded_weights(rotate(unit_key_rows * key_norm_gain, cosine, sine))
    key_rep = jnp.repeat(key_rot, query_group_width, axis=1)
    repeated_value = jnp.repeat(rounded_weights(flattened_value).reshape(packed_length, KEY_VALUE_HEADS, HEAD_SIZE), query_group_width, axis=1)
    token_index = jnp.arange(packed_length, dtype=jnp.int32)
    allowed = ((segments[:, None] == segments[None, :]) & (token_index[:, None] >= token_index[None, :]))[None]
    scores = jnp.einsum('qhd,khd->hqk', rotated_query, key_rep) * score_scale
    scores = jnp.where(allowed, scores, -jnp.inf)
    row_peak = lax.optimization_barrier(jnp.max(scores, axis=-1, keepdims=True))
    log_total = row_peak + jnp.log(lax.optimization_barrier(jnp.sum(jnp.exp(scores - row_peak), axis=-1, keepdims=True)))
    soft_exact = jnp.exp(scores - log_total)
    rounded_softmax = rounded_weights(soft_exact)
    attended = jnp.einsum('hqk,khd->qhd', rounded_softmax, repeated_value).astype(jnp.bfloat16).reshape(packed_length, QUERY_HEAD_COUNT * HEAD_SIZE)
    residual_mid = residual_in + jnp.dot(attended, w_out, preferred_element_type=jnp.float32)
    unit_two, scale_two = norm_moments(residual_mid)
    normed_two = (unit_two * gain_mlp).astype(jnp.bfloat16)
    gate_pre = jnp.dot(normed_two, w_gate, preferred_element_type=jnp.float32)
    up_pre = jnp.dot(normed_two, w_up, preferred_element_type=jnp.float32)
    gate_sig = jax.nn.sigmoid(gate_pre)
    gate_act = gate_pre * gate_sig
    mixed = (gate_act * up_pre).astype(jnp.bfloat16)
    hidden_out = residual_mid + jnp.dot(mixed, w_down, preferred_element_type=jnp.float32)
    grad_mixed = jnp.dot(cotangent, w_down.T, preferred_element_type=jnp.float32)
    grad_gate = (grad_mixed * up_pre * gate_sig * (1.0 + gate_pre * (1.0 - gate_sig))).astype(jnp.bfloat16)
    grad_up = (grad_mixed * gate_act).astype(jnp.bfloat16)
    grad_w_gate = jnp.dot(normed_two.T, grad_gate, preferred_element_type=jnp.float32)
    grad_w_up = jnp.dot(normed_two.T, grad_up, preferred_element_type=jnp.float32)
    grad_w_down = jnp.dot(mixed.T, cotangent, preferred_element_type=jnp.float32)
    grad_norm_two = jnp.dot(grad_gate, w_gate.T, preferred_element_type=jnp.float32) + jnp.dot(grad_up, w_up.T, preferred_element_type=jnp.float32)
    grad_gain_mlp = lax.optimization_barrier(jnp.sum(grad_norm_two * unit_two, axis=0))
    grad_mid = cotangent.astype(jnp.float32) + norm_backward_step(grad_norm_two, unit_two, scale_two, gain_mlp)
    grad_mid_b = grad_mid.astype(jnp.bfloat16)
    grad_w_out = jnp.dot(attended.T, grad_mid_b, preferred_element_type=jnp.float32)
    attention_grad = rounded_weights(jnp.dot(grad_mid_b, w_out.T, preferred_element_type=jnp.float32)).reshape(packed_length, QUERY_HEAD_COUNT, HEAD_SIZE)
    attended_wide = attended.astype(jnp.float32).reshape(packed_length, QUERY_HEAD_COUNT, HEAD_SIZE)
    delta = lax.optimization_barrier(jnp.sum(attention_grad * attended_wide, axis=-1))
    grad_soft = jnp.einsum('qhd,khd->hqk', attention_grad, repeated_value)
    score_gradient = rounded_weights(soft_exact * (grad_soft - delta.T[:, :, None]) * score_scale)
    grad_query_rot = jnp.einsum('hqk,khd->qhd', score_gradient, key_rep)
    rotated_key_grad = jnp.einsum('fie,ifo->efo', score_gradient, rotated_query).reshape(packed_length, KEY_VALUE_HEADS, query_group_width, HEAD_SIZE).sum(axis=2)
    value_grad_total = jnp.einsum('fie,ifo->efo', rounded_softmax, attention_grad).reshape(packed_length, KEY_VALUE_HEADS, query_group_width, HEAD_SIZE).sum(axis=2)
    grad_unit_q = rotate_back(grad_query_rot, cosine, sine)
    unit_key_grad = rotate_back(rotated_key_grad, cosine, sine)
    grad_gain_query = lax.optimization_barrier(jnp.sum(grad_unit_q * unit_q, axis=(0, 1)))
    grad_gain_key = lax.optimization_barrier(jnp.sum(unit_key_grad * unit_key_rows, axis=(0, 1)))
    grad_query = norm_backward_step(grad_unit_q, unit_q, scale_q, gain_query).astype(jnp.bfloat16).reshape(packed_length, QUERY_HEAD_COUNT * HEAD_SIZE)
    key_gradient = norm_backward_step(unit_key_grad, unit_key_rows, key_norm_scale, key_norm_gain).astype(jnp.bfloat16).reshape(packed_length, KEY_VALUE_HEADS * HEAD_SIZE)
    value_gradient = value_grad_total.astype(jnp.bfloat16).reshape(packed_length, KEY_VALUE_HEADS * HEAD_SIZE)
    grad_w_query = jnp.dot(normed_one.T, grad_query, preferred_element_type=jnp.float32)
    grad_w_key = jnp.dot(normed_one.T, key_gradient, preferred_element_type=jnp.float32)
    grad_w_value = jnp.dot(normed_one.T, value_gradient, preferred_element_type=jnp.float32)
    grad_norm_one = jnp.dot(grad_query, w_query.T, preferred_element_type=jnp.float32) + jnp.dot(key_gradient, key_projection_weight.T, preferred_element_type=jnp.float32) + jnp.dot(value_gradient, value_projection_weight.T, preferred_element_type=jnp.float32)
    grad_gain_attn = lax.optimization_barrier(jnp.sum(grad_norm_one * unit_one, axis=0))
    grad_input = grad_mid + norm_backward_step(grad_norm_one, unit_one, scale_one, gain_attn)
    return (hidden_out, grad_input, grad_w_query, grad_w_key, grad_w_value, grad_w_out, grad_w_gate, grad_w_up, grad_w_down, grad_gain_attn, grad_gain_mlp, grad_gain_query, grad_gain_key)

def reference(hidden_in, cotangent, segments, w_query, key_projection_weight, value_projection_weight, w_out, w_gate, w_up, w_down, gain_attn, gain_mlp, gain_query, key_norm_gain):
    seq_count = hidden_in.shape[0] // L
    stacked = (hidden_in.reshape(seq_count, L, MODEL_WIDTH), cotangent.reshape(seq_count, L, MODEL_WIDTH), segments.reshape(seq_count, L))
    initial = (jnp.zeros(w_query.shape, jnp.float32), jnp.zeros(key_projection_weight.shape, jnp.float32), jnp.zeros(value_projection_weight.shape, jnp.float32), jnp.zeros(w_out.shape, jnp.float32), jnp.zeros(w_gate.shape, jnp.float32), jnp.zeros(w_up.shape, jnp.float32), jnp.zeros(w_down.shape, jnp.float32), jnp.zeros(gain_attn.shape, jnp.float32), jnp.zeros(gain_mlp.shape, jnp.float32), jnp.zeros(gain_query.shape, jnp.float32), jnp.zeros(key_norm_gain.shape, jnp.float32))

    def advance(carry, item):
        result = one_sequence(item[0], item[1], item[2], w_query, key_projection_weight, value_projection_weight, w_out, w_gate, w_up, w_down, gain_attn, gain_mlp, gain_query, key_norm_gain)
        updated = tuple((total + piece for total, piece in zip(carry, result[2:])))
        return (updated, (result[0], result[1]))
    totals, rows_out = lax.scan(advance, initial, stacked)
    return (rows_out[0].reshape(seq_count * L, MODEL_WIDTH), rows_out[1].reshape(seq_count * L, MODEL_WIDTH), totals[0], totals[1], totals[2], totals[3], totals[4], totals[5], totals[6], totals[7], totals[8], totals[9], totals[10])
```

```python
import functools

import jax
import jax.numpy as jnp
from jax import lax
from jax.experimental import pallas as pl
from jax.experimental.pallas import tpu as pltpu
from jax.sharding import PartitionSpec as P

EPS = 1e-06
THETA = 1000000.0
AXES = ("fsdp", "ctx", "tp")
MESH = pl.DeviceIdType.MESH
BF16 = jnp.bfloat16
F32 = jnp.float32
TP_BIT, CTX_BIT = 1, 2
PAIR = 2
PAIR_BIT = PAIR * 4


def dot_rows(left, right):
    return lax.dot_general(left, right, (((0,), (0,)), ((), ())), preferred_element_type=F32)


def dot_cols(left, right):
    return lax.dot_general(left, right, (((1,), (1,)), ((), ())), preferred_element_type=F32)


def dot(left, right):
    return lax.dot_general(left, right, (((1,), (0,)), ((), ())), preferred_element_type=F32)


def places():
    f, c, t = lax.axis_index("fsdp"), lax.axis_index("ctx"), lax.axis_index("tp")
    pair = (f // PAIR) % 2
    other_f, other_c, other_t = f + PAIR - 2 * PAIR * pair, 1 - c, 1 - t
    mine = pair * 4 + c * 2
    blocks = [mine, pair * 4 + other_c * 2, (1 - pair) * 4 + c * 2, (1 - pair) * 4 + other_c * 2]
    chips = [None, {"ctx": other_c}, {"fsdp": other_f}, {"fsdp": other_f, "ctx": other_c}]
    return t, other_t, blocks, chips, {"tp": other_t}


def greet(chips, sibling):
    barrier = pltpu.get_barrier_semaphore()
    for device in [*chips[1:], sibling]:
        pl.semaphore_signal(barrier, inc=1, device_id=device, device_id_type=MESH)
    pl.semaphore_wait(barrier, 4)


def remote(src, dst, send, recv, device):
    return pltpu.make_async_remote_copy(
        src_ref=src, dst_ref=dst, send_sem=send, recv_sem=recv, device_id=device, device_id_type=MESH
    )


def spread(own, out, sems):
    send, recv, local = sems
    t, other_t, blocks, chips, sibling = places()
    here = pltpu.make_async_copy(own, out.at[blocks[0] + t], local)
    here.start()
    copies = [None] + [
        remote(own, out.at[blocks[0] + t], send.at[j], recv.at[j], chips[j]) for j in (1, 2, 3)
    ]
    for j in (3, 1, 2):
        copies[j].start()
    beside = remote(own, out.at[blocks[0] + t], send.at[0], recv.at[0], sibling)
    beside.start()
    forwards = []
    for j in (1, 2, 3):
        remote(own, out.at[blocks[j] + t], send.at[j], recv.at[j], chips[j]).wait_recv()
        hand = remote(
            out.at[blocks[j] + t], out.at[blocks[j] + t], send.at[j + 4], recv.at[j + 4], sibling
        )
        hand.start()
        forwards.append(hand)
    here.wait()
    beside.wait_send()
    remote(own, out.at[blocks[0] + other_t], send.at[0], recv.at[0], sibling).wait_recv()
    for j in (1, 2, 3):
        copies[j].wait_send()
        forwards[j - 1].wait_send()
        remote(
            own, out.at[blocks[j] + other_t], send.at[j + 4], recv.at[j + 4], sibling
        ).wait_recv()


def collect(partial, held, first, second, sending, sems):
    send, recv, local = sems
    t, other_t, blocks, chips, sibling = places()
    order = (3, 1, 2, 0)
    loads, hands = {}, {}
    for j in order:
        hands[j] = remote(
            partial.at[blocks[j] + other_t], first.at[j], send.at[j], recv.at[j], sibling
        )
        hands[j].start()
        loads[j] = pltpu.make_async_copy(partial.at[blocks[j] + t], held.at[j], local.at[j])
        loads[j].start()
    rows = held.shape[1]
    step = 16
    across = {}
    for j in order:
        loads[j].wait()
        hands[j].wait()
        if j == 0:
            continue

        @pl.loop(0, rows // step)
        def _(i):
            at = pl.ds(pl.multiple_of(i * step, step), step)
            sending[j - 1, at] = (held[j, at].astype(F32) + first[j, at].astype(F32)).astype(BF16)

        across[j] = remote(
            sending.at[j - 1], second.at[j - 1], send.at[j + 3], recv.at[j + 3], chips[j]
        )
        across[j].start()
    for j in (3, 1, 2):
        across[j].wait()


def collected(held, first, second, at):
    return (held[0, at].astype(F32) + first[0, at].astype(F32)) + (
        second[0, at].astype(F32) + second[1, at].astype(F32) + second[2, at].astype(F32)
    )


def row_loop(rows, body):
    step = 16

    @pl.loop(0, rows // step)
    def _(i):
        body(pl.ds(pl.multiple_of(i * step, step), step))


def unit_and_scale(x):
    scale = lax.rsqrt(jnp.mean(x * x, axis=-1, keepdims=True) + EPS)
    return x * scale, scale


def first_kernel(hidden, gain, out, own, send, recv, local):
    def norm(at):
        unit, _ = unit_and_scale(hidden[at].astype(F32))
        own[at] = (unit * gain[...]).astype(BF16)

    row_loop(hidden.shape[0], norm)
    _, _, _, chips, sibling = places()
    greet(chips, sibling)
    spread(own, out, (send, recv, local.at[0]))


def middle_kernel(
    partial, hidden, gain, mid, out, own, held, first, second, sending, s1, r1, l1, s2, r2, l2
):
    _, _, _, chips, sibling = places()
    greet(chips, sibling)
    collect(partial, held, first, second, sending, (s1, r1, l1))

    def norm(at):
        x = hidden[at].astype(F32) + collected(held, first, second, at)
        mid[at] = x
        unit, _ = unit_and_scale(x)
        own[at] = (unit * gain[...]).astype(BF16)

    row_loop(hidden.shape[0], norm)
    spread(own, out, (s2, r2, l2.at[0]))


def norm_back(grad, x, gain, gain_grad):
    unit, scale = unit_and_scale(x)
    gain_grad[...] += jnp.sum((grad * unit).reshape(-1, 8, grad.shape[-1]), axis=0)
    e = grad * gain
    return scale * (e - unit * jnp.mean(e * unit, axis=-1, keepdims=True))


def turn_kernel(
    partial, mid, cot, gain, grad_mid, gain_grad, out,
    own, held, first, second, sending, s1, r1, l1, s2, r2, l2,
):
    _, _, _, chips, sibling = places()
    greet(chips, sibling)
    collect(partial, held, first, second, sending, (s1, r1, l1))
    gain_grad[...] = jnp.zeros_like(gain_grad)

    def back(at):
        grad = collected(held, first, second, at)
        g = cot[at].astype(F32) + norm_back(grad, mid[at], gain[...], gain_grad)
        grad_mid[at] = g
        own[at] = g.astype(BF16)

    row_loop(mid.shape[0], back)
    spread(own, out, (s2, r2, l2.at[0]))


def last_kernel(
    partial, hidden, grad_mid, gain, grad_in, gain_grad, held, first, second, sending, s1, r1, l1
):
    _, _, _, chips, sibling = places()
    greet(chips, sibling)
    collect(partial, held, first, second, sending, (s1, r1, l1))
    gain_grad[...] = jnp.zeros_like(gain_grad)

    def back(at):
        grad = collected(held, first, second, at)
        grad_in[at] = grad_mid[at] + norm_back(
            grad, hidden[at].astype(F32), gain[...], gain_grad
        )

    row_loop(hidden.shape[0], back)


VMEM_SPEC = pl.BlockSpec(memory_space=pltpu.VMEM)
ANY_SPEC = pl.BlockSpec(memory_space=pl.ANY)


def comm_call(kernel, collective_id, operands, in_specs, outs, out_specs, scratch, nbytes):
    return pl.pallas_call(
        kernel,
        out_shape=outs,
        in_specs=in_specs,
        out_specs=out_specs,
        scratch_shapes=scratch,
        compiler_params=pltpu.CompilerParams(
            collective_id=collective_id, has_side_effects=True, vmem_limit_bytes=32 << 20
        ),
        cost_estimate=pl.CostEstimate(flops=nbytes * 20, bytes_accessed=nbytes, transcendentals=0),
        name=kernel.__name__,
    )(*operands)


def spread_scratch():
    return [
        pltpu.SemaphoreType.DMA((8,)),
        pltpu.SemaphoreType.DMA((8,)),
        pltpu.SemaphoreType.DMA((1,)),
    ]


def collect_buffers(rows, width):
    return [
        pltpu.VMEM((4, rows, width), BF16),
        pltpu.VMEM((4, rows, width), BF16),
        pltpu.VMEM((3, rows, width), BF16),
        pltpu.VMEM((3, rows, width), BF16),
    ]


def collect_sems():
    return [
        pltpu.SemaphoreType.DMA((8,)),
        pltpu.SemaphoreType.DMA((8,)),
        pltpu.SemaphoreType.DMA((4,)),
    ]


def head_unit(x):
    scale = lax.rsqrt(jnp.mean(x * x, axis=-1, keepdims=True) + EPS)
    return x * scale, scale


def rot(a, cos, sin):
    return a * cos + pltpu.roll(a, a.shape[-1] // 2, 1) * sin


def rot_back(b, cos, sin):
    return b * cos - pltpu.roll(b, b.shape[-1] // 2, 1) * sin


def allowed_keys(seg_col, seg_row):
    length = seg_col.shape[0]
    row = lax.broadcasted_iota(jnp.int32, (length, length), 0)
    col = lax.broadcasted_iota(jnp.int32, (length, length), 1)
    return (seg_col == seg_row) & (row >= col)


def soft_of(scores):
    peak = jnp.max(scores, axis=-1, keepdims=True)
    lse = peak + jnp.log(jnp.sum(jnp.exp(scores - peak), axis=-1, keepdims=True))
    return jnp.exp(scores - lse)


def attend_kernel(groups, qkv, seg_col, seg_row, cos_ref, sin_ref, gain_q, gain_k, out):
    d = gain_q.shape[-1]
    cos, sin = cos_ref[0], sin_ref[0]
    allowed = allowed_keys(seg_col[0], seg_row[0])
    unit_k, _ = head_unit(qkv[0, :, groups * d : (groups + 1) * d].astype(F32))
    key = rot(unit_k * gain_k[...], cos, sin).astype(BF16)
    value = qkv[0, :, (groups + 1) * d : (groups + 2) * d]
    for g in range(groups):
        unit_q, _ = head_unit(qkv[0, :, g * d : (g + 1) * d].astype(F32))
        query = rot(unit_q * gain_q[...], cos, sin).astype(BF16)
        scores = jnp.where(allowed, dot_cols(query, key) * d**-0.5, -jnp.inf)
        soft = soft_of(scores).astype(BF16)
        out[0, :, g * d : (g + 1) * d] = dot(soft, value).astype(BF16)


def attend_back_kernel(
    groups, qkv, att, datt, seg_col, seg_row, cos_ref, sin_ref, gain_q, gain_k, grad, gains
):
    d = gain_q.shape[-1]
    cos, sin = cos_ref[0], sin_ref[0]
    scale = d**-0.5
    allowed = allowed_keys(seg_col[0], seg_row[0])
    unit_k, scale_k = head_unit(qkv[0, :, groups * d : (groups + 1) * d].astype(F32))
    key = rot(unit_k * gain_k[...], cos, sin).astype(BF16)
    value = qkv[0, :, (groups + 1) * d : (groups + 2) * d]
    key_grad = jnp.zeros(unit_k.shape, F32)
    value_grad = jnp.zeros(unit_k.shape, F32)
    gq = jnp.zeros((8, d), F32)

    def through_norm(b, unit, scale_, gain):
        e = b * gain
        return scale_ * (e - unit * jnp.mean(e * unit, axis=-1, keepdims=True))

    for g in range(groups):
        at = slice(g * d, (g + 1) * d)
        unit_q, scale_q = head_unit(qkv[0, :, at].astype(F32))
        query = rot(unit_q * gain_q[...], cos, sin).astype(BF16)
        scores = jnp.where(allowed, dot_cols(query, key) * scale, -jnp.inf)
        soft = soft_of(scores)
        up = datt[0, :, at]
        delta = jnp.sum(up.astype(F32) * att[0, :, at].astype(F32), axis=-1, keepdims=True)
        ds = (soft * (dot_cols(up, value) - delta) * scale).astype(BF16)
        value_grad += dot_rows(soft.astype(BF16), up)
        key_grad += dot_rows(ds, query)
        b = rot_back(dot(ds, key), cos, sin)
        gq += jnp.sum((b * unit_q).reshape(-1, 8, d), axis=0)
        grad[0, :, at] = through_norm(b, unit_q, scale_q, gain_q[...]).astype(BF16)
    b = rot_back(key_grad, cos, sin)
    gk = jnp.sum((b * unit_k).reshape(-1, 8, d), axis=0)
    grad[0, :, groups * d : (groups + 1) * d] = through_norm(b, unit_k, scale_k, gain_k[...]).astype(BF16)
    grad[0, :, (groups + 1) * d : (groups + 2) * d] = value_grad.astype(BF16)
    gains[0, 0] = gq
    gains[0, 1] = gk


def per_sequence(*shape):
    return pl.BlockSpec((1, *shape), lambda s: (s,) + (0,) * len(shape))


def attention_specs(length, d):
    return [
        per_sequence(length, 1),
        per_sequence(1, length),
        per_sequence(length, d),
        per_sequence(length, d),
        pl.BlockSpec((1, d), lambda s: (0, 0)),
        pl.BlockSpec((1, d), lambda s: (0, 0)),
    ]


def attend(groups, qkv, common):
    n, length, width = qkv.shape
    d = width // (groups + 2)
    return pl.pallas_call(
        functools.partial(attend_kernel, groups),
        grid=(n,),
        out_shape=jax.ShapeDtypeStruct((n, length, groups * d), BF16),
        in_specs=[per_sequence(length, width), *attention_specs(length, d)],
        out_specs=per_sequence(length, groups * d),
        compiler_params=pltpu.CompilerParams(vmem_limit_bytes=40 << 20),
        cost_estimate=pl.CostEstimate(
            flops=n * groups * length * length * (4 * d + 20),
            bytes_accessed=n * length * width * 4,
            transcendentals=n * groups * length * length * 2,
        ),
        name="attend",
    )(qkv, *common)


def attend_back(groups, qkv, att, datt, common):
    n, length, width = qkv.shape
    d = width // (groups + 2)
    return pl.pallas_call(
        functools.partial(attend_back_kernel, groups),
        grid=(n,),
        out_shape=(
            jax.ShapeDtypeStruct((n, length, width), BF16),
            jax.ShapeDtypeStruct((n, 2, 8, d), F32),
        ),
        in_specs=[
            per_sequence(length, width),
            per_sequence(length, groups * d),
            per_sequence(length, groups * d),
            *attention_specs(length, d),
        ],
        out_specs=(per_sequence(length, width), per_sequence(2, 8, d)),
        compiler_params=pltpu.CompilerParams(vmem_limit_bytes=40 << 20),
        cost_estimate=pl.CostEstimate(
            flops=n * groups * length * length * (10 * d + 30),
            bytes_accessed=n * length * width * 8,
            transcendentals=n * groups * length * length * 2,
        ),
        name="attend_back",
    )(qkv, att, datt, *common)


def build(mesh):
    n = mesh.size
    n_f = mesh.shape["fsdp"]
    spread_bits = [b for b in (1 << i for i in range(n_f.bit_length() - 2, -1, -1)) if b != PAIR]
    all_bits = sorted([*spread_bits, PAIR], reverse=True)

    def swap(v, bit):
        return lax.ppermute(v, AXES, [(i, i ^ bit) for i in range(n)])

    def bit_of(f, b):
        return (f // b) % 2

    def in_order(bit, own, other, axis):
        low = jnp.where(bit == 0, own, other)
        high = jnp.where(bit == 0, other, own)
        return jnp.stack([low, high], axis=axis)

    def pick(v, index, axis):
        return lax.dynamic_index_in_dim(v, index, axis, keepdims=False)

    def gather(v, f):
        have = [PAIR]
        for b in spread_bits:
            have = sorted([*have, b], reverse=True)
            v = in_order(bit_of(f, b), v, swap(v, b * 4), have.index(b))
        return v.reshape(n_f, *v.shape[len(have) :])

    def halves(f, b, width):
        return [n_f // (2 * b), 2, b * width]

    def scatter(keep, got, f, width):
        v = keep + got.astype(F32)
        have = [b for b in all_bits if b != 1]
        v = v.reshape(*([2] * len(have)), width, v.shape[-1])
        for b in [b for b in reversed(spread_bits) if b != 1]:
            axis = have.index(b)
            bit = bit_of(f, b)
            v = pick(v, bit, axis) + swap(pick(v, 1 - bit, axis).astype(BF16), b * 4).astype(F32)
            have.remove(b)
        return v

    def body(
        hidden_in,
        cotangent,
        segments,
        w_query,
        key_projection_weight,
        value_projection_weight,
        w_out,
        w_gate,
        w_up,
        w_down,
        gain_attn,
        gain_mlp,
        gain_query,
        key_norm_gain,
    ):
        rows, width = hidden_in.shape
        d = gain_query.shape[0]
        length = segments.shape[0]
        f, c = lax.axis_index("fsdp"), lax.axis_index("ctx")
        pair = bit_of(f, PAIR)
        at_rows = w_query.shape[0]
        ff_rows = w_gate.shape[0]
        ff_cols = w_gate.shape[1] // 2
        q_cols, kv_cols = w_query.shape[1] // 4, key_projection_weight.shape[1] // 4
        groups = q_cols // kv_cols

        def chunks4(w):
            return jnp.moveaxis(w.reshape(at_rows, 4, w.shape[1] // 4), 1, 0)

        def attn_weights(chunks):
            cols = chunks.shape[-1]
            chunks = chunks.reshape(2, 2, at_rows, cols)
            mine = pick(pick(chunks, c, 0), pair, 0)
            by_ctx = swap(pick(pick(chunks, 1 - c, 0), pair, 0), CTX_BIT)
            by_pair = swap(pick(pick(chunks, c, 0), 1 - pair, 0), PAIR_BIT)
            by_both = swap(pick(pick(chunks, 1 - c, 0), 1 - pair, 0), CTX_BIT | PAIR_BIT)
            near = in_order(c, mine, by_ctx, 0)
            far = in_order(c, by_pair, by_both, 0)
            both = in_order(pair, near, far, 0)
            return gather(both.reshape(2, 2 * at_rows, cols), f).reshape(-1, cols)

        full_qkv = attn_weights(
            jnp.concatenate(
                [chunks4(w_query), chunks4(key_projection_weight), chunks4(value_projection_weight)], axis=2
            )
        )
        full_out = attn_weights(chunks4(w_out.T))

        def ff_weights(w):
            w = w.reshape(ff_rows, 2, ff_cols)
            other = swap(pick(w, 1 - pair, 1), PAIR_BIT)
            return gather(in_order(pair, pick(w, pair, 1), other, 0), f).reshape(-1, ff_cols)

        full_gate = ff_weights(w_gate)
        full_up = ff_weights(w_up)
        full_down = ff_weights(w_down.T)

        seg = in_order(pair, segments, swap(segments, PAIR_BIT), 0)
        before = jnp.sum((seg[:, None, :] < seg[:, :, None]).astype(jnp.int32), axis=-1)
        positions = jnp.arange(length, dtype=jnp.int32)[None] - before
        freqs = THETA ** (-2.0 * jnp.arange(d // 2, dtype=F32) / d)
        angles = positions.astype(F32)[..., None] * freqs
        cos, sin = jnp.cos(angles), jnp.sin(angles)
        common = (
            seg[:, :, None],
            seg[:, None, :],
            jnp.concatenate([cos, cos], axis=-1),
            jnp.concatenate([-sin, sin], axis=-1),
            gain_query[None],
            key_norm_gain[None],
        )

        all_rows = jax.ShapeDtypeStruct((8, rows, width), BF16)
        own_rows = jax.ShapeDtypeStruct((rows, width), F32)
        gain_rows = jax.ShapeDtypeStruct((8, width), F32)
        block = pltpu.VMEM((rows, width), BF16)
        nbytes = rows * width * 16

        normed_one = comm_call(
            first_kernel, 0, (hidden_in, gain_attn[None]), [VMEM_SPEC] * 2,
            all_rows, ANY_SPEC, [block, *spread_scratch()], nbytes,
        ).reshape(8 * rows, width)
        qkv = dot(normed_one, full_qkv).astype(BF16)
        qkv3 = qkv.reshape(2, length, qkv.shape[1])
        attended3 = attend(groups, qkv3, common)
        attended = attended3.reshape(8 * rows, q_cols)
        out_part = dot_cols(attended, full_out).astype(BF16).reshape(8, rows, width)
        residual_mid, normed_two = comm_call(
            middle_kernel, 1, (out_part, hidden_in, gain_mlp[None]),
            [ANY_SPEC, VMEM_SPEC, VMEM_SPEC], (own_rows, all_rows), (VMEM_SPEC, ANY_SPEC),
            [block, *collect_buffers(rows, width), *collect_sems(), *spread_scratch()], 2 * nbytes,
        )
        normed_two = normed_two.reshape(8 * rows, width)

        teams = sorted(
            sorted(i ^ b ^ p for b in range(4) for p in (0, PAIR_BIT))
            for i in range(0, n, 4)
            if not i & PAIR_BIT
        )
        grad_rows = lax.all_gather(cotangent, AXES, axis_index_groups=teams, tiled=True)

        gate_pre = dot(normed_two, full_gate)
        up_pre = dot(normed_two, full_up)
        gate_sig = jax.nn.sigmoid(gate_pre)
        gate_act = gate_pre * gate_sig
        mixed = (gate_act * up_pre).astype(BF16)
        grad_mixed = dot(grad_rows, full_down)
        grad_gate = (grad_mixed * up_pre * gate_sig * (1.0 + gate_pre * (1.0 - gate_sig))).astype(BF16)
        grad_up = (grad_mixed * gate_act).astype(BF16)
        norm_two_part = (dot_cols(grad_gate, full_gate) + dot_cols(grad_up, full_up)).astype(BF16)
        grad_mid, gain_mlp_part, grad_mid_rows = comm_call(
            turn_kernel, 2, (norm_two_part.reshape(8, rows, width), residual_mid, cotangent, gain_mlp[None]),
            [ANY_SPEC, VMEM_SPEC, VMEM_SPEC, VMEM_SPEC], (own_rows, gain_rows, all_rows),
            (VMEM_SPEC, VMEM_SPEC, ANY_SPEC),
            [block, *collect_buffers(rows, width), *collect_sems(), *spread_scratch()], 2 * nbytes,
        )
        grad_mid_rows = grad_mid_rows.reshape(8 * rows, width)

        down_part = dot_cols(mixed, full_down).astype(BF16)
        hidden_out = residual_mid + lax.psum_scatter(
            down_part, AXES, scatter_dimension=0, axis_index_groups=teams, tiled=True
        ).astype(F32)

        low = bit_of(f, 1)

        def weight_grad(acts, grads):
            split = acts.reshape(acts.shape[0], n_f // 2, 2, width // n_f)
            mine = pick(split, low, 2).reshape(acts.shape[0], -1)
            theirs = pick(split, 1 - low, 2).reshape(acts.shape[0], -1)
            got = swap(dot_rows(theirs, grads).astype(BF16), 4)
            return scatter(dot_rows(mine, grads), got, f, width // n_f)

        def ff_grad(acts, grads):
            v = weight_grad(acts, grads)
            other = swap(pick(v, 1 - pair, 0).astype(BF16), PAIR_BIT).astype(F32)
            return in_order(pair, pick(v, pair, 0), other, 1).reshape(ff_rows, 2 * ff_cols)

        grad_w_gate = ff_grad(normed_two, grad_gate)
        grad_w_up = ff_grad(normed_two, grad_up)
        grad_w_down = ff_grad(grad_rows, mixed).T

        def attn_grad(acts, grads):
            v = weight_grad(acts, grads)
            v = v.reshape(2, 2, at_rows, v.shape[-1])
            mine = pick(pick(v, pair, 0), c, 0)
            by_ctx = swap(pick(pick(v, pair, 0), 1 - c, 0).astype(BF16), CTX_BIT).astype(F32)
            by_pair = swap(pick(pick(v, 1 - pair, 0), c, 0).astype(BF16), PAIR_BIT).astype(F32)
            by_both = swap(pick(pick(v, 1 - pair, 0), 1 - c, 0).astype(BF16), CTX_BIT | PAIR_BIT).astype(F32)
            near = in_order(pair, mine, by_pair, 1)
            far = in_order(pair, by_ctx, by_both, 1)
            return in_order(c, near, far, 1)

        grad_w_out = attn_grad(grad_mid_rows, attended).reshape(at_rows, 4 * q_cols).T

        datt = dot(grad_mid_rows, full_out).astype(BF16).reshape(attended3.shape)
        grad_qkv, head_gains = attend_back(groups, qkv3, attended3, datt, common)
        grad_qkv = grad_qkv.reshape(8 * rows, -1)
        norm_one_part = dot_cols(grad_qkv, full_qkv).astype(BF16)
        grad_input, gain_attn_part = comm_call(
            last_kernel, 3, (norm_one_part.reshape(8, rows, width), hidden_in, grad_mid, gain_attn[None]),
            [ANY_SPEC, VMEM_SPEC, VMEM_SPEC, VMEM_SPEC], (own_rows, gain_rows), (VMEM_SPEC, VMEM_SPEC),
            [*collect_buffers(rows, width), *collect_sems()], nbytes,
        )
        grad_qkv_w = attn_grad(normed_one, grad_qkv)
        grad_w_query = grad_qkv_w[..., :q_cols].reshape(at_rows, -1)
        grad_w_key = grad_qkv_w[..., q_cols : q_cols + kv_cols].reshape(at_rows, -1)
        grad_w_value = grad_qkv_w[..., q_cols + kv_cols :].reshape(at_rows, -1)

        head_gains = jnp.sum(head_gains, axis=(0, 2))
        gains = jnp.concatenate(
            [jnp.sum(gain_attn_part, axis=0), jnp.sum(gain_mlp_part, axis=0), head_gains[0], head_gains[1]]
        ).reshape(-1, d)
        for i in range(n.bit_length() - 1):
            gains = gains + swap(gains, 1 << i)
        gains = gains.reshape(-1)
        return (
            hidden_out,
            grad_input,
            grad_w_query,
            grad_w_key,
            grad_w_value,
            grad_w_out,
            grad_w_gate,
            grad_w_up,
            grad_w_down,
            gains[:width],
            gains[width : 2 * width],
            gains[2 * width : 2 * width + d],
            gains[2 * width + d :],
        )

    return body


def solution(mesh):
    everyone = P(("fsdp", "ctx", "tp"), None)
    attn = P(("fsdp", "ctx"), "tp")
    attn_out = P("tp", ("fsdp", "ctx"))
    ff_in = P("fsdp", ("ctx", "tp"))
    ff_out = P(("ctx", "tp"), "fsdp")
    same = P()
    return jax.shard_map(
        build(mesh),
        mesh=mesh,
        in_specs=(
            everyone, everyone, P("fsdp"), attn, attn, attn, attn_out, ff_in, ff_in, ff_out,
            same, same, same, same,
        ),
        out_specs=(
            everyone, everyone, attn, attn, attn, attn_out, ff_in, ff_in, ff_out,
            same, same, same, same,
        ),
        check_vma=False,
    )
```

```python
import functools

import jax
import jax.numpy as jnp
from jax import lax
from jax.experimental import pallas as pl
from jax.experimental.pallas import tpu as pltpu
from jax.sharding import PartitionSpec as P

EPS = 1e-06
THETA = 1000000.0
AXES = ("fsdp", "ctx", "tp")
MESH = pl.DeviceIdType.MESH
BF16 = jnp.bfloat16
F32 = jnp.float32
TP_BIT, CTX_BIT = 1, 2
PAIR = 2
PAIR_BIT = PAIR * 4


def dot_rows(left, right):
    return lax.dot_general(left, right, (((0,), (0,)), ((), ())), preferred_element_type=F32)


def dot_cols(left, right):
    return lax.dot_general(left, right, (((1,), (1,)), ((), ())), preferred_element_type=F32)


def dot(left, right):
    return lax.dot_general(left, right, (((1,), (0,)), ((), ())), preferred_element_type=F32)


def remote(src, dst, send, recv, device):
    return pltpu.make_async_remote_copy(
        src_ref=src, dst_ref=dst, send_sem=send, recv_sem=recv, device_id=device, device_id_type=MESH
    )


class Moves:
    def __init__(self, send, recv, local):
        self.send, self.recv, self.local = send, recv, local
        self.sent, self.loads = 0, 0
        self.open = []

    def swap(self, src, there, here, device):
        k = self.sent
        self.sent += 1
        copy = remote(src, there, self.send.at[k], self.recv.at[k], device)
        copy.start()
        self.open.append(copy.wait_send)
        return remote(src, here, self.send.at[k], self.recv.at[k], device).wait_recv

    def load(self, src, dst):
        k = self.loads
        self.loads += 1
        copy = pltpu.make_async_copy(src, dst, self.local.at[k])
        copy.start()
        return copy.wait

    def store(self, src, dst):
        self.open.append(self.load(src, dst))

    def close(self):
        for wait in self.open:
            wait()


class Place:
    def __init__(self, bits):
        self.bits = bits
        f, c, t = lax.axis_index("fsdp"), lax.axis_index("ctx"), lax.axis_index("tp")
        self.f, self.c, self.t = f, c, t
        self.pair = (f // PAIR) % 2
        far_f = self.block(PAIR)
        fs, cs = [f, f, far_f, far_f], [c, 1 - c, c, 1 - c]
        pairs = [self.pair, self.pair, 1 - self.pair, 1 - self.pair]
        self.at = [(fs[j], cs[j], pairs[j]) for j in range(4)]
        self.rows_of = [pairs[j] * 4 + cs[j] * 2 for j in range(4)]
        self.chunk_of = [cs[j] * 2 + pairs[j] for j in range(4)]
        self.chips = [None, {"ctx": 1 - c}, {"fsdp": far_f}, {"fsdp": far_f, "ctx": 1 - c}]
        self.sibling = {"tp": 1 - t}

    def block(self, mask):
        out = self.f
        for i in range(mask.bit_length()):
            b = 1 << i
            if mask & b:
                out = out + b - 2 * b * ((self.f // b) % 2)
        return out

    def along(self, bit):
        return {"fsdp": self.block(bit)}

    def greet(self):
        barrier = pltpu.get_barrier_semaphore()
        devices = [*self.chips[1:], self.sibling, *[self.along(b) for b in self.bits]]
        for device in devices:
            pl.semaphore_signal(barrier, inc=1, device_id=device, device_id_type=MESH)
        pl.semaphore_wait(barrier, len(devices))


class Spread:
    def __init__(self, moves, place, own, out):
        self.moves, self.place, self.out = moves, place, out
        self.rows = own.shape[0]
        mine = self.at(0, place.t)
        self.here = moves.load(own, mine)
        self.pair = moves.swap(own, mine, self.at(2, place.t), place.chips[2])
        self.ctx = moves.swap(own, mine, self.at(1, place.t), place.chips[1])
        self.beside = [moves.swap(own, mine, self.at(0, 1 - place.t), place.sibling)]

    def at(self, j, t):
        start = (self.place.rows_of[j] + t) * self.rows
        return self.out.at[pl.ds(pl.multiple_of(start, self.rows), self.rows)]

    def hand(self, j):
        block = self.at(j, self.place.t)
        self.beside.append(
            self.moves.swap(block, block, self.at(j, 1 - self.place.t), self.place.sibling)
        )

    def from_pair(self):
        self.pair()
        block = self.at(2, self.place.t)
        self.both = self.moves.swap(block, block, self.at(3, self.place.t), self.place.chips[1])
        self.hand(2)

    def from_ctx(self):
        self.ctx()
        self.hand(1)

    def from_both(self):
        self.both()
        self.hand(3)

    def finish(self):
        self.here()
        for wait in self.beside:
            wait()


class Collect:
    def __init__(self, moves, place, part, held, first, ctx_in, pair_in, sending, load):
        self.moves, self.place = moves, place
        self.first, self.ctx_in, self.pair_in, self.sending = first, ctx_in, pair_in, sending
        t = place.t
        self.hands, self.loads = {}, {}
        for j in (3, 1, 2, 0):
            self.hands[j] = moves.swap(part(j, 1 - t), first.at[j], first.at[j], place.sibling)
            if load:
                self.loads[j] = moves.load(part(j, t), held.at[j])
        self.held = (lambda j: held.at[j]) if load else (lambda j: part(j, t))

    def two(self, j, at):
        return self.held(j)[at].astype(F32) + self.first[j, at].astype(F32)

    def ready(self, j):
        self.hands[j]()
        if j in self.loads:
            self.loads[j]()

    def to_ctx(self):
        self.waits = {}
        for j, slot in ((3, 0), (1, 1)):
            self.ready(j)

            def body(at):
                self.sending[slot, at] = self.two(j, at).astype(BF16)

            row_loop(self.sending.shape[1], body)
            self.waits[j] = self.moves.swap(
                self.sending.at[slot], self.ctx_in.at[slot], self.ctx_in.at[slot], self.place.chips[1]
            )

    def to_pair(self):
        self.ready(2)
        self.waits[3]()

        def body(at):
            self.sending[2, at] = (self.two(2, at) + self.ctx_in[0, at].astype(F32)).astype(BF16)

        row_loop(self.sending.shape[1], body)
        self.waits[2] = self.moves.swap(self.sending.at[2], self.pair_in, self.pair_in, self.place.chips[2])

    def finish(self):
        self.ready(0)
        self.waits[1]()
        self.waits[2]()

    def total(self, at):
        return self.two(0, at) + (self.ctx_in[1, at].astype(F32) + self.pair_in[at].astype(F32))


def collect_buffers(rows, width):
    return [
        pltpu.VMEM((4, rows, width), BF16),
        pltpu.VMEM((2, rows, width), BF16),
        pltpu.VMEM((rows, width), BF16),
        pltpu.VMEM((3, rows, width), BF16),
    ]


def row_loop(rows, body):
    step = 16

    @pl.loop(0, rows // step)
    def _(i):
        body(pl.ds(pl.multiple_of(i * step, step), step))


def unit_and_scale(x):
    scale = lax.rsqrt(jnp.mean(x * x, axis=-1, keepdims=True) + EPS)
    return x * scale, scale


class Gather:
    def __init__(self, moves, place, block):
        self.moves, self.place, self.block = moves, place, block
        self.waits = {}

    def forward(self, mask, src=None):
        done = [i for i, b in enumerate(self.place.bits) if mask & b]
        here = self.block(self.place.block(mask))
        for b in self.place.bits[max(done, default=-1) + 1 :]:
            self.waits[mask | b] = self.moves.swap(
                here if src is None else src, here, self.block(self.place.block(mask | b)), self.place.along(b)
            )

    def masks(self, stage):
        out = [0, PAIR]
        for b in self.place.bits[:stage]:
            out += [m | b for m in out]
        return [m | self.place.bits[stage] for m in out]

    def middle(self):
        for stage in range(len(self.place.bits) - 1):
            for m in self.masks(stage):
                self.waits.pop(m)()
                self.forward(m)

    def finish(self):
        for wait in self.waits.values():
            wait()


def head_unit(x):
    scale = lax.rsqrt(jnp.mean(x * x, axis=-1, keepdims=True) + EPS)
    return x * scale, scale


def rot(a, cos, sin):
    return a * cos + pltpu.roll(a, a.shape[-1] // 2, 1) * sin


def rot_back(b, cos, sin):
    return b * cos - pltpu.roll(b, b.shape[-1] // 2, 1) * sin


def allowed_keys(seg_col, seg_row):
    length = seg_col.shape[0]
    row = lax.broadcasted_iota(jnp.int32, (length, length), 0)
    col = lax.broadcasted_iota(jnp.int32, (length, length), 1)
    return (seg_col == seg_row) & (row >= col)


def soft_of(scores):
    peak = jnp.max(scores, axis=-1, keepdims=True)
    lse = peak + jnp.log(jnp.sum(jnp.exp(scores - peak), axis=-1, keepdims=True))
    return jnp.exp(scores - lse)


def attend_one(groups, s, qkv, seg_col, seg_row, cos_ref, sin_ref, gain_q, gain_k, out):
    d = gain_q.shape[-1]
    length = cos_ref.shape[1]
    rows = pl.ds(pl.multiple_of(s * length, length), length)
    cos, sin = cos_ref[s], sin_ref[s]
    allowed = allowed_keys(seg_col[s], seg_row[s])
    unit_k, _ = head_unit(qkv[rows, groups * d : (groups + 1) * d].astype(F32))
    key = rot(unit_k * gain_k[...], cos, sin).astype(BF16)
    value = qkv[rows, (groups + 1) * d : (groups + 2) * d]
    for g in range(groups):
        unit_q, _ = head_unit(qkv[rows, g * d : (g + 1) * d].astype(F32))
        query = rot(unit_q * gain_q[...], cos, sin).astype(BF16)
        scores = jnp.where(allowed, dot_cols(query, key) * d**-0.5, -jnp.inf)
        soft = soft_of(scores).astype(BF16)
        out[rows, g * d : (g + 1) * d] = dot(soft, value).astype(BF16)


def attend_back_kernel(
    groups, qkv, att, datt, seg_col, seg_row, cos_ref, sin_ref, gain_q, gain_k, grad, gains
):
    d = gain_q.shape[-1]
    cos, sin = cos_ref[0], sin_ref[0]
    scale = d**-0.5
    allowed = allowed_keys(seg_col[0], seg_row[0])
    unit_k, scale_k = head_unit(qkv[0, :, groups * d : (groups + 1) * d].astype(F32))
    key = rot(unit_k * gain_k[...], cos, sin).astype(BF16)
    value = qkv[0, :, (groups + 1) * d : (groups + 2) * d]
    key_grad = jnp.zeros(unit_k.shape, F32)
    value_grad = jnp.zeros(unit_k.shape, F32)
    gq = jnp.zeros((8, d), F32)

    def through_norm(b, unit, scale_, gain):
        e = b * gain
        return scale_ * (e - unit * jnp.mean(e * unit, axis=-1, keepdims=True))

    for g in range(groups):
        at = slice(g * d, (g + 1) * d)
        unit_q, scale_q = head_unit(qkv[0, :, at].astype(F32))
        query = rot(unit_q * gain_q[...], cos, sin).astype(BF16)
        scores = jnp.where(allowed, dot_cols(query, key) * scale, -jnp.inf)
        soft = soft_of(scores)
        up = datt[0, :, at]
        delta = jnp.sum(up.astype(F32) * att[0, :, at].astype(F32), axis=-1, keepdims=True)
        ds = (soft * (dot_cols(up, value) - delta) * scale).astype(BF16)
        value_grad += dot_rows(soft.astype(BF16), up)
        key_grad += dot_rows(ds, query)
        b = rot_back(dot(ds, key), cos, sin)
        gq += jnp.sum((b * unit_q).reshape(-1, 8, d), axis=0)
        grad[0, :, at] = through_norm(b, unit_q, scale_q, gain_q[...]).astype(BF16)
    b = rot_back(key_grad, cos, sin)
    gk = jnp.sum((b * unit_k).reshape(-1, 8, d), axis=0)
    grad[0, :, groups * d : (groups + 1) * d] = through_norm(b, unit_k, scale_k, gain_k[...]).astype(BF16)
    grad[0, :, (groups + 1) * d : (groups + 2) * d] = value_grad.astype(BF16)
    gains[0, 0] = gq
    gains[0, 1] = gk


def per_sequence(*shape):
    return pl.BlockSpec((1, *shape), lambda s: (s,) + (0,) * len(shape))


def attention_specs(length, d):
    return [
        per_sequence(length, 1),
        per_sequence(1, length),
        per_sequence(length, d),
        per_sequence(length, d),
        pl.BlockSpec((1, d), lambda s: (0, 0)),
        pl.BlockSpec((1, d), lambda s: (0, 0)),
    ]


def attend_back(groups, qkv, att, datt, common):
    n, length, width = qkv.shape
    d = width // (groups + 2)
    return pl.pallas_call(
        functools.partial(attend_back_kernel, groups),
        grid=(n,),
        out_shape=(
            jax.ShapeDtypeStruct((n, length, width), BF16),
            jax.ShapeDtypeStruct((n, 2, 8, d), F32),
        ),
        in_specs=[
            per_sequence(length, width),
            per_sequence(length, groups * d),
            per_sequence(length, groups * d),
            *attention_specs(length, d),
        ],
        out_specs=(per_sequence(length, width), per_sequence(2, 8, d)),
        compiler_params=pltpu.CompilerParams(vmem_limit_bytes=40 << 20),
        cost_estimate=pl.CostEstimate(
            flops=n * groups * length * length * (10 * d + 30),
            bytes_accessed=n * length * width * 8,
            transcendentals=n * groups * length * length * 2,
        ),
        name="attend_back",
    )(qkv, att, datt, *common)


def forward_kernel(
    bits, groups, natural,
    hidden, cot, gain_attn, gain_mlp, seg_col, seg_row, cos, sin, gain_q, gain_k, wq, wk, wv, wo, wg, wu, wd,
    mid, normed_one, normed_two, cot_rows, qkv_out, att_out, qkv_weight, out_weight, gate_weight, up_weight, down_weight,
    own_one, own_two, rows_one, w_qkv, w_out, qkv, att, part, first, ctx_in, pair_in, sending, send, recv, local,
):
    place = Place(bits)
    moves = Moves(send, recv, local)
    rows, width = hidden.shape
    at_rows, ff_rows, ff_cols = wq.shape[0], wg.shape[0], wg.shape[1] // 2
    q_cols, kv_cols = wq.shape[1] // 4, wk.shape[1] // 4

    def lanes(start, size):
        return pl.ds(pl.multiple_of(start, size), size)

    def qkv_rows(f, c=None):
        if c is None:
            return lanes(f * 2 * at_rows, 2 * at_rows)
        return lanes((f * 2 + c) * at_rows, at_rows)

    place.greet()

    def out_block(f, c=None):
        return w_out.at[:, qkv_rows(f, c)] if natural else w_out.at[qkv_rows(f, c)]

    def out_chunk(j):
        at = lanes(place.chunk_of[j] * q_cols, q_cols)
        return wo.at[at] if natural else wo.at[:, at]

    pieces = (
        (wq, q_cols, pl.ds(0, q_cols)),
        (wk, kv_cols, pl.ds(q_cols, kv_cols)),
        (wv, kv_cols, pl.ds(q_cols + kv_cols, kv_cols)),
    )
    f0, c0, _ = place.at[0]
    qkv_in, out_in = {}, {}
    for j in (3, 2, 1):
        fj, cj, _ = place.at[j]
        qkv_in[j] = [
            moves.swap(
                w.at[:, lanes(place.chunk_of[j] * size, size)],
                w_qkv.at[qkv_rows(f0, c0), to],
                w_qkv.at[qkv_rows(fj, cj), to],
                place.chips[j],
            )
            for w, size, to in pieces
        ]
    qkv_in[0] = [
        moves.load(w.at[:, lanes(place.chunk_of[0] * size, size)], w_qkv.at[qkv_rows(f0, c0), to])
        for w, size, to in pieces
    ]
    for j in (3, 2, 1):
        fj, cj, _ = place.at[j]
        out_in[j] = moves.swap(out_chunk(j), out_block(f0, c0), out_block(fj, cj), place.chips[j])
    out_in[0] = moves.load(out_chunk(0), out_block(f0, c0))

    def rows_block(w):
        return lambda f: w.at[lanes(f * ff_rows, ff_rows)]

    def cols_block(w):
        return lambda f: w.at[:, lanes(f * ff_rows, ff_rows)]

    mine, theirs = lanes(place.pair * ff_cols, ff_cols), lanes((1 - place.pair) * ff_cols, ff_cols)
    feed = [
        (Gather(moves, place, rows_block(gate_weight)), wg.at[:, mine], wg.at[:, theirs]),
        (Gather(moves, place, rows_block(up_weight)), wu.at[:, mine], wu.at[:, theirs]),
        (Gather(moves, place, cols_block(down_weight)), wd.at[mine], wd.at[theirs])
        if natural
        else (Gather(moves, place, rows_block(down_weight)), wd.at[:, mine], wd.at[:, theirs]),
    ]

    def swap_pair(i):
        gather, own, other = feed[i]
        gather.waits[PAIR] = moves.swap(
            other, gather.block(place.f), gather.block(place.block(PAIR)), place.along(PAIR)
        )
        moves.store(own, gather.block(place.f))

    def norm_one(at):
        unit, _ = unit_and_scale(hidden[at].astype(F32))
        own_one[at] = (unit * gain_attn[...]).astype(BF16)

    row_loop(rows, norm_one)
    spread_one = Spread(moves, place, own_one, rows_one)

    qkv_gather = Gather(moves, place, lambda f: w_qkv.at[qkv_rows(f)])
    out_gather = Gather(moves, place, out_block)
    for gather, arrivals in ((qkv_gather, qkv_in), (out_gather, {j: [w] for j, w in out_in.items()})):
        for wait in (*arrivals[0], *arrivals[1]):
            wait()
        gather.forward(0)
        for wait in (*arrivals[2], *arrivals[3]):
            wait()
        gather.forward(PAIR)
    swap_pair(0)
    spread_one.from_pair()
    spread_one.from_ctx()
    qkv_gather.middle()
    out_gather.middle()
    feed[0][0].forward(0, feed[0][1])
    feed[0][0].waits.pop(PAIR)()
    feed[0][0].forward(PAIR)
    swap_pair(1)
    spread_one.from_both()
    spread_one.finish()
    qkv_gather.finish()

    moves.store(rows_one, normed_one)
    moves.store(w_qkv, qkv_weight)
    step = 2 * rows

    @pl.loop(0, 8 * rows // step)
    def _(i):
        at = lanes(i * step, step)
        qkv[at] = dot(rows_one[at], w_qkv[...]).astype(BF16)

    moves.store(qkv, qkv_out)
    spread_cot = Spread(moves, place, cot, cot_rows)
    swap_pair(2)

    def pump(i):
        feed[i][0].middle()
        if i + 1 < len(feed):
            gather, own, _ = feed[i + 1]
            gather.forward(0, own)
            gather.waits.pop(PAIR)()
            gather.forward(PAIR)

    @pl.loop(0, cos.shape[0])
    def _(s):
        attend_one(groups, s, qkv, seg_col, seg_row, cos, sin, gain_q, gain_k, att)

    moves.store(att, att_out)
    spread_cot.from_pair()
    out_gather.finish()
    moves.store(w_out, out_weight)

    @pl.loop(0, 8)
    def _(i):
        part[i] = (dot if natural else dot_cols)(att[lanes(i * rows, rows)], w_out[...]).astype(BF16)

    collect = Collect(
        moves, place, lambda j, t: part.at[place.rows_of[j] + t], None, first, ctx_in, pair_in, sending, False
    )
    collect.to_ctx()
    spread_cot.from_ctx()
    pump(0)
    collect.to_pair()
    spread_cot.from_both()
    collect.finish()

    def norm_two(at):
        x = hidden[at].astype(F32) + collect.total(at)
        mid[at] = x
        unit, _ = unit_and_scale(x)
        own_two[at] = (unit * gain_mlp[...]).astype(BF16)

    row_loop(rows, norm_two)
    spread_two = Spread(moves, place, own_two, normed_two)
    spread_two.from_pair()
    pump(1)
    spread_two.from_ctx()
    spread_two.from_both()
    spread_two.finish()
    spread_cot.finish()
    pump(2)
    for gather, _, _ in feed:
        gather.finish()
    moves.close()


def norm_back(grad, x, gain, gain_grad):
    unit, scale = unit_and_scale(x)
    gain_grad[...] += jnp.sum((grad * unit).reshape(-1, 8, grad.shape[-1]), axis=0)
    e = grad * gain
    return scale * (e - unit * jnp.mean(e * unit, axis=-1, keepdims=True))


def turn_kernel(
    bits, partial, mid, cot, gain, grad_mid, gain_grad, out,
    own, held, first, ctx_in, pair_in, sending, send, recv, local,
):
    place = Place(bits)
    moves = Moves(send, recv, local)
    place.greet()
    collect = Collect(
        moves, place, lambda j, t: partial.at[place.rows_of[j] + t], held, first, ctx_in, pair_in, sending, True
    )
    collect.to_ctx()
    collect.to_pair()
    collect.finish()
    gain_grad[...] = jnp.zeros_like(gain_grad)

    def back(at):
        g = cot[at].astype(F32) + norm_back(collect.total(at), mid[at], gain[...], gain_grad)
        grad_mid[at] = g
        own[at] = g.astype(BF16)

    row_loop(mid.shape[0], back)
    spread = Spread(moves, place, own, out)
    spread.from_pair()
    spread.from_ctx()
    spread.from_both()
    spread.finish()
    moves.close()


def last_kernel(
    bits, partial, hidden, grad_mid, gain, grad_in, gain_grad,
    held, first, ctx_in, pair_in, sending, send, recv, local,
):
    place = Place(bits)
    moves = Moves(send, recv, local)
    place.greet()
    collect = Collect(
        moves, place, lambda j, t: partial.at[place.rows_of[j] + t], held, first, ctx_in, pair_in, sending, True
    )
    collect.to_ctx()
    collect.to_pair()
    collect.finish()
    gain_grad[...] = jnp.zeros_like(gain_grad)

    def back(at):
        grad_in[at] = grad_mid[at] + norm_back(
            collect.total(at), hidden[at].astype(F32), gain[...], gain_grad
        )

    row_loop(hidden.shape[0], back)
    moves.close()


VMEM_SPEC = pl.BlockSpec(memory_space=pltpu.VMEM)
ANY_SPEC = pl.BlockSpec(memory_space=pl.ANY)


def comm_call(kernel, bits, collective_id, operands, in_specs, outs, out_specs, scratch, nbytes, copies, *more):
    return pl.pallas_call(
        functools.partial(kernel, bits, *more),
        out_shape=outs,
        in_specs=in_specs,
        out_specs=out_specs,
        scratch_shapes=[
            *scratch,
            pltpu.SemaphoreType.DMA((copies,)),
            pltpu.SemaphoreType.DMA((copies,)),
            pltpu.SemaphoreType.DMA((40,)),
        ],
        compiler_params=pltpu.CompilerParams(
            collective_id=collective_id, has_side_effects=True, vmem_limit_bytes=56 << 20
        ),
        cost_estimate=pl.CostEstimate(flops=nbytes * 20, bytes_accessed=nbytes, transcendentals=0),
        name=kernel.__name__,
    )(*operands)


def build(mesh):
    n = mesh.size
    n_f = mesh.shape["fsdp"]
    spread_bits = [b for b in (1 << i for i in range(n_f.bit_length() - 2, -1, -1)) if b != PAIR]
    all_bits = sorted([*spread_bits, PAIR], reverse=True)

    def swap(v, bit):
        return lax.ppermute(v, AXES, [(i, i ^ bit) for i in range(n)])

    def bit_of(f, b):
        return (f // b) % 2

    def in_order(bit, own, other, axis):
        low = jnp.where(bit == 0, own, other)
        high = jnp.where(bit == 0, other, own)
        return jnp.stack([low, high], axis=axis)

    def pick(v, index, axis):
        return lax.dynamic_index_in_dim(v, index, axis, keepdims=False)

    def scatter(keep, got, f, width):
        v = keep + got.astype(F32)
        have = [b for b in all_bits if b != 1]
        v = v.reshape(*([2] * len(have)), width, v.shape[-1])
        for b in [b for b in reversed(spread_bits) if b != 1]:
            axis = have.index(b)
            bit = bit_of(f, b)
            v = pick(v, bit, axis) + swap(pick(v, 1 - bit, axis).astype(BF16), b * 4).astype(F32)
            have.remove(b)
        return v

    def body(
        hidden_in,
        cotangent,
        segments,
        w_query,
        key_projection_weight,
        value_projection_weight,
        w_out,
        w_gate,
        w_up,
        w_down,
        gain_attn,
        gain_mlp,
        gain_query,
        key_norm_gain,
    ):
        rows, width = hidden_in.shape
        d = gain_query.shape[0]
        length = segments.shape[0]
        f, c = lax.axis_index("fsdp"), lax.axis_index("ctx")
        pair = bit_of(f, PAIR)
        at_rows = w_query.shape[0]
        ff_rows = w_gate.shape[0]
        ff_cols = w_gate.shape[1] // 2
        q_cols, kv_cols = w_query.shape[1] // 4, key_projection_weight.shape[1] // 4
        groups = q_cols // kv_cols

        seg = in_order(pair, segments, swap(segments, PAIR_BIT), 0)
        before = jnp.sum((seg[:, None, :] < seg[:, :, None]).astype(jnp.int32), axis=-1)
        positions = jnp.arange(length, dtype=jnp.int32)[None] - before
        freqs = THETA ** (-2.0 * jnp.arange(d // 2, dtype=F32) / d)
        angles = positions.astype(F32)[..., None] * freqs
        cos, sin = jnp.cos(angles), jnp.sin(angles)
        common = (
            seg[:, :, None],
            seg[:, None, :],
            jnp.concatenate([cos, cos], axis=-1),
            jnp.concatenate([-sin, sin], axis=-1),
            gain_query[None],
            key_norm_gain[None],
        )

        n_rows = 8 * rows
        all_rows = jax.ShapeDtypeStruct((n_rows, width), BF16)
        own_rows = jax.ShapeDtypeStruct((rows, width), F32)
        gain_rows = jax.ShapeDtypeStruct((8, width), F32)
        block = pltpu.VMEM((rows, width), BF16)
        nbytes = rows * width * 16
        qkv_cols = q_cols + 2 * kv_cols

        def shape(*dims):
            return jax.ShapeDtypeStruct(dims, BF16)

        copies = 120 + 10 * n_f
        natural = at_rows % 128 == 0 and ff_rows % 128 == 0
        out_dims = (q_cols, width) if natural else (width, q_cols)
        down_dims = (ff_cols, width) if natural else (width, ff_cols)
        times, times_t = (dot, dot_cols) if natural else (dot_cols, dot)
        (
            residual_mid, normed_one, normed_two, grad_rows, qkv, attended, full_qkv, full_out,
            full_gate, full_up, full_down,
        ) = comm_call(
            forward_kernel, spread_bits, 0,
            (hidden_in, cotangent, gain_attn[None], gain_mlp[None], *common, w_query, key_projection_weight,
             value_projection_weight, w_out if natural else w_out.T, w_gate, w_up, w_down if natural else w_down.T),
            [VMEM_SPEC] * 10 + [ANY_SPEC] * 7,
            (own_rows, all_rows, all_rows, all_rows, shape(n_rows, qkv_cols), shape(n_rows, q_cols),
             shape(width, qkv_cols), shape(*out_dims), shape(width, ff_cols), shape(width, ff_cols),
             shape(*down_dims)),
            (VMEM_SPEC, *[ANY_SPEC] * 10),
            [block, block, pltpu.VMEM((n_rows, width), BF16), pltpu.VMEM((width, qkv_cols), BF16),
             pltpu.VMEM(out_dims, BF16), pltpu.VMEM((n_rows, qkv_cols), BF16),
             pltpu.VMEM((n_rows, q_cols), BF16), pltpu.VMEM((8, rows, width), BF16),
             *collect_buffers(rows, width)],
            16 * nbytes, copies, groups, natural,
        )
        qkv3 = qkv.reshape(2, length, qkv_cols)
        attended3 = attended.reshape(2, length, q_cols)
        teams = sorted(
            sorted(i ^ b ^ p for b in range(4) for p in (0, PAIR_BIT))
            for i in range(0, n, 4)
            if not i & PAIR_BIT
        )

        gate_pre = dot(normed_two, full_gate)
        up_pre = dot(normed_two, full_up)
        gate_sig = jax.nn.sigmoid(gate_pre)
        gate_act = gate_pre * gate_sig
        mixed = (gate_act * up_pre).astype(BF16)
        grad_mixed = times_t(grad_rows, full_down)
        grad_gate = (grad_mixed * up_pre * gate_sig * (1.0 + gate_pre * (1.0 - gate_sig))).astype(BF16)
        grad_up = (grad_mixed * gate_act).astype(BF16)
        norm_two_part = (dot_cols(grad_gate, full_gate) + dot_cols(grad_up, full_up)).astype(BF16)
        grad_mid, gain_mlp_part, grad_mid_rows = comm_call(
            turn_kernel, spread_bits, 2, (norm_two_part.reshape(8, rows, width), residual_mid, cotangent, gain_mlp[None]),
            [ANY_SPEC, VMEM_SPEC, VMEM_SPEC, VMEM_SPEC], (own_rows, gain_rows, all_rows),
            (VMEM_SPEC, VMEM_SPEC, ANY_SPEC),
            [block, pltpu.VMEM((4, rows, width), BF16), *collect_buffers(rows, width)], 2 * nbytes, 40,
        )

        down_part = times(mixed, full_down).astype(BF16)
        hidden_out = residual_mid + lax.psum_scatter(
            down_part, AXES, scatter_dimension=0, axis_index_groups=teams, tiled=True
        ).astype(F32)

        low = bit_of(f, 1)

        def weight_grad(acts, grads):
            split = acts.reshape(acts.shape[0], n_f // 2, 2, width // n_f)
            mine = pick(split, low, 2).reshape(acts.shape[0], -1)
            theirs = pick(split, 1 - low, 2).reshape(acts.shape[0], -1)
            got = swap(dot_rows(theirs, grads).astype(BF16), 4)
            return scatter(dot_rows(mine, grads), got, f, width // n_f)

        def ff_grad(acts, grads):
            v = weight_grad(acts, grads)
            other = swap(pick(v, 1 - pair, 0).astype(BF16), PAIR_BIT).astype(F32)
            return in_order(pair, pick(v, pair, 0), other, 1).reshape(ff_rows, 2 * ff_cols)

        grad_w_gate = ff_grad(normed_two, grad_gate)
        grad_w_up = ff_grad(normed_two, grad_up)
        grad_w_down = ff_grad(grad_rows, mixed).T

        def attn_grad(acts, grads):
            v = weight_grad(acts, grads)
            v = v.reshape(2, 2, at_rows, v.shape[-1])
            mine = pick(pick(v, pair, 0), c, 0)
            by_ctx = swap(pick(pick(v, pair, 0), 1 - c, 0).astype(BF16), CTX_BIT).astype(F32)
            by_pair = swap(pick(pick(v, 1 - pair, 0), c, 0).astype(BF16), PAIR_BIT).astype(F32)
            by_both = swap(pick(pick(v, 1 - pair, 0), 1 - c, 0).astype(BF16), CTX_BIT | PAIR_BIT).astype(F32)
            near = in_order(pair, mine, by_pair, 1)
            far = in_order(pair, by_ctx, by_both, 1)
            return in_order(c, near, far, 1)

        grad_w_out = attn_grad(grad_mid_rows, attended).reshape(at_rows, 4 * q_cols).T

        datt = times_t(grad_mid_rows, full_out).astype(BF16).reshape(attended3.shape)
        grad_qkv, head_gains = attend_back(groups, qkv3, attended3, datt, common)
        grad_qkv = grad_qkv.reshape(8 * rows, -1)
        norm_one_part = dot_cols(grad_qkv, full_qkv).astype(BF16)
        grad_input, gain_attn_part = comm_call(
            last_kernel, spread_bits, 3, (norm_one_part.reshape(8, rows, width), hidden_in, grad_mid, gain_attn[None]),
            [ANY_SPEC, VMEM_SPEC, VMEM_SPEC, VMEM_SPEC], (own_rows, gain_rows), (VMEM_SPEC, VMEM_SPEC),
            [pltpu.VMEM((4, rows, width), BF16), *collect_buffers(rows, width)], nbytes, 40,
        )
        grad_qkv_w = attn_grad(normed_one, grad_qkv)
        grad_w_query = grad_qkv_w[..., :q_cols].reshape(at_rows, -1)
        grad_w_key = grad_qkv_w[..., q_cols : q_cols + kv_cols].reshape(at_rows, -1)
        grad_w_value = grad_qkv_w[..., q_cols + kv_cols :].reshape(at_rows, -1)

        head_gains = jnp.sum(head_gains, axis=(0, 2))
        gains = jnp.concatenate(
            [jnp.sum(gain_attn_part, axis=0), jnp.sum(gain_mlp_part, axis=0), head_gains[0], head_gains[1]]
        ).reshape(-1, d)
        for i in range(n.bit_length() - 1):
            gains = gains + swap(gains, 1 << i)
        gains = gains.reshape(-1)
        return (
            hidden_out,
            grad_input,
            grad_w_query,
            grad_w_key,
            grad_w_value,
            grad_w_out,
            grad_w_gate,
            grad_w_up,
            grad_w_down,
            gains[:width],
            gains[width : 2 * width],
            gains[2 * width : 2 * width + d],
            gains[2 * width + d :],
        )

    return body


def solution(mesh):
    everyone = P(("fsdp", "ctx", "tp"), None)
    attn = P(("fsdp", "ctx"), "tp")
    attn_out = P("tp", ("fsdp", "ctx"))
    ff_in = P("fsdp", ("ctx", "tp"))
    ff_out = P(("ctx", "tp"), "fsdp")
    same = P()
    return jax.shard_map(
        build(mesh),
        mesh=mesh,
        in_specs=(
            everyone, everyone, P("fsdp"), attn, attn, attn, attn_out, ff_in, ff_in, ff_out,
            same, same, same, same,
        ),
        out_specs=(
            everyone, everyone, attn, attn, attn, attn_out, ff_in, ff_in, ff_out,
            same, same, same, same,
        ),
        check_vma=False,
    )
```

```python
import functools

import jax
import jax.numpy as jnp
from jax import lax
from jax.experimental import pallas as pl
from jax.experimental.pallas import tpu as pltpu
from jax.sharding import PartitionSpec as P

EPS = 1e-06
THETA = 1000000.0
AXES = ("fsdp", "ctx", "tp")
MESH = pl.DeviceIdType.MESH
BF16 = jnp.bfloat16
F32 = jnp.float32
TP_BIT, CTX_BIT = 1, 2
PAIR = 2
PAIR_BIT = PAIR * 4


def dot_rows(left, right):
    return lax.dot_general(left, right, (((0,), (0,)), ((), ())), preferred_element_type=F32)


def dot_cols(left, right):
    return lax.dot_general(left, right, (((1,), (1,)), ((), ())), preferred_element_type=F32)


def dot(left, right):
    return lax.dot_general(left, right, (((1,), (0,)), ((), ())), preferred_element_type=F32)


def remote(src, dst, send, recv, device):
    return pltpu.make_async_remote_copy(
        src_ref=src, dst_ref=dst, send_sem=send, recv_sem=recv, device_id=device, device_id_type=MESH
    )


class Moves:
    def __init__(self, send, recv, local):
        self.send, self.recv, self.local = send, recv, local
        self.sent, self.loads = 0, 0
        self.open = []

    def swap(self, src, there, here, device, open_=None):
        k = self.sent
        self.sent += 1
        copy = remote(src, there, self.send.at[k], self.recv.at[k], device)
        copy.start()
        (self.open if open_ is None else open_).append(copy.wait_send)
        return remote(src, here, self.send.at[k], self.recv.at[k], device).wait_recv

    def load(self, src, dst):
        k = self.loads
        self.loads += 1
        copy = pltpu.make_async_copy(src, dst, self.local.at[k])
        copy.start()
        return copy.wait

    def store(self, src, dst):
        self.open.append(self.load(src, dst))

    def close(self):
        for wait in self.open:
            wait()


class Place:
    def __init__(self, bits):
        self.bits = bits
        f, c, t = lax.axis_index("fsdp"), lax.axis_index("ctx"), lax.axis_index("tp")
        self.f, self.c, self.t = f, c, t
        self.pair = (f // PAIR) % 2
        far_f = self.block(PAIR)
        fs, cs = [f, f, far_f, far_f], [c, 1 - c, c, 1 - c]
        pairs = [self.pair, self.pair, 1 - self.pair, 1 - self.pair]
        self.at = [(fs[j], cs[j], pairs[j]) for j in range(4)]
        self.rows_of = [pairs[j] * 4 + cs[j] * 2 for j in range(4)]
        self.chunk_of = [cs[j] * 2 + pairs[j] for j in range(4)]
        self.chips = [None, {"ctx": 1 - c}, {"fsdp": far_f}, {"fsdp": far_f, "ctx": 1 - c}]
        self.sibling = {"tp": 1 - t}

    def block(self, mask):
        out = self.f
        for i in range(mask.bit_length()):
            b = 1 << i
            if mask & b:
                out = out + b - 2 * b * ((self.f // b) % 2)
        return out

    def along(self, bit):
        return {"fsdp": self.block(bit)}

    def greet(self):
        barrier = pltpu.get_barrier_semaphore()
        devices = [*self.chips[1:], self.sibling, *[self.along(b) for b in self.bits]]
        for device in devices:
            pl.semaphore_signal(barrier, inc=1, device_id=device, device_id_type=MESH)
        pl.semaphore_wait(barrier, len(devices))


class Spread:
    def __init__(self, moves, place, own, out):
        self.moves, self.place, self.out = moves, place, out
        self.rows = own.shape[0]
        mine = self.at(0, place.t)
        self.here = moves.load(own, mine)
        self.pair = moves.swap(own, mine, self.at(2, place.t), place.chips[2])
        self.ctx = moves.swap(own, mine, self.at(1, place.t), place.chips[1])
        self.beside = [moves.swap(own, mine, self.at(0, 1 - place.t), place.sibling)]

    def at(self, j, t):
        start = (self.place.rows_of[j] + t) * self.rows
        return self.out.at[pl.ds(pl.multiple_of(start, self.rows), self.rows)]

    def hand(self, j):
        block = self.at(j, self.place.t)
        self.beside.append(
            self.moves.swap(block, block, self.at(j, 1 - self.place.t), self.place.sibling)
        )

    def from_pair(self):
        self.pair()
        block = self.at(2, self.place.t)
        self.both = self.moves.swap(block, block, self.at(3, self.place.t), self.place.chips[1])
        self.hand(2)

    def from_ctx(self):
        self.ctx()
        self.hand(1)

    def from_both(self):
        self.both()
        self.hand(3)

    def finish(self):
        self.here()
        for wait in self.beside:
            wait()


class Collect:
    def __init__(self, moves, place, part, held, first, ctx_in, pair_in, sending, load):
        self.moves, self.place = moves, place
        self.first, self.ctx_in, self.pair_in, self.sending = first, ctx_in, pair_in, sending
        t = place.t
        self.hands, self.loads, self.open = {}, {}, []
        for j in (3, 1, 2, 0):
            self.hands[j] = moves.swap(part(j, 1 - t), first.at[j], first.at[j], place.sibling, self.open)
            if load:
                self.loads[j] = moves.load(part(j, t), held.at[j])
        self.held = (lambda j: held.at[j]) if load else (lambda j: part(j, t))

    def two(self, j, at):
        return self.held(j)[at].astype(F32) + self.first[j, at].astype(F32)

    def ready(self, j):
        self.hands[j]()
        if j in self.loads:
            self.loads[j]()

    def to_ctx(self):
        self.waits = {}
        for j, slot in ((3, 0), (1, 1)):
            self.ready(j)

            def body(at):
                self.sending[slot, at] = self.two(j, at).astype(BF16)

            row_loop(self.sending.shape[1], body)
            self.waits[j] = self.moves.swap(
                self.sending.at[slot], self.ctx_in.at[slot], self.ctx_in.at[slot], self.place.chips[1], self.open
            )

    def to_pair(self):
        self.ready(2)
        self.waits[3]()

        def body(at):
            self.sending[2, at] = (self.two(2, at) + self.ctx_in[0, at].astype(F32)).astype(BF16)

        row_loop(self.sending.shape[1], body)
        self.waits[2] = self.moves.swap(
            self.sending.at[2], self.pair_in, self.pair_in, self.place.chips[2], self.open
        )

    def finish(self):
        self.ready(0)
        self.waits[1]()
        self.waits[2]()
        for wait in self.open:
            wait()

    def total(self, at):
        return self.two(0, at) + (self.ctx_in[1, at].astype(F32) + self.pair_in[at].astype(F32))


def collect_buffers(rows, width):
    return [
        pltpu.VMEM((4, rows, width), BF16),
        pltpu.VMEM((2, rows, width), BF16),
        pltpu.VMEM((rows, width), BF16),
        pltpu.VMEM((3, rows, width), BF16),
    ]


def row_loop(rows, body):
    step = 16

    @pl.loop(0, rows // step)
    def _(i):
        body(pl.ds(pl.multiple_of(i * step, step), step))


def unit_and_scale(x):
    scale = lax.rsqrt(jnp.mean(x * x, axis=-1, keepdims=True) + EPS)
    return x * scale, scale


class Gather:
    def __init__(self, moves, place, block):
        self.moves, self.place, self.block = moves, place, block
        self.waits = {}

    def forward(self, mask, src=None):
        done = [i for i, b in enumerate(self.place.bits) if mask & b]
        here = self.block(self.place.block(mask))
        for b in self.place.bits[max(done, default=-1) + 1 :]:
            self.waits[mask | b] = self.moves.swap(
                here if src is None else src, here, self.block(self.place.block(mask | b)), self.place.along(b)
            )

    def masks(self, stage):
        out = [0, PAIR]
        for b in self.place.bits[:stage]:
            out += [m | b for m in out]
        return [m | self.place.bits[stage] for m in out]

    def middle(self):
        for stage in range(len(self.place.bits) - 1):
            for m in self.masks(stage):
                self.waits.pop(m)()
                self.forward(m)

    def finish(self):
        for wait in self.waits.values():
            wait()


def head_unit(x):
    scale = lax.rsqrt(jnp.mean(x * x, axis=-1, keepdims=True) + EPS)
    return x * scale, scale


def rot(a, cos, sin):
    return a * cos + pltpu.roll(a, a.shape[-1] // 2, 1) * sin


def rot_back(b, cos, sin):
    return b * cos - pltpu.roll(b, b.shape[-1] // 2, 1) * sin


def allowed_keys(seg_col, seg_row):
    length = seg_col.shape[0]
    row = lax.broadcasted_iota(jnp.int32, (length, length), 0)
    col = lax.broadcasted_iota(jnp.int32, (length, length), 1)
    return (seg_col == seg_row) & (row >= col)


def soft_of(scores):
    peak = jnp.max(scores, axis=-1, keepdims=True)
    lse = peak + jnp.log(jnp.sum(jnp.exp(scores - peak), axis=-1, keepdims=True))
    return jnp.exp(scores - lse)


def attend_one(groups, s, qkv, seg_col, seg_row, cos_ref, sin_ref, gain_q, gain_k, out):
    d = gain_q.shape[-1]
    length = cos_ref.shape[1]
    rows = pl.ds(pl.multiple_of(s * length, length), length)
    cos, sin = cos_ref[s], sin_ref[s]
    allowed = allowed_keys(seg_col[s], seg_row[s])
    unit_k, _ = head_unit(qkv[rows, groups * d : (groups + 1) * d].astype(F32))
    key = rot(unit_k * gain_k[...], cos, sin).astype(BF16)
    value = qkv[rows, (groups + 1) * d : (groups + 2) * d]
    for g in range(groups):
        unit_q, _ = head_unit(qkv[rows, g * d : (g + 1) * d].astype(F32))
        query = rot(unit_q * gain_q[...], cos, sin).astype(BF16)
        scores = jnp.where(allowed, dot_cols(query, key) * d**-0.5, -jnp.inf)
        soft = soft_of(scores).astype(BF16)
        out[rows, g * d : (g + 1) * d] = dot(soft, value).astype(BF16)


def through_norm(b, unit, scale, gain):
    e = b * gain
    return scale * (e - unit * jnp.mean(e * unit, axis=-1, keepdims=True))


def attend_back_one(
    groups, s, qkv, att, datt, seg_col, seg_row, cos_ref, sin_ref, gain_q, gain_k, grad, gains
):
    d = gain_q.shape[-1]
    length = cos_ref.shape[1]
    rows = pl.ds(pl.multiple_of(s * length, length), length)
    cos, sin = cos_ref[s], sin_ref[s]
    scale = d**-0.5
    allowed = allowed_keys(seg_col[s], seg_row[s])
    at_k, at_v = slice(groups * d, (groups + 1) * d), slice((groups + 1) * d, (groups + 2) * d)
    unit_k, scale_k = head_unit(qkv[rows, at_k].astype(F32))
    key = rot(unit_k * gain_k[...], cos, sin).astype(BF16)
    value = qkv[rows, at_v]
    key_grad = jnp.zeros(unit_k.shape, F32)
    value_grad = jnp.zeros(unit_k.shape, F32)
    for g in range(groups):
        at = slice(g * d, (g + 1) * d)
        unit_q, scale_q = head_unit(qkv[rows, at].astype(F32))
        query = rot(unit_q * gain_q[...], cos, sin).astype(BF16)
        scores = jnp.where(allowed, dot_cols(query, key) * scale, -jnp.inf)
        soft = soft_of(scores)
        up = datt[rows, at]
        delta = jnp.sum(up.astype(F32) * att[rows, at].astype(F32), axis=-1, keepdims=True)
        ds = (soft * (dot_cols(up, value) - delta) * scale).astype(BF16)
        value_grad += dot_rows(soft.astype(BF16), up)
        key_grad += dot_rows(ds, query)
        b = rot_back(dot(ds, key), cos, sin)
        gains[0] += jnp.sum((b * unit_q).reshape(-1, 8, d), axis=0)
        grad[rows, at] = through_norm(b, unit_q, scale_q, gain_q[...]).astype(BF16)
    b = rot_back(key_grad, cos, sin)
    gains[1] += jnp.sum((b * unit_k).reshape(-1, 8, d), axis=0)
    grad[rows, at_k] = through_norm(b, unit_k, scale_k, gain_k[...]).astype(BF16)
    grad[rows, at_v] = value_grad.astype(BF16)


def attend_back_kernel(
    groups, qkv, att, datt, seg_col, seg_row, cos, sin, gain_q, gain_k, grad, gains
):
    gains[...] = jnp.zeros_like(gains)

    @pl.loop(0, cos.shape[0])
    def _(s):
        attend_back_one(
            groups, s, qkv, att, datt, seg_col, seg_row, cos, sin, gain_q, gain_k, grad, gains
        )


def attend_back(groups, qkv, att, datt, common):
    n_rows, width = qkv.shape
    d = width // (groups + 2)
    length = n_rows // 2
    return pl.pallas_call(
        functools.partial(attend_back_kernel, groups),
        out_shape=(jax.ShapeDtypeStruct(qkv.shape, BF16), jax.ShapeDtypeStruct((2, 8, d), F32)),
        compiler_params=pltpu.CompilerParams(vmem_limit_bytes=40 << 20),
        cost_estimate=pl.CostEstimate(
            flops=n_rows * groups * length * (10 * d + 30),
            bytes_accessed=n_rows * width * 8,
            transcendentals=n_rows * groups * length * 2,
        ),
        name="attend_back",
    )(qkv, att, datt, *common)


def forward_kernel(
    bits, groups, natural,
    hidden, cot, gain_attn, gain_mlp, seg_col, seg_row, cos, sin, gain_q, gain_k, wq, wk, wv, wo, wg, wu, wd,
    mid, normed_one, normed_two, cot_rows, qkv_out, att_out, qkv_weight, out_weight, gate_weight, up_weight, down_weight,
    own_one, own_two, rows_one, w_qkv, w_out, qkv, att, part, first, ctx_in, pair_in, sending, send, recv, local,
):
    place = Place(bits)
    moves = Moves(send, recv, local)
    rows, width = hidden.shape
    at_rows, ff_rows, ff_cols = wq.shape[0], wg.shape[0], wg.shape[1] // 2
    q_cols, kv_cols = wq.shape[1] // 4, wk.shape[1] // 4

    def lanes(start, size):
        return pl.ds(pl.multiple_of(start, size), size)

    def qkv_rows(f, c=None):
        if c is None:
            return lanes(f * 2 * at_rows, 2 * at_rows)
        return lanes((f * 2 + c) * at_rows, at_rows)

    place.greet()

    def out_block(f, c=None):
        return w_out.at[:, qkv_rows(f, c)] if natural else w_out.at[qkv_rows(f, c)]

    def out_chunk(j):
        at = lanes(place.chunk_of[j] * q_cols, q_cols)
        return wo.at[at] if natural else wo.at[:, at]

    pieces = (
        (wq, q_cols, pl.ds(0, q_cols)),
        (wk, kv_cols, pl.ds(q_cols, kv_cols)),
        (wv, kv_cols, pl.ds(q_cols + kv_cols, kv_cols)),
    )
    f0, c0, _ = place.at[0]
    qkv_in, out_in = {}, {}
    for j in (3, 2, 1):
        fj, cj, _ = place.at[j]
        qkv_in[j] = [
            moves.swap(
                w.at[:, lanes(place.chunk_of[j] * size, size)],
                w_qkv.at[qkv_rows(f0, c0), to],
                w_qkv.at[qkv_rows(fj, cj), to],
                place.chips[j],
            )
            for w, size, to in pieces
        ]
    qkv_in[0] = [
        moves.load(w.at[:, lanes(place.chunk_of[0] * size, size)], w_qkv.at[qkv_rows(f0, c0), to])
        for w, size, to in pieces
    ]
    for j in (3, 2, 1):
        fj, cj, _ = place.at[j]
        out_in[j] = moves.swap(out_chunk(j), out_block(f0, c0), out_block(fj, cj), place.chips[j])
    out_in[0] = moves.load(out_chunk(0), out_block(f0, c0))

    def rows_block(w):
        return lambda f: w.at[lanes(f * ff_rows, ff_rows)]

    def cols_block(w):
        return lambda f: w.at[:, lanes(f * ff_rows, ff_rows)]

    mine, theirs = lanes(place.pair * ff_cols, ff_cols), lanes((1 - place.pair) * ff_cols, ff_cols)
    feed = [
        (Gather(moves, place, rows_block(gate_weight)), wg.at[:, mine], wg.at[:, theirs]),
        (Gather(moves, place, rows_block(up_weight)), wu.at[:, mine], wu.at[:, theirs]),
        (Gather(moves, place, cols_block(down_weight)), wd.at[mine], wd.at[theirs])
        if natural
        else (Gather(moves, place, rows_block(down_weight)), wd.at[:, mine], wd.at[:, theirs]),
    ]

    def swap_pair(i):
        gather, own, other = feed[i]
        gather.waits[PAIR] = moves.swap(
            other, gather.block(place.f), gather.block(place.block(PAIR)), place.along(PAIR)
        )
        moves.store(own, gather.block(place.f))

    def norm_one(at):
        unit, _ = unit_and_scale(hidden[at].astype(F32))
        own_one[at] = (unit * gain_attn[...]).astype(BF16)

    row_loop(rows, norm_one)
    spread_one = Spread(moves, place, own_one, rows_one)

    qkv_gather = Gather(moves, place, lambda f: w_qkv.at[qkv_rows(f)])
    out_gather = Gather(moves, place, out_block)
    for gather, arrivals in ((qkv_gather, qkv_in), (out_gather, {j: [w] for j, w in out_in.items()})):
        for wait in (*arrivals[0], *arrivals[1]):
            wait()
        gather.forward(0)
        for wait in (*arrivals[2], *arrivals[3]):
            wait()
        gather.forward(PAIR)
    swap_pair(0)
    spread_one.from_pair()
    spread_one.from_ctx()
    qkv_gather.middle()
    out_gather.middle()
    feed[0][0].forward(0, feed[0][1])
    feed[0][0].waits.pop(PAIR)()
    feed[0][0].forward(PAIR)
    swap_pair(1)
    spread_one.from_both()
    spread_one.finish()
    qkv_gather.finish()

    moves.store(rows_one, normed_one)
    moves.store(w_qkv, qkv_weight)
    step = 2 * rows

    @pl.loop(0, 8 * rows // step)
    def _(i):
        at = lanes(i * step, step)
        qkv[at] = dot(rows_one[at], w_qkv[...]).astype(BF16)

    moves.store(qkv, qkv_out)
    spread_cot = Spread(moves, place, cot, cot_rows)
    swap_pair(2)

    def pump(i):
        feed[i][0].middle()
        if i + 1 < len(feed):
            gather, own, _ = feed[i + 1]
            gather.forward(0, own)
            gather.waits.pop(PAIR)()
            gather.forward(PAIR)

    @pl.loop(0, cos.shape[0])
    def _(s):
        attend_one(groups, s, qkv, seg_col, seg_row, cos, sin, gain_q, gain_k, att)

    moves.store(att, att_out)
    spread_cot.from_pair()
    out_gather.finish()
    moves.store(w_out, out_weight)

    @pl.loop(0, 8)
    def _(i):
        part[i] = (dot if natural else dot_cols)(att[lanes(i * rows, rows)], w_out[...]).astype(BF16)

    collect = Collect(
        moves, place, lambda j, t: part.at[place.rows_of[j] + t], None, first, ctx_in, pair_in, sending, False
    )
    collect.to_ctx()
    spread_cot.from_ctx()
    pump(0)
    collect.to_pair()
    spread_cot.from_both()
    collect.finish()

    def norm_two(at):
        x = hidden[at].astype(F32) + collect.total(at)
        mid[at] = x
        unit, _ = unit_and_scale(x)
        own_two[at] = (unit * gain_mlp[...]).astype(BF16)

    row_loop(rows, norm_two)
    spread_two = Spread(moves, place, own_two, normed_two)
    spread_two.from_pair()
    pump(1)
    spread_two.from_ctx()
    spread_two.from_both()
    spread_two.finish()
    spread_cot.finish()
    pump(2)
    for gather, _, _ in feed:
        gather.finish()
    moves.close()


def norm_back(grad, x, gain, gain_grad):
    unit, scale = unit_and_scale(x)
    gain_grad[...] += jnp.sum((grad * unit).reshape(-1, 8, grad.shape[-1]), axis=0)
    e = grad * gain
    return scale * (e - unit * jnp.mean(e * unit, axis=-1, keepdims=True))


def turn_kernel(
    bits, partial, mid, cot, gain, grad_mid, gain_grad, out,
    own, held, first, ctx_in, pair_in, sending, send, recv, local,
):
    place = Place(bits)
    moves = Moves(send, recv, local)
    place.greet()
    collect = Collect(
        moves, place, lambda j, t: partial.at[place.rows_of[j] + t], held, first, ctx_in, pair_in, sending, True
    )
    collect.to_ctx()
    collect.to_pair()
    collect.finish()
    gain_grad[...] = jnp.zeros_like(gain_grad)

    def back(at):
        g = cot[at].astype(F32) + norm_back(collect.total(at), mid[at], gain[...], gain_grad)
        grad_mid[at] = g
        own[at] = g.astype(BF16)

    row_loop(mid.shape[0], back)
    spread = Spread(moves, place, own, out)
    spread.from_pair()
    spread.from_ctx()
    spread.from_both()
    spread.finish()
    moves.close()


def last_kernel(
    bits, partial, hidden, grad_mid, gain, grad_in, gain_grad,
    held, first, ctx_in, pair_in, sending, send, recv, local,
):
    place = Place(bits)
    moves = Moves(send, recv, local)
    place.greet()
    collect = Collect(
        moves, place, lambda j, t: partial.at[place.rows_of[j] + t], held, first, ctx_in, pair_in, sending, True
    )
    collect.to_ctx()
    collect.to_pair()
    collect.finish()
    gain_grad[...] = jnp.zeros_like(gain_grad)

    def back(at):
        grad_in[at] = grad_mid[at] + norm_back(
            collect.total(at), hidden[at].astype(F32), gain[...], gain_grad
        )

    row_loop(hidden.shape[0], back)
    moves.close()


class Scatter:
    def __init__(self, moves, place, product, out0, in0, out1, in1, acc):
        self.moves, self.place, self.product = moves, place, product
        self.out0, self.in0, self.out1, self.in1, self.acc = out0, in0, out1, in1, acc
        self.low, self.high = place.bits[1], place.bits[0]
        self.order = [self.high, self.high | PAIR, 0, PAIR]
        self.first, self.second = {}, {}

    def send(self, i):
        def emit(at, value):
            self.out0[(i, *at)] = value.astype(BF16)

        self.product(self.order[i] | self.low, emit)
        self.first[i] = self.moves.swap(
            self.out0.at[i], self.in0.at[i], self.in0.at[i], self.place.along(self.low)
        )

    def take(self, i):
        self.first[i]()

        def emit(at, value):
            value = value + self.in0[(i, *at)].astype(F32)
            if i < 2:
                self.out1[(i, *at)] = value.astype(BF16)
            else:
                self.acc[(i - 2, *at)] = value

        self.product(self.order[i], emit)
        if i < 2:
            self.second[i] = self.moves.swap(
                self.out1.at[i], self.in1.at[i], self.in1.at[i], self.place.along(self.high)
            )

    def take_high(self, i):
        self.second[i]()
        rows = self.acc.shape[1]
        step = 64

        @pl.loop(0, rows // step)
        def _(k):
            at = pl.ds(pl.multiple_of(k * step, step), step)
            self.acc[i, at] += self.in1[i, at].astype(F32)


class Blocks:
    def __init__(self, moves, place, slots, order):
        self.moves, self.place, self.slots, self.order = moves, place, slots, order
        self.next, self.waits = 0, {}
        self.start(0)

    def start(self, k):
        if k < len(self.order):
            ref, mask = self.order[k]
            size = self.slots.shape[2]
            at = pl.ds(pl.multiple_of(self.place.block(mask) * size, size), size)
            self.waits[k] = self.moves.load(ref.at[:, at], self.slots.at[k % 2])

    def get(self, ref, mask):
        k = self.next
        assert self.order[k][0] is ref and self.order[k][1] == mask
        self.next += 1
        self.waits.pop(k)()
        self.start(k + 1)
        return self.slots[k % 2]


def backward_kernel(
    bits, groups,
    mid, hidden, cot, gain_attn, gain_mlp, seg_col, seg_row, cos, sin, gain_q, gain_k,
    part_two, normed_one, normed_two, cot_rows, qkv_in, att_in, qkv_weight, out_weight, grad_gate, grad_up, mixed_t,
    grad_in, gains, feed_own, feed_other, down_own, down_other, qkv_own, qkv_other, out_own, out_other,
    own, rows_mid, feed, mixed, lhs, lhs_t, part, w_qkv, w_out, qkv, att, datt, dqkv,
    first, ctx_in, pair_in, sending, gain_a, gain_m, gain_h, tree, tree_in,
    f_out0, f_in0, f_out1, f_in1, f_acc, d_out0, d_in0, d_out1, d_in1, d_acc,
    q_out0, q_in0, q_out1, q_in1, q_acc, o_out0, o_in0, o_out1, o_in1, o_acc,
    send, recv, local,
):
    place = Place(bits)
    moves = Moves(send, recv, local)
    rows, width = hidden.shape
    cols = mixed.shape[0]
    tile = lhs.shape[2]
    half = tile // 2
    high, low = bits
    place.greet()

    def lanes(start, size):
        return pl.ds(pl.multiple_of(start, size), size)

    ready_feed = [
        moves.load(grad_gate, feed.at[:, pl.ds(0, cols)]),
        moves.load(grad_up, feed.at[:, pl.ds(cols, cols)]),
    ]
    collect_two = Collect(
        moves, place, lambda j, t: part_two.at[place.rows_of[j] + t], part, first, ctx_in, pair_in, sending, True
    )
    masks = [high, high | PAIR, 0, PAIR]
    sends = [m | low for m in masks]
    order = (
        [(normed_two, m) for m in [*sends, masks[0], masks[1]]]
        + [(cot_rows, m) for m in sends]
        + [(normed_one, m) for m in sends]
        + [(normed_two, m) for m in masks[2:]]
        + [(cot_rows, m) for m in masks]
        + [(normed_one, m) for m in masks]
    )
    blocks = Blocks(moves, place, lhs, order)
    ready_mixed = moves.load(mixed_t, mixed)
    ready_late = [
        moves.load(out_weight, w_out),
        moves.load(att_in, att),
        moves.load(qkv_in, qkv),
        moves.load(qkv_weight, w_qkv),
    ]

    def by_rows(source, right):
        def product(mask, emit):
            lhs_t[...] = blocks.get(source, mask).T
            step = min(512, right.shape[1])

            @pl.loop(0, right.shape[1] // step)
            def _(i):
                at = lanes(i * step, step)
                emit((slice(None), at), dot(lhs_t[...], right[:, at]))

        return product

    def down_product(mask, emit):
        block = blocks.get(cot_rows, mask)
        step = min(256, cols)

        @pl.loop(0, cols // step)
        def _(i):
            at = lanes(i * step, step)
            emit((at, slice(None)), dot(mixed[at], block))

    def out_product(mask, emit):
        at = lanes(place.block(mask) * tile, tile)
        emit((slice(None), slice(None)), dot_rows(att[...], rows_mid[:, at]))

    feed_s = Scatter(moves, place, by_rows(normed_two, feed), f_out0, f_in0, f_out1, f_in1, f_acc)
    down_s = Scatter(moves, place, down_product, d_out0, d_in0, d_out1, d_in1, d_acc)
    qkv_s = Scatter(moves, place, by_rows(normed_one, dqkv), q_out0, q_in0, q_out1, q_in1, q_acc)
    out_s = Scatter(moves, place, out_product, o_out0, o_in0, o_out1, o_in1, o_acc)

    for wait in ready_feed:
        wait()
    feed_s.send(0)
    collect_two.to_ctx()
    feed_s.send(1)
    feed_s.send(2)
    collect_two.to_pair()
    feed_s.send(3)
    feed_s.take(0)
    collect_two.finish()
    gain_m[...] = jnp.zeros_like(gain_m)
    gain_a[...] = jnp.zeros_like(gain_a)
    gain_h[...] = jnp.zeros_like(gain_h)

    def back_two(at):
        g = cot[at].astype(F32) + norm_back(collect_two.total(at), mid[at], gain_mlp[...], gain_m)
        grad_in[at] = g
        own[at] = g.astype(BF16)

    row_loop(rows, back_two)
    spread = Spread(moves, place, own, rows_mid)
    feed_s.take(1)
    spread.from_pair()
    ready_mixed()
    down_s.send(0)
    down_s.send(1)
    spread.from_ctx()
    spread.from_both()
    down_s.send(2)
    down_s.send(3)
    for wait in ready_late:
        wait()
    spread.finish()

    @pl.loop(0, 8 // 2)
    def _(i):
        at = lanes(i * 2 * rows, 2 * rows)
        datt[at] = dot_cols(rows_mid[at], w_out[...]).astype(BF16)

    @pl.loop(0, cos.shape[0])
    def _(s):
        attend_back_one(
            groups, s, qkv, att, datt, seg_col, seg_row, cos, sin, gain_q, gain_k, dqkv, gain_h
        )

    @pl.loop(0, 8)
    def _(i):
        part[i] = dot_cols(dqkv[lanes(i * rows, rows)], w_qkv[...]).astype(BF16)

    collect_one = Collect(
        moves, place, lambda j, t: part.at[place.rows_of[j] + t], None, first, ctx_in, pair_in, sending, False
    )
    for i in range(4):
        out_s.send(i)
    collect_one.to_ctx()
    for i in range(4):
        qkv_s.send(i)
    collect_one.to_pair()
    feed_s.take(2)
    feed_s.take(3)
    down_s.take(0)
    down_s.take(1)
    collect_one.finish()

    def back_one(at):
        grad_in[at] += norm_back(collect_one.total(at), hidden[at].astype(F32), gain_attn[...], gain_a)

    row_loop(rows, back_one)

    d = gain_q.shape[1]
    tree[0, :, 0:width] = jnp.sum(gain_a[...], axis=0, keepdims=True)
    tree[0, :, width : 2 * width] = jnp.sum(gain_m[...], axis=0, keepdims=True)
    tree[0, :, 2 * width : 2 * width + d] = jnp.sum(gain_h[0], axis=0, keepdims=True)
    tree[0, :, 2 * width + d : 2 * width + 2 * d] = jnp.sum(gain_h[1], axis=0, keepdims=True)
    for k, device in enumerate([place.sibling, place.chips[1], place.chips[2], *[place.along(b) for b in bits]]):
        moves.swap(tree.at[k], tree_in.at[k], tree_in.at[k], device)()
        tree[k + 1] = tree[k] + tree_in[k]
    gains[...] = tree[3 + len(bits)]

    finals = []

    def feed_final(scatter, mine, other):
        scatter.take_high(1)
        pair_out = scatter.in0.at[0]
        n, step = pair_out.shape[0], 64

        @pl.loop(0, n // step)
        def _(k):
            at = lanes(k * step, step)
            pair_out[at] = scatter.acc[1, at].astype(BF16)

        finals.append(moves.swap(pair_out, other, other, place.chips[2]))
        scatter.take_high(0)
        moves.store(scatter.acc.at[0], mine)

    def mates_final(scatter, piece, spare, mine, other):
        scatter.take_high(1)
        scatter.take_high(0)
        for j in (3, 2, 1):
            out = spare(j)
            out[...] = piece(j // 2, place.at[j][1]).astype(BF16)
            finals.append(moves.swap(out, other.at[j - 1], other.at[j - 1], place.chips[j]))
        mine[...] = piece(0, place.c)

    feed_final(feed_s, feed_own, feed_other)
    down_s.take(2)
    down_s.take(3)
    for i in range(4):
        out_s.take(i)
    for i in range(4):
        qkv_s.take(i)
    feed_final(down_s, down_own, down_other)
    mates_final(
        out_s, lambda slot, c: o_acc[slot, :, lanes(c * half, half)],
        lambda j: o_in0.at[j, :, pl.ds(0, half)], out_own, out_other,
    )
    mates_final(
        qkv_s, lambda slot, c: q_acc[slot, lanes(c * half, half)],
        lambda j: q_in0.at[j, pl.ds(0, half)], qkv_own, qkv_other,
    )
    for wait in finals:
        wait()
    moves.close()


VMEM_SPEC = pl.BlockSpec(memory_space=pltpu.VMEM)
ANY_SPEC = pl.BlockSpec(memory_space=pl.ANY)


def comm_call(kernel, bits, collective_id, operands, in_specs, outs, out_specs, scratch, nbytes, copies, *more):
    return pl.pallas_call(
        functools.partial(kernel, bits, *more),
        out_shape=outs,
        in_specs=in_specs,
        out_specs=out_specs,
        scratch_shapes=[
            *scratch,
            pltpu.SemaphoreType.DMA((copies,)),
            pltpu.SemaphoreType.DMA((copies,)),
            pltpu.SemaphoreType.DMA((80,)),
        ],
        compiler_params=pltpu.CompilerParams(
            collective_id=collective_id, has_side_effects=True, vmem_limit_bytes=61 << 20
        ),
        cost_estimate=pl.CostEstimate(flops=nbytes * 20, bytes_accessed=nbytes, transcendentals=0),
        name=kernel.__name__,
    )(*operands)


def build(mesh):
    n = mesh.size
    n_f = mesh.shape["fsdp"]
    spread_bits = [b for b in (1 << i for i in range(n_f.bit_length() - 2, -1, -1)) if b != PAIR]
    all_bits = sorted([*spread_bits, PAIR], reverse=True)

    def swap(v, bit):
        return lax.ppermute(v, AXES, [(i, i ^ bit) for i in range(n)])

    def bit_of(f, b):
        return (f // b) % 2

    def in_order(bit, own, other, axis):
        low = jnp.where(bit == 0, own, other)
        high = jnp.where(bit == 0, other, own)
        return jnp.stack([low, high], axis=axis)

    def pick(v, index, axis):
        return lax.dynamic_index_in_dim(v, index, axis, keepdims=False)

    def scatter(keep, got, f, width):
        v = keep + got.astype(F32)
        have = [b for b in all_bits if b != 1]
        v = v.reshape(*([2] * len(have)), width, v.shape[-1])
        for b in [b for b in reversed(spread_bits) if b != 1]:
            axis = have.index(b)
            bit = bit_of(f, b)
            v = pick(v, bit, axis) + swap(pick(v, 1 - bit, axis).astype(BF16), b * 4).astype(F32)
            have.remove(b)
        return v

    def body(
        hidden_in,
        cotangent,
        segments,
        w_query,
        key_projection_weight,
        value_projection_weight,
        w_out,
        w_gate,
        w_up,
        w_down,
        gain_attn,
        gain_mlp,
        gain_query,
        key_norm_gain,
    ):
        rows, width = hidden_in.shape
        d = gain_query.shape[0]
        length = segments.shape[0]
        f, c = lax.axis_index("fsdp"), lax.axis_index("ctx")
        pair = bit_of(f, PAIR)
        at_rows = w_query.shape[0]
        ff_rows = w_gate.shape[0]
        ff_cols = w_gate.shape[1] // 2
        q_cols, kv_cols = w_query.shape[1] // 4, key_projection_weight.shape[1] // 4
        groups = q_cols // kv_cols

        seg = in_order(pair, segments, swap(segments, PAIR_BIT), 0)
        before = jnp.sum((seg[:, None, :] < seg[:, :, None]).astype(jnp.int32), axis=-1)
        positions = jnp.arange(length, dtype=jnp.int32)[None] - before
        freqs = THETA ** (-2.0 * jnp.arange(d // 2, dtype=F32) / d)
        angles = positions.astype(F32)[..., None] * freqs
        cos, sin = jnp.cos(angles), jnp.sin(angles)
        common = (
            seg[:, :, None],
            seg[:, None, :],
            jnp.concatenate([cos, cos], axis=-1),
            jnp.concatenate([-sin, sin], axis=-1),
            gain_query[None],
            key_norm_gain[None],
        )

        n_rows = 8 * rows
        all_rows = jax.ShapeDtypeStruct((n_rows, width), BF16)
        own_rows = jax.ShapeDtypeStruct((rows, width), F32)
        gain_rows = jax.ShapeDtypeStruct((8, width), F32)
        block = pltpu.VMEM((rows, width), BF16)
        nbytes = rows * width * 16
        qkv_cols = q_cols + 2 * kv_cols

        def shape(*dims):
            return jax.ShapeDtypeStruct(dims, BF16)

        copies = 120 + 10 * n_f
        natural = at_rows % 128 == 0 and ff_rows % 128 == 0
        out_dims = (q_cols, width) if natural else (width, q_cols)
        down_dims = (ff_cols, width) if natural else (width, ff_cols)
        times, times_t = (dot, dot_cols) if natural else (dot_cols, dot)
        (
            residual_mid, normed_one, normed_two, grad_rows, qkv, attended, full_qkv, full_out,
            full_gate, full_up, full_down,
        ) = comm_call(
            forward_kernel, spread_bits, 0,
            (hidden_in, cotangent, gain_attn[None], gain_mlp[None], *common, w_query, key_projection_weight,
             value_projection_weight, w_out if natural else w_out.T, w_gate, w_up, w_down if natural else w_down.T),
            [VMEM_SPEC] * 10 + [ANY_SPEC] * 7,
            (own_rows, all_rows, all_rows, all_rows, shape(n_rows, qkv_cols), shape(n_rows, q_cols),
             shape(width, qkv_cols), shape(*out_dims), shape(width, ff_cols), shape(width, ff_cols),
             shape(*down_dims)),
            (VMEM_SPEC, *[ANY_SPEC] * 10),
            [block, block, pltpu.VMEM((n_rows, width), BF16), pltpu.VMEM((width, qkv_cols), BF16),
             pltpu.VMEM(out_dims, BF16), pltpu.VMEM((n_rows, qkv_cols), BF16),
             pltpu.VMEM((n_rows, q_cols), BF16), pltpu.VMEM((8, rows, width), BF16),
             *collect_buffers(rows, width)],
            16 * nbytes, copies, groups, natural,
        )
        teams = sorted(
            sorted(i ^ b ^ p for b in range(4) for p in (0, PAIR_BIT))
            for i in range(0, n, 4)
            if not i & PAIR_BIT
        )

        gate_pre = dot(normed_two, full_gate)
        up_pre = dot(normed_two, full_up)
        gate_sig = jax.nn.sigmoid(gate_pre)
        gate_act = gate_pre * gate_sig
        mixed = (gate_act * up_pre).astype(BF16)
        grad_mixed = times_t(grad_rows, full_down)
        grad_gate = (grad_mixed * up_pre * gate_sig * (1.0 + gate_pre * (1.0 - gate_sig))).astype(BF16)
        grad_up = (grad_mixed * gate_act).astype(BF16)
        norm_two_part = (dot_cols(grad_gate, full_gate) + dot_cols(grad_up, full_up)).astype(BF16)
        down_part = times(mixed, full_down).astype(BF16)
        hidden_out = residual_mid + lax.psum_scatter(
            down_part, AXES, scatter_dimension=0, axis_index_groups=teams, tiled=True
        ).astype(F32)
        backward = one_kernel if natural and len(spread_bits) == 2 else by_steps
        return hidden_out, *backward(
            hidden_in, cotangent, residual_mid, gain_attn, gain_mlp, common, norm_two_part, normed_one, normed_two,
            grad_rows, qkv, attended, full_qkv, full_out, grad_gate, grad_up, mixed, (at_rows, ff_rows),
        )

    def one_kernel(
        hidden_in, cotangent, residual_mid, gain_attn, gain_mlp, common, norm_two_part, normed_one, normed_two,
        grad_rows, qkv, attended, full_qkv, full_out, grad_gate, grad_up, mixed, sizes,
    ):
        rows, width = hidden_in.shape
        n_rows, cols = mixed.shape
        (at_rows, ff_rows), q_cols, qkv_cols = sizes, attended.shape[1], qkv.shape[1]
        d = common[-1].shape[1]
        kv_cols = (qkv_cols - q_cols) // 2
        groups = q_cols // kv_cols

        def out(dtype, *dims):
            return jax.ShapeDtypeStruct(dims, dtype)

        def v(*dims, dtype=BF16):
            return pltpu.VMEM(dims, dtype)

        def scatter(*block):
            return [v(4, *block), v(4, *block), v(2, *block), v(2, *block), v(2, *block, dtype=F32)]

        n_gain = 2 * width + 2 * d
        nbytes = n_rows * width * 20
        (
            grad_input, gains, feed_own, feed_other, down_own, down_other, qkv_own, qkv_other, out_own, out_other,
        ) = comm_call(
            backward_kernel, spread_bits, 2,
            (residual_mid, hidden_in, cotangent, gain_attn[None], gain_mlp[None], *common,
             norm_two_part.reshape(8, rows, width), normed_one, normed_two, grad_rows, qkv, attended, full_qkv,
             full_out, grad_gate, grad_up, mixed.T),
            [VMEM_SPEC] * 11 + [ANY_SPEC] * 11,
            (out(F32, rows, width), out(F32, 1, n_gain), out(F32, ff_rows, 2 * cols), out(BF16, ff_rows, 2 * cols),
             out(F32, cols, ff_rows), out(BF16, cols, ff_rows), out(F32, at_rows, qkv_cols),
             out(BF16, 3, at_rows, qkv_cols), out(F32, q_cols, at_rows), out(BF16, 3, q_cols, at_rows)),
            (VMEM_SPEC, VMEM_SPEC, ANY_SPEC, ANY_SPEC, ANY_SPEC, ANY_SPEC, VMEM_SPEC, ANY_SPEC, VMEM_SPEC, ANY_SPEC),
            [v(rows, width), v(n_rows, width), v(n_rows, 2 * cols), v(cols, n_rows), v(2, n_rows, ff_rows),
             v(ff_rows, n_rows), v(8, rows, width), v(width, qkv_cols), v(q_cols, width), v(n_rows, qkv_cols),
             v(n_rows, q_cols), v(n_rows, q_cols), v(n_rows, qkv_cols),
             *collect_buffers(rows, width), v(8, width, dtype=F32), v(8, width, dtype=F32), v(2, 8, d, dtype=F32),
             v(4 + len(spread_bits), 1, n_gain, dtype=F32), v(3 + len(spread_bits), 1, n_gain, dtype=F32),
             *scatter(ff_rows, 2 * cols), *scatter(cols, ff_rows), *scatter(ff_rows, qkv_cols),
             *scatter(q_cols, ff_rows)],
            nbytes, 80, groups,
        )
        pair = bit_of(lax.axis_index("fsdp"), PAIR)
        c = lax.axis_index("ctx")

        def feed(mine, other, axis):
            return in_order(pair, mine, other.astype(F32), axis)

        def heads(mine, other, axis):
            other = other.astype(F32)
            near = in_order(pair, mine, other[1], axis)
            far = in_order(pair, other[0], other[2], axis)
            return in_order(c, near, far, axis)

        grad_w_gate = feed(feed_own[:, :cols], feed_other[:, :cols], 1).reshape(ff_rows, 2 * cols)
        grad_w_up = feed(feed_own[:, cols:], feed_other[:, cols:], 1).reshape(ff_rows, 2 * cols)
        grad_w_down = feed(down_own, down_other, 0).reshape(2 * cols, ff_rows)
        grad_w_out = heads(out_own, out_other, 0).reshape(4 * q_cols, at_rows)

        def columns(start, size):
            at = slice(start, start + size)
            return heads(qkv_own[:, at], qkv_other[:, :, at], 1).reshape(at_rows, 4 * size)

        gains = gains[0]
        return (
            grad_input,
            columns(0, q_cols),
            columns(q_cols, kv_cols),
            columns(q_cols + kv_cols, kv_cols),
            grad_w_out,
            grad_w_gate,
            grad_w_up,
            grad_w_down,
            gains[:width],
            gains[width : 2 * width],
            gains[2 * width : 2 * width + d],
            gains[2 * width + d :],
        )

    def by_steps(
        hidden_in, cotangent, residual_mid, gain_attn, gain_mlp, common, norm_two_part, normed_one, normed_two,
        grad_rows, qkv, attended, full_qkv, full_out, grad_gate, grad_up, mixed, sizes,
    ):
        rows, width = hidden_in.shape
        (at_rows, ff_rows), ff_cols, q_cols = sizes, mixed.shape[1], attended.shape[1]
        d = common[-1].shape[1]
        kv_cols = (qkv.shape[1] - q_cols) // 2
        groups = q_cols // kv_cols
        natural = full_out.shape[0] != width
        times_t = dot_cols if natural else dot
        f, c = lax.axis_index("fsdp"), lax.axis_index("ctx")
        pair = bit_of(f, PAIR)
        all_rows = jax.ShapeDtypeStruct((8 * rows, width), BF16)
        own_rows = jax.ShapeDtypeStruct((rows, width), F32)
        gain_rows = jax.ShapeDtypeStruct((8, width), F32)
        block = pltpu.VMEM((rows, width), BF16)
        nbytes = rows * width * 16
        grad_mid, gain_mlp_part, grad_mid_rows = comm_call(
            turn_kernel, spread_bits, 2, (norm_two_part.reshape(8, rows, width), residual_mid, cotangent, gain_mlp[None]),
            [ANY_SPEC, VMEM_SPEC, VMEM_SPEC, VMEM_SPEC], (own_rows, gain_rows, all_rows),
            (VMEM_SPEC, VMEM_SPEC, ANY_SPEC),
            [block, pltpu.VMEM((4, rows, width), BF16), *collect_buffers(rows, width)], 2 * nbytes, 40,
        )

        low = bit_of(f, 1)

        def weight_grad(acts, grads):
            split = acts.reshape(acts.shape[0], n_f // 2, 2, width // n_f)
            mine = pick(split, low, 2).reshape(acts.shape[0], -1)
            theirs = pick(split, 1 - low, 2).reshape(acts.shape[0], -1)
            got = swap(dot_rows(theirs, grads).astype(BF16), 4)
            return scatter(dot_rows(mine, grads), got, f, width // n_f)

        def ff_grad(acts, grads):
            v = weight_grad(acts, grads)
            other = swap(pick(v, 1 - pair, 0).astype(BF16), PAIR_BIT).astype(F32)
            return in_order(pair, pick(v, pair, 0), other, 1).reshape(ff_rows, 2 * ff_cols)

        grad_w_gate = ff_grad(normed_two, grad_gate)
        grad_w_up = ff_grad(normed_two, grad_up)
        grad_w_down = ff_grad(grad_rows, mixed).T

        def attn_grad(acts, grads):
            v = weight_grad(acts, grads)
            v = v.reshape(2, 2, at_rows, v.shape[-1])
            mine = pick(pick(v, pair, 0), c, 0)
            by_ctx = swap(pick(pick(v, pair, 0), 1 - c, 0).astype(BF16), CTX_BIT).astype(F32)
            by_pair = swap(pick(pick(v, 1 - pair, 0), c, 0).astype(BF16), PAIR_BIT).astype(F32)
            by_both = swap(pick(pick(v, 1 - pair, 0), 1 - c, 0).astype(BF16), CTX_BIT | PAIR_BIT).astype(F32)
            near = in_order(pair, mine, by_pair, 1)
            far = in_order(pair, by_ctx, by_both, 1)
            return in_order(c, near, far, 1)

        grad_w_out = attn_grad(grad_mid_rows, attended).reshape(at_rows, 4 * q_cols).T

        datt = times_t(grad_mid_rows, full_out).astype(BF16)
        grad_qkv, head_gains = attend_back(groups, qkv, attended, datt, common)
        norm_one_part = dot_cols(grad_qkv, full_qkv).astype(BF16)
        grad_input, gain_attn_part = comm_call(
            last_kernel, spread_bits, 3, (norm_one_part.reshape(8, rows, width), hidden_in, grad_mid, gain_attn[None]),
            [ANY_SPEC, VMEM_SPEC, VMEM_SPEC, VMEM_SPEC], (own_rows, gain_rows), (VMEM_SPEC, VMEM_SPEC),
            [pltpu.VMEM((4, rows, width), BF16), *collect_buffers(rows, width)], nbytes, 40,
        )
        grad_qkv_w = attn_grad(normed_one, grad_qkv)
        grad_w_query = grad_qkv_w[..., :q_cols].reshape(at_rows, -1)
        grad_w_key = grad_qkv_w[..., q_cols : q_cols + kv_cols].reshape(at_rows, -1)
        grad_w_value = grad_qkv_w[..., q_cols + kv_cols :].reshape(at_rows, -1)

        head_gains = jnp.sum(head_gains, axis=1)
        gains = jnp.concatenate(
            [jnp.sum(gain_attn_part, axis=0), jnp.sum(gain_mlp_part, axis=0), head_gains[0], head_gains[1]]
        ).reshape(-1, d)
        for i in range(n.bit_length() - 1):
            gains = gains + swap(gains, 1 << i)
        gains = gains.reshape(-1)
        return (
            grad_input,
            grad_w_query,
            grad_w_key,
            grad_w_value,
            grad_w_out,
            grad_w_gate,
            grad_w_up,
            grad_w_down,
            gains[:width],
            gains[width : 2 * width],
            gains[2 * width : 2 * width + d],
            gains[2 * width + d :],
        )

    return body


def solution(mesh):
    everyone = P(("fsdp", "ctx", "tp"), None)
    attn = P(("fsdp", "ctx"), "tp")
    attn_out = P("tp", ("fsdp", "ctx"))
    ff_in = P("fsdp", ("ctx", "tp"))
    ff_out = P(("ctx", "tp"), "fsdp")
    same = P()
    return jax.shard_map(
        build(mesh),
        mesh=mesh,
        in_specs=(
            everyone, everyone, P("fsdp"), attn, attn, attn, attn_out, ff_in, ff_in, ff_out,
            same, same, same, same,
        ),
        out_specs=(
            everyone, everyone, attn, attn, attn, attn_out, ff_in, ff_in, ff_out,
            same, same, same, same,
        ),
        check_vma=False,
    )
```

```python
import functools

import jax
import jax.numpy as jnp
from jax import lax
from jax.experimental import pallas as pl
from jax.experimental.pallas import tpu as pltpu
from jax.sharding import PartitionSpec as P

EPS = 1e-06
THETA = 1000000.0
AXES = ("fsdp", "ctx", "tp")
MESH = pl.DeviceIdType.MESH
BF16 = jnp.bfloat16
F32 = jnp.float32
TP_BIT, CTX_BIT = 1, 2
PAIR = 2
PAIR_BIT = PAIR * 4


def dot_rows(left, right):
    return lax.dot_general(left, right, (((0,), (0,)), ((), ())), preferred_element_type=F32)


def dot_cols(left, right):
    return lax.dot_general(left, right, (((1,), (1,)), ((), ())), preferred_element_type=F32)


def dot(left, right):
    return lax.dot_general(left, right, (((1,), (0,)), ((), ())), preferred_element_type=F32)


def remote(src, dst, send, recv, device):
    return pltpu.make_async_remote_copy(
        src_ref=src, dst_ref=dst, send_sem=send, recv_sem=recv, device_id=device, device_id_type=MESH
    )


class Moves:
    def __init__(self, send, recv, local):
        self.send, self.recv, self.local = send, recv, local
        self.sent, self.loads = 0, 0
        self.open = []

    def swap(self, src, there, here, device, open_=None):
        k = self.sent
        self.sent += 1
        copy = remote(src, there, self.send.at[k], self.recv.at[k], device)
        copy.start()
        (self.open if open_ is None else open_).append(copy.wait_send)
        return remote(src, here, self.send.at[k], self.recv.at[k], device).wait_recv

    def load(self, src, dst):
        k = self.loads
        self.loads += 1
        copy = pltpu.make_async_copy(src, dst, self.local.at[k])
        copy.start()
        return copy.wait

    def store(self, src, dst):
        self.open.append(self.load(src, dst))

    def close(self):
        for wait in self.open:
            wait()


class Place:
    def __init__(self, bits):
        self.bits = bits
        f, c, t = lax.axis_index("fsdp"), lax.axis_index("ctx"), lax.axis_index("tp")
        self.f, self.c, self.t = f, c, t
        self.pair = (f // PAIR) % 2
        far_f = self.block(PAIR)
        fs, cs = [f, f, far_f, far_f], [c, 1 - c, c, 1 - c]
        pairs = [self.pair, self.pair, 1 - self.pair, 1 - self.pair]
        self.at = [(fs[j], cs[j], pairs[j]) for j in range(4)]
        self.rows_of = [pairs[j] * 4 + cs[j] * 2 for j in range(4)]
        self.chunk_of = [cs[j] * 2 + pairs[j] for j in range(4)]
        self.relay = len(bits) == 2
        self.across_mask = bits[0] | PAIR
        self.inner = (f // bits[0]) % 2 != self.pair
        self.chips = [None, {"ctx": 1 - c}, {"fsdp": far_f}, {"fsdp": far_f, "ctx": 1 - c}]
        self.sibling = {"tp": 1 - t}

    def block(self, mask):
        out = self.f
        for i in range(mask.bit_length()):
            b = 1 << i
            if mask & b:
                out = out + b - 2 * b * ((self.f // b) % 2)
        return out

    def along(self, bit):
        return {"fsdp": self.block(bit)}

    def greet(self):
        barrier = pltpu.get_barrier_semaphore()
        devices = [*self.chips[1:], self.sibling, *[self.along(b) for b in self.bits]]
        if self.relay:
            devices.append(self.along(self.across_mask))
        for device in devices:
            pl.semaphore_signal(barrier, inc=1, device_id=device, device_id_type=MESH)
        pl.semaphore_wait(barrier, len(devices))


class Cross:
    def __init__(self, moves, place, src, here, came_in, across_to, came_out, pair_to):
        self.place, self.here = place, here
        self.came_in, self.came_out = came_in, came_out
        k = moves.sent
        moves.sent += 4
        pair, across = place.chips[2], place.along(place.across_mask)

        def copy(i, source, to, device):
            return remote(source, to, moves.send.at[k + i], moves.recv.at[k + i], device)

        self.hand = copy(0, src, came_in, pair)
        self.own = copy(1, src, came_out, across)
        self.on = copy(2, came_in, across_to, across)
        self.back = copy(3, came_out, pair_to, pair)
        self.came = [copy(0, came_in, came_in, pair), copy(1, came_out, came_out, across)]
        self.landed = [copy(2, here, here, across), copy(3, here, here, pair)]
        moves.open.append(self.left)

        @pl.when(place.inner)
        def _():
            self.own.start()

        @pl.when(jnp.logical_not(place.inner))
        def _():
            self.hand.start()

    def relay(self):
        @pl.when(self.place.inner)
        def _():
            self.came[0].wait_recv()
            self.on.start()
            self.came[1].wait_recv()
            self.back.start()

    def arrive(self):
        @pl.when(self.place.inner)
        def _():
            self.landed[0].wait_recv()

        @pl.when(jnp.logical_not(self.place.inner))
        def _():
            self.landed[1].wait_recv()

    def left(self):
        @pl.when(self.place.inner)
        def _():
            self.own.wait_send()
            self.on.wait_send()
            self.back.wait_send()

        @pl.when(jnp.logical_not(self.place.inner))
        def _():
            self.hand.wait_send()


class Spread:
    def __init__(self, moves, place, own, out):
        self.moves, self.place, self.out = moves, place, out
        self.rows = own.shape[0]
        self.open = []
        mine = self.at(0, place.t)
        self.here = moves.load(own, mine)
        self.pair = moves.swap(own, mine, self.at(2, place.t), place.chips[2], self.open)
        self.ctx = moves.swap(own, mine, self.at(1, place.t), place.chips[1], self.open)
        self.beside = [moves.swap(own, mine, self.at(0, 1 - place.t), place.sibling, self.open)]

    def at(self, j, t):
        start = (self.place.rows_of[j] + t) * self.rows
        return self.out.at[pl.ds(pl.multiple_of(start, self.rows), self.rows)]

    def hand(self, j):
        block = self.at(j, self.place.t)
        self.beside.append(
            self.moves.swap(block, block, self.at(j, 1 - self.place.t), self.place.sibling, self.open)
        )

    def from_pair(self):
        self.pair()
        block = self.at(2, self.place.t)
        self.both = self.moves.swap(block, block, self.at(3, self.place.t), self.place.chips[1], self.open)
        self.hand(2)

    def from_ctx(self):
        self.ctx()
        self.hand(1)

    def from_both(self):
        self.both()
        self.hand(3)

    def finish(self):
        self.here()
        for wait in (*self.beside, *self.open):
            wait()


class Collect:
    def __init__(self, moves, place, part, held, first, ctx_in, pair_in, sending, load):
        self.moves, self.place = moves, place
        self.first, self.ctx_in, self.pair_in, self.sending = first, ctx_in, pair_in, sending
        t = place.t
        self.hands, self.loads, self.open = {}, {}, []
        for j in (3, 1, 2, 0):
            self.hands[j] = moves.swap(part(j, 1 - t), first.at[j], first.at[j], place.sibling, self.open)
            if load:
                self.loads[j] = moves.load(part(j, t), held.at[j])
        self.held = (lambda j: held.at[j]) if load else (lambda j: part(j, t))

    def two(self, j, at):
        return self.held(j)[at].astype(F32) + self.first[j, at].astype(F32)

    def ready(self, j):
        self.hands[j]()
        if j in self.loads:
            self.loads[j]()

    def to_ctx(self):
        self.waits = {}
        for j, slot in ((3, 0), (1, 1)):
            self.ready(j)

            def body(at):
                self.sending[slot, at] = self.two(j, at).astype(BF16)

            row_loop(self.sending.shape[1], body)
            self.waits[j] = self.moves.swap(
                self.sending.at[slot], self.ctx_in.at[slot], self.ctx_in.at[slot], self.place.chips[1], self.open
            )

    def to_pair(self):
        self.ready(2)
        self.waits[3]()

        def body(at):
            self.sending[2, at] = (self.two(2, at) + self.ctx_in[0, at].astype(F32)).astype(BF16)

        row_loop(self.sending.shape[1], body)
        self.waits[2] = self.moves.swap(
            self.sending.at[2], self.pair_in, self.pair_in, self.place.chips[2], self.open
        )

    def finish(self):
        self.ready(0)
        self.waits[1]()
        self.waits[2]()
        for wait in self.open:
            wait()

    def total(self, at):
        return self.two(0, at) + (self.ctx_in[1, at].astype(F32) + self.pair_in[at].astype(F32))


def collect_buffers(rows, width):
    return [
        pltpu.VMEM((4, rows, width), BF16),
        pltpu.VMEM((2, rows, width), BF16),
        pltpu.VMEM((rows, width), BF16),
        pltpu.VMEM((3, rows, width), BF16),
    ]


def row_loop(rows, body):
    step = 16

    @pl.loop(0, rows // step)
    def _(i):
        body(pl.ds(pl.multiple_of(i * step, step), step))


def unit_and_scale(x):
    scale = lax.rsqrt(jnp.mean(x * x, axis=-1, keepdims=True) + EPS)
    return x * scale, scale


class Gather:
    def __init__(self, moves, place, block, spare):
        self.moves, self.place, self.block, self.spare = moves, place, block, spare
        self.waits, self.crosses = {}, {}

    def forward(self, mask, src=None):
        done = [i for i, b in enumerate(self.place.bits) if mask & b]
        here = self.block(self.place.block(mask))
        for b in self.place.bits[max(done, default=-1) + 1 :]:
            if self.place.relay and b == self.place.bits[0]:
                far = self.place.across_mask
                slot = 0 if mask == 0 else 2
                self.crosses[mask] = Cross(
                    self.moves, self.place, here if src is None else src, self.block(self.place.block(mask | b)),
                    self.spare.at[slot], self.block(self.place.block(mask ^ PAIR)),
                    self.spare.at[slot + 1], self.block(self.place.block(mask ^ far)),
                )
                self.waits[mask | b] = self.crosses[mask].arrive
                continue
            self.waits[mask | b] = self.moves.swap(
                here if src is None else src, here, self.block(self.place.block(mask | b)), self.place.along(b)
            )

    def masks(self, stage):
        out = [0, PAIR]
        for b in self.place.bits[:stage]:
            out += [m | b for m in out]
        return [m | self.place.bits[stage] for m in out]

    def relay(self):
        for m in list(self.crosses):
            self.crosses.pop(m).relay()

    def pass_on(self, m):
        self.waits.pop(m)()
        self.forward(m)

    def middle(self):
        self.relay()
        for stage in range(len(self.place.bits) - 1):
            for m in self.masks(stage):
                if m in self.waits:
                    self.pass_on(m)

    def finish(self):
        for wait in self.waits.values():
            wait()


def head_unit(x):
    scale = lax.rsqrt(jnp.mean(x * x, axis=-1, keepdims=True) + EPS)
    return x * scale, scale


def rot(a, cos, sin):
    return a * cos + pltpu.roll(a, a.shape[-1] // 2, 1) * sin


def rot_back(b, cos, sin):
    return b * cos - pltpu.roll(b, b.shape[-1] // 2, 1) * sin


def allowed_keys(start):
    length = start.shape[0]
    row = lax.broadcasted_iota(jnp.int32, (length, length), 0)
    col = lax.broadcasted_iota(jnp.int32, (length, length), 1)
    return (col.astype(F32) >= start) & (row >= col)


def soft_of(scores):
    peak = jnp.max(scores, axis=-1, keepdims=True)
    lse = peak + jnp.log(jnp.sum(jnp.exp(scores - peak), axis=-1, keepdims=True))
    return jnp.exp(scores - lse)


def attend_one(groups, s, qkv, starts, cos_ref, sin_ref, gain_q, gain_k, out):
    d = gain_q.shape[-1]
    length = cos_ref.shape[0] // 2
    rows = pl.ds(pl.multiple_of(s * length, length), length)
    cos, sin = cos_ref[rows], sin_ref[rows]
    allowed = allowed_keys(starts[rows, 0:1])
    unit_k, _ = head_unit(qkv[rows, groups * d : (groups + 1) * d].astype(F32))
    key = rot(unit_k * gain_k[...], cos, sin).astype(BF16)
    value = qkv[rows, (groups + 1) * d : (groups + 2) * d]
    for g in range(groups):
        unit_q, _ = head_unit(qkv[rows, g * d : (g + 1) * d].astype(F32))
        query = rot(unit_q * gain_q[...], cos, sin).astype(BF16)
        scores = jnp.where(allowed, dot_cols(query, key) * d**-0.5, -jnp.inf)
        soft = soft_of(scores).astype(BF16)
        out[rows, g * d : (g + 1) * d] = dot(soft, value).astype(BF16)


def through_norm(b, unit, scale, gain):
    e = b * gain
    return scale * (e - unit * jnp.mean(e * unit, axis=-1, keepdims=True))


def attend_back_one(
    groups, s, qkv, att, datt, starts, cos_ref, sin_ref, gain_q, gain_k, grad, gains
):
    d = gain_q.shape[-1]
    length = cos_ref.shape[0] // 2
    rows = pl.ds(pl.multiple_of(s * length, length), length)
    cos, sin = cos_ref[rows], sin_ref[rows]
    scale = d**-0.5
    allowed = allowed_keys(starts[rows, 0:1])
    at_k, at_v = slice(groups * d, (groups + 1) * d), slice((groups + 1) * d, (groups + 2) * d)
    unit_k, scale_k = head_unit(qkv[rows, at_k].astype(F32))
    key = rot(unit_k * gain_k[...], cos, sin).astype(BF16)
    value = qkv[rows, at_v]
    key_grad = jnp.zeros(unit_k.shape, F32)
    value_grad = jnp.zeros(unit_k.shape, F32)
    for g in range(groups):
        at = slice(g * d, (g + 1) * d)
        unit_q, scale_q = head_unit(qkv[rows, at].astype(F32))
        query = rot(unit_q * gain_q[...], cos, sin).astype(BF16)
        scores = jnp.where(allowed, dot_cols(query, key) * scale, -jnp.inf)
        soft = soft_of(scores)
        up = datt[rows, at]
        delta = jnp.sum(up.astype(F32) * att[rows, at].astype(F32), axis=-1, keepdims=True)
        ds = (soft * (dot_cols(up, value) - delta) * scale).astype(BF16)
        value_grad += dot_rows(soft.astype(BF16), up)
        key_grad += dot_rows(ds, query)
        b = rot_back(dot(ds, key), cos, sin)
        gains[0] += jnp.sum((b * unit_q).reshape(-1, 8, d), axis=0)
        grad[rows, at] = through_norm(b, unit_q, scale_q, gain_q[...]).astype(BF16)
    b = rot_back(key_grad, cos, sin)
    gains[1] += jnp.sum((b * unit_k).reshape(-1, 8, d), axis=0)
    grad[rows, at_k] = through_norm(b, unit_k, scale_k, gain_k[...]).astype(BF16)
    grad[rows, at_v] = value_grad.astype(BF16)


def attend_back_kernel(
    groups, qkv, att, datt, starts, cos, sin, gain_q, gain_k, grad, gains
):
    gains[...] = jnp.zeros_like(gains)

    @pl.loop(0, 2)
    def _(s):
        attend_back_one(groups, s, qkv, att, datt, starts, cos, sin, gain_q, gain_k, grad, gains)


def attend_back(groups, qkv, att, datt, common):
    n_rows, width = qkv.shape
    d = width // (groups + 2)
    length = n_rows // 2
    return pl.pallas_call(
        functools.partial(attend_back_kernel, groups),
        out_shape=(jax.ShapeDtypeStruct(qkv.shape, BF16), jax.ShapeDtypeStruct((2, 8, d), F32)),
        compiler_params=pltpu.CompilerParams(vmem_limit_bytes=40 << 20),
        cost_estimate=pl.CostEstimate(
            flops=n_rows * groups * length * (10 * d + 30),
            bytes_accessed=n_rows * width * 8,
            transcendentals=n_rows * groups * length * 2,
        ),
        name="attend_back",
    )(qkv, att, datt, *common)


def forward_kernel(
    bits, groups, natural,
    hidden, cot, gain_attn, gain_mlp, seg, table, gain_q, gain_k, wq, wk, wv, wo, wg, wu, wd,
    mid, normed_one, normed_two, cot_out, qkv_out, att_out, qkv_weight, out_weight, starts_out, cos_out, sin_out,
    grad_gate_out, grad_up_out, mixed_out, part_out, down_out, spare_qkv, spare_out, spare_gate, spare_up, spare_down,
    own_one, own_two, rows_one, rows_two, rows_cot, w_qkv, w_out, w_gate, w_up, w_down, qkv, att, part,
    gate, up, grad_gate, grad_up, mixed, mixed_t, starts, cos, sin, seg_in, first, ctx_in, pair_in, sending,
    send, recv, local,
):
    place = Place(bits)
    moves = Moves(send, recv, local)
    rows, width = hidden.shape
    at_rows, ff_rows, ff_cols = wq.shape[0], wg.shape[0], wg.shape[1] // 2
    q_cols, kv_cols = wq.shape[1] // 4, wk.shape[1] // 4
    n_rows, length = rows_one.shape[0], seg.shape[1]

    def lanes(start, size):
        return pl.ds(pl.multiple_of(start, size), size)

    def qkv_rows(f, c=None):
        if c is None:
            return lanes(f * 2 * at_rows, 2 * at_rows)
        return lanes((f * 2 + c) * at_rows, at_rows)

    place.greet()

    def out_block(f, c=None):
        return w_out.at[:, qkv_rows(f, c)] if natural else w_out.at[qkv_rows(f, c)]

    def out_chunk(j):
        at = lanes(place.chunk_of[j] * q_cols, q_cols)
        return wo.at[at] if natural else wo.at[:, at]

    pieces = (
        (wq, q_cols, pl.ds(0, q_cols)),
        (wk, kv_cols, pl.ds(q_cols, kv_cols)),
        (wv, kv_cols, pl.ds(q_cols + kv_cols, kv_cols)),
    )
    f0, c0, _ = place.at[0]
    qkv_in, out_in = {}, {}
    for j in (1, 3, 2):
        fj, cj, _ = place.at[j]
        qkv_in[j] = [
            moves.swap(
                w.at[:, lanes(place.chunk_of[j] * size, size)],
                w_qkv.at[qkv_rows(f0, c0), to],
                w_qkv.at[qkv_rows(fj, cj), to],
                place.chips[j],
            )
            for w, size, to in pieces
        ]
    qkv_in[0] = [
        moves.load(w.at[:, lanes(place.chunk_of[0] * size, size)], w_qkv.at[qkv_rows(f0, c0), to])
        for w, size, to in pieces
    ]
    seg_wait = moves.swap(seg, seg_in, seg_in, place.chips[2])

    def norm_one(at):
        unit, _ = unit_and_scale(hidden[at].astype(F32))
        own_one[at] = (unit * gain_attn[...]).astype(BF16)

    row_loop(rows, norm_one)
    def rows_block(w):
        return lambda f: w.at[lanes(f * ff_rows, ff_rows)]

    def cols_block(w):
        return lambda f: w.at[:, lanes(f * ff_rows, ff_rows)]

    mine, theirs = lanes(place.pair * ff_cols, ff_cols), lanes((1 - place.pair) * ff_cols, ff_cols)
    feed = [
        (Gather(moves, place, rows_block(w_gate), spare_gate), wg.at[:, mine], wg.at[:, theirs]),
        (Gather(moves, place, rows_block(w_up), spare_up), wu.at[:, mine], wu.at[:, theirs]),
        (Gather(moves, place, cols_block(w_down), spare_down), wd.at[mine], wd.at[theirs])
        if natural
        else (Gather(moves, place, rows_block(w_down), spare_down), wd.at[:, mine], wd.at[:, theirs]),
    ]
    own_feed = [moves.load(own, gather.block(place.f)) for gather, own, _ in feed]

    def swap_pair(i):
        gather, _, other = feed[i]
        gather.waits[PAIR] = moves.swap(
            other, gather.block(place.f), gather.block(place.block(PAIR)), place.along(PAIR)
        )

    def send_feed(i):
        gather, own, _ = feed[i]
        gather.forward(0, own)
        gather.pass_on(PAIR)

    qkv_gather = Gather(moves, place, lambda f: w_qkv.at[qkv_rows(f)], spare_qkv)
    out_gather = Gather(moves, place, out_block, spare_out)

    def send_attn(gather, arrivals):
        for wait in (*arrivals[0], *arrivals[1]):
            wait()
        gather.forward(0)
        for wait in (*arrivals[2], *arrivals[3]):
            wait()
        gather.forward(PAIR)

    send_attn(qkv_gather, qkv_in)
    for j in (3, 2, 1):
        fj, cj, _ = place.at[j]
        out_in[j] = moves.swap(out_chunk(j), out_block(f0, c0), out_block(fj, cj), place.chips[j])
    out_in[0] = moves.load(out_chunk(0), out_block(f0, c0))
    spread_one = Spread(moves, place, own_one, rows_one)
    swap_pair(0)
    seg_wait()
    pair_first = place.pair == 0
    own_seg, far_seg = seg[...].astype(F32), seg_in[...].astype(F32)
    for i in range(2):
        here = pair_first if i == 0 else jnp.logical_not(pair_first)
        flags = jnp.where(here, own_seg, far_seg)
        both = jnp.broadcast_to(flags, (128, length)).T[:, 0:1]
        start = jnp.sum((flags < both).astype(F32), axis=1, keepdims=True)
        row = lax.broadcasted_iota(jnp.int32, (length, length), 0).astype(F32)
        col = lax.broadcasted_iota(jnp.int32, (length, length), 1).astype(F32)
        chosen = (row - start == col).astype(F32)
        at = pl.ds(i * length, length)
        both_tables = lax.dot_general(
            chosen, table[...], (((1,), (0,)), ((), ())),
            precision=lax.Precision.HIGHEST, preferred_element_type=F32,
        )
        d = gain_q.shape[1]
        starts[at] = jnp.broadcast_to(start, (length, 128))
        cos[at] = both_tables[:, :d]
        sin[at] = both_tables[:, d:]
    moves.store(starts, starts_out)
    moves.store(cos, cos_out)
    moves.store(sin, sin_out)
    qkv_gather.relay()
    spread_one.from_pair()
    send_attn(out_gather, {j: [w] for j, w in out_in.items()})
    qkv_gather.middle()
    spread_one.from_ctx()
    send_feed(0)
    swap_pair(1)
    out_gather.relay()
    spread_one.from_both()
    spread_one.finish()
    qkv_gather.finish()
    step = 2 * rows

    @pl.loop(0, n_rows // step)
    def _(i):
        at = lanes(i * step, step)
        qkv[at] = dot(rows_one[at], w_qkv[...]).astype(BF16)

    moves.store(qkv, qkv_out)
    normed_stored = moves.load(rows_one, normed_one)
    moves.store(w_qkv, qkv_weight)
    spread_cot = Spread(moves, place, cot, rows_cot)
    out_gather.middle()
    feed[0][0].relay()
    send_feed(1)

    @pl.loop(0, 2)
    def _(s):
        attend_one(groups, s, qkv, starts, cos, sin, gain_q, gain_k, att)

    moves.store(att, att_out)
    out_gather.finish()
    swap_pair(2)

    @pl.loop(0, 8)
    def _(i):
        part[i] = (dot if natural else dot_cols)(att[lanes(i * rows, rows)], w_out[...]).astype(BF16)

    moves.store(w_out, out_weight)
    collect = Collect(
        moves, place, lambda j, t: part.at[place.rows_of[j] + t], None, first, ctx_in, pair_in, sending, False
    )
    collect.to_ctx()
    feed[0][0].middle()
    feed[1][0].relay()
    spread_cot.from_pair()
    collect.to_pair()
    send_feed(2)
    spread_cot.from_ctx()
    collect.finish()

    def norm_two(at):
        x = hidden[at].astype(F32) + collect.total(at)
        mid[at] = x
        unit, _ = unit_and_scale(x)
        own_two[at] = (unit * gain_mlp[...]).astype(BF16)

    row_loop(rows, norm_two)
    spread_two = Spread(moves, place, own_two, rows_two)
    feed[1][0].middle()
    feed[2][0].relay()
    spread_cot.from_both()
    spread_two.from_pair()
    spread_two.from_ctx()
    spread_two.from_both()
    spread_two.finish()
    moves.store(rows_two, normed_two)
    for wait in own_feed:
        wait()
    feed[0][0].finish()

    @pl.loop(0, n_rows // step)
    def _(i):
        at = lanes(i * step, step)
        gate[at] = dot(rows_two[at], w_gate[...])

    spread_cot.finish()
    moves.store(rows_cot, cot_out)
    feed[2][0].middle()
    feed[1][0].finish()

    @pl.loop(0, n_rows // step)
    def _(i):
        at = lanes(i * step, step)
        u = dot(rows_two[at], w_up[...])
        up[at] = u
        g = gate[at]
        mix = g * jax.nn.sigmoid(g) * u
        mixed[at] = mix.astype(BF16)
        mixed_t[:, at] = mix.T.astype(BF16)

    moves.store(mixed_t, mixed_out)
    normed_stored()
    feed[2][0].finish()

    @pl.loop(0, n_rows // step)
    def _(i):
        at = lanes(i * step, step)
        m = (dot_cols if natural else dot)(rows_cot[at], w_down[...])
        g = gate[at]
        s = jax.nn.sigmoid(g)
        grad_gate[at] = (m * up[at] * s * (1.0 + g * (1.0 - s))).astype(BF16)
        grad_up[at] = (m * (g * s)).astype(BF16)

    moves.store(grad_gate, grad_gate_out)
    moves.store(grad_up, grad_up_out)

    @pl.loop(0, 8)
    def _(i):
        at = lanes(i * rows, rows)
        part[i] = (dot_cols(grad_gate[at], w_gate[...]) + dot_cols(grad_up[at], w_up[...])).astype(BF16)

    moves.store(part, part_out)

    @pl.loop(0, 8)
    def _(i):
        at = lanes(i * rows, rows)
        rows_one[at] = (dot if natural else dot_cols)(mixed[at], w_down[...]).astype(BF16)

    moves.store(rows_one, down_out)
    moves.close()


def norm_back(grad, x, gain, gain_grad):
    unit, scale = unit_and_scale(x)
    gain_grad[...] += jnp.sum((grad * unit).reshape(-1, 8, grad.shape[-1]), axis=0)
    e = grad * gain
    return scale * (e - unit * jnp.mean(e * unit, axis=-1, keepdims=True))


def turn_kernel(
    bits, partial, mid, cot, gain, grad_mid, gain_grad, out,
    own, held, first, ctx_in, pair_in, sending, send, recv, local,
):
    place = Place(bits)
    moves = Moves(send, recv, local)
    place.greet()
    collect = Collect(
        moves, place, lambda j, t: partial.at[place.rows_of[j] + t], held, first, ctx_in, pair_in, sending, True
    )
    collect.to_ctx()
    collect.to_pair()
    collect.finish()
    gain_grad[...] = jnp.zeros_like(gain_grad)

    def back(at):
        g = cot[at].astype(F32) + norm_back(collect.total(at), mid[at], gain[...], gain_grad)
        grad_mid[at] = g
        own[at] = g.astype(BF16)

    row_loop(mid.shape[0], back)
    spread = Spread(moves, place, own, out)
    spread.from_pair()
    spread.from_ctx()
    spread.from_both()
    spread.finish()
    moves.close()


def last_kernel(
    bits, partial, hidden, grad_mid, gain, grad_in, gain_grad,
    held, first, ctx_in, pair_in, sending, send, recv, local,
):
    place = Place(bits)
    moves = Moves(send, recv, local)
    place.greet()
    collect = Collect(
        moves, place, lambda j, t: partial.at[place.rows_of[j] + t], held, first, ctx_in, pair_in, sending, True
    )
    collect.to_ctx()
    collect.to_pair()
    collect.finish()
    gain_grad[...] = jnp.zeros_like(gain_grad)

    def back(at):
        grad_in[at] = grad_mid[at] + norm_back(
            collect.total(at), hidden[at].astype(F32), gain[...], gain_grad
        )

    row_loop(hidden.shape[0], back)
    moves.close()


class Scatter:
    def __init__(self, moves, place, product, out0, in0, out1, in1, acc, spare):
        self.moves, self.place, self.product, self.spare = moves, place, product, spare
        self.out0, self.in0, self.out1, self.in1, self.acc = out0, in0, out1, in1, acc
        self.low, self.high = place.bits[1], place.bits[0]
        self.order = [self.high, self.high | PAIR, 0, PAIR]
        self.first, self.second, self.leaving = {}, {}, {}

    def send(self, i):
        slot = i % 2
        for wait in self.leaving.pop(slot, []):
            wait()

        def emit(at, value):
            self.out0[(slot, *at)] = value.astype(BF16)

        self.product(self.order[i] | self.low, emit)
        self.leaving[slot] = []
        self.first[i] = self.moves.swap(
            self.out0.at[slot], self.in0.at[i], self.in0.at[i], self.place.along(self.low), self.leaving[slot]
        )

    def take(self, i):
        self.first[i]()

        def emit(at, value):
            value = value + self.in0[(i, *at)].astype(F32)
            if i < 2:
                self.out1[(i, *at)] = value.astype(BF16)
            else:
                self.acc[(i - 2, *at)] = value

        self.product(self.order[i], emit)
        if i < 2:
            to = self.in1.at[i]
            self.second[i] = Cross(
                self.moves, self.place, self.out1.at[i], to, self.spare.at[2 * i], to, self.spare.at[2 * i + 1], to
            )

    def relay(self, i):
        self.second[i].relay()

    def take_high(self, i):
        self.second[i].arrive()
        rows = self.acc.shape[1]
        step = 64

        @pl.loop(0, rows // step)
        def _(k):
            at = pl.ds(pl.multiple_of(k * step, step), step)
            self.acc[i, at] += self.in1[i, at].astype(F32)

    def close(self):
        for waits in self.leaving.values():
            for wait in waits:
                wait()


class Blocks:
    def __init__(self, moves, place, slots, order):
        self.moves, self.place, self.slots, self.order = moves, place, slots, order
        self.next, self.waits = 0, {}
        self.start(0)

    def start(self, k):
        if k < len(self.order):
            ref, mask = self.order[k]
            size = self.slots.shape[2]
            at = pl.ds(pl.multiple_of(self.place.block(mask) * size, size), size)
            self.waits[k] = self.moves.load(ref.at[:, at], self.slots.at[k % 2])

    def get(self, ref, mask):
        k = self.next
        assert self.order[k][0] is ref and self.order[k][1] == mask
        self.next += 1
        self.waits.pop(k)()
        self.start(k + 1)
        return self.slots[k % 2]


def backward_kernel(
    bits, groups,
    mid, hidden, cot, gain_attn, gain_mlp, starts, cos, sin, gain_q, gain_k,
    part_two, part_hidden, normed_one, normed_two, cot_rows, qkv_in, att_in, qkv_weight, out_weight, grad_gate, grad_up,
    mixed_t,
    grad_in, hidden_out, gains, feed_own, feed_other, down_own, down_other, qkv_own, qkv_other, out_own, out_other,
    spare_feed, spare_down, spare_qkv, spare_out,
    own, rows_mid, feed, mixed, lhs, lhs_t, part, w_qkv, w_out, qkv, att, datt, dqkv,
    first, ctx_in, pair_in, sending, gain_a, gain_m, gain_h, tree, tree_in,
    f_out0, f_in0, f_out1, f_in1, f_acc, d_out0, d_in0, d_out1, d_in1, d_acc,
    q_out0, q_in0, q_out1, q_in1, q_acc, o_out0, o_in0, o_out1, o_in1, o_acc,
    send, recv, local,
):
    place = Place(bits)
    moves = Moves(send, recv, local)
    rows, width = hidden.shape
    cols = mixed.shape[0]
    tile = lhs.shape[2]
    half = tile // 2
    high, low = bits
    place.greet()

    def lanes(start, size):
        return pl.ds(pl.multiple_of(start, size), size)

    ready_feed = [
        moves.load(grad_gate, feed.at[:, pl.ds(0, cols)]),
        moves.load(grad_up, feed.at[:, pl.ds(cols, cols)]),
    ]
    collect_two = Collect(
        moves, place, lambda j, t: part_two.at[place.rows_of[j] + t], part, first, ctx_in, pair_in, sending, True
    )
    masks = [high, high | PAIR, 0, PAIR]
    sends = [m | low for m in masks]
    order = [
        (cot_rows, sends[0]), (cot_rows, sends[1]), (normed_two, sends[0]), (cot_rows, masks[0]),
        (normed_two, sends[1]), (cot_rows, masks[1]), (normed_two, masks[0]),
        (cot_rows, sends[2]), (cot_rows, sends[3]), (normed_two, sends[2]), (normed_two, sends[3]),
        (normed_two, masks[1]),
        (normed_one, sends[0]), (normed_one, sends[1]), (cot_rows, masks[2]), (cot_rows, masks[3]),
        (normed_one, sends[2]), (normed_one, sends[3]), (normed_two, masks[2]), (normed_two, masks[3]),
        *[(normed_one, m) for m in masks],
    ]
    blocks = Blocks(moves, place, lhs, order)
    ready_mixed = moves.load(mixed_t, mixed)
    ready_late = [
        moves.load(out_weight, w_out),
        moves.load(att_in, att),
        moves.load(qkv_in, qkv),
        moves.load(qkv_weight, w_qkv),
    ]

    def by_rows(source, right):
        def product(mask, emit):
            lhs_t[...] = blocks.get(source, mask).T
            step = min(512, right.shape[1])

            @pl.loop(0, right.shape[1] // step)
            def _(i):
                at = lanes(i * step, step)
                emit((slice(None), at), dot(lhs_t[...], right[:, at]))

        return product

    def down_product(mask, emit):
        block = blocks.get(cot_rows, mask)
        step = min(256, cols)

        @pl.loop(0, cols // step)
        def _(i):
            at = lanes(i * step, step)
            emit((at, slice(None)), dot(mixed[at], block))

    def out_product(mask, emit):
        at = lanes(place.block(mask) * tile, tile)
        emit((slice(None), slice(None)), dot_rows(att[...], rows_mid[:, at]))

    feed_s = Scatter(moves, place, by_rows(normed_two, feed), f_out0, f_in0, f_out1, f_in1, f_acc, spare_feed)
    down_s = Scatter(moves, place, down_product, d_out0, d_in0, d_out1, d_in1, d_acc, spare_down)
    qkv_s = Scatter(moves, place, by_rows(normed_one, dqkv), q_out0, q_in0, q_out1, q_in1, q_acc, spare_qkv)
    out_s = Scatter(moves, place, out_product, o_out0, o_in0, o_out1, o_in1, o_acc, spare_out)

    ready_mixed()
    down_s.send(0)
    down_s.send(1)
    collect_two.to_ctx()
    for wait in ready_feed:
        wait()
    feed_s.send(0)
    down_s.take(0)
    collect_two.to_pair()
    feed_s.send(1)
    down_s.relay(0)
    down_s.take(1)
    collect_two.finish()
    gain_m[...] = jnp.zeros_like(gain_m)
    gain_a[...] = jnp.zeros_like(gain_a)
    gain_h[...] = jnp.zeros_like(gain_h)

    def back_two(at):
        g = cot[at].astype(F32) + norm_back(collect_two.total(at), mid[at], gain_mlp[...], gain_m)
        grad_in[at] = g
        own[at] = g.astype(BF16)

    row_loop(rows, back_two)
    spread = Spread(moves, place, own, rows_mid)
    feed_s.take(0)
    down_s.relay(1)
    spread.from_pair()
    down_s.send(2)
    down_s.send(3)
    spread.from_ctx()
    feed_s.send(2)
    feed_s.send(3)
    spread.from_both()
    feed_s.relay(0)
    for wait in ready_late:
        wait()
    spread.finish()

    @pl.loop(0, 8 // 2)
    def _(i):
        at = lanes(i * 2 * rows, 2 * rows)
        datt[at] = dot_cols(rows_mid[at], w_out[...]).astype(BF16)

    feed_s.take(1)

    @pl.loop(0, 2)
    def _(s):
        attend_back_one(groups, s, qkv, att, datt, starts, cos, sin, gain_q, gain_k, dqkv, gain_h)

    @pl.loop(0, 8)
    def _(i):
        part[i] = dot_cols(dqkv[lanes(i * rows, rows)], w_qkv[...]).astype(BF16)

    collect_one = Collect(
        moves, place, lambda j, t: part.at[place.rows_of[j] + t], None, first, ctx_in, pair_in, sending, False
    )
    qkv_s.send(0)
    qkv_s.send(1)
    out_s.send(0)
    out_s.send(1)
    collect_one.to_ctx()
    feed_s.relay(1)
    down_s.take(2)
    down_s.take(3)
    collect_one.to_pair()
    qkv_s.send(2)
    qkv_s.send(3)
    out_s.send(2)
    out_s.send(3)
    collect_one.finish()

    def back_one(at):
        grad_in[at] += norm_back(collect_one.total(at), hidden[at].astype(F32), gain_attn[...], gain_a)

    row_loop(rows, back_one)
    feed_s.take(2)
    feed_s.take(3)
    qkv_s.take(0)
    qkv_s.take(1)
    out_s.take(0)
    out_s.take(1)
    qkv_s.relay(0)
    qkv_s.relay(1)
    out_s.relay(0)
    out_s.relay(1)

    d = gain_q.shape[1]
    tree[0, :, 0:width] = jnp.sum(gain_a[...], axis=0, keepdims=True)
    tree[0, :, width : 2 * width] = jnp.sum(gain_m[...], axis=0, keepdims=True)
    tree[0, :, 2 * width : 2 * width + d] = jnp.sum(gain_h[0], axis=0, keepdims=True)
    tree[0, :, 2 * width + d : 2 * width + 2 * d] = jnp.sum(gain_h[1], axis=0, keepdims=True)
    for k, device in enumerate([place.sibling, place.chips[1], place.chips[2], *[place.along(b) for b in bits]]):
        moves.swap(tree.at[k], tree_in.at[k], tree_in.at[k], device)()
        tree[k + 1] = tree[k] + tree_in[k]
    gains[...] = tree[3 + len(bits)]
    collect_hidden = Collect(
        moves, place, lambda j, t: part_hidden.at[place.rows_of[j] + t], part, first, ctx_in, pair_in, sending, True
    )
    collect_hidden.to_ctx()
    finals = []

    def feed_final(scatter, mine, other):
        scatter.take_high(1)
        pair_out = scatter.in0.at[0]
        n, step = pair_out.shape[0], 64

        @pl.loop(0, n // step)
        def _(k):
            at = lanes(k * step, step)
            pair_out[at] = scatter.acc[1, at].astype(BF16)

        finals.append(moves.swap(pair_out, other, other, place.chips[2]))
        scatter.take_high(0)
        moves.store(scatter.acc.at[0], mine)

    def mates_final(scatter, piece, spare, mine, other):
        scatter.take_high(1)
        scatter.take_high(0)
        for j in (3, 2, 1):
            out = spare(j)
            out[...] = piece(j // 2, place.at[j][1]).astype(BF16)
            finals.append(moves.swap(out, other.at[j - 1], other.at[j - 1], place.chips[j]))
        mine[...] = piece(0, place.c)

    feed_final(down_s, down_own, down_other)
    collect_hidden.to_pair()
    qkv_s.take(2)
    qkv_s.take(3)
    out_s.take(2)
    out_s.take(3)
    collect_hidden.finish()

    def add_hidden(at):
        hidden_out[at] = mid[at] + collect_hidden.total(at)

    row_loop(rows, add_hidden)
    feed_final(feed_s, feed_own, feed_other)
    mates_final(
        qkv_s, lambda slot, c: q_acc[slot, lanes(c * half, half)],
        lambda j: q_in0.at[j, pl.ds(0, half)], qkv_own, qkv_other,
    )
    mates_final(
        out_s, lambda slot, c: o_acc[slot, :, lanes(c * half, half)],
        lambda j: o_in0.at[j, :, pl.ds(0, half)], out_own, out_other,
    )
    for scatter in (feed_s, down_s, qkv_s, out_s):
        scatter.close()
    for wait in finals:
        wait()
    moves.close()


def join_kernel(
    feed_own, feed_other, down_own, down_other, qkv_own, qkv_other, out_own, out_other, grad_in, hidden, gains,
    g_query, g_key, g_value, g_out, g_gate, g_up, g_down, g_in, h_out, gain_a, gain_m, gain_q, gain_k,
):
    c = lax.axis_index("ctx")
    pair = (lax.axis_index("fsdp") // PAIR) % 2
    cols, n_q = down_own.shape[0], out_own.shape[0]
    n_kv = (qkv_own.shape[1] - n_q) // 2

    def lanes(start, size):
        return pl.ds(pl.multiple_of(start, size), size)

    mine, theirs = lanes(pair * cols, cols), lanes((1 - pair) * cols, cols)
    g_gate[:, mine] = feed_own[:, :cols]
    g_up[:, mine] = feed_own[:, cols:]
    g_down[mine] = down_own[...]
    g_gate[:, theirs] = feed_other[:, :cols].astype(F32)
    g_up[:, theirs] = feed_other[:, cols:].astype(F32)
    g_down[theirs] = down_other[...].astype(F32)
    chunks = [c * 2 + pair, (1 - c) * 2 + pair, c * 2 + 1 - pair, (1 - c) * 2 + 1 - pair]
    for j, chunk in enumerate(chunks):
        qkv = qkv_own[...] if j == 0 else qkv_other[j - 1].astype(F32)
        g_query[:, lanes(chunk * n_q, n_q)] = qkv[:, :n_q]
        g_key[:, lanes(chunk * n_kv, n_kv)] = qkv[:, n_q : n_q + n_kv]
        g_value[:, lanes(chunk * n_kv, n_kv)] = qkv[:, n_q + n_kv :]
        g_out[lanes(chunk * n_q, n_q)] = out_own[...] if j == 0 else out_other[j - 1].astype(F32)
    g_in[...] = grad_in[...]
    h_out[...] = hidden[...]
    width, d = gain_a.shape[1], gain_q.shape[1]
    gain_a[...] = gains[:, :width]
    gain_m[...] = gains[:, width : 2 * width]
    gain_q[...] = gains[:, 2 * width : 2 * width + d]
    gain_k[...] = gains[:, 2 * width + d :]


VMEM_SPEC = pl.BlockSpec(memory_space=pltpu.VMEM)
ANY_SPEC = pl.BlockSpec(memory_space=pl.ANY)


def comm_call(kernel, bits, collective_id, operands, in_specs, outs, out_specs, scratch, nbytes, copies, *more):
    return pl.pallas_call(
        functools.partial(kernel, bits, *more),
        out_shape=outs,
        in_specs=in_specs,
        out_specs=out_specs,
        scratch_shapes=[
            *scratch,
            pltpu.SemaphoreType.DMA((copies,)),
            pltpu.SemaphoreType.DMA((copies,)),
            pltpu.SemaphoreType.DMA((96,)),
        ],
        compiler_params=pltpu.CompilerParams(
            collective_id=collective_id, has_side_effects=True, vmem_limit_bytes=61 << 20
        ),
        cost_estimate=pl.CostEstimate(flops=nbytes * 20, bytes_accessed=nbytes, transcendentals=0),
        name=kernel.__name__,
    )(*operands)


def build(mesh):
    n = mesh.size
    n_f = mesh.shape["fsdp"]
    spread_bits = [b for b in (1 << i for i in range(n_f.bit_length() - 2, -1, -1)) if b != PAIR]
    all_bits = sorted([*spread_bits, PAIR], reverse=True)

    def swap(v, bit):
        return lax.ppermute(v, AXES, [(i, i ^ bit) for i in range(n)])

    def bit_of(f, b):
        return (f // b) % 2

    def in_order(bit, own, other, axis):
        low = jnp.where(bit == 0, own, other)
        high = jnp.where(bit == 0, other, own)
        return jnp.stack([low, high], axis=axis)

    def pick(v, index, axis):
        return lax.dynamic_index_in_dim(v, index, axis, keepdims=False)

    def scatter(keep, got, f, width):
        v = keep + got.astype(F32)
        have = [b for b in all_bits if b != 1]
        v = v.reshape(*([2] * len(have)), width, v.shape[-1])
        for b in [b for b in reversed(spread_bits) if b != 1]:
            axis = have.index(b)
            bit = bit_of(f, b)
            v = pick(v, bit, axis) + swap(pick(v, 1 - bit, axis).astype(BF16), b * 4).astype(F32)
            have.remove(b)
        return v

    def body(
        hidden_in,
        cotangent,
        segments,
        w_query,
        key_projection_weight,
        value_projection_weight,
        w_out,
        w_gate,
        w_up,
        w_down,
        gain_attn,
        gain_mlp,
        gain_query,
        key_norm_gain,
    ):
        rows, width = hidden_in.shape
        d = gain_query.shape[0]
        length = segments.shape[0]
        f, c = lax.axis_index("fsdp"), lax.axis_index("ctx")
        pair = bit_of(f, PAIR)
        at_rows = w_query.shape[0]
        ff_rows = w_gate.shape[0]
        ff_cols = w_gate.shape[1] // 2
        q_cols, kv_cols = w_query.shape[1] // 4, key_projection_weight.shape[1] // 4
        groups = q_cols // kv_cols

        freqs = THETA ** (-2.0 * jnp.arange(d // 2, dtype=F32) / d)
        angles = jnp.arange(length, dtype=jnp.int32).astype(F32)[:, None] * freqs
        table_cos, table_sin = jnp.cos(angles), jnp.sin(angles)
        table = jnp.concatenate([table_cos, table_cos, -table_sin, table_sin], axis=-1)

        n_rows = 8 * rows
        all_rows = jax.ShapeDtypeStruct((n_rows, width), BF16)
        own_rows = jax.ShapeDtypeStruct((rows, width), F32)
        gain_rows = jax.ShapeDtypeStruct((8, width), F32)
        block = pltpu.VMEM((rows, width), BF16)
        nbytes = rows * width * 16
        qkv_cols = q_cols + 2 * kv_cols

        def shape(*dims):
            return jax.ShapeDtypeStruct(dims, BF16)

        copies = 160 + 10 * n_f
        natural = at_rows % 128 == 0 and ff_rows % 128 == 0
        out_dims = (q_cols, width) if natural else (width, q_cols)
        down_dims = (ff_cols, width) if natural else (width, ff_cols)
        out_part = (q_cols, 2 * at_rows) if natural else (2 * at_rows, q_cols)
        down_part_dims = (ff_cols, ff_rows) if natural else (ff_rows, ff_cols)
        n_seq = 2 * length
        all_tables = jax.ShapeDtypeStruct((n_seq, d), F32)

        def v(*dims, dtype=BF16):
            return pltpu.VMEM(dims, dtype)

        (
            residual_mid, normed_one, normed_two, grad_rows, qkv, attended, full_qkv, full_out, starts, cos, sin,
            grad_gate, grad_up, mixed_t, norm_two_part, down_part, *_,
        ) = comm_call(
            forward_kernel, spread_bits, 0,
            (hidden_in, cotangent, gain_attn[None], gain_mlp[None], segments[None], table, gain_query[None],
             key_norm_gain[None], w_query, key_projection_weight, value_projection_weight,
             w_out if natural else w_out.T, w_gate, w_up, w_down if natural else w_down.T),
            [VMEM_SPEC] * 8 + [ANY_SPEC] * 7,
            (own_rows, all_rows, all_rows, all_rows, shape(n_rows, qkv_cols), shape(n_rows, q_cols),
             shape(width, qkv_cols), shape(*out_dims), jax.ShapeDtypeStruct((n_seq, 128), F32), all_tables, all_tables,
             shape(n_rows, ff_cols), shape(n_rows, ff_cols), shape(ff_cols, n_rows), shape(8, rows, width), all_rows,
             shape(4, 2 * at_rows, qkv_cols), shape(4, *out_part), shape(4, ff_rows, ff_cols),
             shape(4, ff_rows, ff_cols), shape(4, *down_part_dims)),
            (VMEM_SPEC, *[ANY_SPEC] * 20),
            [block, block, v(n_rows, width), v(n_rows, width), v(n_rows, width), v(width, qkv_cols), v(*out_dims),
             v(width, ff_cols), v(width, ff_cols), v(*down_dims), v(n_rows, qkv_cols), v(n_rows, q_cols),
             v(8, rows, width), v(n_rows, ff_cols, dtype=F32), v(n_rows, ff_cols, dtype=F32), v(n_rows, ff_cols),
             v(n_rows, ff_cols), v(n_rows, ff_cols), v(ff_cols, n_rows), v(n_seq, 128, dtype=F32),
             v(n_seq, d, dtype=F32), v(n_seq, d, dtype=F32), v(1, length, dtype=jnp.int32),
             *collect_buffers(rows, width)],
            16 * nbytes, copies, groups, natural,
        )
        common = (starts, cos, sin, gain_query[None], key_norm_gain[None])
        backward = one_kernel if natural and len(spread_bits) == 2 else by_steps
        return backward(
            hidden_in, cotangent, residual_mid, gain_attn, gain_mlp, common, norm_two_part, down_part, normed_one,
            normed_two, grad_rows, qkv, attended, full_qkv, full_out, grad_gate, grad_up, mixed_t, (at_rows, ff_rows),
        )

    def one_kernel(
        hidden_in, cotangent, residual_mid, gain_attn, gain_mlp, common, norm_two_part, down_part, normed_one,
        normed_two, grad_rows, qkv, attended, full_qkv, full_out, grad_gate, grad_up, mixed_t, sizes,
    ):
        rows, width = hidden_in.shape
        cols, n_rows = mixed_t.shape
        (at_rows, ff_rows), q_cols, qkv_cols = sizes, attended.shape[1], qkv.shape[1]
        d = common[-1].shape[1]
        kv_cols = (qkv_cols - q_cols) // 2
        groups = q_cols // kv_cols

        def out(dtype, *dims):
            return jax.ShapeDtypeStruct(dims, dtype)

        def v(*dims, dtype=BF16):
            return pltpu.VMEM(dims, dtype)

        def scatter(*block):
            return [v(2, *block), v(4, *block), v(2, *block), v(2, *block), v(2, *block, dtype=F32)]

        n_gain = 2 * width + 2 * d
        nbytes = n_rows * width * 20
        (
            grad_input, hidden_out, gains, feed_own, feed_other, down_own, down_other, qkv_own, qkv_other, out_own,
            out_other, *_,
        ) = comm_call(
            backward_kernel, spread_bits, 2,
            (residual_mid, hidden_in, cotangent, gain_attn[None], gain_mlp[None], *common, norm_two_part,
             down_part.reshape(8, rows, width), normed_one, normed_two, grad_rows, qkv, attended, full_qkv, full_out,
             grad_gate, grad_up, mixed_t),
            [VMEM_SPEC] * 10 + [ANY_SPEC] * 12,
            (out(F32, rows, width), out(F32, rows, width), out(F32, 1, n_gain), out(F32, ff_rows, 2 * cols),
             out(BF16, ff_rows, 2 * cols), out(F32, cols, ff_rows), out(BF16, cols, ff_rows),
             out(F32, at_rows, qkv_cols), out(BF16, 3, at_rows, qkv_cols), out(F32, q_cols, at_rows),
             out(BF16, 3, q_cols, at_rows), out(BF16, 4, ff_rows, 2 * cols), out(BF16, 4, cols, ff_rows),
             out(BF16, 4, ff_rows, qkv_cols), out(BF16, 4, q_cols, ff_rows)),
            (VMEM_SPEC, VMEM_SPEC, VMEM_SPEC, ANY_SPEC, ANY_SPEC, ANY_SPEC, ANY_SPEC, VMEM_SPEC, ANY_SPEC, VMEM_SPEC,
             *[ANY_SPEC] * 5),
            [v(rows, width), v(n_rows, width), v(n_rows, 2 * cols), v(cols, n_rows), v(2, n_rows, ff_rows),
             v(ff_rows, n_rows), v(8, rows, width), v(width, qkv_cols), v(q_cols, width), v(n_rows, qkv_cols),
             v(n_rows, q_cols), v(n_rows, q_cols), v(n_rows, qkv_cols),
             *collect_buffers(rows, width), v(8, width, dtype=F32), v(8, width, dtype=F32), v(2, 8, d, dtype=F32),
             v(4 + len(spread_bits), 1, n_gain, dtype=F32), v(3 + len(spread_bits), 1, n_gain, dtype=F32),
             *scatter(ff_rows, 2 * cols), *scatter(cols, ff_rows), *scatter(ff_rows, qkv_cols),
             *scatter(q_cols, ff_rows)],
            nbytes, 110, groups,
        )
        own_rows = out(F32, rows, width)
        made = (
            out(F32, at_rows, 4 * q_cols), out(F32, at_rows, 4 * kv_cols), out(F32, at_rows, 4 * kv_cols),
            out(F32, 4 * q_cols, at_rows), out(F32, ff_rows, 2 * cols), out(F32, ff_rows, 2 * cols),
            out(F32, 2 * cols, ff_rows), own_rows, own_rows, out(F32, 1, width), out(F32, 1, width), out(F32, 1, d),
            out(F32, 1, d),
        )
        pieces = pl.pallas_call(
            join_kernel,
            out_shape=made,
            compiler_params=pltpu.CompilerParams(vmem_limit_bytes=40 << 20),
            name="join_kernel",
        )(feed_own, feed_other, down_own, down_other, qkv_own, qkv_other, out_own, out_other, grad_input, hidden_out, gains)
        grads, (grad_input, hidden_out), gains = pieces[:7], pieces[7:9], pieces[9:]
        return hidden_out, grad_input, *grads, *(g[0] for g in gains)

    def by_steps(
        hidden_in, cotangent, residual_mid, gain_attn, gain_mlp, common, norm_two_part, down_part, normed_one,
        normed_two, grad_rows, qkv, attended, full_qkv, full_out, grad_gate, grad_up, mixed_t, sizes,
    ):
        rows, width = hidden_in.shape
        (at_rows, ff_rows), ff_cols, q_cols = sizes, mixed_t.shape[0], attended.shape[1]
        d = common[-1].shape[1]
        kv_cols = (qkv.shape[1] - q_cols) // 2
        groups = q_cols // kv_cols
        natural = full_out.shape[0] != width
        times_t = dot_cols if natural else dot
        f, c = lax.axis_index("fsdp"), lax.axis_index("ctx")
        pair = bit_of(f, PAIR)
        all_rows = jax.ShapeDtypeStruct((8 * rows, width), BF16)
        own_rows = jax.ShapeDtypeStruct((rows, width), F32)
        gain_rows = jax.ShapeDtypeStruct((8, width), F32)
        block = pltpu.VMEM((rows, width), BF16)
        nbytes = rows * width * 16
        grad_mid, gain_mlp_part, grad_mid_rows = comm_call(
            turn_kernel, spread_bits, 2, (norm_two_part.reshape(8, rows, width), residual_mid, cotangent, gain_mlp[None]),
            [ANY_SPEC, VMEM_SPEC, VMEM_SPEC, VMEM_SPEC], (own_rows, gain_rows, all_rows),
            (VMEM_SPEC, VMEM_SPEC, ANY_SPEC),
            [block, pltpu.VMEM((4, rows, width), BF16), *collect_buffers(rows, width)], 2 * nbytes, 40,
        )

        low = bit_of(f, 1)

        def weight_grad(acts, grads):
            split = acts.reshape(acts.shape[0], n_f // 2, 2, width // n_f)
            mine = pick(split, low, 2).reshape(acts.shape[0], -1)
            theirs = pick(split, 1 - low, 2).reshape(acts.shape[0], -1)
            got = swap(dot_rows(theirs, grads).astype(BF16), 4)
            return scatter(dot_rows(mine, grads), got, f, width // n_f)

        def ff_grad(acts, grads):
            v = weight_grad(acts, grads)
            other = swap(pick(v, 1 - pair, 0).astype(BF16), PAIR_BIT).astype(F32)
            return in_order(pair, pick(v, pair, 0), other, 1).reshape(ff_rows, 2 * ff_cols)

        grad_w_gate = ff_grad(normed_two, grad_gate)
        grad_w_up = ff_grad(normed_two, grad_up)
        grad_w_down = ff_grad(grad_rows, mixed_t.T).T

        def attn_grad(acts, grads):
            v = weight_grad(acts, grads)
            v = v.reshape(2, 2, at_rows, v.shape[-1])
            mine = pick(pick(v, pair, 0), c, 0)
            by_ctx = swap(pick(pick(v, pair, 0), 1 - c, 0).astype(BF16), CTX_BIT).astype(F32)
            by_pair = swap(pick(pick(v, 1 - pair, 0), c, 0).astype(BF16), PAIR_BIT).astype(F32)
            by_both = swap(pick(pick(v, 1 - pair, 0), 1 - c, 0).astype(BF16), CTX_BIT | PAIR_BIT).astype(F32)
            near = in_order(pair, mine, by_pair, 1)
            far = in_order(pair, by_ctx, by_both, 1)
            return in_order(c, near, far, 1)

        grad_w_out = attn_grad(grad_mid_rows, attended).reshape(at_rows, 4 * q_cols).T

        datt = times_t(grad_mid_rows, full_out).astype(BF16)
        grad_qkv, head_gains = attend_back(groups, qkv, attended, datt, common)
        norm_one_part = dot_cols(grad_qkv, full_qkv).astype(BF16)
        grad_input, gain_attn_part = comm_call(
            last_kernel, spread_bits, 3, (norm_one_part.reshape(8, rows, width), hidden_in, grad_mid, gain_attn[None]),
            [ANY_SPEC, VMEM_SPEC, VMEM_SPEC, VMEM_SPEC], (own_rows, gain_rows), (VMEM_SPEC, VMEM_SPEC),
            [pltpu.VMEM((4, rows, width), BF16), *collect_buffers(rows, width)], nbytes, 40,
        )
        grad_qkv_w = attn_grad(normed_one, grad_qkv)
        grad_w_query = grad_qkv_w[..., :q_cols].reshape(at_rows, -1)
        grad_w_key = grad_qkv_w[..., q_cols : q_cols + kv_cols].reshape(at_rows, -1)
        grad_w_value = grad_qkv_w[..., q_cols + kv_cols :].reshape(at_rows, -1)

        head_gains = jnp.sum(head_gains, axis=1)
        gains = jnp.concatenate(
            [jnp.sum(gain_attn_part, axis=0), jnp.sum(gain_mlp_part, axis=0), head_gains[0], head_gains[1]]
        ).reshape(-1, d)
        for i in range(n.bit_length() - 1):
            gains = gains + swap(gains, 1 << i)
        gains = gains.reshape(-1)
        teams = sorted(
            sorted(i ^ b ^ p for b in range(4) for p in (0, PAIR_BIT))
            for i in range(0, n, 4)
            if not i & PAIR_BIT
        )
        hidden_out = residual_mid + lax.psum_scatter(
            down_part, AXES, scatter_dimension=0, axis_index_groups=teams, tiled=True
        ).astype(F32)
        return (
            hidden_out,
            grad_input,
            grad_w_query,
            grad_w_key,
            grad_w_value,
            grad_w_out,
            grad_w_gate,
            grad_w_up,
            grad_w_down,
            gains[:width],
            gains[width : 2 * width],
            gains[2 * width : 2 * width + d],
            gains[2 * width + d :],
        )

    return body


def solution(mesh):
    everyone = P(("fsdp", "ctx", "tp"), None)
    attn = P(("fsdp", "ctx"), "tp")
    attn_out = P("tp", ("fsdp", "ctx"))
    ff_in = P("fsdp", ("ctx", "tp"))
    ff_out = P(("ctx", "tp"), "fsdp")
    same = P()
    return jax.shard_map(
        build(mesh),
        mesh=mesh,
        in_specs=(
            everyone, everyone, P("fsdp"), attn, attn, attn, attn_out, ff_in, ff_in, ff_out,
            same, same, same, same,
        ),
        out_specs=(
            everyone, everyone, attn, attn, attn, attn_out, ff_in, ff_in, ff_out,
            same, same, same, same,
        ),
        check_vma=False,
    )
```

```python
import functools

import jax
import jax.numpy as jnp
from jax import lax
from jax.experimental import pallas as pl
from jax.experimental.pallas import tpu as pltpu
from jax.sharding import PartitionSpec as P

EPS = 1e-06
THETA = 1000000.0
AXES = ("fsdp", "ctx", "tp")
MESH = pl.DeviceIdType.MESH
BF16 = jnp.bfloat16
F32 = jnp.float32
TP_BIT, CTX_BIT = 1, 2
PAIR = 2
PAIR_BIT = PAIR * 4


def dot_rows(left, right):
    return lax.dot_general(left, right, (((0,), (0,)), ((), ())), preferred_element_type=F32)


def dot_cols(left, right):
    return lax.dot_general(left, right, (((1,), (1,)), ((), ())), preferred_element_type=F32)


def dot(left, right):
    return lax.dot_general(left, right, (((1,), (0,)), ((), ())), preferred_element_type=F32)


def remote(src, dst, send, recv, device):
    return pltpu.make_async_remote_copy(
        src_ref=src, dst_ref=dst, send_sem=send, recv_sem=recv, device_id=device, device_id_type=MESH
    )


class Moves:
    def __init__(self, send, recv, local):
        self.send, self.recv, self.local = send, recv, local
        self.sent, self.loads = 0, 0
        self.open = []

    def swap(self, src, there, here, device, open_=None):
        k = self.sent
        self.sent += 1
        copy = remote(src, there, self.send.at[k], self.recv.at[k], device)
        copy.start()
        (self.open if open_ is None else open_).append(copy.wait_send)
        return remote(src, here, self.send.at[k], self.recv.at[k], device).wait_recv

    def load(self, src, dst):
        k = self.loads
        self.loads += 1
        copy = pltpu.make_async_copy(src, dst, self.local.at[k])
        copy.start()
        return copy.wait

    def store(self, src, dst):
        self.open.append(self.load(src, dst))

    def close(self):
        for wait in self.open:
            wait()


class Place:
    def __init__(self, bits):
        self.bits = bits
        f, c, t = lax.axis_index("fsdp"), lax.axis_index("ctx"), lax.axis_index("tp")
        self.f, self.c, self.t = f, c, t
        self.pair = (f // PAIR) % 2
        far_f = self.block(PAIR)
        fs, cs = [f, f, far_f, far_f], [c, 1 - c, c, 1 - c]
        pairs = [self.pair, self.pair, 1 - self.pair, 1 - self.pair]
        self.at = [(fs[j], cs[j], pairs[j]) for j in range(4)]
        self.rows_of = [pairs[j] * 4 + cs[j] * 2 for j in range(4)]
        self.chunk_of = [cs[j] * 2 + pairs[j] for j in range(4)]
        self.relay = len(bits) == 2
        self.across_mask = bits[0] | PAIR
        self.inner = (f // bits[0]) % 2 != self.pair
        self.chips = [None, {"ctx": 1 - c}, {"fsdp": far_f}, {"fsdp": far_f, "ctx": 1 - c}]
        self.sibling = {"tp": 1 - t}

    def block(self, mask):
        out = self.f
        for i in range(mask.bit_length()):
            b = 1 << i
            if mask & b:
                out = out + b - 2 * b * ((self.f // b) % 2)
        return out

    def along(self, bit):
        return {"fsdp": self.block(bit)}

    def greet(self):
        barrier = pltpu.get_barrier_semaphore()
        devices = [*self.chips[1:], self.sibling, *[self.along(b) for b in self.bits]]
        if self.relay:
            devices.append(self.along(self.across_mask))
        for device in devices:
            pl.semaphore_signal(barrier, inc=1, device_id=device, device_id_type=MESH)
        pl.semaphore_wait(barrier, len(devices))


class Cross:
    def __init__(self, moves, place, src, here, came_in, across_to, came_out, pair_to):
        self.place, self.here = place, here
        self.came_in, self.came_out = came_in, came_out
        k = moves.sent
        moves.sent += 4
        pair, across = place.chips[2], place.along(place.across_mask)

        def copy(i, source, to, device):
            return remote(source, to, moves.send.at[k + i], moves.recv.at[k + i], device)

        self.hand = copy(0, src, came_in, pair)
        self.own = copy(1, src, came_out, across)
        self.on = copy(2, came_in, across_to, across)
        self.back = copy(3, came_out, pair_to, pair)
        self.came = [copy(0, came_in, came_in, pair), copy(1, came_out, came_out, across)]
        self.landed = [copy(2, here, here, across), copy(3, here, here, pair)]
        moves.open.append(self.left)

        @pl.when(place.inner)
        def _():
            self.own.start()

        @pl.when(jnp.logical_not(place.inner))
        def _():
            self.hand.start()

    def relay(self):
        @pl.when(self.place.inner)
        def _():
            self.came[0].wait_recv()
            self.on.start()
            self.came[1].wait_recv()
            self.back.start()

    def arrive(self):
        @pl.when(self.place.inner)
        def _():
            self.landed[0].wait_recv()

        @pl.when(jnp.logical_not(self.place.inner))
        def _():
            self.landed[1].wait_recv()

    def left(self):
        @pl.when(self.place.inner)
        def _():
            self.own.wait_send()
            self.on.wait_send()
            self.back.wait_send()

        @pl.when(jnp.logical_not(self.place.inner))
        def _():
            self.hand.wait_send()


class Spread:
    def __init__(self, moves, place, own, out):
        self.moves, self.place, self.out = moves, place, out
        self.rows = own.shape[0]
        self.open = []
        mine = self.at(0, place.t)
        self.here = moves.load(own, mine)
        self.pair = moves.swap(own, mine, self.at(2, place.t), place.chips[2], self.open)
        self.ctx = moves.swap(own, mine, self.at(1, place.t), place.chips[1], self.open)
        self.beside = [moves.swap(own, mine, self.at(0, 1 - place.t), place.sibling, self.open)]

    def at(self, j, t):
        start = (self.place.rows_of[j] + t) * self.rows
        return self.out.at[pl.ds(pl.multiple_of(start, self.rows), self.rows)]

    def hand(self, j):
        block = self.at(j, self.place.t)
        self.beside.append(
            self.moves.swap(block, block, self.at(j, 1 - self.place.t), self.place.sibling, self.open)
        )

    def from_pair(self):
        self.pair()
        block = self.at(2, self.place.t)
        self.both = self.moves.swap(block, block, self.at(3, self.place.t), self.place.chips[1], self.open)
        self.hand(2)

    def from_ctx(self):
        self.ctx()
        self.hand(1)

    def from_both(self):
        self.both()
        self.hand(3)

    def finish(self):
        self.here()
        for wait in (*self.beside, *self.open):
            wait()


class Collect:
    def __init__(self, moves, place, part, held, first, ctx_in, pair_in, sending, load):
        self.moves, self.place = moves, place
        self.first, self.ctx_in, self.pair_in, self.sending = first, ctx_in, pair_in, sending
        t = place.t
        self.hands, self.loads, self.open = {}, {}, []
        for j in (3, 1, 2, 0):
            self.hands[j] = moves.swap(part(j, 1 - t), first.at[j], first.at[j], place.sibling, self.open)
            if load:
                self.loads[j] = moves.load(part(j, t), held.at[j])
        self.held = (lambda j: held.at[j]) if load else (lambda j: part(j, t))

    def two(self, j, at):
        return self.held(j)[at].astype(F32) + self.first[j, at].astype(F32)

    def ready(self, j):
        self.hands[j]()
        if j in self.loads:
            self.loads[j]()

    def to_ctx(self):
        self.waits = {}
        for j, slot in ((3, 0), (1, 1)):
            self.ready(j)

            def body(at):
                self.sending[slot, at] = self.two(j, at).astype(BF16)

            row_loop(self.sending.shape[1], body)
            self.waits[j] = self.moves.swap(
                self.sending.at[slot], self.ctx_in.at[slot], self.ctx_in.at[slot], self.place.chips[1], self.open
            )

    def to_pair(self):
        self.ready(2)
        self.waits[3]()

        def body(at):
            self.sending[2, at] = (self.two(2, at) + self.ctx_in[0, at].astype(F32)).astype(BF16)

        row_loop(self.sending.shape[1], body)
        self.waits[2] = self.moves.swap(
            self.sending.at[2], self.pair_in, self.pair_in, self.place.chips[2], self.open
        )

    def fold(self):
        for j, slot in ((3, 0), (1, 1), (2, 2)):
            self.ready(j)

            def body(at):
                self.sending[slot, at] = self.two(j, at).astype(BF16)

            row_loop(self.sending.shape[1], body)
        self.ready(0)

    def post_ctx(self):
        self.waits = {}
        for j, slot in ((3, 0), (1, 1)):
            self.waits[j] = self.moves.swap(
                self.sending.at[slot], self.ctx_in.at[slot], self.ctx_in.at[slot], self.place.chips[1], self.open
            )

    def post_pair(self):
        self.waits[3]()

        def body(at):
            self.sending[2, at] = (self.sending[2, at].astype(F32) + self.ctx_in[0, at].astype(F32)).astype(BF16)

        row_loop(self.sending.shape[1], body)
        self.waits[2] = self.moves.swap(
            self.sending.at[2], self.pair_in, self.pair_in, self.place.chips[2], self.open
        )

    def came(self):
        for wait in (self.waits[1], self.waits[2], *self.open):
            wait()

    def finish(self):
        self.ready(0)
        self.waits[1]()
        self.waits[2]()
        for wait in self.open:
            wait()

    def total(self, at):
        return self.two(0, at) + (self.ctx_in[1, at].astype(F32) + self.pair_in[at].astype(F32))


def collect_buffers(rows, width):
    return [
        pltpu.VMEM((4, rows, width), BF16),
        pltpu.VMEM((2, rows, width), BF16),
        pltpu.VMEM((rows, width), BF16),
        pltpu.VMEM((3, rows, width), BF16),
    ]


def row_loop(rows, body):
    step = 16

    @pl.loop(0, rows // step)
    def _(i):
        body(pl.ds(pl.multiple_of(i * step, step), step))


def unit_and_scale(x):
    scale = lax.rsqrt(jnp.mean(x * x, axis=-1, keepdims=True) + EPS)
    return x * scale, scale


class Gather:
    def __init__(self, moves, place, block, spare):
        self.moves, self.place, self.block, self.spare = moves, place, block, spare
        self.waits, self.crosses = {}, {}

    def forward(self, mask, src=None):
        done = [i for i, b in enumerate(self.place.bits) if mask & b]
        here = self.block(self.place.block(mask))
        for b in self.place.bits[max(done, default=-1) + 1 :]:
            if self.place.relay and b == self.place.bits[0]:
                far = self.place.across_mask
                slot = 0 if mask == 0 else 2
                self.crosses[mask] = Cross(
                    self.moves, self.place, here if src is None else src, self.block(self.place.block(mask | b)),
                    self.spare.at[slot], self.block(self.place.block(mask ^ PAIR)),
                    self.spare.at[slot + 1], self.block(self.place.block(mask ^ far)),
                )
                self.waits[mask | b] = self.crosses[mask].arrive
                continue
            self.waits[mask | b] = self.moves.swap(
                here if src is None else src, here, self.block(self.place.block(mask | b)), self.place.along(b)
            )

    def masks(self, stage):
        out = [0, PAIR]
        for b in self.place.bits[:stage]:
            out += [m | b for m in out]
        return [m | self.place.bits[stage] for m in out]

    def relay(self):
        for m in list(self.crosses):
            self.crosses.pop(m).relay()

    def pass_on(self, m):
        self.waits.pop(m)()
        self.forward(m)

    def middle(self):
        self.relay()
        for stage in range(len(self.place.bits) - 1):
            for m in self.masks(stage):
                if m in self.waits:
                    self.pass_on(m)

    def finish(self):
        for wait in self.waits.values():
            wait()


def head_unit(x):
    scale = lax.rsqrt(jnp.mean(x * x, axis=-1, keepdims=True) + EPS)
    return x * scale, scale


def rot(a, cos, sin):
    return a * cos + pltpu.roll(a, a.shape[-1] // 2, 1) * sin


def rot_back(b, cos, sin):
    return b * cos - pltpu.roll(b, b.shape[-1] // 2, 1) * sin


def allowed_keys(start):
    length = start.shape[0]
    row = lax.broadcasted_iota(jnp.int32, (length, length), 0)
    col = lax.broadcasted_iota(jnp.int32, (length, length), 1)
    return (col.astype(F32) >= start) & (row >= col)


def soft_of(scores):
    peak = jnp.max(scores, axis=-1, keepdims=True)
    lse = peak + jnp.log(jnp.sum(jnp.exp(scores - peak), axis=-1, keepdims=True))
    return jnp.exp(scores - lse)


def attend_one(groups, s, qkv, starts, cos_ref, sin_ref, gain_q, gain_k, out):
    d = gain_q.shape[-1]
    length = cos_ref.shape[0] // 2
    rows = pl.ds(pl.multiple_of(s * length, length), length)
    cos, sin = cos_ref[rows], sin_ref[rows]
    allowed = allowed_keys(starts[rows, 0:1])
    unit_k, _ = head_unit(qkv[rows, groups * d : (groups + 1) * d].astype(F32))
    key = rot(unit_k * gain_k[...], cos, sin).astype(BF16)
    value = qkv[rows, (groups + 1) * d : (groups + 2) * d]
    for g in range(groups):
        unit_q, _ = head_unit(qkv[rows, g * d : (g + 1) * d].astype(F32))
        query = rot(unit_q * gain_q[...], cos, sin).astype(BF16)
        scores = jnp.where(allowed, dot_cols(query, key) * d**-0.5, -jnp.inf)
        soft = soft_of(scores).astype(BF16)
        out[rows, g * d : (g + 1) * d] = dot(soft, value).astype(BF16)


def through_norm(b, unit, scale, gain):
    e = b * gain
    return scale * (e - unit * jnp.mean(e * unit, axis=-1, keepdims=True))


def attend_back_one(
    groups, s, qkv, att, datt, starts, cos_ref, sin_ref, gain_q, gain_k, grad, gains
):
    d = gain_q.shape[-1]
    length = cos_ref.shape[0] // 2
    rows = pl.ds(pl.multiple_of(s * length, length), length)
    cos, sin = cos_ref[rows], sin_ref[rows]
    scale = d**-0.5
    allowed = allowed_keys(starts[rows, 0:1])
    at_k, at_v = slice(groups * d, (groups + 1) * d), slice((groups + 1) * d, (groups + 2) * d)
    unit_k, scale_k = head_unit(qkv[rows, at_k].astype(F32))
    key = rot(unit_k * gain_k[...], cos, sin).astype(BF16)
    value = qkv[rows, at_v]
    key_grad = jnp.zeros(unit_k.shape, F32)
    value_grad = jnp.zeros(unit_k.shape, F32)
    for g in range(groups):
        at = slice(g * d, (g + 1) * d)
        unit_q, scale_q = head_unit(qkv[rows, at].astype(F32))
        query = rot(unit_q * gain_q[...], cos, sin).astype(BF16)
        scores = jnp.where(allowed, dot_cols(query, key) * scale, -jnp.inf)
        soft = soft_of(scores)
        up = datt[rows, at]
        delta = jnp.sum(up.astype(F32) * att[rows, at].astype(F32), axis=-1, keepdims=True)
        ds = (soft * (dot_cols(up, value) - delta) * scale).astype(BF16)
        value_grad += dot_rows(soft.astype(BF16), up)
        key_grad += dot_rows(ds, query)
        b = rot_back(dot(ds, key), cos, sin)
        gains[0] += jnp.sum((b * unit_q).reshape(-1, 8, d), axis=0)
        grad[rows, at] = through_norm(b, unit_q, scale_q, gain_q[...]).astype(BF16)
    b = rot_back(key_grad, cos, sin)
    gains[1] += jnp.sum((b * unit_k).reshape(-1, 8, d), axis=0)
    grad[rows, at_k] = through_norm(b, unit_k, scale_k, gain_k[...]).astype(BF16)
    grad[rows, at_v] = value_grad.astype(BF16)


def attend_back_kernel(
    groups, qkv, att, datt, starts, cos, sin, gain_q, gain_k, grad, gains
):
    gains[...] = jnp.zeros_like(gains)

    @pl.loop(0, 2)
    def _(s):
        attend_back_one(groups, s, qkv, att, datt, starts, cos, sin, gain_q, gain_k, grad, gains)


def attend_back(groups, qkv, att, datt, common):
    n_rows, width = qkv.shape
    d = width // (groups + 2)
    length = n_rows // 2
    return pl.pallas_call(
        functools.partial(attend_back_kernel, groups),
        out_shape=(jax.ShapeDtypeStruct(qkv.shape, BF16), jax.ShapeDtypeStruct((2, 8, d), F32)),
        compiler_params=pltpu.CompilerParams(vmem_limit_bytes=40 << 20),
        cost_estimate=pl.CostEstimate(
            flops=n_rows * groups * length * (10 * d + 30),
            bytes_accessed=n_rows * width * 8,
            transcendentals=n_rows * groups * length * 2,
        ),
        name="attend_back",
    )(qkv, att, datt, *common)


def forward_kernel(
    bits, groups, natural,
    hidden, cot, gain_attn, gain_mlp, seg, table, gain_q, gain_k, wq, wk, wv, wo, wg, wu, wd,
    mid, normed_one, normed_two, cot_out, qkv_out, att_out, qkv_weight, out_weight, starts_out, cos_out, sin_out,
    grad_gate_out, grad_up_out, mixed_out, part_out, down_out, spare_qkv, spare_out, spare_gate, spare_up, spare_down,
    own_one, own_two, rows_one, rows_two, rows_cot, w_qkv, w_out, w_gate, w_up, w_down, qkv, att, part,
    gate, up, grad_gate, grad_up, mixed, mixed_t, starts, cos, sin, seg_in, first, ctx_in, pair_in, sending,
    send, recv, local,
):
    place = Place(bits)
    moves = Moves(send, recv, local)
    rows, width = hidden.shape
    at_rows, ff_rows, ff_cols = wq.shape[0], wg.shape[0], wg.shape[1] // 2
    q_cols, kv_cols = wq.shape[1] // 4, wk.shape[1] // 4
    n_rows, length = rows_one.shape[0], seg.shape[1]

    def lanes(start, size):
        return pl.ds(pl.multiple_of(start, size), size)

    def qkv_rows(f, c=None):
        if c is None:
            return lanes(f * 2 * at_rows, 2 * at_rows)
        return lanes((f * 2 + c) * at_rows, at_rows)

    place.greet()

    def out_block(f, c=None):
        return w_out.at[:, qkv_rows(f, c)] if natural else w_out.at[qkv_rows(f, c)]

    def out_chunk(j):
        at = lanes(place.chunk_of[j] * q_cols, q_cols)
        return wo.at[at] if natural else wo.at[:, at]

    pieces = (
        (wq, q_cols, pl.ds(0, q_cols)),
        (wk, kv_cols, pl.ds(q_cols, kv_cols)),
        (wv, kv_cols, pl.ds(q_cols + kv_cols, kv_cols)),
    )
    f0, c0, _ = place.at[0]
    qkv_in, out_in = {}, {}
    for j in (1, 3, 2):
        fj, cj, _ = place.at[j]
        qkv_in[j] = [
            moves.swap(
                w.at[:, lanes(place.chunk_of[j] * size, size)],
                w_qkv.at[qkv_rows(f0, c0), to],
                w_qkv.at[qkv_rows(fj, cj), to],
                place.chips[j],
            )
            for w, size, to in pieces
        ]
    qkv_in[0] = [
        moves.load(w.at[:, lanes(place.chunk_of[0] * size, size)], w_qkv.at[qkv_rows(f0, c0), to])
        for w, size, to in pieces
    ]
    seg_wait = moves.swap(seg, seg_in, seg_in, place.chips[2])

    def norm_one(at):
        unit, _ = unit_and_scale(hidden[at].astype(F32))
        own_one[at] = (unit * gain_attn[...]).astype(BF16)

    row_loop(rows, norm_one)
    def rows_block(w):
        return lambda f: w.at[lanes(f * ff_rows, ff_rows)]

    def cols_block(w):
        return lambda f: w.at[:, lanes(f * ff_rows, ff_rows)]

    mine, theirs = lanes(place.pair * ff_cols, ff_cols), lanes((1 - place.pair) * ff_cols, ff_cols)
    feed = [
        (Gather(moves, place, rows_block(w_gate), spare_gate), wg.at[:, mine], wg.at[:, theirs]),
        (Gather(moves, place, rows_block(w_up), spare_up), wu.at[:, mine], wu.at[:, theirs]),
        (Gather(moves, place, cols_block(w_down), spare_down), wd.at[mine], wd.at[theirs])
        if natural
        else (Gather(moves, place, rows_block(w_down), spare_down), wd.at[:, mine], wd.at[:, theirs]),
    ]
    own_feed = [moves.load(own, gather.block(place.f)) for gather, own, _ in feed]

    def swap_pair(i):
        gather, _, other = feed[i]
        gather.waits[PAIR] = moves.swap(
            other, gather.block(place.f), gather.block(place.block(PAIR)), place.along(PAIR)
        )

    def send_feed(i):
        gather, own, _ = feed[i]
        gather.forward(0, own)
        gather.pass_on(PAIR)

    qkv_gather = Gather(moves, place, lambda f: w_qkv.at[qkv_rows(f)], spare_qkv)
    out_gather = Gather(moves, place, out_block, spare_out)

    def send_attn(gather, arrivals):
        for wait in (*arrivals[0], *arrivals[1]):
            wait()
        gather.forward(0)
        for wait in (*arrivals[2], *arrivals[3]):
            wait()
        gather.forward(PAIR)

    send_attn(qkv_gather, qkv_in)
    for j in (3, 2, 1):
        fj, cj, _ = place.at[j]
        out_in[j] = moves.swap(out_chunk(j), out_block(f0, c0), out_block(fj, cj), place.chips[j])
    out_in[0] = moves.load(out_chunk(0), out_block(f0, c0))
    spread_one = Spread(moves, place, own_one, rows_one)
    swap_pair(0)
    swap_pair(1)
    seg_wait()
    pair_first = place.pair == 0
    own_seg, far_seg = seg[...].astype(F32), seg_in[...].astype(F32)
    for i in range(2):
        here = pair_first if i == 0 else jnp.logical_not(pair_first)
        flags = jnp.where(here, own_seg, far_seg)
        both = jnp.broadcast_to(flags, (128, length)).T[:, 0:1]
        start = jnp.sum((flags < both).astype(F32), axis=1, keepdims=True)
        row = lax.broadcasted_iota(jnp.int32, (length, length), 0).astype(F32)
        col = lax.broadcasted_iota(jnp.int32, (length, length), 1).astype(F32)
        chosen = (row - start == col).astype(F32)
        at = pl.ds(i * length, length)
        both_tables = lax.dot_general(
            chosen, table[...], (((1,), (0,)), ((), ())),
            precision=lax.Precision.HIGHEST, preferred_element_type=F32,
        )
        d = gain_q.shape[1]
        starts[at] = jnp.broadcast_to(start, (length, 128))
        cos[at] = both_tables[:, :d]
        sin[at] = both_tables[:, d:]
    moves.store(starts, starts_out)
    moves.store(cos, cos_out)
    moves.store(sin, sin_out)
    qkv_gather.relay()
    spread_one.from_pair()
    send_attn(out_gather, {j: [w] for j, w in out_in.items()})
    qkv_gather.middle()
    spread_one.from_ctx()
    send_feed(0)
    out_gather.relay()
    spread_one.from_both()
    spread_one.finish()
    send_feed(1)
    swap_pair(2)
    qkv_gather.finish()
    step = 2 * rows

    wide = min(256, w_qkv.shape[1])

    @pl.loop(0, w_qkv.shape[1] // wide)
    def _(i):
        at = lanes(i * wide, wide)
        qkv[:, at] = dot(rows_one[...], w_qkv[:, at]).astype(BF16)

    moves.store(qkv, qkv_out)
    normed_stored = moves.load(rows_one, normed_one)
    moves.store(w_qkv, qkv_weight)
    out_gather.middle()
    feed[0][0].relay()

    @pl.loop(0, 2)
    def _(s):
        attend_one(groups, s, qkv, starts, cos, sin, gain_q, gain_k, att)

    moves.store(att, att_out)
    out_gather.finish()

    def columns_of(weight, at):
        return (dot, weight[:, at]) if natural else (dot_cols, weight[at])

    @pl.loop(0, width // 256)
    def _(i):
        at = lanes(i * 256, 256)
        times, block = columns_of(w_out, at)
        part[:, :, at] = times(att[...], block).astype(BF16).reshape(8, rows, 256)

    moves.store(w_out, out_weight)
    collect = Collect(
        moves, place, lambda j, t: part.at[place.rows_of[j] + t], None, first, ctx_in, pair_in, sending, False
    )
    collect.to_ctx()
    feed[0][0].middle()
    feed[1][0].relay()
    collect.to_pair()
    send_feed(2)
    feed[1][0].middle()
    collect.finish()

    def norm_two(at):
        x = hidden[at].astype(F32) + collect.total(at)
        mid[at] = x
        unit, _ = unit_and_scale(x)
        own_two[at] = (unit * gain_mlp[...]).astype(BF16)

    row_loop(rows, norm_two)
    spread_two = Spread(moves, place, own_two, rows_two)
    spread_cot = Spread(moves, place, cot, rows_cot)
    feed[2][0].relay()
    spread_two.from_pair()
    spread_two.from_ctx()
    spread_two.from_both()
    feed[2][0].middle()
    spread_two.finish()
    moves.store(rows_two, normed_two)
    for wait in own_feed:
        wait()
    feed[0][0].finish()

    @pl.loop(0, n_rows // step)
    def _(i):
        at = lanes(i * step, step)
        gate[at] = dot(rows_two[at], w_gate[...])

    spread_cot.from_pair()
    spread_cot.from_ctx()
    feed[1][0].finish()

    @pl.loop(0, n_rows // step)
    def _(i):
        at = lanes(i * step, step)
        u = dot(rows_two[at], w_up[...])
        up[at] = u
        g = gate[at]
        mix = g * jax.nn.sigmoid(g) * u
        mixed[at] = mix.astype(BF16)
        mixed_t[:, at] = mix.T.astype(BF16)

    moves.store(mixed_t, mixed_out)
    spread_cot.from_both()
    spread_cot.finish()
    moves.store(rows_cot, cot_out)
    normed_stored()
    feed[2][0].finish()

    @pl.loop(0, n_rows // step)
    def _(i):
        at = lanes(i * step, step)
        m = (dot_cols if natural else dot)(rows_cot[at], w_down[...])
        g = gate[at]
        s = jax.nn.sigmoid(g)
        grad_gate[at] = (m * up[at] * s * (1.0 + g * (1.0 - s))).astype(BF16)
        grad_up[at] = (m * (g * s)).astype(BF16)

    moves.store(grad_gate, grad_gate_out)
    moves.store(grad_up, grad_up_out)

    @pl.loop(0, width // 256)
    def _(i):
        at = lanes(i * 256, 256)
        both = dot_cols(grad_gate[...], w_gate[at]) + dot_cols(grad_up[...], w_up[at])
        part[:, :, at] = both.astype(BF16).reshape(8, rows, 256)

    moves.store(part, part_out)

    @pl.loop(0, width // 256)
    def _(i):
        at = lanes(i * 256, 256)
        times, block = columns_of(w_down, at)
        rows_one[:, at] = times(mixed[...], block).astype(BF16)

    moves.store(rows_one, down_out)
    moves.close()


def norm_back(grad, x, gain, gain_grad):
    unit, scale = unit_and_scale(x)
    gain_grad[...] += jnp.sum((grad * unit).reshape(-1, 8, grad.shape[-1]), axis=0)
    e = grad * gain
    return scale * (e - unit * jnp.mean(e * unit, axis=-1, keepdims=True))


def turn_kernel(
    bits, partial, mid, cot, gain, grad_mid, gain_grad, out,
    own, held, first, ctx_in, pair_in, sending, send, recv, local,
):
    place = Place(bits)
    moves = Moves(send, recv, local)
    place.greet()
    collect = Collect(
        moves, place, lambda j, t: partial.at[place.rows_of[j] + t], held, first, ctx_in, pair_in, sending, True
    )
    collect.to_ctx()
    collect.to_pair()
    collect.finish()
    gain_grad[...] = jnp.zeros_like(gain_grad)

    def back(at):
        g = cot[at].astype(F32) + norm_back(collect.total(at), mid[at], gain[...], gain_grad)
        grad_mid[at] = g
        own[at] = g.astype(BF16)

    row_loop(mid.shape[0], back)
    spread = Spread(moves, place, own, out)
    spread.from_pair()
    spread.from_ctx()
    spread.from_both()
    spread.finish()
    moves.close()


def last_kernel(
    bits, partial, hidden, grad_mid, gain, grad_in, gain_grad,
    held, first, ctx_in, pair_in, sending, send, recv, local,
):
    place = Place(bits)
    moves = Moves(send, recv, local)
    place.greet()
    collect = Collect(
        moves, place, lambda j, t: partial.at[place.rows_of[j] + t], held, first, ctx_in, pair_in, sending, True
    )
    collect.to_ctx()
    collect.to_pair()
    collect.finish()
    gain_grad[...] = jnp.zeros_like(gain_grad)

    def back(at):
        grad_in[at] = grad_mid[at] + norm_back(
            collect.total(at), hidden[at].astype(F32), gain[...], gain_grad
        )

    row_loop(hidden.shape[0], back)
    moves.close()


class Scatter:
    def __init__(self, moves, place, product, out0, in0, out1, in1, acc, acc_pair, spare):
        self.moves, self.place, self.product, self.spare = moves, place, product, spare
        self.out0, self.in0, self.out1, self.in1, self.acc, self.acc_pair = out0, in0, out1, in1, acc, acc_pair
        self.low, self.high = place.bits[1], place.bits[0]
        self.order = [self.high, self.high | PAIR, 0, PAIR]
        self.first, self.second, self.leaving = {}, {}, {}

    def send(self, i):
        slot = i % 2
        for wait in self.leaving.pop(slot, []):
            wait()

        def emit(at, value):
            self.out0[(slot, *at)] = value.astype(BF16)

        self.product(self.order[i] | self.low, emit)
        self.leaving[slot] = []
        self.first[i] = self.moves.swap(
            self.out0.at[slot], self.in0.at[i], self.in0.at[i], self.place.along(self.low), self.leaving[slot]
        )

    def take(self, i):
        self.first[i]()

        def emit(at, value):
            value = value + self.in0[(i, *at)].astype(F32)
            if i < 2:
                self.out1[(i, *at)] = value.astype(BF16)
            elif i == 2:
                self.acc[at] = value
            else:
                self.acc_pair[at] = value.astype(BF16)

        self.product(self.order[i], emit)
        if i < 2:
            to = self.in1.at[i]
            self.second[i] = Cross(
                self.moves, self.place, self.out1.at[i], to, self.spare.at[2 * i], to, self.spare.at[2 * i + 1], to
            )

    def relay(self, i):
        self.second[i].relay()

    def take_high(self, i):
        self.second[i].arrive()
        total = self.acc_pair if i else self.acc
        step = 64

        @pl.loop(0, total.shape[0] // step)
        def _(k):
            at = pl.ds(pl.multiple_of(k * step, step), step)
            total[at] = (total[at].astype(F32) + self.in1[i, at].astype(F32)).astype(total.dtype)

    def close(self):
        for waits in self.leaving.values():
            for wait in waits:
                wait()


class Blocks:
    def __init__(self, moves, place, slots, order):
        self.moves, self.place, self.slots, self.order = moves, place, slots, order
        self.next, self.waits = 0, {}
        self.start(0)

    def start(self, k):
        if k < len(self.order):
            ref, mask = self.order[k]
            size = self.slots.shape[2]
            at = pl.ds(pl.multiple_of(self.place.block(mask) * size, size), size)
            self.waits[k] = self.moves.load(ref.at[:, at], self.slots.at[k % 2])

    def get(self, ref, mask):
        k = self.next
        assert self.order[k][0] is ref and self.order[k][1] == mask
        self.next += 1
        self.waits.pop(k)()
        self.start(k + 1)
        return self.slots[k % 2]


def backward_kernel(
    bits, groups,
    cot, gain_attn, gain_mlp, starts, cos, sin, gain_q, gain_k,
    mid, hidden, part_two, part_hidden, normed_one, normed_two, cot_rows, qkv_in, att_in, qkv_weight, out_weight, grad_gate, grad_up,
    mixed_t,
    grad_in, hidden_out, gains, feed_own, feed_other, down_own, down_other, qkv_own, qkv_other, out_own, out_other,
    spare_feed, spare_down, spare_qkv, spare_out,
    own, rows_mid, feed, mixed, lhs, lhs_t, part, w_qkv, w_out, qkv, att, datt, dqkv,
    first, ctx_in, pair_in, sending, first_h, ctx_h, pair_h, sending_h, gain_a, gain_m, gain_h, tree, tree_in,
    f_out0, f_in0, f_out1, f_in1, f_acc, f_pair, d_out0, d_in0, d_out1, d_in1, d_acc, d_pair,
    q_out0, q_in0, q_out1, q_in1, q_acc, q_pair, o_out0, o_in0, o_out1, o_in1, o_acc, o_pair,
    send, recv, local,
):
    place = Place(bits)
    moves = Moves(send, recv, local)
    rows, width = cot.shape
    cols = mixed.shape[0]
    tile = lhs.shape[2]
    half = tile // 2
    high, low = bits
    place.greet()

    def lanes(start, size):
        return pl.ds(pl.multiple_of(start, size), size)

    ready_mid = moves.load(mid, hidden_out)
    ready_feed = [
        moves.load(grad_gate, feed.at[:, pl.ds(0, cols)]),
        moves.load(grad_up, feed.at[:, pl.ds(cols, cols)]),
    ]
    collect_two = Collect(
        moves, place, lambda j, t: part_two.at[place.rows_of[j] + t], part, first, ctx_in, pair_in, sending, True
    )
    masks = [high, high | PAIR, 0, PAIR]
    sends = [m | low for m in masks]
    a, b, c, e = range(4)
    order = [
        (cot_rows, sends[a]), (cot_rows, sends[b]), (normed_two, sends[a]), (cot_rows, masks[a]),
        (normed_two, sends[b]), (cot_rows, masks[b]), (normed_two, masks[a]), (cot_rows, sends[e]),
        (cot_rows, sends[c]), (normed_two, sends[e]), (normed_two, masks[b]), (normed_one, sends[a]),
        (normed_one, sends[b]), (normed_one, sends[e]), (cot_rows, masks[e]), (cot_rows, masks[c]),
        (normed_two, masks[e]), (normed_two, sends[c]), (normed_one, sends[c]), (normed_one, masks[a]),
        (normed_one, masks[b]), (normed_one, masks[e]), (normed_two, masks[c]), (normed_one, masks[c]),
    ]
    blocks = Blocks(moves, place, lhs, order)
    ready_mixed = moves.load(mixed_t, mixed)
    ready_late = [
        moves.load(out_weight, w_out),
        moves.load(att_in, att),
        moves.load(qkv_in, qkv),
        moves.load(qkv_weight, w_qkv),
    ]

    def by_rows(source, right):
        def product(mask, emit):
            lhs_t[...] = blocks.get(source, mask).T
            step = min(512, right.shape[1])

            @pl.loop(0, right.shape[1] // step)
            def _(i):
                at = lanes(i * step, step)
                emit((slice(None), at), dot(lhs_t[...], right[:, at]))

        return product

    def down_product(mask, emit):
        block = blocks.get(cot_rows, mask)
        step = min(256, cols)

        @pl.loop(0, cols // step)
        def _(i):
            at = lanes(i * step, step)
            emit((at, slice(None)), dot(mixed[at], block))

    def out_product(mask, emit):
        at = lanes(place.block(mask) * tile, tile)
        emit((slice(None), slice(None)), dot_rows(att[...], rows_mid[:, at]))

    feed_s = Scatter(moves, place, by_rows(normed_two, feed), f_out0, f_in0, f_out1, f_in1, f_acc, f_pair, spare_feed)
    down_s = Scatter(moves, place, down_product, d_out0, d_in0, d_out1, d_in1, d_acc, d_pair, spare_down)
    qkv_s = Scatter(moves, place, by_rows(normed_one, dqkv), q_out0, q_in0, q_out1, q_in1, q_acc, q_pair, spare_qkv)
    out_s = Scatter(moves, place, out_product, o_out0, o_in0, o_out1, o_in1, o_acc, o_pair, spare_out)

    ready_mixed()
    down_s.send(a)
    down_s.send(b)
    collect_two.to_ctx()
    for wait in ready_feed:
        wait()
    feed_s.send(a)
    down_s.take(a)
    feed_s.send(b)
    collect_two.to_pair()
    collect_hidden = Collect(
        moves, place, lambda j, t: part_hidden.at[place.rows_of[j] + t], part.at[pl.ds(4, 4)],
        first_h, ctx_h, pair_h, sending_h, True,
    )
    down_s.relay(a)
    down_s.take(b)

    collect_hidden.fold()
    ready_mid()
    collect_two.finish()
    gain_m[...] = jnp.zeros_like(gain_m)
    gain_a[...] = jnp.zeros_like(gain_a)
    gain_h[...] = jnp.zeros_like(gain_h)

    def back_two(at):
        x = hidden_out[at]
        g = cot[at].astype(F32) + norm_back(collect_two.total(at), x, gain_mlp[...], gain_m)
        hidden_out[at] = x + collect_hidden.two(0, at)
        grad_in[at] = g
        own[at] = g.astype(BF16)

    row_loop(rows, back_two)
    spread = Spread(moves, place, own, rows_mid)
    down_s.relay(b)
    feed_s.take(a)
    down_s.send(e)
    spread.from_pair()
    down_s.send(c)
    spread.from_ctx()
    feed_s.send(e)
    feed_s.relay(a)
    spread.from_both()
    for wait in ready_late:
        wait()
    spread.finish()
    ready_hidden = moves.load(hidden, own)
    collect_hidden.post_ctx()

    @pl.loop(0, 4)
    def _(i):
        at = lanes(i * 2 * rows, 2 * rows)
        datt[at] = dot_cols(rows_mid[at], w_out[...]).astype(BF16)

    feed_s.take(b)

    @pl.loop(0, 2)
    def _(s):
        attend_back_one(groups, s, qkv, att, datt, starts, cos, sin, gain_q, gain_k, dqkv, gain_h)

    @pl.loop(0, width // tile)
    def _(i):
        at = lanes(i * tile, tile)
        part[:, :, at] = dot_cols(dqkv[...], w_qkv[at]).astype(BF16).reshape(8, rows, tile)

    collect_one = Collect(
        moves, place, lambda j, t: part.at[place.rows_of[j] + t], None, first, ctx_in, pair_in, sending, False
    )
    qkv_s.send(a)
    qkv_s.send(b)
    out_s.send(a)
    out_s.send(b)
    collect_one.to_ctx()
    feed_s.relay(b)
    collect_hidden.post_pair()
    qkv_s.send(e)
    out_s.send(e)
    down_s.take(e)
    down_s.take(c)
    feed_s.take(e)
    collect_one.to_pair()
    feed_s.send(c)
    qkv_s.send(c)
    out_s.send(c)
    qkv_s.take(a)
    qkv_s.take(b)
    out_s.take(a)
    out_s.take(b)
    collect_one.finish()

    ready_hidden()

    def back_one(at):
        grad_in[at] += norm_back(collect_one.total(at), own[at].astype(F32), gain_attn[...], gain_a)

    row_loop(rows, back_one)

    d = gain_q.shape[1]
    tree[0, :, 0:width] = jnp.sum(gain_a[...], axis=0, keepdims=True)
    tree[0, :, width : 2 * width] = jnp.sum(gain_m[...], axis=0, keepdims=True)
    tree[0, :, 2 * width : 2 * width + d] = jnp.sum(gain_h[0], axis=0, keepdims=True)
    tree[0, :, 2 * width + d : 2 * width + 2 * d] = jnp.sum(gain_h[1], axis=0, keepdims=True)
    partners = [place.sibling, place.chips[1], *[place.along(x) for x in bits], place.chips[2]]
    tree_waits = []

    def climb():
        k = len(tree_waits)
        if k:
            tree_waits[-1]()
            tree[k] = tree[k - 1] + tree_in[k - 1]
        if k < len(partners):
            tree_waits.append(moves.swap(tree.at[k], tree_in.at[k], tree_in.at[k], partners[k]))

    finals = []

    def pair_final(scatter, other):
        scatter.take_high(1)
        finals.append(moves.swap(scatter.acc_pair, other, other, place.chips[2]))

    def own_final(scatter, mine):
        scatter.take_high(0)
        moves.store(scatter.acc, mine)

    def mates_final(scatter, slot, piece, spare, other):
        scatter.take_high(slot)
        for j in (3, 2) if slot else (1,):
            out = spare(j)
            out[...] = piece(slot, place.at[j][1]).astype(BF16)
            finals.append(moves.swap(out, other.at[j - 1], other.at[j - 1], place.chips[j]))

    def qkv_piece(slot, c):
        return (q_pair if slot else q_acc)[lanes(c * half, half)]

    def out_piece(slot, c):
        return (o_pair if slot else o_acc)[:, lanes(c * half, half)]

    def qkv_spare(j):
        return q_in0.at[j, pl.ds(0, half)]

    def out_spare(j):
        return o_in0.at[j, :, pl.ds(0, half)]

    climb()
    qkv_s.relay(a)
    qkv_s.relay(b)
    out_s.relay(a)
    out_s.relay(b)
    climb()
    pair_final(down_s, down_other)
    climb()
    own_final(down_s, down_own)
    qkv_s.take(e)
    out_s.take(e)
    climb()
    collect_hidden.came()

    def end_hidden(at):
        hidden_out[at] += ctx_h[1, at].astype(F32) + pair_h[at].astype(F32)

    row_loop(rows, end_hidden)
    pair_final(feed_s, feed_other)
    climb()
    feed_s.take(c)
    qkv_s.take(c)
    out_s.take(c)
    mates_final(qkv_s, 1, qkv_piece, qkv_spare, qkv_other)
    mates_final(out_s, 1, out_piece, out_spare, out_other)
    own_final(feed_s, feed_own)
    mates_final(qkv_s, 0, qkv_piece, qkv_spare, qkv_other)
    mates_final(out_s, 0, out_piece, out_spare, out_other)
    qkv_own[...] = qkv_piece(0, place.c)
    out_own[...] = out_piece(0, place.c)
    climb()
    gains[...] = tree[len(partners)]
    for scatter in (feed_s, down_s, qkv_s, out_s):
        scatter.close()
    for wait in finals:
        wait()
    moves.close()


def join_kernel(
    feed_own, feed_other, down_own, down_other, qkv_own, qkv_other, out_own, out_other, grad_in, hidden, gains,
    g_query, g_key, g_value, g_out, g_gate, g_up, g_down, g_in, h_out, gain_a, gain_m, gain_q, gain_k,
):
    c = lax.axis_index("ctx")
    pair = (lax.axis_index("fsdp") // PAIR) % 2
    cols, n_q = down_own.shape[0], out_own.shape[0]
    n_kv = (qkv_own.shape[1] - n_q) // 2

    def lanes(start, size):
        return pl.ds(pl.multiple_of(start, size), size)

    mine, theirs = lanes(pair * cols, cols), lanes((1 - pair) * cols, cols)
    g_gate[:, mine] = feed_own[:, :cols]
    g_up[:, mine] = feed_own[:, cols:]
    g_down[mine] = down_own[...]
    g_gate[:, theirs] = feed_other[:, :cols].astype(F32)
    g_up[:, theirs] = feed_other[:, cols:].astype(F32)
    g_down[theirs] = down_other[...].astype(F32)
    chunks = [c * 2 + pair, (1 - c) * 2 + pair, c * 2 + 1 - pair, (1 - c) * 2 + 1 - pair]
    for j, chunk in enumerate(chunks):
        qkv = qkv_own[...] if j == 0 else qkv_other[j - 1].astype(F32)
        g_query[:, lanes(chunk * n_q, n_q)] = qkv[:, :n_q]
        g_key[:, lanes(chunk * n_kv, n_kv)] = qkv[:, n_q : n_q + n_kv]
        g_value[:, lanes(chunk * n_kv, n_kv)] = qkv[:, n_q + n_kv :]
        g_out[lanes(chunk * n_q, n_q)] = out_own[...] if j == 0 else out_other[j - 1].astype(F32)
    g_in[...] = grad_in[...]
    h_out[...] = hidden[...]
    width, d = gain_a.shape[1], gain_q.shape[1]
    gain_a[...] = gains[:, :width]
    gain_m[...] = gains[:, width : 2 * width]
    gain_q[...] = gains[:, 2 * width : 2 * width + d]
    gain_k[...] = gains[:, 2 * width + d :]


VMEM_SPEC = pl.BlockSpec(memory_space=pltpu.VMEM)
ANY_SPEC = pl.BlockSpec(memory_space=pl.ANY)


def comm_call(kernel, bits, collective_id, operands, in_specs, outs, out_specs, scratch, nbytes, copies, *more):
    return pl.pallas_call(
        functools.partial(kernel, bits, *more),
        out_shape=outs,
        in_specs=in_specs,
        out_specs=out_specs,
        scratch_shapes=[
            *scratch,
            pltpu.SemaphoreType.DMA((copies,)),
            pltpu.SemaphoreType.DMA((copies,)),
            pltpu.SemaphoreType.DMA((96,)),
        ],
        compiler_params=pltpu.CompilerParams(
            collective_id=collective_id, has_side_effects=True, vmem_limit_bytes=61 << 20
        ),
        cost_estimate=pl.CostEstimate(flops=nbytes * 20, bytes_accessed=nbytes, transcendentals=0),
        name=kernel.__name__,
    )(*operands)


def build(mesh):
    n = mesh.size
    n_f = mesh.shape["fsdp"]
    spread_bits = [b for b in (1 << i for i in range(n_f.bit_length() - 2, -1, -1)) if b != PAIR]
    all_bits = sorted([*spread_bits, PAIR], reverse=True)

    def swap(v, bit):
        return lax.ppermute(v, AXES, [(i, i ^ bit) for i in range(n)])

    def bit_of(f, b):
        return (f // b) % 2

    def in_order(bit, own, other, axis):
        low = jnp.where(bit == 0, own, other)
        high = jnp.where(bit == 0, other, own)
        return jnp.stack([low, high], axis=axis)

    def pick(v, index, axis):
        return lax.dynamic_index_in_dim(v, index, axis, keepdims=False)

    def scatter(keep, got, f, width):
        v = keep + got.astype(F32)
        have = [b for b in all_bits if b != 1]
        v = v.reshape(*([2] * len(have)), width, v.shape[-1])
        for b in [b for b in reversed(spread_bits) if b != 1]:
            axis = have.index(b)
            bit = bit_of(f, b)
            v = pick(v, bit, axis) + swap(pick(v, 1 - bit, axis).astype(BF16), b * 4).astype(F32)
            have.remove(b)
        return v

    def body(
        hidden_in,
        cotangent,
        segments,
        w_query,
        key_projection_weight,
        value_projection_weight,
        w_out,
        w_gate,
        w_up,
        w_down,
        gain_attn,
        gain_mlp,
        gain_query,
        key_norm_gain,
    ):
        rows, width = hidden_in.shape
        d = gain_query.shape[0]
        length = segments.shape[0]
        f, c = lax.axis_index("fsdp"), lax.axis_index("ctx")
        pair = bit_of(f, PAIR)
        at_rows = w_query.shape[0]
        ff_rows = w_gate.shape[0]
        ff_cols = w_gate.shape[1] // 2
        q_cols, kv_cols = w_query.shape[1] // 4, key_projection_weight.shape[1] // 4
        groups = q_cols // kv_cols

        freqs = THETA ** (-2.0 * jnp.arange(d // 2, dtype=F32) / d)
        angles = jnp.arange(length, dtype=jnp.int32).astype(F32)[:, None] * freqs
        table_cos, table_sin = jnp.cos(angles), jnp.sin(angles)
        table = jnp.concatenate([table_cos, table_cos, -table_sin, table_sin], axis=-1)

        n_rows = 8 * rows
        all_rows = jax.ShapeDtypeStruct((n_rows, width), BF16)
        own_rows = jax.ShapeDtypeStruct((rows, width), F32)
        gain_rows = jax.ShapeDtypeStruct((8, width), F32)
        block = pltpu.VMEM((rows, width), BF16)
        nbytes = rows * width * 16
        qkv_cols = q_cols + 2 * kv_cols

        def shape(*dims):
            return jax.ShapeDtypeStruct(dims, BF16)

        copies = 160 + 10 * n_f
        natural = at_rows % 128 == 0 and ff_rows % 128 == 0
        out_dims = (q_cols, width) if natural else (width, q_cols)
        down_dims = (ff_cols, width) if natural else (width, ff_cols)
        out_part = (q_cols, 2 * at_rows) if natural else (2 * at_rows, q_cols)
        down_part_dims = (ff_cols, ff_rows) if natural else (ff_rows, ff_cols)
        n_seq = 2 * length
        all_tables = jax.ShapeDtypeStruct((n_seq, d), F32)

        def v(*dims, dtype=BF16):
            return pltpu.VMEM(dims, dtype)

        (
            residual_mid, normed_one, normed_two, grad_rows, qkv, attended, full_qkv, full_out, starts, cos, sin,
            grad_gate, grad_up, mixed_t, norm_two_part, down_part, *_,
        ) = comm_call(
            forward_kernel, spread_bits, 0,
            (hidden_in, cotangent, gain_attn[None], gain_mlp[None], segments[None], table, gain_query[None],
             key_norm_gain[None], w_query, key_projection_weight, value_projection_weight,
             w_out if natural else w_out.T, w_gate, w_up, w_down if natural else w_down.T),
            [VMEM_SPEC] * 8 + [ANY_SPEC] * 7,
            (own_rows, all_rows, all_rows, all_rows, shape(n_rows, qkv_cols), shape(n_rows, q_cols),
             shape(width, qkv_cols), shape(*out_dims), jax.ShapeDtypeStruct((n_seq, 128), F32), all_tables, all_tables,
             shape(n_rows, ff_cols), shape(n_rows, ff_cols), shape(ff_cols, n_rows), shape(8, rows, width), all_rows,
             shape(4, 2 * at_rows, qkv_cols), shape(4, *out_part), shape(4, ff_rows, ff_cols),
             shape(4, ff_rows, ff_cols), shape(4, *down_part_dims)),
            (VMEM_SPEC, *[ANY_SPEC] * 20),
            [block, block, v(n_rows, width), v(n_rows, width), v(n_rows, width), v(width, qkv_cols), v(*out_dims),
             v(width, ff_cols), v(width, ff_cols), v(*down_dims), v(n_rows, qkv_cols), v(n_rows, q_cols),
             v(8, rows, width), v(n_rows, ff_cols, dtype=F32), v(n_rows, ff_cols, dtype=F32), v(n_rows, ff_cols),
             v(n_rows, ff_cols), v(n_rows, ff_cols), v(ff_cols, n_rows), v(n_seq, 128, dtype=F32),
             v(n_seq, d, dtype=F32), v(n_seq, d, dtype=F32), v(1, length, dtype=jnp.int32),
             *collect_buffers(rows, width)],
            16 * nbytes, copies, groups, natural,
        )
        common = (starts, cos, sin, gain_query[None], key_norm_gain[None])
        backward = one_kernel if natural and len(spread_bits) == 2 else by_steps
        return backward(
            hidden_in, cotangent, residual_mid, gain_attn, gain_mlp, common, norm_two_part, down_part, normed_one,
            normed_two, grad_rows, qkv, attended, full_qkv, full_out, grad_gate, grad_up, mixed_t, (at_rows, ff_rows),
        )

    def one_kernel(
        hidden_in, cotangent, residual_mid, gain_attn, gain_mlp, common, norm_two_part, down_part, normed_one,
        normed_two, grad_rows, qkv, attended, full_qkv, full_out, grad_gate, grad_up, mixed_t, sizes,
    ):
        rows, width = hidden_in.shape
        cols, n_rows = mixed_t.shape
        (at_rows, ff_rows), q_cols, qkv_cols = sizes, attended.shape[1], qkv.shape[1]
        d = common[-1].shape[1]
        kv_cols = (qkv_cols - q_cols) // 2
        groups = q_cols // kv_cols

        def out(dtype, *dims):
            return jax.ShapeDtypeStruct(dims, dtype)

        def v(*dims, dtype=BF16):
            return pltpu.VMEM(dims, dtype)

        def scatter(*block):
            return [v(2, *block), v(4, *block), v(2, *block), v(2, *block), v(*block, dtype=F32), v(*block)]

        n_gain = 2 * width + 2 * d
        nbytes = n_rows * width * 20
        (
            grad_input, hidden_out, gains, feed_own, feed_other, down_own, down_other, qkv_own, qkv_other, out_own,
            out_other, *_,
        ) = comm_call(
            backward_kernel, spread_bits, 2,
            (cotangent, gain_attn[None], gain_mlp[None], *common, residual_mid, hidden_in, norm_two_part,
             down_part.reshape(8, rows, width), normed_one, normed_two, grad_rows, qkv, attended, full_qkv, full_out,
             grad_gate, grad_up, mixed_t),
            [VMEM_SPEC] * 8 + [ANY_SPEC] * 14,
            (out(F32, rows, width), out(F32, rows, width), out(F32, 1, n_gain), out(F32, ff_rows, 2 * cols),
             out(BF16, ff_rows, 2 * cols), out(F32, cols, ff_rows), out(BF16, cols, ff_rows),
             out(F32, at_rows, qkv_cols), out(BF16, 3, at_rows, qkv_cols), out(F32, q_cols, at_rows),
             out(BF16, 3, q_cols, at_rows), out(BF16, 4, ff_rows, 2 * cols), out(BF16, 4, cols, ff_rows),
             out(BF16, 4, ff_rows, qkv_cols), out(BF16, 4, q_cols, ff_rows)),
            (VMEM_SPEC, VMEM_SPEC, VMEM_SPEC, ANY_SPEC, ANY_SPEC, ANY_SPEC, ANY_SPEC, VMEM_SPEC, ANY_SPEC, VMEM_SPEC,
             *[ANY_SPEC] * 5),
            [v(rows, width), v(n_rows, width), v(n_rows, 2 * cols), v(cols, n_rows), v(2, n_rows, ff_rows),
             v(ff_rows, n_rows), v(8, rows, width), v(width, qkv_cols), v(q_cols, width), v(n_rows, qkv_cols),
             v(n_rows, q_cols), v(n_rows, q_cols), v(n_rows, qkv_cols),
             *collect_buffers(rows, width), *collect_buffers(rows, width), v(8, width, dtype=F32), v(8, width, dtype=F32), v(2, 8, d, dtype=F32),
             v(4 + len(spread_bits), 1, n_gain, dtype=F32), v(3 + len(spread_bits), 1, n_gain, dtype=F32),
             *scatter(ff_rows, 2 * cols), *scatter(cols, ff_rows), *scatter(ff_rows, qkv_cols),
             *scatter(q_cols, ff_rows)],
            nbytes, 110, groups,
        )
        own_rows = out(F32, rows, width)
        made = (
            out(F32, at_rows, 4 * q_cols), out(F32, at_rows, 4 * kv_cols), out(F32, at_rows, 4 * kv_cols),
            out(F32, 4 * q_cols, at_rows), out(F32, ff_rows, 2 * cols), out(F32, ff_rows, 2 * cols),
            out(F32, 2 * cols, ff_rows), own_rows, own_rows, out(F32, 1, width), out(F32, 1, width), out(F32, 1, d),
            out(F32, 1, d),
        )
        pieces = pl.pallas_call(
            join_kernel,
            out_shape=made,
            compiler_params=pltpu.CompilerParams(vmem_limit_bytes=61 << 20),
            name="join_kernel",
        )(feed_own, feed_other, down_own, down_other, qkv_own, qkv_other, out_own, out_other, grad_input, hidden_out, gains)
        grads, (grad_input, hidden_out), gains = pieces[:7], pieces[7:9], pieces[9:]
        return hidden_out, grad_input, *grads, *(g[0] for g in gains)

    def by_steps(
        hidden_in, cotangent, residual_mid, gain_attn, gain_mlp, common, norm_two_part, down_part, normed_one,
        normed_two, grad_rows, qkv, attended, full_qkv, full_out, grad_gate, grad_up, mixed_t, sizes,
    ):
        rows, width = hidden_in.shape
        (at_rows, ff_rows), ff_cols, q_cols = sizes, mixed_t.shape[0], attended.shape[1]
        d = common[-1].shape[1]
        kv_cols = (qkv.shape[1] - q_cols) // 2
        groups = q_cols // kv_cols
        natural = full_out.shape[0] != width
        times_t = dot_cols if natural else dot
        f, c = lax.axis_index("fsdp"), lax.axis_index("ctx")
        pair = bit_of(f, PAIR)
        all_rows = jax.ShapeDtypeStruct((8 * rows, width), BF16)
        own_rows = jax.ShapeDtypeStruct((rows, width), F32)
        gain_rows = jax.ShapeDtypeStruct((8, width), F32)
        block = pltpu.VMEM((rows, width), BF16)
        nbytes = rows * width * 16
        grad_mid, gain_mlp_part, grad_mid_rows = comm_call(
            turn_kernel, spread_bits, 2, (norm_two_part.reshape(8, rows, width), residual_mid, cotangent, gain_mlp[None]),
            [ANY_SPEC, VMEM_SPEC, VMEM_SPEC, VMEM_SPEC], (own_rows, gain_rows, all_rows),
            (VMEM_SPEC, VMEM_SPEC, ANY_SPEC),
            [block, pltpu.VMEM((4, rows, width), BF16), *collect_buffers(rows, width)], 2 * nbytes, 40,
        )

        low = bit_of(f, 1)

        def weight_grad(acts, grads):
            split = acts.reshape(acts.shape[0], n_f // 2, 2, width // n_f)
            mine = pick(split, low, 2).reshape(acts.shape[0], -1)
            theirs = pick(split, 1 - low, 2).reshape(acts.shape[0], -1)
            got = swap(dot_rows(theirs, grads).astype(BF16), 4)
            return scatter(dot_rows(mine, grads), got, f, width // n_f)

        def ff_grad(acts, grads):
            v = weight_grad(acts, grads)
            other = swap(pick(v, 1 - pair, 0).astype(BF16), PAIR_BIT).astype(F32)
            return in_order(pair, pick(v, pair, 0), other, 1).reshape(ff_rows, 2 * ff_cols)

        grad_w_gate = ff_grad(normed_two, grad_gate)
        grad_w_up = ff_grad(normed_two, grad_up)
        grad_w_down = ff_grad(grad_rows, mixed_t.T).T

        def attn_grad(acts, grads):
            v = weight_grad(acts, grads)
            v = v.reshape(2, 2, at_rows, v.shape[-1])
            mine = pick(pick(v, pair, 0), c, 0)
            by_ctx = swap(pick(pick(v, pair, 0), 1 - c, 0).astype(BF16), CTX_BIT).astype(F32)
            by_pair = swap(pick(pick(v, 1 - pair, 0), c, 0).astype(BF16), PAIR_BIT).astype(F32)
            by_both = swap(pick(pick(v, 1 - pair, 0), 1 - c, 0).astype(BF16), CTX_BIT | PAIR_BIT).astype(F32)
            near = in_order(pair, mine, by_pair, 1)
            far = in_order(pair, by_ctx, by_both, 1)
            return in_order(c, near, far, 1)

        grad_w_out = attn_grad(grad_mid_rows, attended).reshape(at_rows, 4 * q_cols).T

        datt = times_t(grad_mid_rows, full_out).astype(BF16)
        grad_qkv, head_gains = attend_back(groups, qkv, attended, datt, common)
        norm_one_part = dot_cols(grad_qkv, full_qkv).astype(BF16)
        grad_input, gain_attn_part = comm_call(
            last_kernel, spread_bits, 3, (norm_one_part.reshape(8, rows, width), hidden_in, grad_mid, gain_attn[None]),
            [ANY_SPEC, VMEM_SPEC, VMEM_SPEC, VMEM_SPEC], (own_rows, gain_rows), (VMEM_SPEC, VMEM_SPEC),
            [pltpu.VMEM((4, rows, width), BF16), *collect_buffers(rows, width)], nbytes, 40,
        )
        grad_qkv_w = attn_grad(normed_one, grad_qkv)
        grad_w_query = grad_qkv_w[..., :q_cols].reshape(at_rows, -1)
        grad_w_key = grad_qkv_w[..., q_cols : q_cols + kv_cols].reshape(at_rows, -1)
        grad_w_value = grad_qkv_w[..., q_cols + kv_cols :].reshape(at_rows, -1)

        head_gains = jnp.sum(head_gains, axis=1)
        gains = jnp.concatenate(
            [jnp.sum(gain_attn_part, axis=0), jnp.sum(gain_mlp_part, axis=0), head_gains[0], head_gains[1]]
        ).reshape(-1, d)
        for i in range(n.bit_length() - 1):
            gains = gains + swap(gains, 1 << i)
        gains = gains.reshape(-1)
        teams = sorted(
            sorted(i ^ b ^ p for b in range(4) for p in (0, PAIR_BIT))
            for i in range(0, n, 4)
            if not i & PAIR_BIT
        )
        hidden_out = residual_mid + lax.psum_scatter(
            down_part, AXES, scatter_dimension=0, axis_index_groups=teams, tiled=True
        ).astype(F32)
        return (
            hidden_out,
            grad_input,
            grad_w_query,
            grad_w_key,
            grad_w_value,
            grad_w_out,
            grad_w_gate,
            grad_w_up,
            grad_w_down,
            gains[:width],
            gains[width : 2 * width],
            gains[2 * width : 2 * width + d],
            gains[2 * width + d :],
        )

    return body


def solution(mesh):
    everyone = P(("fsdp", "ctx", "tp"), None)
    attn = P(("fsdp", "ctx"), "tp")
    attn_out = P("tp", ("fsdp", "ctx"))
    ff_in = P("fsdp", ("ctx", "tp"))
    ff_out = P(("ctx", "tp"), "fsdp")
    same = P()
    return jax.shard_map(
        build(mesh),
        mesh=mesh,
        in_specs=(
            everyone, everyone, P("fsdp"), attn, attn, attn, attn_out, ff_in, ff_in, ff_out,
            same, same, same, same,
        ),
        out_specs=(
            everyone, everyone, attn, attn, attn, attn_out, ff_in, ff_in, ff_out,
            same, same, same, same,
        ),
        check_vma=False,
    )
```

```python
import functools

import jax
import jax.numpy as jnp
from jax import lax
from jax.experimental import pallas as pl
from jax.experimental.pallas import tpu as pltpu
from jax.sharding import PartitionSpec as P

EPS = 1e-06
THETA = 1000000.0
AXES = ("fsdp", "ctx", "tp")
MESH = pl.DeviceIdType.MESH
BF16 = jnp.bfloat16
F32 = jnp.float32
TP_BIT, CTX_BIT = 1, 2
PAIR = 2
PAIR_BIT = PAIR * 4


def dot_rows(left, right):
    return lax.dot_general(left, right, (((0,), (0,)), ((), ())), preferred_element_type=F32)


def dot_cols(left, right):
    return lax.dot_general(left, right, (((1,), (1,)), ((), ())), preferred_element_type=F32)


def dot(left, right):
    return lax.dot_general(left, right, (((1,), (0,)), ((), ())), preferred_element_type=F32)


def remote(src, dst, send, recv, device):
    return pltpu.make_async_remote_copy(
        src_ref=src, dst_ref=dst, send_sem=send, recv_sem=recv, device_id=device, device_id_type=MESH
    )


class Moves:
    def __init__(self, send, recv, local):
        self.send, self.recv, self.local = send, recv, local
        self.sent, self.loads = 0, 0
        self.open = []

    def swap(self, src, there, here, device, open_=None):
        k = self.sent
        self.sent += 1
        copy = remote(src, there, self.send.at[k], self.recv.at[k], device)
        copy.start()
        (self.open if open_ is None else open_).append(copy.wait_send)
        return remote(src, here, self.send.at[k], self.recv.at[k], device).wait_recv

    def load(self, src, dst):
        k = self.loads
        self.loads += 1
        copy = pltpu.make_async_copy(src, dst, self.local.at[k])
        copy.start()
        return copy.wait

    def store(self, src, dst):
        self.open.append(self.load(src, dst))

    def close(self):
        for wait in self.open:
            wait()


class Place:
    def __init__(self, bits):
        self.bits = bits
        f, c, t = lax.axis_index("fsdp"), lax.axis_index("ctx"), lax.axis_index("tp")
        self.f, self.c, self.t = f, c, t
        self.pair = (f // PAIR) % 2
        far_f = self.block(PAIR)
        fs, cs = [f, f, far_f, far_f], [c, 1 - c, c, 1 - c]
        pairs = [self.pair, self.pair, 1 - self.pair, 1 - self.pair]
        self.at = [(fs[j], cs[j], pairs[j]) for j in range(4)]
        self.rows_of = [pairs[j] * 4 + cs[j] * 2 for j in range(4)]
        self.chunk_of = [cs[j] * 2 + pairs[j] for j in range(4)]
        self.relay = len(bits) == 2
        self.across_mask = bits[0] | PAIR
        self.inner = (f // bits[0]) % 2 != self.pair
        self.chips = [None, {"ctx": 1 - c}, {"fsdp": far_f}, {"fsdp": far_f, "ctx": 1 - c}]
        self.sibling = {"tp": 1 - t}

    def block(self, mask):
        out = self.f
        for i in range(mask.bit_length()):
            b = 1 << i
            if mask & b:
                out = out + b - 2 * b * ((self.f // b) % 2)
        return out

    def along(self, bit):
        return {"fsdp": self.block(bit)}

    def greet(self):
        barrier = pltpu.get_barrier_semaphore()
        devices = [*self.chips[1:], self.sibling, *[self.along(b) for b in self.bits]]
        if self.relay:
            devices.append(self.along(self.across_mask))
        for device in devices:
            pl.semaphore_signal(barrier, inc=1, device_id=device, device_id_type=MESH)
        pl.semaphore_wait(barrier, len(devices))


class Cross:
    def __init__(self, moves, place, src, here, came_in, across_to, came_out, pair_to):
        self.place, self.here = place, here
        self.came_in, self.came_out = came_in, came_out
        k = moves.sent
        moves.sent += 4
        pair, across = place.chips[2], place.along(place.across_mask)

        def copy(i, source, to, device):
            return remote(source, to, moves.send.at[k + i], moves.recv.at[k + i], device)

        self.hand = copy(0, src, came_in, pair)
        self.own = copy(1, src, came_out, across)
        self.on = copy(2, came_in, across_to, across)
        self.back = copy(3, came_out, pair_to, pair)
        self.came = [copy(0, came_in, came_in, pair), copy(1, came_out, came_out, across)]
        self.landed = [copy(2, here, here, across), copy(3, here, here, pair)]
        moves.open.append(self.left)

        @pl.when(place.inner)
        def _():
            self.own.start()

        @pl.when(jnp.logical_not(place.inner))
        def _():
            self.hand.start()

    def relay(self):
        @pl.when(self.place.inner)
        def _():
            self.came[0].wait_recv()
            self.on.start()
            self.came[1].wait_recv()
            self.back.start()

    def arrive(self):
        @pl.when(self.place.inner)
        def _():
            self.landed[0].wait_recv()

        @pl.when(jnp.logical_not(self.place.inner))
        def _():
            self.landed[1].wait_recv()

    def left(self):
        @pl.when(self.place.inner)
        def _():
            self.own.wait_send()
            self.on.wait_send()
            self.back.wait_send()

        @pl.when(jnp.logical_not(self.place.inner))
        def _():
            self.hand.wait_send()


class Spread:
    def __init__(self, moves, place, own, out):
        self.moves, self.place, self.out = moves, place, out
        self.rows = own.shape[0]
        self.open = []
        mine = self.at(0, place.t)
        self.here = moves.load(own, mine)
        self.pair = moves.swap(own, mine, self.at(2, place.t), place.chips[2], self.open)
        self.ctx = moves.swap(own, mine, self.at(1, place.t), place.chips[1], self.open)
        self.beside = [moves.swap(own, mine, self.at(0, 1 - place.t), place.sibling, self.open)]

    def at(self, j, t):
        start = (self.place.rows_of[j] + t) * self.rows
        return self.out.at[pl.ds(pl.multiple_of(start, self.rows), self.rows)]

    def hand(self, j):
        block = self.at(j, self.place.t)
        self.beside.append(
            self.moves.swap(block, block, self.at(j, 1 - self.place.t), self.place.sibling, self.open)
        )

    def from_pair(self):
        self.pair()
        block = self.at(2, self.place.t)
        self.both = self.moves.swap(block, block, self.at(3, self.place.t), self.place.chips[1], self.open)
        self.hand(2)

    def from_ctx(self):
        self.ctx()
        self.hand(1)

    def from_both(self):
        self.both()
        self.hand(3)

    def finish(self):
        self.here()
        for wait in (*self.beside, *self.open):
            wait()


class Collect:
    def __init__(self, moves, place, part, held, first, ctx_in, pair_in, sending, load):
        self.moves, self.place = moves, place
        self.first, self.ctx_in, self.pair_in, self.sending = first, ctx_in, pair_in, sending
        t = place.t
        self.hands, self.loads, self.open = {}, {}, []
        for j in (3, 1, 2, 0):
            self.hands[j] = moves.swap(part(j, 1 - t), first.at[j], first.at[j], place.sibling, self.open)
            if load:
                self.loads[j] = moves.load(part(j, t), held.at[j])
        self.held = (lambda j: held.at[j]) if load else (lambda j: part(j, t))

    def two(self, j, at):
        return self.held(j)[at].astype(F32) + self.first[j, at].astype(F32)

    def ready(self, j):
        self.hands[j]()
        if j in self.loads:
            self.loads[j]()

    def to_ctx(self):
        self.waits = {}
        for j, slot in ((3, 0), (1, 1)):
            self.ready(j)

            def body(at):
                self.sending[slot, at] = self.two(j, at).astype(BF16)

            row_loop(self.sending.shape[1], body)
            self.waits[j] = self.moves.swap(
                self.sending.at[slot], self.ctx_in.at[slot], self.ctx_in.at[slot], self.place.chips[1], self.open
            )

    def to_pair(self):
        self.ready(2)
        self.waits[3]()

        def body(at):
            self.sending[2, at] = (self.two(2, at) + self.ctx_in[0, at].astype(F32)).astype(BF16)

        row_loop(self.sending.shape[1], body)
        self.waits[2] = self.moves.swap(
            self.sending.at[2], self.pair_in, self.pair_in, self.place.chips[2], self.open
        )

    def fold(self):
        for j, slot in ((3, 0), (1, 1), (2, 2)):
            self.ready(j)

            def body(at):
                self.sending[slot, at] = self.two(j, at).astype(BF16)

            row_loop(self.sending.shape[1], body)
        self.ready(0)

    def post_ctx(self):
        self.waits = {}
        for j, slot in ((3, 0), (1, 1)):
            self.waits[j] = self.moves.swap(
                self.sending.at[slot], self.ctx_in.at[slot], self.ctx_in.at[slot], self.place.chips[1], self.open
            )

    def post_pair(self):
        self.waits[3]()

        def body(at):
            self.sending[2, at] = (self.sending[2, at].astype(F32) + self.ctx_in[0, at].astype(F32)).astype(BF16)

        row_loop(self.sending.shape[1], body)
        self.waits[2] = self.moves.swap(
            self.sending.at[2], self.pair_in, self.pair_in, self.place.chips[2], self.open
        )

    def came(self):
        for wait in (self.waits[1], self.waits[2], *self.open):
            wait()

    def finish(self):
        self.ready(0)
        self.waits[1]()
        self.waits[2]()
        for wait in self.open:
            wait()

    def total(self, at):
        return self.two(0, at) + (self.ctx_in[1, at].astype(F32) + self.pair_in[at].astype(F32))


def collect_buffers(rows, width):
    return [
        pltpu.VMEM((4, rows, width), BF16),
        pltpu.VMEM((2, rows, width), BF16),
        pltpu.VMEM((rows, width), BF16),
        pltpu.VMEM((3, rows, width), BF16),
    ]


def row_loop(rows, body):
    step = 16

    @pl.loop(0, rows // step)
    def _(i):
        body(pl.ds(pl.multiple_of(i * step, step), step))


def unit_and_scale(x):
    scale = lax.rsqrt(jnp.mean(x * x, axis=-1, keepdims=True) + EPS)
    return x * scale, scale


class Gather:
    def __init__(self, moves, place, block, spare):
        self.moves, self.place, self.block, self.spare = moves, place, block, spare
        self.waits, self.crosses = {}, {}

    def forward(self, mask, src=None):
        done = [i for i, b in enumerate(self.place.bits) if mask & b]
        here = self.block(self.place.block(mask))
        for b in self.place.bits[max(done, default=-1) + 1 :]:
            if self.place.relay and b == self.place.bits[0]:
                far = self.place.across_mask
                slot = 0 if mask == 0 else 2
                self.crosses[mask] = Cross(
                    self.moves, self.place, here if src is None else src, self.block(self.place.block(mask | b)),
                    self.spare.at[slot], self.block(self.place.block(mask ^ PAIR)),
                    self.spare.at[slot + 1], self.block(self.place.block(mask ^ far)),
                )
                self.waits[mask | b] = self.crosses[mask].arrive
                continue
            self.waits[mask | b] = self.moves.swap(
                here if src is None else src, here, self.block(self.place.block(mask | b)), self.place.along(b)
            )

    def masks(self, stage):
        out = [0, PAIR]
        for b in self.place.bits[:stage]:
            out += [m | b for m in out]
        return [m | self.place.bits[stage] for m in out]

    def relay(self, m):
        if self.place.relay:
            self.crosses[m].relay()

    def hop(self, m):
        if self.place.relay:
            self.pass_on(m | self.place.bits[0])
        elif m == PAIR:
            self.middle()

    def pass_on(self, m):
        self.waits.pop(m)()
        self.forward(m)

    def middle(self):
        for stage in range(len(self.place.bits) - 1):
            for m in self.masks(stage):
                if m in self.waits:
                    self.pass_on(m)

    def finish(self):
        for wait in self.waits.values():
            wait()


def head_unit(x):
    scale = lax.rsqrt(jnp.mean(x * x, axis=-1, keepdims=True) + EPS)
    return x * scale, scale


def rot(a, cos, sin):
    return a * cos + pltpu.roll(a, a.shape[-1] // 2, 1) * sin


def rot_back(b, cos, sin):
    return b * cos - pltpu.roll(b, b.shape[-1] // 2, 1) * sin


def allowed_keys(start):
    length = start.shape[0]
    row = lax.broadcasted_iota(jnp.int32, (length, length), 0)
    col = lax.broadcasted_iota(jnp.int32, (length, length), 1)
    return (col.astype(F32) >= start) & (row >= col)


def soft_of(scores):
    peak = jnp.max(scores, axis=-1, keepdims=True)
    lse = peak + jnp.log(jnp.sum(jnp.exp(scores - peak), axis=-1, keepdims=True))
    return jnp.exp(scores - lse)


def attend_one(groups, s, qkv, starts, cos_ref, sin_ref, gain_q, gain_k, out):
    d = gain_q.shape[-1]
    length = cos_ref.shape[0] // 2
    rows = pl.ds(pl.multiple_of(s * length, length), length)
    cos, sin = cos_ref[rows], sin_ref[rows]
    allowed = allowed_keys(starts[rows, 0:1])
    unit_k, _ = head_unit(qkv[rows, groups * d : (groups + 1) * d].astype(F32))
    key = rot(unit_k * gain_k[...], cos, sin).astype(BF16)
    value = qkv[rows, (groups + 1) * d : (groups + 2) * d]
    for g in range(groups):
        unit_q, _ = head_unit(qkv[rows, g * d : (g + 1) * d].astype(F32))
        query = rot(unit_q * gain_q[...], cos, sin).astype(BF16)
        scores = jnp.where(allowed, dot_cols(query, key) * d**-0.5, -jnp.inf)
        soft = soft_of(scores).astype(BF16)
        out[rows, g * d : (g + 1) * d] = dot(soft, value).astype(BF16)


def through_norm(b, unit, scale, gain):
    e = b * gain
    return scale * (e - unit * jnp.mean(e * unit, axis=-1, keepdims=True))


def attend_back_one(
    groups, s, qkv, att, datt, starts, cos_ref, sin_ref, gain_q, gain_k, grad, gains
):
    d = gain_q.shape[-1]
    length = cos_ref.shape[0] // 2
    rows = pl.ds(pl.multiple_of(s * length, length), length)
    cos, sin = cos_ref[rows], sin_ref[rows]
    scale = d**-0.5
    allowed = allowed_keys(starts[rows, 0:1])
    at_k, at_v = slice(groups * d, (groups + 1) * d), slice((groups + 1) * d, (groups + 2) * d)
    unit_k, scale_k = head_unit(qkv[rows, at_k].astype(F32))
    key = rot(unit_k * gain_k[...], cos, sin).astype(BF16)
    value = qkv[rows, at_v]
    key_grad = jnp.zeros(unit_k.shape, F32)
    value_grad = jnp.zeros(unit_k.shape, F32)
    for g in range(groups):
        at = slice(g * d, (g + 1) * d)
        unit_q, scale_q = head_unit(qkv[rows, at].astype(F32))
        query = rot(unit_q * gain_q[...], cos, sin).astype(BF16)
        scores = jnp.where(allowed, dot_cols(query, key) * scale, -jnp.inf)
        soft = soft_of(scores)
        up = datt[rows, at]
        delta = jnp.sum(up.astype(F32) * att[rows, at].astype(F32), axis=-1, keepdims=True)
        ds = (soft * (dot_cols(up, value) - delta) * scale).astype(BF16)
        value_grad += dot_rows(soft.astype(BF16), up)
        key_grad += dot_rows(ds, query)
        b = rot_back(dot(ds, key), cos, sin)
        gains[0] += jnp.sum((b * unit_q).reshape(-1, 8, d), axis=0)
        grad[rows, at] = through_norm(b, unit_q, scale_q, gain_q[...]).astype(BF16)
    b = rot_back(key_grad, cos, sin)
    gains[1] += jnp.sum((b * unit_k).reshape(-1, 8, d), axis=0)
    grad[rows, at_k] = through_norm(b, unit_k, scale_k, gain_k[...]).astype(BF16)
    grad[rows, at_v] = value_grad.astype(BF16)


def attend_back_kernel(
    groups, qkv, att, datt, starts, cos, sin, gain_q, gain_k, grad, gains
):
    gains[...] = jnp.zeros_like(gains)

    @pl.loop(0, 2)
    def _(s):
        attend_back_one(groups, s, qkv, att, datt, starts, cos, sin, gain_q, gain_k, grad, gains)


def attend_back(groups, qkv, att, datt, common):
    n_rows, width = qkv.shape
    d = width // (groups + 2)
    length = n_rows // 2
    return pl.pallas_call(
        functools.partial(attend_back_kernel, groups),
        out_shape=(jax.ShapeDtypeStruct(qkv.shape, BF16), jax.ShapeDtypeStruct((2, 8, d), F32)),
        compiler_params=pltpu.CompilerParams(vmem_limit_bytes=40 << 20),
        cost_estimate=pl.CostEstimate(
            flops=n_rows * groups * length * (10 * d + 30),
            bytes_accessed=n_rows * width * 8,
            transcendentals=n_rows * groups * length * 2,
        ),
        name="attend_back",
    )(qkv, att, datt, *common)


def forward_kernel(
    bits, groups, natural,
    hidden, cot, gain_attn, gain_mlp, seg, table, gain_q, gain_k, wq, wk, wv, wo, wg, wu, wd,
    mid, normed_one, normed_two, cot_out, qkv_out, att_out, qkv_weight, out_weight, starts_out, cos_out, sin_out,
    grad_gate_out, grad_up_out, mixed_out, part_out, down_out, spare_qkv, spare_out, spare_gate, spare_up, spare_down,
    own_one, own_two, rows_one, rows_two, rows_cot, w_qkv, w_out, w_gate, w_up, w_down, qkv, att, part,
    gate, up, grad_gate, grad_up, mixed, mixed_t, starts, cos, sin, seg_in, first, ctx_in, pair_in, sending,
    send, recv, local,
):
    place = Place(bits)
    moves = Moves(send, recv, local)
    rows, width = hidden.shape
    at_rows, ff_rows, ff_cols = wq.shape[0], wg.shape[0], wg.shape[1] // 2
    q_cols, kv_cols = wq.shape[1] // 4, wk.shape[1] // 4
    n_rows, length = rows_one.shape[0], seg.shape[1]

    def lanes(start, size):
        return pl.ds(pl.multiple_of(start, size), size)

    def qkv_rows(f, c=None):
        if c is None:
            return lanes(f * 2 * at_rows, 2 * at_rows)
        return lanes((f * 2 + c) * at_rows, at_rows)

    place.greet()

    def out_block(f, c=None):
        return w_out.at[:, qkv_rows(f, c)] if natural else w_out.at[qkv_rows(f, c)]

    def out_chunk(j):
        at = lanes(place.chunk_of[j] * q_cols, q_cols)
        return wo.at[at] if natural else wo.at[:, at]

    pieces = (
        (wq, q_cols, pl.ds(0, q_cols)),
        (wk, kv_cols, pl.ds(q_cols, kv_cols)),
        (wv, kv_cols, pl.ds(q_cols + kv_cols, kv_cols)),
    )
    f0, c0, _ = place.at[0]
    qkv_in, out_in = {}, {}

    def rows_block(w):
        return lambda f: w.at[lanes(f * ff_rows, ff_rows)]

    def cols_block(w):
        return lambda f: w.at[:, lanes(f * ff_rows, ff_rows)]

    mine, theirs = lanes(place.pair * ff_cols, ff_cols), lanes((1 - place.pair) * ff_cols, ff_cols)
    feed = [
        (Gather(moves, place, rows_block(w_gate), spare_gate), wg.at[:, mine], wg.at[:, theirs]),
        (Gather(moves, place, rows_block(w_up), spare_up), wu.at[:, mine], wu.at[:, theirs]),
        (Gather(moves, place, cols_block(w_down), spare_down), wd.at[mine], wd.at[theirs])
        if natural
        else (Gather(moves, place, rows_block(w_down), spare_down), wd.at[:, mine], wd.at[:, theirs]),
    ]
    own_feed = [moves.load(own, gather.block(place.f)) for gather, own, _ in feed]

    def swap_pair(i):
        gather, _, other = feed[i]
        gather.waits[PAIR] = moves.swap(
            other, gather.block(place.f), gather.block(place.block(PAIR)), place.along(PAIR)
        )

    def send_feed(i):
        gather, own, _ = feed[i]
        gather.forward(0, own)
        gather.pass_on(PAIR)

    step = 2 * rows
    wide = min(256, w_qkv.shape[1])
    qkv_gather = Gather(moves, place, lambda f: w_qkv.at[qkv_rows(f)], spare_qkv)
    out_gather = Gather(moves, place, out_block, spare_out)

    def norm_one(at):
        unit, _ = unit_and_scale(hidden[at].astype(F32))
        own_one[at] = (unit * gain_attn[...]).astype(BF16)

    def norm_two(at):
        x = hidden[at].astype(F32) + collect.total(at)
        mid[at] = x
        unit, _ = unit_and_scale(x)
        own_two[at] = (unit * gain_mlp[...]).astype(BF16)

    def columns_of(weight, at):
        return (dot, weight[:, at]) if natural else (dot_cols, weight[at])

    def attend_part(s):
        attend_one(groups, s, qkv, starts, cos, sin, gain_q, gain_k, att)

    def gate_part(i):
        at = pl.ds(i * step, step)
        gate[at] = dot(rows_two[at], w_gate[...])

    def up_part(i):
        at = pl.ds(i * step, step)
        u = dot(rows_two[at], w_up[...])
        up[at] = u
        g = gate[at]
        mix = g * jax.nn.sigmoid(g) * u
        mixed[at] = mix.astype(BF16)
        mixed_t[:, at] = mix.T.astype(BF16)

    def back_part(i):
        at = pl.ds(i * step, step)
        m = (dot_cols if natural else dot)(rows_cot[at], w_down[...])
        g = gate[at]
        s = jax.nn.sigmoid(g)
        grad_gate[at] = (m * up[at] * s * (1.0 + g * (1.0 - s))).astype(BF16)
        grad_up[at] = (m * (g * s)).astype(BF16)

    for j in (3, 2, 1):
        fj, cj, _ = place.at[j]
        out_in[j] = moves.swap(out_chunk(j), out_block(f0, c0), out_block(fj, cj), place.chips[j])
    out_in[0] = moves.load(out_chunk(0), out_block(f0, c0))
    row_loop(rows, norm_one)
    for j in (1, 3, 2):
        fj, cj, _ = place.at[j]
        qkv_in[j] = [
            moves.swap(
                w.at[:, lanes(place.chunk_of[j] * size, size)],
                w_qkv.at[qkv_rows(f0, c0), to],
                w_qkv.at[qkv_rows(fj, cj), to],
                place.chips[j],
            )
            for w, size, to in pieces
        ]
    qkv_in[0] = [
        moves.load(w.at[:, lanes(place.chunk_of[0] * size, size)], w_qkv.at[qkv_rows(f0, c0), to])
        for w, size, to in pieces
    ]
    out_in[0]()
    out_in[1]()
    out_gather.forward(0)
    for wait in (*qkv_in[0], *qkv_in[1]):
        wait()
    qkv_gather.forward(0)
    spread_one = Spread(moves, place, own_one, rows_one)
    qkv_gather.relay(0)
    spread_one.from_ctx()
    out_gather.relay(0)
    out_in[2]()
    out_in[3]()
    out_gather.forward(PAIR)
    for wait in (*qkv_in[2], *qkv_in[3]):
        wait()
    qkv_gather.forward(PAIR)
    feed[0][0].forward(0, feed[0][1])
    out_gather.hop(0)
    spread_cot = Spread(moves, place, cot, rows_cot)
    seg_wait = moves.swap(seg, seg_in, seg_in, place.chips[2])
    spread_one.from_pair()
    out_gather.relay(PAIR)
    qkv_gather.hop(0)
    qkv_gather.relay(PAIR)
    feed[0][0].relay(0)
    out_gather.hop(PAIR)
    qkv_gather.hop(PAIR)
    swap_pair(0)
    spread_one.from_both()
    spread_cot.from_pair()
    feed[1][0].forward(0, feed[1][1])
    seg_wait()
    pair_first = place.pair == 0
    own_seg, far_seg = seg[...].astype(F32), seg_in[...].astype(F32)
    for i in range(2):
        here = pair_first if i == 0 else jnp.logical_not(pair_first)
        flags = jnp.where(here, own_seg, far_seg)
        both = jnp.broadcast_to(flags, (128, length)).T[:, 0:1]
        start = jnp.sum((flags < both).astype(F32), axis=1, keepdims=True)
        row = lax.broadcasted_iota(jnp.int32, (length, length), 0).astype(F32)
        col = lax.broadcasted_iota(jnp.int32, (length, length), 1).astype(F32)
        chosen = (row - start == col).astype(F32)
        at = pl.ds(i * length, length)
        both_tables = lax.dot_general(
            chosen, table[...], (((1,), (0,)), ((), ())),
            precision=lax.Precision.HIGHEST, preferred_element_type=F32,
        )
        d = gain_q.shape[1]
        starts[at] = jnp.broadcast_to(start, (length, 128))
        cos[at] = both_tables[:, :d]
        sin[at] = both_tables[:, d:]
    moves.store(starts, starts_out)
    moves.store(cos, cos_out)
    moves.store(sin, sin_out)
    swap_pair(1)
    spread_one.finish()
    normed_stored = moves.load(rows_one, normed_one)
    out_gather.finish()
    moves.store(w_out, out_weight)
    qkv_gather.finish()
    moves.store(w_qkv, qkv_weight)
    @pl.loop(0, w_qkv.shape[1] // wide)
    def _(i):
        at = lanes(i * wide, wide)
        qkv[:, at] = dot(rows_one[...], w_qkv[:, at]).astype(BF16)

    moves.store(qkv, qkv_out)
    attend_part(0)
    attend_part(1)
    moves.store(att, att_out)
    feed[0][0].pass_on(PAIR)
    feed[1][0].relay(0)
    @pl.loop(0, width // 256)
    def _(i):
        at = lanes(i * 256, 256)
        times, block = columns_of(w_out, at)
        part[:, :, at] = times(att[...], block).astype(BF16).reshape(8, rows, 256)

    collect = Collect(
        moves, place, lambda j, t: part.at[place.rows_of[j] + t], None, first, ctx_in, pair_in, sending, False
    )
    feed[0][0].hop(0)
    collect.to_ctx()
    feed[0][0].relay(PAIR)
    feed[2][0].forward(0, feed[2][1])
    collect.to_pair()
    spread_cot.from_ctx()
    feed[1][0].pass_on(PAIR)
    feed[0][0].hop(PAIR)
    swap_pair(2)
    collect.finish()
    feed[2][0].relay(0)
    row_loop(rows, norm_two)
    spread_two = Spread(moves, place, own_two, rows_two)
    spread_cot.from_both()
    spread_cot.finish()
    moves.store(rows_cot, cot_out)
    feed[1][0].hop(0)
    spread_two.from_ctx()
    feed[2][0].pass_on(PAIR)
    feed[2][0].hop(0)
    feed[1][0].relay(PAIR)
    spread_two.from_pair()
    feed[2][0].relay(PAIR)
    own_feed[0]()
    feed[0][0].finish()
    feed[1][0].hop(PAIR)
    spread_two.from_both()
    feed[2][0].hop(PAIR)
    spread_two.finish()
    moves.store(rows_two, normed_two)
    gate_part(0)
    gate_part(1)
    own_feed[1]()
    feed[1][0].finish()
    up_part(0)
    gate_part(2)
    up_part(1)
    gate_part(3)
    up_part(2)
    up_part(3)
    moves.store(mixed_t, mixed_out)
    own_feed[2]()
    feed[2][0].finish()
    normed_stored()

    @pl.loop(0, width // 256)
    def _(i):
        at = lanes(i * 256, 256)
        times, block = columns_of(w_down, at)
        rows_one[:, at] = times(mixed[...], block).astype(BF16)

    moves.store(rows_one, down_out)
    back_part(0)
    back_part(1)
    back_part(2)
    back_part(3)
    moves.store(grad_gate, grad_gate_out)
    moves.store(grad_up, grad_up_out)
    @pl.loop(0, width // 256)
    def _(i):
        at = lanes(i * 256, 256)
        both = dot_cols(grad_gate[...], w_gate[at]) + dot_cols(grad_up[...], w_up[at])
        part[:, :, at] = both.astype(BF16).reshape(8, rows, 256)

    moves.store(part, part_out)
    moves.close()


def norm_back(grad, x, gain, gain_grad):
    unit, scale = unit_and_scale(x)
    gain_grad[...] += jnp.sum((grad * unit).reshape(-1, 8, grad.shape[-1]), axis=0)
    e = grad * gain
    return scale * (e - unit * jnp.mean(e * unit, axis=-1, keepdims=True))


def turn_kernel(
    bits, partial, mid, cot, gain, grad_mid, gain_grad, out,
    own, held, first, ctx_in, pair_in, sending, send, recv, local,
):
    place = Place(bits)
    moves = Moves(send, recv, local)
    place.greet()
    collect = Collect(
        moves, place, lambda j, t: partial.at[place.rows_of[j] + t], held, first, ctx_in, pair_in, sending, True
    )
    collect.to_ctx()
    collect.to_pair()
    collect.finish()
    gain_grad[...] = jnp.zeros_like(gain_grad)

    def back(at):
        g = cot[at].astype(F32) + norm_back(collect.total(at), mid[at], gain[...], gain_grad)
        grad_mid[at] = g
        own[at] = g.astype(BF16)

    row_loop(mid.shape[0], back)
    spread = Spread(moves, place, own, out)
    spread.from_pair()
    spread.from_ctx()
    spread.from_both()
    spread.finish()
    moves.close()


def last_kernel(
    bits, partial, hidden, grad_mid, gain, grad_in, gain_grad,
    held, first, ctx_in, pair_in, sending, send, recv, local,
):
    place = Place(bits)
    moves = Moves(send, recv, local)
    place.greet()
    collect = Collect(
        moves, place, lambda j, t: partial.at[place.rows_of[j] + t], held, first, ctx_in, pair_in, sending, True
    )
    collect.to_ctx()
    collect.to_pair()
    collect.finish()
    gain_grad[...] = jnp.zeros_like(gain_grad)

    def back(at):
        grad_in[at] = grad_mid[at] + norm_back(
            collect.total(at), hidden[at].astype(F32), gain[...], gain_grad
        )

    row_loop(hidden.shape[0], back)
    moves.close()


class Scatter:
    def __init__(self, moves, place, product, out0, in0, out1, in1, acc, acc_pair, spare):
        self.moves, self.place, self.product, self.spare = moves, place, product, spare
        self.out0, self.in0, self.out1, self.in1, self.acc, self.acc_pair = out0, in0, out1, in1, acc, acc_pair
        self.low, self.high = place.bits[1], place.bits[0]
        self.order = [self.high, self.high | PAIR, 0, PAIR]
        self.first, self.second, self.leaving = {}, {}, {}

    def send(self, i):
        slot = i % 2
        for wait in self.leaving.pop(slot, []):
            wait()

        def emit(at, value):
            self.out0[(slot, *at)] = value.astype(BF16)

        self.product(self.order[i] | self.low, emit)
        self.leaving[slot] = []
        self.first[i] = self.moves.swap(
            self.out0.at[slot], self.in0.at[i], self.in0.at[i], self.place.along(self.low), self.leaving[slot]
        )

    def take(self, i):
        self.first[i]()

        def emit(at, value):
            value = value + self.in0[(i, *at)].astype(F32)
            if i < 2:
                self.out1[(i, *at)] = value.astype(BF16)
            elif i == 2:
                self.acc[at] = value
            else:
                self.acc_pair[at] = value.astype(BF16)

        self.product(self.order[i], emit)
        if i < 2:
            to = self.in1.at[i]
            self.second[i] = Cross(
                self.moves, self.place, self.out1.at[i], to, self.spare.at[2 * i], to, self.spare.at[2 * i + 1], to
            )

    def relay(self, i):
        self.second[i].relay()

    def take_high(self, i):
        self.second[i].arrive()
        total = self.acc_pair if i else self.acc
        step = 64

        @pl.loop(0, total.shape[0] // step)
        def _(k):
            at = pl.ds(pl.multiple_of(k * step, step), step)
            total[at] = (total[at].astype(F32) + self.in1[i, at].astype(F32)).astype(total.dtype)

    def close(self):
        for waits in self.leaving.values():
            for wait in waits:
                wait()


class Blocks:
    def __init__(self, moves, place, slots, order):
        self.moves, self.place, self.slots, self.order = moves, place, slots, order
        self.next, self.waits = 0, {}
        self.start(0)

    def start(self, k):
        if k < len(self.order):
            ref, mask = self.order[k]
            size = self.slots.shape[2]
            at = pl.ds(pl.multiple_of(self.place.block(mask) * size, size), size)
            self.waits[k] = self.moves.load(ref.at[:, at], self.slots.at[k % 2])

    def get(self, ref, mask):
        k = self.next
        assert self.order[k][0] is ref and self.order[k][1] == mask
        self.next += 1
        self.waits.pop(k)()
        self.start(k + 1)
        return self.slots[k % 2]


def backward_kernel(
    bits, groups,
    cot, gain_attn, gain_mlp, starts, cos, sin, gain_q, gain_k,
    mid, hidden, part_two, part_hidden, normed_one, normed_two, cot_rows, qkv_in, att_in, qkv_weight, out_weight, grad_gate, grad_up,
    mixed_t,
    grad_in, hidden_out, gains, feed_own, feed_other, down_own, down_other, qkv_own, qkv_other, out_own, out_other,
    spare_feed, spare_down, spare_qkv, spare_out,
    own, rows_mid, feed, mixed, lhs, lhs_t, part, w_qkv, w_out, qkv, att, datt, dqkv,
    first, ctx_in, pair_in, sending, first_h, ctx_h, pair_h, sending_h, gain_a, gain_m, gain_h, tree, tree_in,
    f_out0, f_in0, f_out1, f_in1, f_acc, f_pair, d_out0, d_in0, d_out1, d_in1, d_acc, d_pair,
    q_out0, q_in0, q_out1, q_in1, q_acc, q_pair, o_out0, o_in0, o_out1, o_in1, o_acc, o_pair,
    send, recv, local,
):
    place = Place(bits)
    moves = Moves(send, recv, local)
    rows, width = cot.shape
    cols = mixed.shape[0]
    tile = lhs.shape[2]
    half = tile // 2
    high, low = bits
    place.greet()

    def lanes(start, size):
        return pl.ds(pl.multiple_of(start, size), size)

    ready_mid = moves.load(mid, hidden_out)
    ready_feed = [
        moves.load(grad_gate, feed.at[:, pl.ds(0, cols)]),
        moves.load(grad_up, feed.at[:, pl.ds(cols, cols)]),
    ]
    masks = [high, high | PAIR, 0, PAIR]
    sends = [m | low for m in masks]
    a, b, c, e = range(4)
    order = [
        (cot_rows, sends[a]), (cot_rows, sends[b]), (cot_rows, masks[a]), (normed_two, sends[a]),
        (cot_rows, sends[e]), (cot_rows, masks[b]), (normed_two, sends[b]), (cot_rows, masks[e]),
        (normed_two, masks[a]), (cot_rows, sends[c]), (normed_two, masks[b]), (normed_one, sends[a]),
        (normed_one, sends[b]), (normed_two, sends[e]), (normed_one, masks[b]), (normed_two, sends[c]),
        (cot_rows, masks[c]), (normed_one, masks[a]), (normed_two, masks[e]), (normed_one, sends[e]),
        (normed_two, masks[c]), (normed_one, sends[c]), (normed_one, masks[e]), (normed_one, masks[c]),
    ]
    blocks = Blocks(moves, place, lhs, order)
    ready_mixed = moves.load(mixed_t, mixed)
    ready_late = [
        moves.load(out_weight, w_out),
        moves.load(att_in, att),
        moves.load(qkv_in, qkv),
        moves.load(qkv_weight, w_qkv),
    ]

    def by_rows(source, right):
        def product(mask, emit):
            lhs_t[...] = blocks.get(source, mask).T
            step = min(512, right.shape[1])

            @pl.loop(0, right.shape[1] // step)
            def _(i):
                at = lanes(i * step, step)
                emit((slice(None), at), dot(lhs_t[...], right[:, at]))

        return product

    def down_product(mask, emit):
        block = blocks.get(cot_rows, mask)
        step = min(256, cols)

        @pl.loop(0, cols // step)
        def _(i):
            at = lanes(i * step, step)
            emit((at, slice(None)), dot(mixed[at], block))

    def out_product(mask, emit):
        at = lanes(place.block(mask) * tile, tile)
        emit((slice(None), slice(None)), dot_rows(att[...], rows_mid[:, at]))

    feed_s = Scatter(moves, place, by_rows(normed_two, feed), f_out0, f_in0, f_out1, f_in1, f_acc, f_pair, spare_feed)
    down_s = Scatter(moves, place, down_product, d_out0, d_in0, d_out1, d_in1, d_acc, d_pair, spare_down)
    qkv_s = Scatter(moves, place, by_rows(normed_one, dqkv), q_out0, q_in0, q_out1, q_in1, q_acc, q_pair, spare_qkv)
    out_s = Scatter(moves, place, out_product, o_out0, o_in0, o_out1, o_in1, o_acc, o_pair, spare_out)

    d = gain_q.shape[1]
    gain_m[...] = jnp.zeros_like(gain_m)
    gain_a[...] = jnp.zeros_like(gain_a)
    gain_h[...] = jnp.zeros_like(gain_h)

    def back_two(at):
        x = hidden_out[at]
        g = cot[at].astype(F32) + norm_back(collect_two.total(at), x, gain_mlp[...], gain_m)
        hidden_out[at] = x + collect_hidden.two(0, at)
        grad_in[at] = g
        own[at] = g.astype(BF16)

    def back_one(at):
        grad_in[at] += norm_back(collect_one.total(at), own[at].astype(F32), gain_attn[...], gain_a)

    def end_hidden(at):
        hidden_out[at] += ctx_h[1, at].astype(F32) + pair_h[at].astype(F32)

    partners = [place.sibling, place.chips[1], *[place.along(x) for x in bits], place.chips[2]]
    tree_waits = []

    def climb():
        k = len(tree_waits)
        if k:
            tree_waits[-1]()
            tree[k] = tree[k - 1] + tree_in[k - 1]
        if k < len(partners):
            tree_waits.append(moves.swap(tree.at[k], tree_in.at[k], tree_in.at[k], partners[k]))

    finals = []

    def pair_final(scatter, other):
        scatter.take_high(1)
        finals.append(moves.swap(scatter.acc_pair, other, other, place.chips[2]))

    def own_final(scatter, mine):
        scatter.take_high(0)
        moves.store(scatter.acc, mine)

    def mates_final(scatter, slot, piece, spare, other):
        scatter.take_high(slot)
        for j in (3, 2) if slot else (1,):
            out = spare(j)
            out[...] = piece(slot, place.at[j][1]).astype(BF16)
            finals.append(moves.swap(out, other.at[j - 1], other.at[j - 1], place.chips[j]))

    def qkv_piece(slot, c):
        return (q_pair if slot else q_acc)[lanes(c * half, half)]

    def out_piece(slot, c):
        return (o_pair if slot else o_acc)[:, lanes(c * half, half)]

    def qkv_spare(j):
        return q_in0.at[j, pl.ds(0, half)]

    def out_spare(j):
        return o_in0.at[j, :, pl.ds(0, half)]

    def attend_part(s):
        attend_back_one(groups, s, qkv, att, datt, starts, cos, sin, gain_q, gain_k, dqkv, gain_h)

    ready_mixed()
    down_s.send(a)
    for wait in ready_feed:
        wait()
    down_s.send(b)
    collect_two = Collect(
        moves, place, lambda j, t: part_two.at[place.rows_of[j] + t], part, first, ctx_in, pair_in, sending, True
    )
    collect_two.to_ctx()
    down_s.take(a)
    collect_hidden = Collect(
        moves, place, lambda j, t: part_hidden.at[place.rows_of[j] + t], part.at[pl.ds(4, 4)],
        first_h, ctx_h, pair_h, sending_h, True,
    )
    feed_s.send(a)
    collect_hidden.fold()
    collect_two.to_pair()
    down_s.send(e)
    down_s.relay(a)
    for wait in ready_late:
        wait()
    down_s.take(b)
    collect_two.finish()
    ready_mid()
    row_loop(rows, back_two)
    spread = Spread(moves, place, own, rows_mid)
    down_s.relay(b)
    feed_s.send(b)
    down_s.take(e)
    feed_s.take(a)
    down_s.send(c)
    spread.from_pair()
    collect_hidden.post_ctx()
    spread.from_ctx()
    pair_final(down_s, down_other)
    spread.from_both()
    feed_s.take(b)
    feed_s.relay(a)
    spread.finish()
    ready_hidden = moves.load(hidden, own)
    @pl.loop(0, 4)
    def _(i):
        at = lanes(i * 2 * rows, 2 * rows)
        datt[at] = dot_cols(rows_mid[at], w_out[...]).astype(BF16)

    attend_part(0)
    collect_hidden.post_pair()
    attend_part(1)
    out_s.send(a)
    out_s.send(b)
    @pl.loop(0, width // tile)
    def _(i):
        at = lanes(i * tile, tile)
        part[:, :, at] = dot_cols(dqkv[...], w_qkv[at]).astype(BF16).reshape(8, rows, tile)

    collect_one = Collect(
        moves, place, lambda j, t: part.at[place.rows_of[j] + t], None, first, ctx_in, pair_in, sending, False
    )
    qkv_s.send(a)
    qkv_s.send(b)
    out_s.send(e)
    feed_s.relay(b)
    feed_s.send(e)
    out_s.take(b)
    collect_one.to_ctx()
    qkv_s.take(b)
    feed_s.send(c)
    collect_one.to_pair()
    out_s.take(e)
    down_s.take(c)
    out_s.send(c)
    qkv_s.take(a)
    feed_s.take(e)
    pair_final(feed_s, feed_other)
    collect_one.finish()
    qkv_s.send(e)
    ready_hidden()
    row_loop(rows, back_one)
    tree[0, :, 0:width] = jnp.sum(gain_a[...], axis=0, keepdims=True)
    tree[0, :, width : 2 * width] = jnp.sum(gain_m[...], axis=0, keepdims=True)
    tree[0, :, 2 * width : 2 * width + d] = jnp.sum(gain_h[0], axis=0, keepdims=True)
    tree[0, :, 2 * width + d : 2 * width + 2 * d] = jnp.sum(gain_h[1], axis=0, keepdims=True)
    climb()
    out_s.relay(b)
    qkv_s.relay(a)
    climb()
    out_s.take(a)
    qkv_s.relay(b)
    climb()
    feed_s.take(c)
    qkv_s.send(c)
    collect_hidden.came()
    row_loop(rows, end_hidden)
    own_final(down_s, down_own)
    climb()
    own_final(feed_s, feed_own)
    out_s.take(c)
    mates_final(out_s, 1, out_piece, out_spare, out_other)
    climb()
    climb()
    gains[...] = tree[len(partners)]
    qkv_s.take(e)
    qkv_s.take(c)
    mates_final(qkv_s, 0, qkv_piece, qkv_spare, qkv_other)
    qkv_own[...] = qkv_piece(0, place.c)
    out_s.relay(a)
    mates_final(qkv_s, 1, qkv_piece, qkv_spare, qkv_other)
    mates_final(out_s, 0, out_piece, out_spare, out_other)
    out_own[...] = out_piece(0, place.c)
    for scatter in (feed_s, down_s, qkv_s, out_s):
        scatter.close()
    for wait in finals:
        wait()
    moves.close()


def join_kernel(
    feed_own, feed_other, down_own, down_other, qkv_own, qkv_other, out_own, out_other, grad_in, hidden, gains,
    g_query, g_key, g_value, g_out, g_gate, g_up, g_down, g_in, h_out, gain_a, gain_m, gain_q, gain_k,
):
    c = lax.axis_index("ctx")
    pair = (lax.axis_index("fsdp") // PAIR) % 2
    cols, n_q = down_own.shape[0], out_own.shape[0]
    n_kv = (qkv_own.shape[1] - n_q) // 2

    def lanes(start, size):
        return pl.ds(pl.multiple_of(start, size), size)

    mine, theirs = lanes(pair * cols, cols), lanes((1 - pair) * cols, cols)
    g_gate[:, mine] = feed_own[:, :cols]
    g_up[:, mine] = feed_own[:, cols:]
    g_down[mine] = down_own[...]
    g_gate[:, theirs] = feed_other[:, :cols].astype(F32)
    g_up[:, theirs] = feed_other[:, cols:].astype(F32)
    g_down[theirs] = down_other[...].astype(F32)
    chunks = [c * 2 + pair, (1 - c) * 2 + pair, c * 2 + 1 - pair, (1 - c) * 2 + 1 - pair]
    for j, chunk in enumerate(chunks):
        qkv = qkv_own[...] if j == 0 else qkv_other[j - 1].astype(F32)
        g_query[:, lanes(chunk * n_q, n_q)] = qkv[:, :n_q]
        g_key[:, lanes(chunk * n_kv, n_kv)] = qkv[:, n_q : n_q + n_kv]
        g_value[:, lanes(chunk * n_kv, n_kv)] = qkv[:, n_q + n_kv :]
        g_out[lanes(chunk * n_q, n_q)] = out_own[...] if j == 0 else out_other[j - 1].astype(F32)
    g_in[...] = grad_in[...]
    h_out[...] = hidden[...]
    width, d = gain_a.shape[1], gain_q.shape[1]
    gain_a[...] = gains[:, :width]
    gain_m[...] = gains[:, width : 2 * width]
    gain_q[...] = gains[:, 2 * width : 2 * width + d]
    gain_k[...] = gains[:, 2 * width + d :]


VMEM_SPEC = pl.BlockSpec(memory_space=pltpu.VMEM)
ANY_SPEC = pl.BlockSpec(memory_space=pl.ANY)


def comm_call(kernel, bits, collective_id, operands, in_specs, outs, out_specs, scratch, nbytes, copies, *more):
    return pl.pallas_call(
        functools.partial(kernel, bits, *more),
        out_shape=outs,
        in_specs=in_specs,
        out_specs=out_specs,
        scratch_shapes=[
            *scratch,
            pltpu.SemaphoreType.DMA((copies,)),
            pltpu.SemaphoreType.DMA((copies,)),
            pltpu.SemaphoreType.DMA((96,)),
        ],
        compiler_params=pltpu.CompilerParams(
            collective_id=collective_id, has_side_effects=True, vmem_limit_bytes=61 << 20
        ),
        cost_estimate=pl.CostEstimate(flops=nbytes * 20, bytes_accessed=nbytes, transcendentals=0),
        name=kernel.__name__,
    )(*operands)


def build(mesh):
    n = mesh.size
    n_f = mesh.shape["fsdp"]
    spread_bits = [b for b in (1 << i for i in range(n_f.bit_length() - 2, -1, -1)) if b != PAIR]
    all_bits = sorted([*spread_bits, PAIR], reverse=True)

    def swap(v, bit):
        return lax.ppermute(v, AXES, [(i, i ^ bit) for i in range(n)])

    def bit_of(f, b):
        return (f // b) % 2

    def in_order(bit, own, other, axis):
        low = jnp.where(bit == 0, own, other)
        high = jnp.where(bit == 0, other, own)
        return jnp.stack([low, high], axis=axis)

    def pick(v, index, axis):
        return lax.dynamic_index_in_dim(v, index, axis, keepdims=False)

    def scatter(keep, got, f, width):
        v = keep + got.astype(F32)
        have = [b for b in all_bits if b != 1]
        v = v.reshape(*([2] * len(have)), width, v.shape[-1])
        for b in [b for b in reversed(spread_bits) if b != 1]:
            axis = have.index(b)
            bit = bit_of(f, b)
            v = pick(v, bit, axis) + swap(pick(v, 1 - bit, axis).astype(BF16), b * 4).astype(F32)
            have.remove(b)
        return v

    def body(
        hidden_in,
        cotangent,
        segments,
        w_query,
        key_projection_weight,
        value_projection_weight,
        w_out,
        w_gate,
        w_up,
        w_down,
        gain_attn,
        gain_mlp,
        gain_query,
        key_norm_gain,
    ):
        rows, width = hidden_in.shape
        d = gain_query.shape[0]
        length = segments.shape[0]
        f, c = lax.axis_index("fsdp"), lax.axis_index("ctx")
        pair = bit_of(f, PAIR)
        at_rows = w_query.shape[0]
        ff_rows = w_gate.shape[0]
        ff_cols = w_gate.shape[1] // 2
        q_cols, kv_cols = w_query.shape[1] // 4, key_projection_weight.shape[1] // 4
        groups = q_cols // kv_cols

        freqs = THETA ** (-2.0 * jnp.arange(d // 2, dtype=F32) / d)
        angles = jnp.arange(length, dtype=jnp.int32).astype(F32)[:, None] * freqs
        table_cos, table_sin = jnp.cos(angles), jnp.sin(angles)
        table = jnp.concatenate([table_cos, table_cos, -table_sin, table_sin], axis=-1)

        n_rows = 8 * rows
        all_rows = jax.ShapeDtypeStruct((n_rows, width), BF16)
        own_rows = jax.ShapeDtypeStruct((rows, width), F32)
        gain_rows = jax.ShapeDtypeStruct((8, width), F32)
        block = pltpu.VMEM((rows, width), BF16)
        nbytes = rows * width * 16
        qkv_cols = q_cols + 2 * kv_cols

        def shape(*dims):
            return jax.ShapeDtypeStruct(dims, BF16)

        copies = 160 + 10 * n_f
        natural = at_rows % 128 == 0 and ff_rows % 128 == 0
        out_dims = (q_cols, width) if natural else (width, q_cols)
        down_dims = (ff_cols, width) if natural else (width, ff_cols)
        out_part = (q_cols, 2 * at_rows) if natural else (2 * at_rows, q_cols)
        down_part_dims = (ff_cols, ff_rows) if natural else (ff_rows, ff_cols)
        n_seq = 2 * length
        all_tables = jax.ShapeDtypeStruct((n_seq, d), F32)

        def v(*dims, dtype=BF16):
            return pltpu.VMEM(dims, dtype)

        (
            residual_mid, normed_one, normed_two, grad_rows, qkv, attended, full_qkv, full_out, starts, cos, sin,
            grad_gate, grad_up, mixed_t, norm_two_part, down_part, *_,
        ) = comm_call(
            forward_kernel, spread_bits, 0,
            (hidden_in, cotangent, gain_attn[None], gain_mlp[None], segments[None], table, gain_query[None],
             key_norm_gain[None], w_query, key_projection_weight, value_projection_weight,
             w_out if natural else w_out.T, w_gate, w_up, w_down if natural else w_down.T),
            [VMEM_SPEC] * 8 + [ANY_SPEC] * 7,
            (own_rows, all_rows, all_rows, all_rows, shape(n_rows, qkv_cols), shape(n_rows, q_cols),
             shape(width, qkv_cols), shape(*out_dims), jax.ShapeDtypeStruct((n_seq, 128), F32), all_tables, all_tables,
             shape(n_rows, ff_cols), shape(n_rows, ff_cols), shape(ff_cols, n_rows), shape(8, rows, width), all_rows,
             shape(4, 2 * at_rows, qkv_cols), shape(4, *out_part), shape(4, ff_rows, ff_cols),
             shape(4, ff_rows, ff_cols), shape(4, *down_part_dims)),
            (VMEM_SPEC, *[ANY_SPEC] * 20),
            [block, block, v(n_rows, width), v(n_rows, width), v(n_rows, width), v(width, qkv_cols), v(*out_dims),
             v(width, ff_cols), v(width, ff_cols), v(*down_dims), v(n_rows, qkv_cols), v(n_rows, q_cols),
             v(8, rows, width), v(n_rows, ff_cols, dtype=F32), v(n_rows, ff_cols, dtype=F32), v(n_rows, ff_cols),
             v(n_rows, ff_cols), v(n_rows, ff_cols), v(ff_cols, n_rows), v(n_seq, 128, dtype=F32),
             v(n_seq, d, dtype=F32), v(n_seq, d, dtype=F32), v(1, length, dtype=jnp.int32),
             *collect_buffers(rows, width)],
            16 * nbytes, copies, groups, natural,
        )
        common = (starts, cos, sin, gain_query[None], key_norm_gain[None])
        backward = one_kernel if natural and len(spread_bits) == 2 else by_steps
        return backward(
            hidden_in, cotangent, residual_mid, gain_attn, gain_mlp, common, norm_two_part, down_part, normed_one,
            normed_two, grad_rows, qkv, attended, full_qkv, full_out, grad_gate, grad_up, mixed_t, (at_rows, ff_rows),
        )

    def one_kernel(
        hidden_in, cotangent, residual_mid, gain_attn, gain_mlp, common, norm_two_part, down_part, normed_one,
        normed_two, grad_rows, qkv, attended, full_qkv, full_out, grad_gate, grad_up, mixed_t, sizes,
    ):
        rows, width = hidden_in.shape
        cols, n_rows = mixed_t.shape
        (at_rows, ff_rows), q_cols, qkv_cols = sizes, attended.shape[1], qkv.shape[1]
        d = common[-1].shape[1]
        kv_cols = (qkv_cols - q_cols) // 2
        groups = q_cols // kv_cols

        def out(dtype, *dims):
            return jax.ShapeDtypeStruct(dims, dtype)

        def v(*dims, dtype=BF16):
            return pltpu.VMEM(dims, dtype)

        def scatter(*block):
            return [v(2, *block), v(4, *block), v(2, *block), v(2, *block), v(*block, dtype=F32), v(*block)]

        n_gain = 2 * width + 2 * d
        nbytes = n_rows * width * 20
        (
            grad_input, hidden_out, gains, feed_own, feed_other, down_own, down_other, qkv_own, qkv_other, out_own,
            out_other, *_,
        ) = comm_call(
            backward_kernel, spread_bits, 2,
            (cotangent, gain_attn[None], gain_mlp[None], *common, residual_mid, hidden_in, norm_two_part,
             down_part.reshape(8, rows, width), normed_one, normed_two, grad_rows, qkv, attended, full_qkv, full_out,
             grad_gate, grad_up, mixed_t),
            [VMEM_SPEC] * 8 + [ANY_SPEC] * 14,
            (out(F32, rows, width), out(F32, rows, width), out(F32, 1, n_gain), out(F32, ff_rows, 2 * cols),
             out(BF16, ff_rows, 2 * cols), out(F32, cols, ff_rows), out(BF16, cols, ff_rows),
             out(F32, at_rows, qkv_cols), out(BF16, 3, at_rows, qkv_cols), out(F32, q_cols, at_rows),
             out(BF16, 3, q_cols, at_rows), out(BF16, 4, ff_rows, 2 * cols), out(BF16, 4, cols, ff_rows),
             out(BF16, 4, ff_rows, qkv_cols), out(BF16, 4, q_cols, ff_rows)),
            (VMEM_SPEC, VMEM_SPEC, VMEM_SPEC, ANY_SPEC, ANY_SPEC, ANY_SPEC, ANY_SPEC, VMEM_SPEC, ANY_SPEC, VMEM_SPEC,
             *[ANY_SPEC] * 5),
            [v(rows, width), v(n_rows, width), v(n_rows, 2 * cols), v(cols, n_rows), v(2, n_rows, ff_rows),
             v(ff_rows, n_rows), v(8, rows, width), v(width, qkv_cols), v(q_cols, width), v(n_rows, qkv_cols),
             v(n_rows, q_cols), v(n_rows, q_cols), v(n_rows, qkv_cols),
             *collect_buffers(rows, width), *collect_buffers(rows, width), v(8, width, dtype=F32), v(8, width, dtype=F32), v(2, 8, d, dtype=F32),
             v(4 + len(spread_bits), 1, n_gain, dtype=F32), v(3 + len(spread_bits), 1, n_gain, dtype=F32),
             *scatter(ff_rows, 2 * cols), *scatter(cols, ff_rows), *scatter(ff_rows, qkv_cols),
             *scatter(q_cols, ff_rows)],
            nbytes, 110, groups,
        )
        own_rows = out(F32, rows, width)
        made = (
            out(F32, at_rows, 4 * q_cols), out(F32, at_rows, 4 * kv_cols), out(F32, at_rows, 4 * kv_cols),
            out(F32, 4 * q_cols, at_rows), out(F32, ff_rows, 2 * cols), out(F32, ff_rows, 2 * cols),
            out(F32, 2 * cols, ff_rows), own_rows, own_rows, out(F32, 1, width), out(F32, 1, width), out(F32, 1, d),
            out(F32, 1, d),
        )
        pieces = pl.pallas_call(
            join_kernel,
            out_shape=made,
            compiler_params=pltpu.CompilerParams(vmem_limit_bytes=61 << 20),
            name="join_kernel",
        )(feed_own, feed_other, down_own, down_other, qkv_own, qkv_other, out_own, out_other, grad_input, hidden_out, gains)
        grads, (grad_input, hidden_out), gains = pieces[:7], pieces[7:9], pieces[9:]
        return hidden_out, grad_input, *grads, *(g[0] for g in gains)

    def by_steps(
        hidden_in, cotangent, residual_mid, gain_attn, gain_mlp, common, norm_two_part, down_part, normed_one,
        normed_two, grad_rows, qkv, attended, full_qkv, full_out, grad_gate, grad_up, mixed_t, sizes,
    ):
        rows, width = hidden_in.shape
        (at_rows, ff_rows), ff_cols, q_cols = sizes, mixed_t.shape[0], attended.shape[1]
        d = common[-1].shape[1]
        kv_cols = (qkv.shape[1] - q_cols) // 2
        groups = q_cols // kv_cols
        natural = full_out.shape[0] != width
        times_t = dot_cols if natural else dot
        f, c = lax.axis_index("fsdp"), lax.axis_index("ctx")
        pair = bit_of(f, PAIR)
        all_rows = jax.ShapeDtypeStruct((8 * rows, width), BF16)
        own_rows = jax.ShapeDtypeStruct((rows, width), F32)
        gain_rows = jax.ShapeDtypeStruct((8, width), F32)
        block = pltpu.VMEM((rows, width), BF16)
        nbytes = rows * width * 16
        grad_mid, gain_mlp_part, grad_mid_rows = comm_call(
            turn_kernel, spread_bits, 2, (norm_two_part.reshape(8, rows, width), residual_mid, cotangent, gain_mlp[None]),
            [ANY_SPEC, VMEM_SPEC, VMEM_SPEC, VMEM_SPEC], (own_rows, gain_rows, all_rows),
            (VMEM_SPEC, VMEM_SPEC, ANY_SPEC),
            [block, pltpu.VMEM((4, rows, width), BF16), *collect_buffers(rows, width)], 2 * nbytes, 40,
        )

        low = bit_of(f, 1)

        def weight_grad(acts, grads):
            split = acts.reshape(acts.shape[0], n_f // 2, 2, width // n_f)
            mine = pick(split, low, 2).reshape(acts.shape[0], -1)
            theirs = pick(split, 1 - low, 2).reshape(acts.shape[0], -1)
            got = swap(dot_rows(theirs, grads).astype(BF16), 4)
            return scatter(dot_rows(mine, grads), got, f, width // n_f)

        def ff_grad(acts, grads):
            v = weight_grad(acts, grads)
            other = swap(pick(v, 1 - pair, 0).astype(BF16), PAIR_BIT).astype(F32)
            return in_order(pair, pick(v, pair, 0), other, 1).reshape(ff_rows, 2 * ff_cols)

        grad_w_gate = ff_grad(normed_two, grad_gate)
        grad_w_up = ff_grad(normed_two, grad_up)
        grad_w_down = ff_grad(grad_rows, mixed_t.T).T

        def attn_grad(acts, grads):
            v = weight_grad(acts, grads)
            v = v.reshape(2, 2, at_rows, v.shape[-1])
            mine = pick(pick(v, pair, 0), c, 0)
            by_ctx = swap(pick(pick(v, pair, 0), 1 - c, 0).astype(BF16), CTX_BIT).astype(F32)
            by_pair = swap(pick(pick(v, 1 - pair, 0), c, 0).astype(BF16), PAIR_BIT).astype(F32)
            by_both = swap(pick(pick(v, 1 - pair, 0), 1 - c, 0).astype(BF16), CTX_BIT | PAIR_BIT).astype(F32)
            near = in_order(pair, mine, by_pair, 1)
            far = in_order(pair, by_ctx, by_both, 1)
            return in_order(c, near, far, 1)

        grad_w_out = attn_grad(grad_mid_rows, attended).reshape(at_rows, 4 * q_cols).T

        datt = times_t(grad_mid_rows, full_out).astype(BF16)
        grad_qkv, head_gains = attend_back(groups, qkv, attended, datt, common)
        norm_one_part = dot_cols(grad_qkv, full_qkv).astype(BF16)
        grad_input, gain_attn_part = comm_call(
            last_kernel, spread_bits, 3, (norm_one_part.reshape(8, rows, width), hidden_in, grad_mid, gain_attn[None]),
            [ANY_SPEC, VMEM_SPEC, VMEM_SPEC, VMEM_SPEC], (own_rows, gain_rows), (VMEM_SPEC, VMEM_SPEC),
            [pltpu.VMEM((4, rows, width), BF16), *collect_buffers(rows, width)], nbytes, 40,
        )
        grad_qkv_w = attn_grad(normed_one, grad_qkv)
        grad_w_query = grad_qkv_w[..., :q_cols].reshape(at_rows, -1)
        grad_w_key = grad_qkv_w[..., q_cols : q_cols + kv_cols].reshape(at_rows, -1)
        grad_w_value = grad_qkv_w[..., q_cols + kv_cols :].reshape(at_rows, -1)

        head_gains = jnp.sum(head_gains, axis=1)
        gains = jnp.concatenate(
            [jnp.sum(gain_attn_part, axis=0), jnp.sum(gain_mlp_part, axis=0), head_gains[0], head_gains[1]]
        ).reshape(-1, d)
        for i in range(n.bit_length() - 1):
            gains = gains + swap(gains, 1 << i)
        gains = gains.reshape(-1)
        teams = sorted(
            sorted(i ^ b ^ p for b in range(4) for p in (0, PAIR_BIT))
            for i in range(0, n, 4)
            if not i & PAIR_BIT
        )
        hidden_out = residual_mid + lax.psum_scatter(
            down_part, AXES, scatter_dimension=0, axis_index_groups=teams, tiled=True
        ).astype(F32)
        return (
            hidden_out,
            grad_input,
            grad_w_query,
            grad_w_key,
            grad_w_value,
            grad_w_out,
            grad_w_gate,
            grad_w_up,
            grad_w_down,
            gains[:width],
            gains[width : 2 * width],
            gains[2 * width : 2 * width + d],
            gains[2 * width + d :],
        )

    return body


def solution(mesh):
    everyone = P(("fsdp", "ctx", "tp"), None)
    attn = P(("fsdp", "ctx"), "tp")
    attn_out = P("tp", ("fsdp", "ctx"))
    ff_in = P("fsdp", ("ctx", "tp"))
    ff_out = P(("ctx", "tp"), "fsdp")
    same = P()
    return jax.shard_map(
        build(mesh),
        mesh=mesh,
        in_specs=(
            everyone, everyone, P("fsdp"), attn, attn, attn, attn_out, ff_in, ff_in, ff_out,
            same, same, same, same,
        ),
        out_specs=(
            everyone, everyone, attn, attn, attn, attn_out, ff_in, ff_in, ff_out,
            same, same, same, same,
        ),
        check_vma=False,
    )
```

```python
import functools

import jax
import jax.numpy as jnp
from jax import lax
from jax.experimental import pallas as pl
from jax.experimental.pallas import tpu as pltpu
from jax.sharding import PartitionSpec as P

EPS = 1e-06
THETA = 1000000.0
AXES = ("fsdp", "ctx", "tp")
MESH = pl.DeviceIdType.MESH
BF16 = jnp.bfloat16
F32 = jnp.float32
TP_BIT, CTX_BIT = 1, 2
PAIR = 2
PAIR_BIT = PAIR * 4


def dot_rows(left, right):
    return lax.dot_general(left, right, (((0,), (0,)), ((), ())), preferred_element_type=F32)


def dot_cols(left, right):
    return lax.dot_general(left, right, (((1,), (1,)), ((), ())), preferred_element_type=F32)


def dot(left, right):
    return lax.dot_general(left, right, (((1,), (0,)), ((), ())), preferred_element_type=F32)


def remote(src, dst, send, recv, device):
    return pltpu.make_async_remote_copy(
        src_ref=src, dst_ref=dst, send_sem=send, recv_sem=recv, device_id=device, device_id_type=MESH
    )


class Moves:
    def __init__(self, send, recv, local):
        self.send, self.recv, self.local = send, recv, local
        self.sent, self.loads = 0, 0
        self.open = []

    def swap(self, src, there, here, device, open_=None):
        k = self.sent
        self.sent += 1
        copy = remote(src, there, self.send.at[k], self.recv.at[k], device)
        copy.start()
        (self.open if open_ is None else open_).append(copy.wait_send)
        return remote(src, here, self.send.at[k], self.recv.at[k], device).wait_recv

    def load(self, src, dst):
        k = self.loads
        self.loads += 1
        copy = pltpu.make_async_copy(src, dst, self.local.at[k])
        copy.start()
        return copy.wait

    def store(self, src, dst):
        self.open.append(self.load(src, dst))

    def close(self):
        for wait in self.open:
            wait()


class Place:
    def __init__(self, bits):
        self.bits = bits
        f, c, t = lax.axis_index("fsdp"), lax.axis_index("ctx"), lax.axis_index("tp")
        self.f, self.c, self.t = f, c, t
        self.pair = (f // PAIR) % 2
        far_f = self.block(PAIR)
        fs, cs = [f, f, far_f, far_f], [c, 1 - c, c, 1 - c]
        pairs = [self.pair, self.pair, 1 - self.pair, 1 - self.pair]
        self.at = [(fs[j], cs[j], pairs[j]) for j in range(4)]
        self.rows_of = [pairs[j] * 4 + cs[j] * 2 for j in range(4)]
        self.chunk_of = [cs[j] * 2 + pairs[j] for j in range(4)]
        self.relay = len(bits) == 2
        self.across_mask = bits[0] | PAIR
        self.inner = (f // bits[0]) % 2 != self.pair
        self.chips = [None, {"ctx": 1 - c}, {"fsdp": far_f}, {"fsdp": far_f, "ctx": 1 - c}]
        self.sibling = {"tp": 1 - t}

    def block(self, mask):
        out = self.f
        for i in range(mask.bit_length()):
            b = 1 << i
            if mask & b:
                out = out + b - 2 * b * ((self.f // b) % 2)
        return out

    def along(self, bit):
        return {"fsdp": self.block(bit)}

    def greet(self):
        barrier = pltpu.get_barrier_semaphore()
        devices = [*self.chips[1:], self.sibling, *[self.along(b) for b in self.bits]]
        if self.relay:
            devices += [self.along(self.across_mask), self.along(self.bits[0] | self.bits[1])]
        for device in devices:
            pl.semaphore_signal(barrier, inc=1, device_id=device, device_id_type=MESH)
        pl.semaphore_wait(barrier, len(devices))


class Cross:
    def __init__(self, moves, place, src, here, came_in, across_to, came_out, pair_to):
        self.place, self.here = place, here
        self.came_in, self.came_out = came_in, came_out
        k = moves.sent
        moves.sent += 4
        pair, across = place.chips[2], place.along(place.across_mask)

        def copy(i, source, to, device):
            return remote(source, to, moves.send.at[k + i], moves.recv.at[k + i], device)

        self.hand = copy(0, src, came_in, pair)
        self.own = copy(1, src, came_out, across)
        self.on = copy(2, came_in, across_to, across)
        self.back = copy(3, came_out, pair_to, pair)
        self.came = [copy(0, came_in, came_in, pair), copy(1, came_out, came_out, across)]
        self.landed = [copy(2, here, here, across), copy(3, here, here, pair)]
        moves.open.append(self.left)

        @pl.when(place.inner)
        def _():
            self.own.start()

        @pl.when(jnp.logical_not(place.inner))
        def _():
            self.hand.start()

    def relay(self):
        @pl.when(self.place.inner)
        def _():
            self.came[0].wait_recv()
            self.on.start()
            self.came[1].wait_recv()
            self.back.start()

    def arrive(self):
        @pl.when(self.place.inner)
        def _():
            self.landed[0].wait_recv()

        @pl.when(jnp.logical_not(self.place.inner))
        def _():
            self.landed[1].wait_recv()

    def left(self):
        @pl.when(self.place.inner)
        def _():
            self.own.wait_send()
            self.on.wait_send()
            self.back.wait_send()

        @pl.when(jnp.logical_not(self.place.inner))
        def _():
            self.hand.wait_send()


class Spread:
    def __init__(self, moves, place, own, out):
        self.moves, self.place, self.out = moves, place, out
        self.rows = own.shape[0]
        self.open = []
        mine = self.at(0, place.t)
        self.here = moves.load(own, mine)
        self.pair = moves.swap(own, mine, self.at(2, place.t), place.chips[2], self.open)
        self.ctx = moves.swap(own, mine, self.at(1, place.t), place.chips[1], self.open)
        self.beside = [moves.swap(own, mine, self.at(0, 1 - place.t), place.sibling, self.open)]

    def at(self, j, t):
        start = (self.place.rows_of[j] + t) * self.rows
        return self.out.at[pl.ds(pl.multiple_of(start, self.rows), self.rows)]

    def hand(self, j):
        block = self.at(j, self.place.t)
        self.beside.append(
            self.moves.swap(block, block, self.at(j, 1 - self.place.t), self.place.sibling, self.open)
        )

    def from_pair(self):
        self.pair()
        block = self.at(2, self.place.t)
        self.both = self.moves.swap(block, block, self.at(3, self.place.t), self.place.chips[1], self.open)
        self.hand(2)

    def from_ctx(self):
        self.ctx()
        self.hand(1)

    def from_both(self):
        self.both()
        self.hand(3)

    def finish(self):
        self.here()
        for wait in (*self.beside, *self.open):
            wait()


class Collect:
    def __init__(self, moves, place, part, held, first, ctx_in, pair_in, sending, load):
        self.moves, self.place = moves, place
        self.first, self.ctx_in, self.pair_in, self.sending = first, ctx_in, pair_in, sending
        t = place.t
        self.hands, self.loads, self.open = {}, {}, []
        for j in (3, 1, 2, 0):
            self.hands[j] = moves.swap(part(j, 1 - t), first.at[j], first.at[j], place.sibling, self.open)
            if load:
                self.loads[j] = moves.load(part(j, t), held.at[j])
        self.held = (lambda j: held.at[j]) if load else (lambda j: part(j, t))

    def two(self, j, at):
        return self.held(j)[at].astype(F32) + self.first[j, at].astype(F32)

    def ready(self, j):
        self.hands[j]()
        if j in self.loads:
            self.loads[j]()

    def to_ctx(self):
        self.waits = {}
        for j, slot in ((3, 0), (1, 1)):
            self.ready(j)

            def body(at):
                self.sending[slot, at] = self.two(j, at).astype(BF16)

            row_loop(self.sending.shape[1], body)
            self.waits[j] = self.moves.swap(
                self.sending.at[slot], self.ctx_in.at[slot], self.ctx_in.at[slot], self.place.chips[1], self.open
            )

    def to_pair(self):
        self.ready(2)
        self.waits[3]()

        def body(at):
            self.sending[2, at] = (self.two(2, at) + self.ctx_in[0, at].astype(F32)).astype(BF16)

        row_loop(self.sending.shape[1], body)
        self.waits[2] = self.moves.swap(
            self.sending.at[2], self.pair_in, self.pair_in, self.place.chips[2], self.open
        )

    def fold(self):
        for j, slot in ((3, 0), (1, 1), (2, 2)):
            self.ready(j)

            def body(at):
                self.sending[slot, at] = self.two(j, at).astype(BF16)

            row_loop(self.sending.shape[1], body)
        self.ready(0)

    def post_ctx(self):
        self.waits = {}
        for j, slot in ((3, 0), (1, 1)):
            self.waits[j] = self.moves.swap(
                self.sending.at[slot], self.ctx_in.at[slot], self.ctx_in.at[slot], self.place.chips[1], self.open
            )

    def post_pair(self):
        self.waits[3]()

        def body(at):
            self.sending[2, at] = (self.sending[2, at].astype(F32) + self.ctx_in[0, at].astype(F32)).astype(BF16)

        row_loop(self.sending.shape[1], body)
        self.waits[2] = self.moves.swap(
            self.sending.at[2], self.pair_in, self.pair_in, self.place.chips[2], self.open
        )

    def came(self):
        for wait in (self.waits[1], self.waits[2], *self.open):
            wait()

    def finish(self):
        self.ready(0)
        self.waits[1]()
        self.waits[2]()
        for wait in self.open:
            wait()

    def total(self, at):
        return self.two(0, at) + (self.ctx_in[1, at].astype(F32) + self.pair_in[at].astype(F32))


def collect_buffers(rows, width):
    return [
        pltpu.VMEM((4, rows, width), BF16),
        pltpu.VMEM((2, rows, width), BF16),
        pltpu.VMEM((rows, width), BF16),
        pltpu.VMEM((3, rows, width), BF16),
    ]


def row_loop(rows, body):
    step = 16

    @pl.loop(0, rows // step)
    def _(i):
        body(pl.ds(pl.multiple_of(i * step, step), step))


def unit_and_scale(x):
    scale = lax.rsqrt(jnp.mean(x * x, axis=-1, keepdims=True) + EPS)
    return x * scale, scale


class Gather:
    def __init__(self, moves, place, block, spare):
        self.moves, self.place, self.block, self.spare = moves, place, block, spare
        self.waits, self.crosses = {}, {}

    def forward(self, mask, src=None):
        done = [i for i, b in enumerate(self.place.bits) if mask & b]
        here = self.block(self.place.block(mask))
        for b in self.place.bits[max(done, default=-1) + 1 :]:
            if self.place.relay and b == self.place.bits[0]:
                far = self.place.across_mask
                slot = 0 if mask == 0 else 2
                self.crosses[mask] = Cross(
                    self.moves, self.place, here if src is None else src, self.block(self.place.block(mask | b)),
                    self.spare.at[slot], self.block(self.place.block(mask ^ PAIR)),
                    self.spare.at[slot + 1], self.block(self.place.block(mask ^ far)),
                )
                self.waits[mask | b] = self.crosses[mask].arrive
                continue
            self.waits[mask | b] = self.moves.swap(
                here if src is None else src, here, self.block(self.place.block(mask | b)), self.place.along(b)
            )

    def masks(self, stage):
        out = [0, PAIR]
        for b in self.place.bits[:stage]:
            out += [m | b for m in out]
        return [m | self.place.bits[stage] for m in out]

    def relay(self, m):
        if self.place.relay:
            self.crosses[m].relay()

    def hop(self, m):
        if self.place.relay:
            self.pass_on(m | self.place.bits[0])
        elif m == PAIR:
            self.middle()

    def pass_on(self, m):
        self.waits.pop(m)()
        self.forward(m)

    def middle(self):
        for stage in range(len(self.place.bits) - 1):
            for m in self.masks(stage):
                if m in self.waits:
                    self.pass_on(m)

    def finish(self):
        for wait in self.waits.values():
            wait()


def head_unit(x):
    scale = lax.rsqrt(jnp.mean(x * x, axis=-1, keepdims=True) + EPS)
    return x * scale, scale


def rot(a, cos, sin):
    return a * cos + pltpu.roll(a, a.shape[-1] // 2, 1) * sin


def rot_back(b, cos, sin):
    return b * cos - pltpu.roll(b, b.shape[-1] // 2, 1) * sin


def allowed_keys(start):
    length = start.shape[0]
    row = lax.broadcasted_iota(jnp.int32, (length, length), 0)
    col = lax.broadcasted_iota(jnp.int32, (length, length), 1)
    return (col.astype(F32) >= start) & (row >= col)


def soft_of(scores):
    peak = jnp.max(scores, axis=-1, keepdims=True)
    lse = peak + jnp.log(jnp.sum(jnp.exp(scores - peak), axis=-1, keepdims=True))
    return jnp.exp(scores - lse)


def attend_one(groups, s, qkv, starts, cos_ref, sin_ref, gain_q, gain_k, out):
    d = gain_q.shape[-1]
    length = cos_ref.shape[0] // 2
    rows = pl.ds(pl.multiple_of(s * length, length), length)
    cos, sin = cos_ref[rows], sin_ref[rows]
    allowed = allowed_keys(starts[rows, 0:1])
    unit_k, _ = head_unit(qkv[rows, groups * d : (groups + 1) * d].astype(F32))
    key = rot(unit_k * gain_k[...], cos, sin).astype(BF16)
    value = qkv[rows, (groups + 1) * d : (groups + 2) * d]
    for g in range(groups):
        unit_q, _ = head_unit(qkv[rows, g * d : (g + 1) * d].astype(F32))
        query = rot(unit_q * gain_q[...], cos, sin).astype(BF16)
        scores = jnp.where(allowed, dot_cols(query, key) * d**-0.5, -jnp.inf)
        soft = soft_of(scores).astype(BF16)
        out[rows, g * d : (g + 1) * d] = dot(soft, value).astype(BF16)


def through_norm(b, unit, scale, gain):
    e = b * gain
    return scale * (e - unit * jnp.mean(e * unit, axis=-1, keepdims=True))


def attend_back_one(
    groups, s, qkv, att, datt, starts, cos_ref, sin_ref, gain_q, gain_k, grad, gains
):
    d = gain_q.shape[-1]
    length = cos_ref.shape[0] // 2
    rows = pl.ds(pl.multiple_of(s * length, length), length)
    cos, sin = cos_ref[rows], sin_ref[rows]
    scale = d**-0.5
    allowed = allowed_keys(starts[rows, 0:1])
    at_k, at_v = slice(groups * d, (groups + 1) * d), slice((groups + 1) * d, (groups + 2) * d)
    unit_k, scale_k = head_unit(qkv[rows, at_k].astype(F32))
    key = rot(unit_k * gain_k[...], cos, sin).astype(BF16)
    value = qkv[rows, at_v]
    key_grad = jnp.zeros(unit_k.shape, F32)
    value_grad = jnp.zeros(unit_k.shape, F32)
    for g in range(groups):
        at = slice(g * d, (g + 1) * d)
        unit_q, scale_q = head_unit(qkv[rows, at].astype(F32))
        query = rot(unit_q * gain_q[...], cos, sin).astype(BF16)
        scores = jnp.where(allowed, dot_cols(query, key) * scale, -jnp.inf)
        soft = soft_of(scores)
        up = datt[rows, at]
        delta = jnp.sum(up.astype(F32) * att[rows, at].astype(F32), axis=-1, keepdims=True)
        ds = (soft * (dot_cols(up, value) - delta) * scale).astype(BF16)
        value_grad += dot_rows(soft.astype(BF16), up)
        key_grad += dot_rows(ds, query)
        b = rot_back(dot(ds, key), cos, sin)
        gains[0] += jnp.sum((b * unit_q).reshape(-1, 8, d), axis=0)
        grad[rows, at] = through_norm(b, unit_q, scale_q, gain_q[...]).astype(BF16)
    b = rot_back(key_grad, cos, sin)
    gains[1] += jnp.sum((b * unit_k).reshape(-1, 8, d), axis=0)
    grad[rows, at_k] = through_norm(b, unit_k, scale_k, gain_k[...]).astype(BF16)
    grad[rows, at_v] = value_grad.astype(BF16)


def attend_back_kernel(
    groups, qkv, att, datt, starts, cos, sin, gain_q, gain_k, grad, gains
):
    gains[...] = jnp.zeros_like(gains)

    @pl.loop(0, 2)
    def _(s):
        attend_back_one(groups, s, qkv, att, datt, starts, cos, sin, gain_q, gain_k, grad, gains)


def attend_back(groups, qkv, att, datt, common):
    n_rows, width = qkv.shape
    d = width // (groups + 2)
    length = n_rows // 2
    return pl.pallas_call(
        functools.partial(attend_back_kernel, groups),
        out_shape=(jax.ShapeDtypeStruct(qkv.shape, BF16), jax.ShapeDtypeStruct((2, 8, d), F32)),
        compiler_params=pltpu.CompilerParams(vmem_limit_bytes=40 << 20),
        cost_estimate=pl.CostEstimate(
            flops=n_rows * groups * length * (10 * d + 30),
            bytes_accessed=n_rows * width * 8,
            transcendentals=n_rows * groups * length * 2,
        ),
        name="attend_back",
    )(qkv, att, datt, *common)


def forward_kernel(
    bits, groups, natural,
    hidden, cot, gain_attn, gain_mlp, seg, table, gain_q, gain_k, wq, wk, wv, wo, wg, wu, wd,
    mid, normed_one, normed_two, cot_out, qkv_out, att_out, qkv_weight, out_weight, starts_out, cos_out, sin_out,
    grad_gate_out, grad_up_out, mixed_out, part_out, down_out, spare_qkv, spare_out, spare_gate, spare_up, spare_down, early_in,
    own_one, own_two, rows_one, rows_two, rows_cot, w_qkv, w_out, w_gate, w_up, w_down, qkv, att, part,
    gate, up, grad_gate, grad_up, mixed, mixed_t, starts, cos, sin, seg_in, early, first, ctx_in, pair_in, sending,
    send, recv, local,
):
    place = Place(bits)
    moves = Moves(send, recv, local)
    rows, width = hidden.shape
    at_rows, ff_rows, ff_cols = wq.shape[0], wg.shape[0], wg.shape[1] // 2
    q_cols, kv_cols = wq.shape[1] // 4, wk.shape[1] // 4
    n_rows, length = rows_one.shape[0], seg.shape[1]

    def lanes(start, size):
        return pl.ds(pl.multiple_of(start, size), size)

    def qkv_rows(f, c=None):
        if c is None:
            return lanes(f * 2 * at_rows, 2 * at_rows)
        return lanes((f * 2 + c) * at_rows, at_rows)

    place.greet()

    def out_block(f, c=None):
        return w_out.at[:, qkv_rows(f, c)] if natural else w_out.at[qkv_rows(f, c)]

    def out_chunk(j):
        at = lanes(place.chunk_of[j] * q_cols, q_cols)
        return wo.at[at] if natural else wo.at[:, at]

    pieces = (
        (wq, q_cols, pl.ds(0, q_cols)),
        (wk, kv_cols, pl.ds(q_cols, kv_cols)),
        (wv, kv_cols, pl.ds(q_cols + kv_cols, kv_cols)),
    )
    f0, c0, _ = place.at[0]
    qkv_in, out_in = {}, {}

    def rows_block(w):
        return lambda f: w.at[lanes(f * ff_rows, ff_rows)]

    def cols_block(w):
        return lambda f: w.at[:, lanes(f * ff_rows, ff_rows)]

    mine, theirs = lanes(place.pair * ff_cols, ff_cols), lanes((1 - place.pair) * ff_cols, ff_cols)
    feed = [
        (Gather(moves, place, rows_block(w_gate), spare_gate), wg.at[:, mine], wg.at[:, theirs]),
        (Gather(moves, place, rows_block(w_up), spare_up), wu.at[:, mine], wu.at[:, theirs]),
        (Gather(moves, place, cols_block(w_down), spare_down), wd.at[mine], wd.at[theirs])
        if natural
        else (Gather(moves, place, rows_block(w_down), spare_down), wd.at[:, mine], wd.at[:, theirs]),
    ]
    own_feed = [moves.load(own, gather.block(place.f)) for gather, own, _ in feed]

    def swap_pair(i):
        gather, _, other = feed[i]
        gather.waits[PAIR] = moves.swap(
            other, gather.block(place.f), gather.block(place.block(PAIR)), place.along(PAIR)
        )

    def send_feed(i):
        gather, own, _ = feed[i]
        gather.forward(0, own)
        gather.pass_on(PAIR)

    early_waits = []

    def send_early(i):
        if place.relay:
            high, low = bits
            mask = (high, high | PAIR)[i] | low
            at = lanes(place.block(mask) * ff_rows, ff_rows)
            early[i] = dot(mixed_t[...], rows_cot[:, at]).astype(BF16)
            early_waits.append(moves.swap(early.at[i], early_in.at[i], early_in.at[i], place.along(low)))

    step = 2 * rows
    wide = min(256, w_qkv.shape[1])
    qkv_gather = Gather(moves, place, lambda f: w_qkv.at[qkv_rows(f)], spare_qkv)
    out_gather = Gather(moves, place, out_block, spare_out)

    def norm_one(at):
        unit, _ = unit_and_scale(hidden[at].astype(F32))
        own_one[at] = (unit * gain_attn[...]).astype(BF16)

    def norm_two(at):
        x = hidden[at].astype(F32) + collect.total(at)
        mid[at] = x
        unit, _ = unit_and_scale(x)
        own_two[at] = (unit * gain_mlp[...]).astype(BF16)

    def columns_of(weight, at):
        return (dot, weight[:, at]) if natural else (dot_cols, weight[at])

    def attend_part(s):
        attend_one(groups, s, qkv, starts, cos, sin, gain_q, gain_k, att)

    def gate_part(i):
        at = pl.ds(i * step, step)
        gate[at] = dot(rows_two[at], w_gate[...])

    def up_part(i):
        at = pl.ds(i * step, step)
        u = dot(rows_two[at], w_up[...])
        up[at] = u
        g = gate[at]
        mix = g * jax.nn.sigmoid(g) * u
        mixed[at] = mix.astype(BF16)
        mixed_t[:, at] = mix.T.astype(BF16)

    def back_part(i):
        at = pl.ds(i * step, step)
        m = (dot_cols if natural else dot)(rows_cot[at], w_down[...])
        g = gate[at]
        s = jax.nn.sigmoid(g)
        grad_gate[at] = (m * up[at] * s * (1.0 + g * (1.0 - s))).astype(BF16)
        grad_up[at] = (m * (g * s)).astype(BF16)

    for j in (3, 2, 1):
        fj, cj, _ = place.at[j]
        out_in[j] = moves.swap(out_chunk(j), out_block(f0, c0), out_block(fj, cj), place.chips[j])
    out_in[0] = moves.load(out_chunk(0), out_block(f0, c0))
    for j in (1, 3, 2):
        fj, cj, _ = place.at[j]
        qkv_in[j] = [
            moves.swap(
                w.at[:, lanes(place.chunk_of[j] * size, size)],
                w_qkv.at[qkv_rows(f0, c0), to],
                w_qkv.at[qkv_rows(fj, cj), to],
                place.chips[j],
            )
            for w, size, to in pieces
        ]
    qkv_in[0] = [
        moves.load(w.at[:, lanes(place.chunk_of[0] * size, size)], w_qkv.at[qkv_rows(f0, c0), to])
        for w, size, to in pieces
    ]
    out_in[0]()
    out_in[1]()
    out_gather.forward(0)
    row_loop(rows, norm_one)
    spread_one = Spread(moves, place, own_one, rows_one)
    out_in[2]()
    out_in[3]()
    out_gather.forward(PAIR)
    for wait in (*qkv_in[0], *qkv_in[1]):
        wait()
    qkv_gather.forward(0)
    for wait in (*qkv_in[2], *qkv_in[3]):
        wait()
    qkv_gather.forward(PAIR)
    feed[0][0].forward(0, feed[0][1])
    seg_wait = moves.swap(seg, seg_in, seg_in, place.chips[2])
    swap_pair(0)
    spread_one.from_pair()
    out_gather.relay(0)
    qkv_gather.relay(0)
    out_gather.hop(0)
    out_gather.relay(PAIR)
    qkv_gather.relay(PAIR)
    out_gather.hop(PAIR)
    spread_one.from_ctx()
    swap_pair(1)
    spread_one.from_both()
    spread_one.finish()
    normed_stored = moves.load(rows_one, normed_one)
    qkv_gather.hop(0)
    qkv_gather.hop(PAIR)
    feed[0][0].relay(0)
    feed[1][0].forward(0, feed[1][1])
    feed[0][0].pass_on(PAIR)
    out_gather.finish()
    moves.store(w_out, out_weight)
    spread_cot = Spread(moves, place, cot, rows_cot)
    qkv_gather.finish()
    moves.store(w_qkv, qkv_weight)
    @pl.loop(0, w_qkv.shape[1] // wide)
    def _(i):
        at = lanes(i * wide, wide)
        qkv[:, at] = dot(rows_one[...], w_qkv[:, at]).astype(BF16)

    moves.store(qkv, qkv_out)
    seg_wait()
    pair_first = place.pair == 0
    own_seg, far_seg = seg[...].astype(F32), seg_in[...].astype(F32)
    for i in range(2):
        here = pair_first if i == 0 else jnp.logical_not(pair_first)
        flags = jnp.where(here, own_seg, far_seg)
        both = jnp.broadcast_to(flags, (128, length)).T[:, 0:1]
        start = jnp.sum((flags < both).astype(F32), axis=1, keepdims=True)
        row = lax.broadcasted_iota(jnp.int32, (length, length), 0).astype(F32)
        col = lax.broadcasted_iota(jnp.int32, (length, length), 1).astype(F32)
        chosen = (row - start == col).astype(F32)
        at = pl.ds(i * length, length)
        both_tables = lax.dot_general(
            chosen, table[...], (((1,), (0,)), ((), ())),
            precision=lax.Precision.HIGHEST, preferred_element_type=F32,
        )
        d = gain_q.shape[1]
        starts[at] = jnp.broadcast_to(start, (length, 128))
        cos[at] = both_tables[:, :d]
        sin[at] = both_tables[:, d:]
    moves.store(starts, starts_out)
    moves.store(cos, cos_out)
    moves.store(sin, sin_out)
    feed[0][0].hop(0)
    attend_part(0)
    attend_part(1)
    moves.store(att, att_out)
    @pl.loop(0, width // 256)
    def _(i):
        at = lanes(i * 256, 256)
        times, block = columns_of(w_out, at)
        part[:, :, at] = times(att[...], block).astype(BF16).reshape(8, rows, 256)

    collect = Collect(
        moves, place, lambda j, t: part.at[place.rows_of[j] + t], None, first, ctx_in, pair_in, sending, False
    )
    feed[1][0].pass_on(PAIR)
    feed[1][0].relay(0)
    collect.to_ctx()
    spread_cot.from_ctx()
    feed[0][0].relay(PAIR)
    collect.to_pair()
    feed[1][0].relay(PAIR)
    feed[0][0].hop(PAIR)
    swap_pair(2)
    collect.finish()
    row_loop(rows, norm_two)
    spread_two = Spread(moves, place, own_two, rows_two)
    spread_cot.from_pair()
    feed[1][0].hop(0)
    feed[1][0].hop(PAIR)
    own_feed[0]()
    feed[0][0].finish()
    feed[2][0].forward(0, feed[2][1])
    feed[2][0].pass_on(PAIR)
    spread_two.from_pair()
    spread_two.from_ctx()
    feed[2][0].relay(0)
    feed[2][0].relay(PAIR)
    feed[2][0].hop(0)
    spread_two.from_both()
    own_feed[1]()
    feed[1][0].finish()
    spread_cot.from_both()
    spread_two.finish()
    moves.store(rows_two, normed_two)
    gate_part(0)
    up_part(0)
    feed[2][0].hop(PAIR)
    gate_part(1)
    gate_part(2)
    up_part(1)
    spread_cot.finish()
    moves.store(rows_cot, cot_out)
    gate_part(3)
    up_part(2)
    up_part(3)
    moves.store(mixed_t, mixed_out)
    send_early(0)
    send_early(1)
    own_feed[2]()
    feed[2][0].finish()
    back_part(0)
    back_part(1)
    back_part(2)
    back_part(3)
    moves.store(grad_gate, grad_gate_out)
    moves.store(grad_up, grad_up_out)
    normed_stored()

    @pl.loop(0, width // 256)
    def _(i):
        at = lanes(i * 256, 256)
        times, block = columns_of(w_down, at)
        rows_one[:, at] = times(mixed[...], block).astype(BF16)

    moves.store(rows_one, down_out)
    for half in range(2):

        @pl.loop(0, width // 512)
        def _(i):
            at = lanes(half * (width // 2) + i * 256, 256)
            both = dot_cols(grad_gate[...], w_gate[at]) + dot_cols(grad_up[...], w_up[at])
            part[:, :, at] = both.astype(BF16).reshape(8, rows, 256)

        at = pl.ds(half * (width // 2), width // 2)
        moves.store(part.at[:, :, at], part_out.at[:, :, at])

    for wait in early_waits:
        wait()
    moves.close()


def norm_back(grad, x, gain, gain_grad):
    unit, scale = unit_and_scale(x)
    gain_grad[...] += jnp.sum((grad * unit).reshape(-1, 8, grad.shape[-1]), axis=0)
    e = grad * gain
    return scale * (e - unit * jnp.mean(e * unit, axis=-1, keepdims=True))


def turn_kernel(
    bits, partial, mid, cot, gain, grad_mid, gain_grad, out,
    own, held, first, ctx_in, pair_in, sending, send, recv, local,
):
    place = Place(bits)
    moves = Moves(send, recv, local)
    place.greet()
    collect = Collect(
        moves, place, lambda j, t: partial.at[place.rows_of[j] + t], held, first, ctx_in, pair_in, sending, True
    )
    collect.to_ctx()
    collect.to_pair()
    collect.finish()
    gain_grad[...] = jnp.zeros_like(gain_grad)

    def back(at):
        g = cot[at].astype(F32) + norm_back(collect.total(at), mid[at], gain[...], gain_grad)
        grad_mid[at] = g
        own[at] = g.astype(BF16)

    row_loop(mid.shape[0], back)
    spread = Spread(moves, place, own, out)
    spread.from_pair()
    spread.from_ctx()
    spread.from_both()
    spread.finish()
    moves.close()


def last_kernel(
    bits, partial, hidden, grad_mid, gain, grad_in, gain_grad,
    held, first, ctx_in, pair_in, sending, send, recv, local,
):
    place = Place(bits)
    moves = Moves(send, recv, local)
    place.greet()
    collect = Collect(
        moves, place, lambda j, t: partial.at[place.rows_of[j] + t], held, first, ctx_in, pair_in, sending, True
    )
    collect.to_ctx()
    collect.to_pair()
    collect.finish()
    gain_grad[...] = jnp.zeros_like(gain_grad)

    def back(at):
        grad_in[at] = grad_mid[at] + norm_back(
            collect.total(at), hidden[at].astype(F32), gain[...], gain_grad
        )

    row_loop(hidden.shape[0], back)
    moves.close()


class Scatter:
    def __init__(self, moves, place, product, out0, in0, out1, in1, acc, acc_pair, spare):
        self.moves, self.place, self.product, self.spare = moves, place, product, spare
        self.out0, self.in0, self.out1, self.in1, self.acc, self.acc_pair = out0, in0, out1, in1, acc, acc_pair
        self.low, self.high = place.bits[1], place.bits[0]
        self.order = [self.high, self.high | PAIR, 0, PAIR]
        self.first, self.second, self.leaving = {}, {}, {}

    def send(self, i):
        slot = i % 2
        for wait in self.leaving.pop(slot, []):
            wait()

        def emit(at, value):
            self.out0[(slot, *at)] = value.astype(BF16)

        self.product(self.order[i] | self.low, emit)
        self.leaving[slot] = []
        self.first[i] = self.moves.swap(
            self.out0.at[slot], self.in0.at[i], self.in0.at[i], self.place.along(self.low), self.leaving[slot]
        )

    def take(self, i):
        self.first[i]()

        def emit(at, value):
            value = value + self.in0[(i, *at)].astype(F32)
            if i < 2:
                self.out1[(i, *at)] = value.astype(BF16)
            elif i == 2:
                self.acc[at] = value
            else:
                self.acc_pair[at] = value.astype(BF16)

        self.product(self.order[i], emit)
        if i < 2:
            to = self.in1.at[i]
            self.second[i] = Cross(
                self.moves, self.place, self.out1.at[i], to, self.spare.at[2 * i], to, self.spare.at[2 * i + 1], to
            )

    def relay(self, i):
        self.second[i].relay()

    def take_high(self, i):
        self.second[i].arrive()
        total = self.acc_pair if i else self.acc
        step = 64

        @pl.loop(0, total.shape[0] // step)
        def _(k):
            at = pl.ds(pl.multiple_of(k * step, step), step)
            total[at] = (total[at].astype(F32) + self.in1[i, at].astype(F32)).astype(total.dtype)

    def close(self):
        for waits in self.leaving.values():
            for wait in waits:
                wait()


class Blocks:
    def __init__(self, moves, place, slots, order):
        self.moves, self.place, self.slots, self.order = moves, place, slots, order
        self.next, self.waits = 0, {}
        self.start(0)

    def start(self, k):
        if k < len(self.order):
            ref, mask = self.order[k]
            size = self.slots.shape[2]
            at = pl.ds(pl.multiple_of(self.place.block(mask) * size, size), size)
            self.waits[k] = self.moves.load(ref.at[:, at], self.slots.at[k % 2])

    def get(self, ref, mask):
        k = self.next
        assert self.order[k][0] is ref and self.order[k][1] == mask
        self.next += 1
        self.waits.pop(k)()
        self.start(k + 1)
        return self.slots[k % 2]


def backward_kernel(
    bits, groups,
    cot, gain_attn, gain_mlp, starts, cos, sin, gain_q, gain_k,
    mid, hidden, part_two, part_hidden, normed_one, normed_two, cot_rows, qkv_in, att_in, qkv_weight, out_weight, grad_gate, grad_up,
    mixed_t, early_in,
    grad_in, hidden_out, gains, feed_own, feed_other, down_own, down_other, qkv_own, qkv_other, out_own, out_other,
    spare_feed, spare_down, spare_qkv, spare_out,
    own, rows_mid, feed, mixed, lhs, lhs_t, part, w_qkv, w_out, qkv, att, datt, dqkv,
    first, ctx_in, pair_in, sending, first_h, ctx_h, pair_h, sending_h, gain_a, gain_m, gain_h, tree, tree_in,
    f_out0, f_in0, f_out1, f_in1, f_acc, f_pair, d_out0, d_in0, d_out1, d_in1, d_acc, d_pair,
    q_out0, q_in0, q_out1, q_in1, q_acc, q_pair, o_out0, o_in0, o_out1, o_in1, o_acc, o_pair,
    send, recv, local,
):
    place = Place(bits)
    moves = Moves(send, recv, local)
    rows, width = cot.shape
    cols = mixed.shape[0]
    tile = lhs.shape[2]
    half = tile // 2
    high, low = bits
    place.greet()

    def lanes(start, size):
        return pl.ds(pl.multiple_of(start, size), size)

    ready_mid = moves.load(mid, hidden_out)
    ready_feed = [
        moves.load(grad_gate, feed.at[:, pl.ds(0, cols)]),
        moves.load(grad_up, feed.at[:, pl.ds(cols, cols)]),
    ]
    masks = [high, high | PAIR, 0, PAIR]
    sends = [m | low for m in masks]
    a, b, c, e = range(4)
    order = [
        (cot_rows, masks[a]), (normed_two, sends[a]), (cot_rows, masks[b]), (normed_two, sends[b]),
        (cot_rows, sends[e]), (normed_two, masks[a]), (normed_two, sends[e]), (normed_two, masks[b]),
        (normed_two, sends[c]), (cot_rows, masks[e]), (cot_rows, sends[c]), (normed_two, masks[e]),
        (normed_one, sends[a]), (normed_one, sends[b]), (normed_one, masks[a]), (normed_one, sends[e]),
        (normed_one, sends[c]), (cot_rows, masks[c]), (normed_one, masks[b]), (normed_one, masks[e]),
        (normed_one, masks[c]), (normed_two, masks[c]),
    ]
    blocks = Blocks(moves, place, lhs, order)
    ready_mixed = moves.load(mixed_t, mixed)
    ready_early = [moves.load(early_in.at[i], d_in0.at[i]) for i in range(2)]
    ready_late = [
        moves.load(out_weight, w_out),
        moves.load(att_in, att),
        moves.load(qkv_in, qkv),
        moves.load(qkv_weight, w_qkv),
    ]

    def by_rows(source, right):
        def product(mask, emit):
            lhs_t[...] = blocks.get(source, mask).T
            step = min(512, right.shape[1])

            @pl.loop(0, right.shape[1] // step)
            def _(i):
                at = lanes(i * step, step)
                emit((slice(None), at), dot(lhs_t[...], right[:, at]))

        return product

    def down_product(mask, emit):
        block = blocks.get(cot_rows, mask)
        step = min(256, cols)

        @pl.loop(0, cols // step)
        def _(i):
            at = lanes(i * step, step)
            emit((at, slice(None)), dot(mixed[at], block))

    def out_product(mask, emit):
        at = lanes(place.block(mask) * tile, tile)
        emit((slice(None), slice(None)), dot_rows(att[...], rows_mid[:, at]))

    feed_s = Scatter(moves, place, by_rows(normed_two, feed), f_out0, f_in0, f_out1, f_in1, f_acc, f_pair, spare_feed)
    down_s = Scatter(moves, place, down_product, d_out0, d_in0, d_out1, d_in1, d_acc, d_pair, spare_down)
    down_s.first = dict(enumerate(ready_early))
    qkv_s = Scatter(moves, place, by_rows(normed_one, dqkv), q_out0, q_in0, q_out1, q_in1, q_acc, q_pair, spare_qkv)
    out_s = Scatter(moves, place, out_product, o_out0, o_in0, o_out1, o_in1, o_acc, o_pair, spare_out)

    d = gain_q.shape[1]
    gain_m[...] = jnp.zeros_like(gain_m)
    gain_a[...] = jnp.zeros_like(gain_a)
    gain_h[...] = jnp.zeros_like(gain_h)

    def back_two(at):
        x = hidden_out[at]
        g = cot[at].astype(F32) + norm_back(collect_two.total(at), x, gain_mlp[...], gain_m)
        hidden_out[at] = x + collect_hidden.two(0, at)
        grad_in[at] = g
        own[at] = g.astype(BF16)

    def back_one(at):
        grad_in[at] += norm_back(collect_one.total(at), own[at].astype(F32), gain_attn[...], gain_a)

    def end_hidden(at):
        hidden_out[at] += ctx_h[1, at].astype(F32) + pair_h[at].astype(F32)

    tree_waits = []

    def climb():
        k = len(tree_waits)
        if k == 1:
            tree_waits[0]()
            tree[1] = tree[0] + tree_in[0]
        if k > 1:
            for wait in tree_waits[-1]:
                wait()
            at = 1 + 4 * (k - 2)
            tree[k] = (tree_in[at] + tree_in[at + 1]) + (tree_in[at + 2] + tree_in[at + 3])
        if k == 0:
            tree_waits.append(moves.swap(tree.at[0], tree_in.at[0], tree_in.at[0], place.sibling))
        elif k < 3:
            mine, others = team(k)
            slots = 1 + 4 * (k - 1)
            tree_in[slots + mine] = tree[k]
            tree_waits.append(
                [
                    moves.swap(tree.at[k], tree_in.at[slots + mine], tree_in.at[slots + index], device)
                    for index, device in others
                ]
            )

    def team(k):
        if k == 1:
            return place.rows_of[0] // 2, [(place.rows_of[j] // 2, place.chips[j]) for j in (3, 2, 1)]

        def index(mask):
            f = place.block(mask)
            return (f // high) % 2 * 2 + f % 2

        return index(0), [(index(m), place.along(m)) for m in (high | low, high, low)]

    finals = []

    def pair_final(scatter, other):
        scatter.take_high(1)
        finals.append(moves.swap(scatter.acc_pair, other, other, place.chips[2]))

    def own_final(scatter, mine):
        scatter.take_high(0)
        moves.store(scatter.acc, mine)

    def mates_final(scatter, slot, piece, spare, other):
        scatter.take_high(slot)
        for j in (3, 2) if slot else (1,):
            out = spare(j)
            out[...] = piece(slot, place.at[j][1]).astype(BF16)
            finals.append(moves.swap(out, other.at[j - 1], other.at[j - 1], place.chips[j]))

    def qkv_piece(slot, c):
        return (q_pair if slot else q_acc)[lanes(c * half, half)]

    def out_piece(slot, c):
        return (o_pair if slot else o_acc)[:, lanes(c * half, half)]

    def qkv_spare(j):
        return q_in0.at[j, pl.ds(0, half)]

    def out_spare(j):
        return o_in0.at[j, :, pl.ds(0, half)]

    def attend_part(s):
        attend_back_one(groups, s, qkv, att, datt, starts, cos, sin, gain_q, gain_k, dqkv, gain_h)

    ready_mixed()
    down_s.take(a)
    for wait in ready_feed:
        wait()
    collect_two = Collect(
        moves, place, lambda j, t: part_two.at[place.rows_of[j] + t], part, first, ctx_in, pair_in, sending, True
    )
    feed_s.send(a)
    down_s.take(b)
    collect_two.to_ctx()
    feed_s.send(b)
    down_s.relay(a)
    collect_hidden = Collect(
        moves, place, lambda j, t: part_hidden.at[place.rows_of[j] + t], part.at[pl.ds(4, 4)],
        first_h, ctx_h, pair_h, sending_h, True,
    )
    collect_two.to_pair()
    down_s.relay(b)
    collect_hidden.fold()
    down_s.send(e)
    feed_s.take(a)
    collect_two.finish()
    ready_mid()
    row_loop(rows, back_two)
    spread = Spread(moves, place, own, rows_mid)
    feed_s.send(e)
    feed_s.take(b)
    spread.from_ctx()
    feed_s.send(c)
    down_s.take(e)
    pair_final(down_s, down_other)
    feed_s.relay(a)
    for wait in ready_late:
        wait()
    spread.from_pair()
    collect_hidden.post_ctx()
    down_s.send(c)
    feed_s.relay(b)
    spread.from_both()
    spread.finish()
    ready_hidden = moves.load(hidden, own)
    @pl.loop(0, 4)
    def _(i):
        at = lanes(i * 2 * rows, 2 * rows)
        datt[at] = dot_cols(rows_mid[at], w_out[...]).astype(BF16)

    attend_part(0)
    out_s.send(a)
    out_s.send(b)
    collect_hidden.post_pair()
    attend_part(1)
    @pl.loop(0, width // tile)
    def _(i):
        at = lanes(i * tile, tile)
        part[:, :, at] = dot_cols(dqkv[...], w_qkv[at]).astype(BF16).reshape(8, rows, tile)

    feed_s.take(e)
    qkv_s.send(a)
    collect_one = Collect(
        moves, place, lambda j, t: part.at[place.rows_of[j] + t], None, first, ctx_in, pair_in, sending, False
    )
    qkv_s.send(b)
    out_s.take(b)
    collect_one.to_ctx()
    pair_final(feed_s, feed_other)
    qkv_s.take(a)
    qkv_s.send(e)
    qkv_s.send(c)
    collect_one.to_pair()
    down_s.take(c)
    out_s.send(e)
    out_s.send(c)
    qkv_s.relay(a)
    out_s.relay(b)
    qkv_s.take(b)
    qkv_s.take(e)
    qkv_s.take(c)
    feed_s.take(c)
    collect_one.finish()
    ready_hidden()
    row_loop(rows, back_one)
    tree[0, :, 0:width] = jnp.sum(gain_a[...], axis=0, keepdims=True)
    tree[0, :, width : 2 * width] = jnp.sum(gain_m[...], axis=0, keepdims=True)
    tree[0, :, 2 * width : 2 * width + d] = jnp.sum(gain_h[0], axis=0, keepdims=True)
    tree[0, :, 2 * width + d : 2 * width + 2 * d] = jnp.sum(gain_h[1], axis=0, keepdims=True)
    out_s.take(c)
    out_s.take(e)
    climb()
    out_s.take(a)
    climb()
    own_final(down_s, down_own)
    mates_final(qkv_s, 0, qkv_piece, qkv_spare, qkv_other)
    qkv_own[...] = qkv_piece(0, place.c)
    qkv_s.relay(b)
    climb()
    mates_final(out_s, 1, out_piece, out_spare, out_other)
    own_final(feed_s, feed_own)
    out_s.relay(a)
    mates_final(qkv_s, 1, qkv_piece, qkv_spare, qkv_other)
    climb()
    gains[...] = tree[3]
    mates_final(out_s, 0, out_piece, out_spare, out_other)
    out_own[...] = out_piece(0, place.c)
    collect_hidden.came()
    row_loop(rows, end_hidden)
    for scatter in (feed_s, down_s, qkv_s, out_s):
        scatter.close()
    for wait in finals:
        wait()
    moves.close()


def join_kernel(
    feed_own, feed_other, down_own, down_other, qkv_own, qkv_other, out_own, out_other, grad_in, hidden, gains,
    g_query, g_key, g_value, g_out, g_gate, g_up, g_down, g_in, h_out, gain_a, gain_m, gain_q, gain_k,
):
    c = lax.axis_index("ctx")
    pair = (lax.axis_index("fsdp") // PAIR) % 2
    cols, n_q = down_own.shape[0], out_own.shape[0]
    n_kv = (qkv_own.shape[1] - n_q) // 2

    def lanes(start, size):
        return pl.ds(pl.multiple_of(start, size), size)

    mine, theirs = lanes(pair * cols, cols), lanes((1 - pair) * cols, cols)
    g_gate[:, mine] = feed_own[:, :cols]
    g_up[:, mine] = feed_own[:, cols:]
    g_down[mine] = down_own[...]
    g_gate[:, theirs] = feed_other[:, :cols].astype(F32)
    g_up[:, theirs] = feed_other[:, cols:].astype(F32)
    g_down[theirs] = down_other[...].astype(F32)
    chunks = [c * 2 + pair, (1 - c) * 2 + pair, c * 2 + 1 - pair, (1 - c) * 2 + 1 - pair]
    for j, chunk in enumerate(chunks):
        qkv = qkv_own[...] if j == 0 else qkv_other[j - 1].astype(F32)
        g_query[:, lanes(chunk * n_q, n_q)] = qkv[:, :n_q]
        g_key[:, lanes(chunk * n_kv, n_kv)] = qkv[:, n_q : n_q + n_kv]
        g_value[:, lanes(chunk * n_kv, n_kv)] = qkv[:, n_q + n_kv :]
        g_out[lanes(chunk * n_q, n_q)] = out_own[...] if j == 0 else out_other[j - 1].astype(F32)
    g_in[...] = grad_in[...]
    h_out[...] = hidden[...]
    width, d = gain_a.shape[1], gain_q.shape[1]
    gain_a[...] = gains[:, :width]
    gain_m[...] = gains[:, width : 2 * width]
    gain_q[...] = gains[:, 2 * width : 2 * width + d]
    gain_k[...] = gains[:, 2 * width + d :]


VMEM_SPEC = pl.BlockSpec(memory_space=pltpu.VMEM)
ANY_SPEC = pl.BlockSpec(memory_space=pl.ANY)


def comm_call(kernel, bits, collective_id, operands, in_specs, outs, out_specs, scratch, nbytes, copies, *more):
    return pl.pallas_call(
        functools.partial(kernel, bits, *more),
        out_shape=outs,
        in_specs=in_specs,
        out_specs=out_specs,
        scratch_shapes=[
            *scratch,
            pltpu.SemaphoreType.DMA((copies,)),
            pltpu.SemaphoreType.DMA((copies,)),
            pltpu.SemaphoreType.DMA((96,)),
        ],
        compiler_params=pltpu.CompilerParams(
            collective_id=collective_id, has_side_effects=True, vmem_limit_bytes=61 << 20
        ),
        cost_estimate=pl.CostEstimate(flops=nbytes * 20, bytes_accessed=nbytes, transcendentals=0),
        name=kernel.__name__,
    )(*operands)


def build(mesh):
    n = mesh.size
    n_f = mesh.shape["fsdp"]
    spread_bits = [b for b in (1 << i for i in range(n_f.bit_length() - 2, -1, -1)) if b != PAIR]
    all_bits = sorted([*spread_bits, PAIR], reverse=True)

    def swap(v, bit):
        return lax.ppermute(v, AXES, [(i, i ^ bit) for i in range(n)])

    def bit_of(f, b):
        return (f // b) % 2

    def in_order(bit, own, other, axis):
        low = jnp.where(bit == 0, own, other)
        high = jnp.where(bit == 0, other, own)
        return jnp.stack([low, high], axis=axis)

    def pick(v, index, axis):
        return lax.dynamic_index_in_dim(v, index, axis, keepdims=False)

    def scatter(keep, got, f, width):
        v = keep + got.astype(F32)
        have = [b for b in all_bits if b != 1]
        v = v.reshape(*([2] * len(have)), width, v.shape[-1])
        for b in [b for b in reversed(spread_bits) if b != 1]:
            axis = have.index(b)
            bit = bit_of(f, b)
            v = pick(v, bit, axis) + swap(pick(v, 1 - bit, axis).astype(BF16), b * 4).astype(F32)
            have.remove(b)
        return v

    def body(
        hidden_in,
        cotangent,
        segments,
        w_query,
        key_projection_weight,
        value_projection_weight,
        w_out,
        w_gate,
        w_up,
        w_down,
        gain_attn,
        gain_mlp,
        gain_query,
        key_norm_gain,
    ):
        rows, width = hidden_in.shape
        d = gain_query.shape[0]
        length = segments.shape[0]
        f, c = lax.axis_index("fsdp"), lax.axis_index("ctx")
        pair = bit_of(f, PAIR)
        at_rows = w_query.shape[0]
        ff_rows = w_gate.shape[0]
        ff_cols = w_gate.shape[1] // 2
        q_cols, kv_cols = w_query.shape[1] // 4, key_projection_weight.shape[1] // 4
        groups = q_cols // kv_cols

        freqs = THETA ** (-2.0 * jnp.arange(d // 2, dtype=F32) / d)
        angles = jnp.arange(length, dtype=jnp.int32).astype(F32)[:, None] * freqs
        table_cos, table_sin = jnp.cos(angles), jnp.sin(angles)
        table = jnp.concatenate([table_cos, table_cos, -table_sin, table_sin], axis=-1)

        n_rows = 8 * rows
        all_rows = jax.ShapeDtypeStruct((n_rows, width), BF16)
        own_rows = jax.ShapeDtypeStruct((rows, width), F32)
        gain_rows = jax.ShapeDtypeStruct((8, width), F32)
        block = pltpu.VMEM((rows, width), BF16)
        nbytes = rows * width * 16
        qkv_cols = q_cols + 2 * kv_cols

        def shape(*dims):
            return jax.ShapeDtypeStruct(dims, BF16)

        copies = 160 + 10 * n_f
        natural = at_rows % 128 == 0 and ff_rows % 128 == 0
        out_dims = (q_cols, width) if natural else (width, q_cols)
        down_dims = (ff_cols, width) if natural else (width, ff_cols)
        out_part = (q_cols, 2 * at_rows) if natural else (2 * at_rows, q_cols)
        down_part_dims = (ff_cols, ff_rows) if natural else (ff_rows, ff_cols)
        n_seq = 2 * length
        all_tables = jax.ShapeDtypeStruct((n_seq, d), F32)

        def v(*dims, dtype=BF16):
            return pltpu.VMEM(dims, dtype)

        (
            residual_mid, normed_one, normed_two, grad_rows, qkv, attended, full_qkv, full_out, starts, cos, sin,
            grad_gate, grad_up, mixed_t, norm_two_part, down_part, *_, early_in,
        ) = comm_call(
            forward_kernel, spread_bits, 0,
            (hidden_in, cotangent, gain_attn[None], gain_mlp[None], segments[None], table, gain_query[None],
             key_norm_gain[None], w_query, key_projection_weight, value_projection_weight,
             w_out if natural else w_out.T, w_gate, w_up, w_down if natural else w_down.T),
            [VMEM_SPEC] * 8 + [ANY_SPEC] * 7,
            (own_rows, all_rows, all_rows, all_rows, shape(n_rows, qkv_cols), shape(n_rows, q_cols),
             shape(width, qkv_cols), shape(*out_dims), jax.ShapeDtypeStruct((n_seq, 128), F32), all_tables, all_tables,
             shape(n_rows, ff_cols), shape(n_rows, ff_cols), shape(ff_cols, n_rows), shape(8, rows, width), all_rows,
             shape(4, 2 * at_rows, qkv_cols), shape(4, *out_part), shape(4, ff_rows, ff_cols),
             shape(4, ff_rows, ff_cols), shape(4, *down_part_dims), shape(2, *down_part_dims)),
            (VMEM_SPEC, *[ANY_SPEC] * 21),
            [block, block, v(n_rows, width), v(n_rows, width), v(n_rows, width), v(width, qkv_cols), v(*out_dims),
             v(width, ff_cols), v(width, ff_cols), v(*down_dims), v(n_rows, qkv_cols), v(n_rows, q_cols),
             v(8, rows, width), v(n_rows, ff_cols, dtype=F32), v(n_rows, ff_cols, dtype=F32), v(n_rows, ff_cols),
             v(n_rows, ff_cols), v(n_rows, ff_cols), v(ff_cols, n_rows), v(n_seq, 128, dtype=F32),
             v(n_seq, d, dtype=F32), v(n_seq, d, dtype=F32), v(1, length, dtype=jnp.int32), v(2, *down_part_dims),
             *collect_buffers(rows, width)],
            16 * nbytes, copies, groups, natural,
        )
        common = (starts, cos, sin, gain_query[None], key_norm_gain[None])
        backward = one_kernel if natural and len(spread_bits) == 2 else by_steps
        return backward(
            hidden_in, cotangent, residual_mid, gain_attn, gain_mlp, common, norm_two_part, down_part, normed_one,
            normed_two, grad_rows, qkv, attended, full_qkv, full_out, grad_gate, grad_up, mixed_t, early_in,
            (at_rows, ff_rows),
        )

    def one_kernel(
        hidden_in, cotangent, residual_mid, gain_attn, gain_mlp, common, norm_two_part, down_part, normed_one,
        normed_two, grad_rows, qkv, attended, full_qkv, full_out, grad_gate, grad_up, mixed_t, early_in, sizes,
    ):
        rows, width = hidden_in.shape
        cols, n_rows = mixed_t.shape
        (at_rows, ff_rows), q_cols, qkv_cols = sizes, attended.shape[1], qkv.shape[1]
        d = common[-1].shape[1]
        kv_cols = (qkv_cols - q_cols) // 2
        groups = q_cols // kv_cols

        def out(dtype, *dims):
            return jax.ShapeDtypeStruct(dims, dtype)

        def v(*dims, dtype=BF16):
            return pltpu.VMEM(dims, dtype)

        def scatter(*block):
            return [v(2, *block), v(4, *block), v(2, *block), v(2, *block), v(*block, dtype=F32), v(*block)]

        n_gain = 2 * width + 2 * d
        nbytes = n_rows * width * 20
        (
            grad_input, hidden_out, gains, feed_own, feed_other, down_own, down_other, qkv_own, qkv_other, out_own,
            out_other, *_,
        ) = comm_call(
            backward_kernel, spread_bits, 2,
            (cotangent, gain_attn[None], gain_mlp[None], *common, residual_mid, hidden_in, norm_two_part,
             down_part.reshape(8, rows, width), normed_one, normed_two, grad_rows, qkv, attended, full_qkv, full_out,
             grad_gate, grad_up, mixed_t, early_in),
            [VMEM_SPEC] * 8 + [ANY_SPEC] * 15,
            (out(F32, rows, width), out(F32, rows, width), out(F32, 1, n_gain), out(F32, ff_rows, 2 * cols),
             out(BF16, ff_rows, 2 * cols), out(F32, cols, ff_rows), out(BF16, cols, ff_rows),
             out(F32, at_rows, qkv_cols), out(BF16, 3, at_rows, qkv_cols), out(F32, q_cols, at_rows),
             out(BF16, 3, q_cols, at_rows), out(BF16, 4, ff_rows, 2 * cols), out(BF16, 4, cols, ff_rows),
             out(BF16, 4, ff_rows, qkv_cols), out(BF16, 4, q_cols, ff_rows)),
            (VMEM_SPEC, VMEM_SPEC, VMEM_SPEC, ANY_SPEC, ANY_SPEC, ANY_SPEC, ANY_SPEC, VMEM_SPEC, ANY_SPEC, VMEM_SPEC,
             *[ANY_SPEC] * 5),
            [v(rows, width), v(n_rows, width), v(n_rows, 2 * cols), v(cols, n_rows), v(2, n_rows, ff_rows),
             v(ff_rows, n_rows), v(8, rows, width), v(width, qkv_cols), v(q_cols, width), v(n_rows, qkv_cols),
             v(n_rows, q_cols), v(n_rows, q_cols), v(n_rows, qkv_cols),
             *collect_buffers(rows, width), *collect_buffers(rows, width), v(8, width, dtype=F32), v(8, width, dtype=F32), v(2, 8, d, dtype=F32),
             v(4, 1, n_gain, dtype=F32), v(9, 1, n_gain, dtype=F32),
             *scatter(ff_rows, 2 * cols), *scatter(cols, ff_rows), *scatter(ff_rows, qkv_cols),
             *scatter(q_cols, ff_rows)],
            nbytes, 110, groups,
        )
        own_rows = out(F32, rows, width)
        made = (
            out(F32, at_rows, 4 * q_cols), out(F32, at_rows, 4 * kv_cols), out(F32, at_rows, 4 * kv_cols),
            out(F32, 4 * q_cols, at_rows), out(F32, ff_rows, 2 * cols), out(F32, ff_rows, 2 * cols),
            out(F32, 2 * cols, ff_rows), own_rows, own_rows, out(F32, 1, width), out(F32, 1, width), out(F32, 1, d),
            out(F32, 1, d),
        )
        pieces = pl.pallas_call(
            join_kernel,
            out_shape=made,
            compiler_params=pltpu.CompilerParams(vmem_limit_bytes=61 << 20),
            name="join_kernel",
        )(feed_own, feed_other, down_own, down_other, qkv_own, qkv_other, out_own, out_other, grad_input, hidden_out, gains)
        grads, (grad_input, hidden_out), gains = pieces[:7], pieces[7:9], pieces[9:]
        return hidden_out, grad_input, *grads, *(g[0] for g in gains)

    def by_steps(
        hidden_in, cotangent, residual_mid, gain_attn, gain_mlp, common, norm_two_part, down_part, normed_one,
        normed_two, grad_rows, qkv, attended, full_qkv, full_out, grad_gate, grad_up, mixed_t, early_in, sizes,
    ):
        rows, width = hidden_in.shape
        (at_rows, ff_rows), ff_cols, q_cols = sizes, mixed_t.shape[0], attended.shape[1]
        d = common[-1].shape[1]
        kv_cols = (qkv.shape[1] - q_cols) // 2
        groups = q_cols // kv_cols
        natural = full_out.shape[0] != width
        times_t = dot_cols if natural else dot
        f, c = lax.axis_index("fsdp"), lax.axis_index("ctx")
        pair = bit_of(f, PAIR)
        all_rows = jax.ShapeDtypeStruct((8 * rows, width), BF16)
        own_rows = jax.ShapeDtypeStruct((rows, width), F32)
        gain_rows = jax.ShapeDtypeStruct((8, width), F32)
        block = pltpu.VMEM((rows, width), BF16)
        nbytes = rows * width * 16
        grad_mid, gain_mlp_part, grad_mid_rows = comm_call(
            turn_kernel, spread_bits, 2, (norm_two_part.reshape(8, rows, width), residual_mid, cotangent, gain_mlp[None]),
            [ANY_SPEC, VMEM_SPEC, VMEM_SPEC, VMEM_SPEC], (own_rows, gain_rows, all_rows),
            (VMEM_SPEC, VMEM_SPEC, ANY_SPEC),
            [block, pltpu.VMEM((4, rows, width), BF16), *collect_buffers(rows, width)], 2 * nbytes, 40,
        )

        low = bit_of(f, 1)

        def weight_grad(acts, grads):
            split = acts.reshape(acts.shape[0], n_f // 2, 2, width // n_f)
            mine = pick(split, low, 2).reshape(acts.shape[0], -1)
            theirs = pick(split, 1 - low, 2).reshape(acts.shape[0], -1)
            got = swap(dot_rows(theirs, grads).astype(BF16), 4)
            return scatter(dot_rows(mine, grads), got, f, width // n_f)

        def ff_grad(acts, grads):
            v = weight_grad(acts, grads)
            other = swap(pick(v, 1 - pair, 0).astype(BF16), PAIR_BIT).astype(F32)
            return in_order(pair, pick(v, pair, 0), other, 1).reshape(ff_rows, 2 * ff_cols)

        grad_w_gate = ff_grad(normed_two, grad_gate)
        grad_w_up = ff_grad(normed_two, grad_up)
        grad_w_down = ff_grad(grad_rows, mixed_t.T).T

        def attn_grad(acts, grads):
            v = weight_grad(acts, grads)
            v = v.reshape(2, 2, at_rows, v.shape[-1])
            mine = pick(pick(v, pair, 0), c, 0)
            by_ctx = swap(pick(pick(v, pair, 0), 1 - c, 0).astype(BF16), CTX_BIT).astype(F32)
            by_pair = swap(pick(pick(v, 1 - pair, 0), c, 0).astype(BF16), PAIR_BIT).astype(F32)
            by_both = swap(pick(pick(v, 1 - pair, 0), 1 - c, 0).astype(BF16), CTX_BIT | PAIR_BIT).astype(F32)
            near = in_order(pair, mine, by_pair, 1)
            far = in_order(pair, by_ctx, by_both, 1)
            return in_order(c, near, far, 1)

        grad_w_out = attn_grad(grad_mid_rows, attended).reshape(at_rows, 4 * q_cols).T

        datt = times_t(grad_mid_rows, full_out).astype(BF16)
        grad_qkv, head_gains = attend_back(groups, qkv, attended, datt, common)
        norm_one_part = dot_cols(grad_qkv, full_qkv).astype(BF16)
        grad_input, gain_attn_part = comm_call(
            last_kernel, spread_bits, 3, (norm_one_part.reshape(8, rows, width), hidden_in, grad_mid, gain_attn[None]),
            [ANY_SPEC, VMEM_SPEC, VMEM_SPEC, VMEM_SPEC], (own_rows, gain_rows), (VMEM_SPEC, VMEM_SPEC),
            [pltpu.VMEM((4, rows, width), BF16), *collect_buffers(rows, width)], nbytes, 40,
        )
        grad_qkv_w = attn_grad(normed_one, grad_qkv)
        grad_w_query = grad_qkv_w[..., :q_cols].reshape(at_rows, -1)
        grad_w_key = grad_qkv_w[..., q_cols : q_cols + kv_cols].reshape(at_rows, -1)
        grad_w_value = grad_qkv_w[..., q_cols + kv_cols :].reshape(at_rows, -1)

        head_gains = jnp.sum(head_gains, axis=1)
        gains = jnp.concatenate(
            [jnp.sum(gain_attn_part, axis=0), jnp.sum(gain_mlp_part, axis=0), head_gains[0], head_gains[1]]
        ).reshape(-1, d)
        for i in range(n.bit_length() - 1):
            gains = gains + swap(gains, 1 << i)
        gains = gains.reshape(-1)
        teams = sorted(
            sorted(i ^ b ^ p for b in range(4) for p in (0, PAIR_BIT))
            for i in range(0, n, 4)
            if not i & PAIR_BIT
        )
        hidden_out = residual_mid + lax.psum_scatter(
            down_part, AXES, scatter_dimension=0, axis_index_groups=teams, tiled=True
        ).astype(F32)
        return (
            hidden_out,
            grad_input,
            grad_w_query,
            grad_w_key,
            grad_w_value,
            grad_w_out,
            grad_w_gate,
            grad_w_up,
            grad_w_down,
            gains[:width],
            gains[width : 2 * width],
            gains[2 * width : 2 * width + d],
            gains[2 * width + d :],
        )

    return body


def solution(mesh):
    everyone = P(("fsdp", "ctx", "tp"), None)
    attn = P(("fsdp", "ctx"), "tp")
    attn_out = P("tp", ("fsdp", "ctx"))
    ff_in = P("fsdp", ("ctx", "tp"))
    ff_out = P(("ctx", "tp"), "fsdp")
    same = P()
    return jax.shard_map(
        build(mesh),
        mesh=mesh,
        in_specs=(
            everyone, everyone, P("fsdp"), attn, attn, attn, attn_out, ff_in, ff_in, ff_out,
            same, same, same, same,
        ),
        out_specs=(
            everyone, everyone, attn, attn, attn, attn_out, ff_in, ff_in, ff_out,
            same, same, same, same,
        ),
        check_vma=False,
    )
```

```python
import functools

import jax
import jax.numpy as jnp
from jax import lax
from jax.experimental import pallas as pl
from jax.experimental.pallas import tpu as pltpu
from jax.sharding import PartitionSpec as P

EPS = 1e-06
THETA = 1000000.0
AXES = ("fsdp", "ctx", "tp")
MESH = pl.DeviceIdType.MESH
BF16 = jnp.bfloat16
F32 = jnp.float32
TP_BIT, CTX_BIT = 1, 2
PAIR = 2
PAIR_BIT = PAIR * 4


def dot_rows(left, right):
    return lax.dot_general(left, right, (((0,), (0,)), ((), ())), preferred_element_type=F32)


def dot_cols(left, right):
    return lax.dot_general(left, right, (((1,), (1,)), ((), ())), preferred_element_type=F32)


def dot(left, right):
    return lax.dot_general(left, right, (((1,), (0,)), ((), ())), preferred_element_type=F32)


def remote(src, dst, send, recv, device):
    return pltpu.make_async_remote_copy(
        src_ref=src, dst_ref=dst, send_sem=send, recv_sem=recv, device_id=device, device_id_type=MESH
    )


class Moves:
    def __init__(self, send, recv, local):
        self.send, self.recv, self.local = send, recv, local
        self.sent, self.loads = 0, 0
        self.open = []

    def swap(self, src, there, here, device, open_=None):
        k = self.sent
        self.sent += 1
        copy = remote(src, there, self.send.at[k], self.recv.at[k], device)
        copy.start()
        (self.open if open_ is None else open_).append(copy.wait_send)
        return remote(src, here, self.send.at[k], self.recv.at[k], device).wait_recv

    def load(self, src, dst):
        k = self.loads
        self.loads += 1
        copy = pltpu.make_async_copy(src, dst, self.local.at[k])
        copy.start()
        return copy.wait

    def store(self, src, dst):
        self.open.append(self.load(src, dst))

    def close(self):
        for wait in self.open:
            wait()


class Place:
    def __init__(self, bits):
        self.bits = bits
        f, c, t = lax.axis_index("fsdp"), lax.axis_index("ctx"), lax.axis_index("tp")
        self.f, self.c, self.t = f, c, t
        self.pair = (f // PAIR) % 2
        far_f = self.block(PAIR)
        fs, cs = [f, f, far_f, far_f], [c, 1 - c, c, 1 - c]
        pairs = [self.pair, self.pair, 1 - self.pair, 1 - self.pair]
        self.at = [(fs[j], cs[j], pairs[j]) for j in range(4)]
        self.rows_of = [pairs[j] * 4 + cs[j] * 2 for j in range(4)]
        self.chunk_of = [cs[j] * 2 + pairs[j] for j in range(4)]
        self.relay = len(bits) == 2
        self.across_mask = bits[0] | PAIR
        self.inner = (f // bits[0]) % 2 != self.pair
        self.chips = [None, {"ctx": 1 - c}, {"fsdp": far_f}, {"fsdp": far_f, "ctx": 1 - c}]
        self.sibling = {"tp": 1 - t}

    def block(self, mask):
        out = self.f
        for i in range(mask.bit_length()):
            b = 1 << i
            if mask & b:
                out = out + b - 2 * b * ((self.f // b) % 2)
        return out

    def along(self, bit):
        return {"fsdp": self.block(bit)}

    def greet(self):
        barrier = pltpu.get_barrier_semaphore()
        devices = [*self.chips[1:], self.sibling, *[self.along(b) for b in self.bits]]
        if self.relay:
            devices += [self.along(self.across_mask), self.along(self.bits[0] | self.bits[1])]
        for device in devices:
            pl.semaphore_signal(barrier, inc=1, device_id=device, device_id_type=MESH)
        pl.semaphore_wait(barrier, len(devices))


class Cross:
    def __init__(self, moves, place, src, here, came_in, across_to, came_out, pair_to):
        self.place, self.here = place, here
        self.came_in, self.came_out = came_in, came_out
        k = moves.sent
        moves.sent += 4
        pair, across = place.chips[2], place.along(place.across_mask)

        def copy(i, source, to, device):
            return remote(source, to, moves.send.at[k + i], moves.recv.at[k + i], device)

        self.hand = copy(0, src, came_in, pair)
        self.own = copy(1, src, came_out, across)
        self.on = copy(2, came_in, across_to, across)
        self.back = copy(3, came_out, pair_to, pair)
        self.came = [copy(0, came_in, came_in, pair), copy(1, came_out, came_out, across)]
        self.landed = [copy(2, here, here, across), copy(3, here, here, pair)]
        moves.open.append(self.left)

        @pl.when(place.inner)
        def _():
            self.own.start()

        @pl.when(jnp.logical_not(place.inner))
        def _():
            self.hand.start()

    def relay(self):
        @pl.when(self.place.inner)
        def _():
            self.came[0].wait_recv()
            self.on.start()
            self.came[1].wait_recv()
            self.back.start()

    def arrive(self):
        @pl.when(self.place.inner)
        def _():
            self.landed[0].wait_recv()

        @pl.when(jnp.logical_not(self.place.inner))
        def _():
            self.landed[1].wait_recv()

    def left(self):
        @pl.when(self.place.inner)
        def _():
            self.own.wait_send()
            self.on.wait_send()
            self.back.wait_send()

        @pl.when(jnp.logical_not(self.place.inner))
        def _():
            self.hand.wait_send()


class Spread:
    def __init__(self, moves, place, own, out, part=0, parts=1):
        self.moves, self.place, self.out = moves, place, out
        self.rows = own.shape[0]
        self.stride, self.offset = self.rows * parts, self.rows * part
        self.open = []
        mine = self.at(0, place.t)
        self.here = moves.load(own, mine)
        self.pair = moves.swap(own, mine, self.at(2, place.t), place.chips[2], self.open)
        self.ctx = moves.swap(own, mine, self.at(1, place.t), place.chips[1], self.open)
        self.beside = [moves.swap(own, mine, self.at(0, 1 - place.t), place.sibling, self.open)]

    def at(self, j, t):
        start = (self.place.rows_of[j] + t) * self.stride + self.offset
        return self.out.at[pl.ds(pl.multiple_of(start, self.rows), self.rows)]

    def hand(self, j):
        block = self.at(j, self.place.t)
        self.beside.append(
            self.moves.swap(block, block, self.at(j, 1 - self.place.t), self.place.sibling, self.open)
        )

    def from_pair(self):
        self.pair()
        block = self.at(2, self.place.t)
        self.both = self.moves.swap(block, block, self.at(3, self.place.t), self.place.chips[1], self.open)
        self.hand(2)

    def from_ctx(self):
        self.ctx()
        self.hand(1)

    def from_both(self):
        self.both()
        self.hand(3)

    def finish(self):
        self.here()
        for wait in (*self.beside, *self.open):
            wait()


class Collect:
    def __init__(self, moves, place, part, held, first, ctx_in, pair_in, sending, load):
        self.moves, self.place = moves, place
        self.first, self.ctx_in, self.pair_in, self.sending = first, ctx_in, pair_in, sending
        t = place.t
        self.hands, self.loads, self.open = {}, {}, []
        for j in (3, 1, 2, 0):
            self.hands[j] = moves.swap(part(j, 1 - t), first.at[j], first.at[j], place.sibling, self.open)
            if load:
                self.loads[j] = moves.load(part(j, t), held.at[j])
        self.held = (lambda j: held.at[j]) if load else (lambda j: part(j, t))

    def two(self, j, at):
        return self.held(j)[at].astype(F32) + self.first[j, at].astype(F32)

    def ready(self, j):
        self.hands[j]()
        if j in self.loads:
            self.loads[j]()

    def to_ctx(self):
        self.waits = {}
        for j, slot in ((3, 0), (1, 1)):
            self.ready(j)

            def body(at):
                self.sending[slot, at] = self.two(j, at).astype(BF16)

            row_loop(self.sending.shape[1], body)
            self.waits[j] = self.moves.swap(
                self.sending.at[slot], self.ctx_in.at[slot], self.ctx_in.at[slot], self.place.chips[1], self.open
            )

    def to_pair(self):
        self.ready(2)
        self.waits[3]()

        def body(at):
            self.sending[2, at] = (self.two(2, at) + self.ctx_in[0, at].astype(F32)).astype(BF16)

        row_loop(self.sending.shape[1], body)
        self.waits[2] = self.moves.swap(
            self.sending.at[2], self.pair_in, self.pair_in, self.place.chips[2], self.open
        )

    def fold(self):
        for j, slot in ((3, 0), (1, 1), (2, 2)):
            self.ready(j)

            def body(at):
                self.sending[slot, at] = self.two(j, at).astype(BF16)

            row_loop(self.sending.shape[1], body)
        self.ready(0)

    def post_ctx(self):
        self.waits = {}
        for j, slot in ((3, 0), (1, 1)):
            self.waits[j] = self.moves.swap(
                self.sending.at[slot], self.ctx_in.at[slot], self.ctx_in.at[slot], self.place.chips[1], self.open
            )

    def post_pair(self):
        self.waits[3]()

        def body(at):
            self.sending[2, at] = (self.sending[2, at].astype(F32) + self.ctx_in[0, at].astype(F32)).astype(BF16)

        row_loop(self.sending.shape[1], body)
        self.waits[2] = self.moves.swap(
            self.sending.at[2], self.pair_in, self.pair_in, self.place.chips[2], self.open
        )

    def came(self):
        for wait in (self.waits[1], self.waits[2], *self.open):
            wait()

    def finish(self):
        self.ready(0)
        self.waits[1]()
        self.waits[2]()
        for wait in self.open:
            wait()

    def total(self, at):
        return self.two(0, at) + (self.ctx_in[1, at].astype(F32) + self.pair_in[at].astype(F32))


def collect_buffers(rows, width):
    return [
        pltpu.VMEM((4, rows, width), BF16),
        pltpu.VMEM((2, rows, width), BF16),
        pltpu.VMEM((rows, width), BF16),
        pltpu.VMEM((3, rows, width), BF16),
    ]


def row_loop(rows, body):
    step = 16

    @pl.loop(0, rows // step)
    def _(i):
        body(pl.ds(pl.multiple_of(i * step, step), step))


def half_loop(part, rows, body):
    step = 16

    @pl.loop(0, rows // step)
    def _(i):
        body(
            pl.ds(pl.multiple_of(i * step, step), step),
            pl.ds(pl.multiple_of(part * rows + i * step, step), step),
        )


def unit_and_scale(x):
    scale = lax.rsqrt(jnp.mean(x * x, axis=-1, keepdims=True) + EPS)
    return x * scale, scale


class Gather:
    def __init__(self, moves, place, block, spare):
        self.moves, self.place, self.block, self.spare = moves, place, block, spare
        self.waits, self.crosses = {}, {}

    def forward(self, mask, src=None):
        done = [i for i, b in enumerate(self.place.bits) if mask & b]
        here = self.block(self.place.block(mask))
        for b in self.place.bits[max(done, default=-1) + 1 :]:
            if self.place.relay and b == self.place.bits[0]:
                far = self.place.across_mask
                slot = 0 if mask == 0 else 2
                self.crosses[mask] = Cross(
                    self.moves, self.place, here if src is None else src, self.block(self.place.block(mask | b)),
                    self.spare.at[slot], self.block(self.place.block(mask ^ PAIR)),
                    self.spare.at[slot + 1], self.block(self.place.block(mask ^ far)),
                )
                self.waits[mask | b] = self.crosses[mask].arrive
                continue
            self.waits[mask | b] = self.moves.swap(
                here if src is None else src, here, self.block(self.place.block(mask | b)), self.place.along(b)
            )

    def masks(self, stage):
        out = [0, PAIR]
        for b in self.place.bits[:stage]:
            out += [m | b for m in out]
        return [m | self.place.bits[stage] for m in out]

    def relay(self, m):
        if self.place.relay:
            self.crosses[m].relay()

    def hop(self, m):
        if self.place.relay:
            self.pass_on(m | self.place.bits[0])
        elif m == PAIR:
            self.middle()

    def pass_on(self, m):
        self.waits.pop(m)()
        self.forward(m)

    def middle(self):
        for stage in range(len(self.place.bits) - 1):
            for m in self.masks(stage):
                if m in self.waits:
                    self.pass_on(m)

    def finish(self):
        for wait in self.waits.values():
            wait()


def head_unit(x):
    scale = lax.rsqrt(jnp.mean(x * x, axis=-1, keepdims=True) + EPS)
    return x * scale, scale


def rot(a, cos, sin):
    return a * cos + pltpu.roll(a, a.shape[-1] // 2, 1) * sin


def rot_back(b, cos, sin):
    return b * cos - pltpu.roll(b, b.shape[-1] // 2, 1) * sin


def allowed_keys(start):
    length = start.shape[0]
    row = lax.broadcasted_iota(jnp.int32, (length, length), 0)
    col = lax.broadcasted_iota(jnp.int32, (length, length), 1)
    return (col.astype(F32) >= start) & (row >= col)


def soft_of(scores):
    peak = jnp.max(scores, axis=-1, keepdims=True)
    lse = peak + jnp.log(jnp.sum(jnp.exp(scores - peak), axis=-1, keepdims=True))
    return jnp.exp(scores - lse)


def attend_one(groups, s, qkv, starts, cos_ref, sin_ref, gain_q, gain_k, out):
    d = gain_q.shape[-1]
    length = cos_ref.shape[0] // 2
    rows = pl.ds(pl.multiple_of(s * length, length), length)
    cos, sin = cos_ref[rows], sin_ref[rows]
    allowed = allowed_keys(starts[rows, 0:1])
    unit_k, _ = head_unit(qkv[rows, groups * d : (groups + 1) * d].astype(F32))
    key = rot(unit_k * gain_k[...], cos, sin).astype(BF16)
    value = qkv[rows, (groups + 1) * d : (groups + 2) * d]
    for g in range(groups):
        unit_q, _ = head_unit(qkv[rows, g * d : (g + 1) * d].astype(F32))
        query = rot(unit_q * gain_q[...], cos, sin).astype(BF16)
        scores = jnp.where(allowed, dot_cols(query, key) * d**-0.5, -jnp.inf)
        soft = soft_of(scores).astype(BF16)
        out[rows, g * d : (g + 1) * d] = dot(soft, value).astype(BF16)


def through_norm(b, unit, scale, gain):
    e = b * gain
    return scale * (e - unit * jnp.mean(e * unit, axis=-1, keepdims=True))


def attend_back_one(
    groups, s, qkv, att, datt, starts, cos_ref, sin_ref, gain_q, gain_k, grad, gains
):
    d = gain_q.shape[-1]
    length = cos_ref.shape[0] // 2
    rows = pl.ds(pl.multiple_of(s * length, length), length)
    cos, sin = cos_ref[rows], sin_ref[rows]
    scale = d**-0.5
    allowed = allowed_keys(starts[rows, 0:1])
    at_k, at_v = slice(groups * d, (groups + 1) * d), slice((groups + 1) * d, (groups + 2) * d)
    unit_k, scale_k = head_unit(qkv[rows, at_k].astype(F32))
    key = rot(unit_k * gain_k[...], cos, sin).astype(BF16)
    value = qkv[rows, at_v]
    key_grad = jnp.zeros(unit_k.shape, F32)
    value_grad = jnp.zeros(unit_k.shape, F32)
    for g in range(groups):
        at = slice(g * d, (g + 1) * d)
        unit_q, scale_q = head_unit(qkv[rows, at].astype(F32))
        query = rot(unit_q * gain_q[...], cos, sin).astype(BF16)
        scores = jnp.where(allowed, dot_cols(query, key) * scale, -jnp.inf)
        soft = soft_of(scores)
        up = datt[rows, at]
        delta = jnp.sum(up.astype(F32) * att[rows, at].astype(F32), axis=-1, keepdims=True)
        ds = (soft * (dot_cols(up, value) - delta) * scale).astype(BF16)
        value_grad += dot_rows(soft.astype(BF16), up)
        key_grad += dot_rows(ds, query)
        b = rot_back(dot(ds, key), cos, sin)
        gains[0] += jnp.sum((b * unit_q).reshape(-1, 8, d), axis=0)
        grad[rows, at] = through_norm(b, unit_q, scale_q, gain_q[...]).astype(BF16)
    b = rot_back(key_grad, cos, sin)
    gains[1] += jnp.sum((b * unit_k).reshape(-1, 8, d), axis=0)
    grad[rows, at_k] = through_norm(b, unit_k, scale_k, gain_k[...]).astype(BF16)
    grad[rows, at_v] = value_grad.astype(BF16)


def attend_back_kernel(
    groups, qkv, att, datt, starts, cos, sin, gain_q, gain_k, grad, gains
):
    gains[...] = jnp.zeros_like(gains)

    @pl.loop(0, 2)
    def _(s):
        attend_back_one(groups, s, qkv, att, datt, starts, cos, sin, gain_q, gain_k, grad, gains)


def attend_back(groups, qkv, att, datt, common):
    n_rows, width = qkv.shape
    d = width // (groups + 2)
    length = n_rows // 2
    return pl.pallas_call(
        functools.partial(attend_back_kernel, groups),
        out_shape=(jax.ShapeDtypeStruct(qkv.shape, BF16), jax.ShapeDtypeStruct((2, 8, d), F32)),
        compiler_params=pltpu.CompilerParams(vmem_limit_bytes=40 << 20),
        cost_estimate=pl.CostEstimate(
            flops=n_rows * groups * length * (10 * d + 30),
            bytes_accessed=n_rows * width * 8,
            transcendentals=n_rows * groups * length * 2,
        ),
        name="attend_back",
    )(qkv, att, datt, *common)


def forward_kernel(
    bits, groups, natural,
    hidden, cot, gain_attn, gain_mlp, seg, table, gain_q, gain_k, wq, wk, wv, wo, wg, wu, wd,
    mid, normed_one, normed_two, cot_out, qkv_out, att_out, qkv_weight, out_weight, starts_out, cos_out, sin_out,
    grad_gate_out, grad_up_out, mixed_out, part_out, down_out, spare_qkv, spare_out,
    spare_gate_a, spare_up_a, spare_down_a, spare_gate_b, spare_up_b, spare_down_b, early_in,
    own_one, own_two, rows_one, rows_two, rows_cot, w_qkv, w_out, w_gate, w_up, w_down, qkv, att, part,
    gate, up, grad_gate, grad_up, mixed, mixed_t, starts, cos, sin, seg_in, early, first, ctx_in, pair_in, sending,
    send, recv, local,
):
    place = Place(bits)
    moves = Moves(send, recv, local)
    rows, width = hidden.shape
    at_rows, ff_rows, ff_cols = wq.shape[0], wg.shape[0], wg.shape[1] // 2
    q_cols, kv_cols = wq.shape[1] // 4, wk.shape[1] // 4
    n_rows, length = rows_one.shape[0], seg.shape[1]

    def lanes(start, size):
        return pl.ds(pl.multiple_of(start, size), size)

    def qkv_rows(f, c=None):
        if c is None:
            return lanes(f * 2 * at_rows, 2 * at_rows)
        return lanes((f * 2 + c) * at_rows, at_rows)

    place.greet()

    def out_block(f, c=None):
        return w_out.at[:, qkv_rows(f, c)] if natural else w_out.at[qkv_rows(f, c)]

    def out_chunk(j):
        at = lanes(place.chunk_of[j] * q_cols, q_cols)
        return wo.at[at] if natural else wo.at[:, at]

    pieces = (
        (wq, q_cols, pl.ds(0, q_cols)),
        (wk, kv_cols, pl.ds(q_cols, kv_cols)),
        (wv, kv_cols, pl.ds(q_cols + kv_cols, kv_cols)),
    )
    f0, c0, _ = place.at[0]
    qkv_in, out_in = {}, {}

    border = ff_cols - 256 if ff_cols % 256 == 0 and ff_cols > 256 else ff_cols // 2
    piece_a, piece_b = pl.ds(0, border), pl.ds(border, ff_cols - border)

    def feed_weight(weight, piece, source, spare, by_rows):
        start, size = (0, border) if piece is piece_a else (border, ff_cols - border)

        def block(f):
            at = lanes(f * ff_rows, ff_rows)
            return weight.at[at, piece] if by_rows else weight.at[piece, at]

        def half(which):
            at = pl.ds(pl.multiple_of(which * ff_cols + start, 128), size)
            return source.at[:, at] if by_rows else source.at[at]

        return Gather(moves, place, block, spare), half(place.pair), half(1 - place.pair)

    feed = []
    for piece, spares in ((piece_a, (spare_gate_a, spare_up_a, spare_down_a)), (piece_b, (spare_gate_b, spare_up_b, spare_down_b))):
        feed.append(feed_weight(w_gate, piece, wg, spares[0], True))
        feed.append(feed_weight(w_up, piece, wu, spares[1], True))
        feed.append(feed_weight(w_down, piece, wd, spares[2], not natural))
    own_feed = [moves.load(own, gather.block(place.f)) for gather, own, _ in feed]

    def swap_pair(i):
        gather, _, other = feed[i]
        gather.waits[PAIR] = moves.swap(
            other, gather.block(place.f), gather.block(place.block(PAIR)), place.along(PAIR)
        )

    early_waits = []

    def send_early(i):
        if place.relay:
            high, low = bits
            mask = (high, high | PAIR)[i] | low
            at = lanes(place.block(mask) * ff_rows, ff_rows)
            early[i] = dot(mixed_t[...], rows_cot[:, at]).astype(BF16)
            early_waits.append(moves.swap(early.at[i], early_in.at[i], early_in.at[i], place.along(low)))

    step = 2 * rows
    wide = min(256, w_qkv.shape[1])
    qkv_gather = Gather(moves, place, lambda f: w_qkv.at[qkv_rows(f)], spare_qkv)
    out_gather = Gather(moves, place, out_block, spare_out)

    def norm_one(at):
        unit, _ = unit_and_scale(hidden[at].astype(F32))
        own_one[at] = (unit * gain_attn[...]).astype(BF16)

    collects = [None, None]

    def collect_part(h):
        at = pl.ds(h * rows // 2, rows // 2)
        return Collect(
            moves, place, lambda j, t: part.at[place.rows_of[j] + t, at], None, first.at[:, at], ctx_in.at[:, at],
            pair_in.at[at], sending.at[:, at], False,
        )

    def norm_two(h):
        def body(there, at):
            x = hidden[at].astype(F32) + collects[h].total(there)
            mid[at] = x
            unit, _ = unit_and_scale(x)
            own_two[at] = (unit * gain_mlp[...]).astype(BF16)

        return body

    def columns_of(weight, at):
        return (dot, weight[:, at]) if natural else (dot_cols, weight[at])

    def gate_part(piece):
        @pl.loop(0, n_rows // step)
        def _(i):
            at = lanes(i * step, step)
            gate[at, piece] = dot(rows_two[at], w_gate[:, piece])

    def up_part(piece):
        @pl.loop(0, n_rows // step)
        def _(i):
            at = lanes(i * step, step)
            u = dot(rows_two[at], w_up[:, piece])
            up[at, piece] = u
            g = gate[at, piece]
            mix = g * jax.nn.sigmoid(g) * u
            mixed[at, piece] = mix.astype(BF16)
            mixed_t[piece, at] = mix.T.astype(BF16)

    def back_part(piece):
        @pl.loop(0, n_rows // step)
        def _(i):
            at = lanes(i * step, step)
            m = dot_cols(rows_cot[at], w_down[piece]) if natural else dot(rows_cot[at], w_down[:, piece])
            g = gate[at, piece]
            s = jax.nn.sigmoid(g)
            grad_gate[at, piece] = (m * up[at, piece] * s * (1.0 + g * (1.0 - s))).astype(BF16)
            grad_up[at, piece] = (m * (g * s)).astype(BF16)

    def grad_part(piece, last):
        for half in range(2):

            @pl.loop(0, width // 512)
            def _(i):
                at = lanes(half * (width // 2) + i * 256, 256)
                both = dot_cols(grad_gate[:, piece], w_gate[at, piece]) + dot_cols(grad_up[:, piece], w_up[at, piece])
                both = both.reshape(8, rows, 256)
                if last:
                    both = both + part[:, :, at].astype(F32)
                part[:, :, at] = both.astype(BF16)

            if last:
                at = pl.ds(half * (width // 2), width // 2)
                moves.store(part.at[:, :, at], part_out.at[:, :, at])

    def down_part(piece, last):
        @pl.loop(0, width // 256)
        def _(i):
            at = lanes(i * 256, 256)
            if natural:
                term = dot(mixed[:, piece], w_down[piece, at])
            else:
                term = dot_cols(mixed[:, piece], w_down[at, piece])
            if last:
                term = term + rows_one[:, at].astype(F32)
            rows_one[:, at] = term.astype(BF16)

        if last:
            moves.store(rows_one, down_out)

    for j in (3, 2, 1):
        fj, cj, _ = place.at[j]
        out_in[j] = moves.swap(out_chunk(j), out_block(f0, c0), out_block(fj, cj), place.chips[j])
    out_in[0] = moves.load(out_chunk(0), out_block(f0, c0))
    for j in (1, 3, 2):
        fj, cj, _ = place.at[j]
        qkv_in[j] = [
            moves.swap(
                w.at[:, lanes(place.chunk_of[j] * size, size)],
                w_qkv.at[qkv_rows(f0, c0), to],
                w_qkv.at[qkv_rows(fj, cj), to],
                place.chips[j],
            )
            for w, size, to in pieces
        ]
    qkv_in[0] = [
        moves.load(w.at[:, lanes(place.chunk_of[0] * size, size)], w_qkv.at[qkv_rows(f0, c0), to])
        for w, size, to in pieces
    ]
    out_in[0]()
    out_in[1]()
    out_gather.forward(0)
    for wait in (*qkv_in[0], *qkv_in[1]):
        wait()
    qkv_gather.forward(0)
    for wait in (*qkv_in[2], *qkv_in[3]):
        wait()
    qkv_gather.forward(PAIR)
    out_in[2]()
    out_in[3]()
    out_gather.forward(PAIR)
    row_loop(rows, norm_one)
    spread_one = Spread(moves, place, own_one, rows_one)
    out_gather.relay(0)
    seg_wait = moves.swap(seg, seg_in, seg_in, place.chips[2])
    qkv_gather.relay(0)
    swap_pair(1)
    qkv_gather.relay(PAIR)
    feed[2][0].forward(0, feed[2][1])
    swap_pair(2)
    qkv_gather.hop(0)
    out_gather.relay(PAIR)
    feed[3][0].forward(0, feed[3][1])
    out_gather.hop(0)
    spread_one.from_pair()
    qkv_gather.hop(PAIR)
    feed[0][0].forward(0, feed[0][1])
    spread_cot = Spread(moves, place, cot, rows_cot)
    spread_one.from_both()
    out_gather.hop(PAIR)
    spread_one.from_ctx()
    feed[1][0].forward(0, feed[1][1])
    seg_wait()
    pair_first = place.pair == 0
    own_seg, far_seg = seg[...].astype(F32), seg_in[...].astype(F32)
    for i in range(2):
        here = pair_first if i == 0 else jnp.logical_not(pair_first)
        flags = jnp.where(here, own_seg, far_seg)
        both = jnp.broadcast_to(flags, (128, length)).T[:, 0:1]
        start = jnp.sum((flags < both).astype(F32), axis=1, keepdims=True)
        row = lax.broadcasted_iota(jnp.int32, (length, length), 0).astype(F32)
        col = lax.broadcasted_iota(jnp.int32, (length, length), 1).astype(F32)
        chosen = (row - start == col).astype(F32)
        at = pl.ds(i * length, length)
        both_tables = lax.dot_general(
            chosen, table[...], (((1,), (0,)), ((), ())),
            precision=lax.Precision.HIGHEST, preferred_element_type=F32,
        )
        d = gain_q.shape[1]
        starts[at] = jnp.broadcast_to(start, (length, 128))
        cos[at] = both_tables[:, :d]
        sin[at] = both_tables[:, d:]
    moves.store(starts, starts_out)
    moves.store(cos, cos_out)
    moves.store(sin, sin_out)
    feed[2][0].pass_on(PAIR)
    spread_one.finish()
    normed_stored = moves.load(rows_one, normed_one)
    feed[2][0].relay(0)
    feed[1][0].pass_on(PAIR)
    swap_pair(0)
    qkv_gather.finish()
    moves.store(w_qkv, qkv_weight)
    swap_pair(3)
    feed[0][0].relay(0)
    @pl.loop(0, w_qkv.shape[1] // wide)
    def _(i):
        at = lanes(i * wide, wide)
        qkv[:, at] = dot(rows_one[...], w_qkv[:, at]).astype(BF16)

    moves.store(qkv, qkv_out)
    @pl.loop(0, 2)
    def _(s):
        attend_one(groups, s, qkv, starts, cos, sin, gain_q, gain_k, att)

    moves.store(att, att_out)
    swap_pair(4)
    out_gather.finish()
    moves.store(w_out, out_weight)
    feed[2][0].hop(0)
    feed[4][0].forward(0, feed[4][1])
    @pl.loop(0, width // 256)
    def _(i):
        at = lanes(i * 256, 256)
        times, block = columns_of(w_out, at)
        part[:, :, at] = times(att[...], block).astype(BF16).reshape(8, rows, 256)

    collects[0] = collect_part(0)
    feed[1][0].relay(0)
    collects[0].to_ctx()
    collects[1] = collect_part(1)
    feed[3][0].relay(0)
    feed[1][0].relay(PAIR)
    feed[1][0].hop(0)
    collects[1].to_ctx()
    feed[2][0].relay(PAIR)
    feed[0][0].pass_on(PAIR)
    spread_cot.from_pair()
    collects[1].to_pair()
    spread_cot.from_ctx()
    collects[0].to_pair()
    feed[3][0].pass_on(PAIR)
    feed[2][0].hop(PAIR)
    feed[0][0].relay(PAIR)
    feed[3][0].hop(0)
    feed[0][0].hop(0)
    collects[1].finish()
    half_loop(1, rows // 2, norm_two(1))
    spread_two_1 = Spread(moves, place, own_two.at[pl.ds(1 * rows // 2, rows // 2)], rows_two, 1, 2)
    feed[1][0].hop(PAIR)
    own_feed[2]()
    feed[2][0].finish()
    collects[0].finish()
    half_loop(0, rows // 2, norm_two(0))
    spread_two_0 = Spread(moves, place, own_two.at[pl.ds(0 * rows // 2, rows // 2)], rows_two, 0, 2)
    feed[0][0].hop(PAIR)
    spread_cot.from_both()
    feed[4][0].pass_on(PAIR)
    feed[3][0].relay(PAIR)
    spread_two_1.from_pair()
    swap_pair(5)
    feed[4][0].relay(0)
    spread_cot.finish()
    moves.store(rows_cot, cot_out)
    own_feed[0]()
    feed[0][0].finish()
    spread_two_0.from_pair()
    feed[3][0].hop(PAIR)
    spread_two_0.from_ctx()
    spread_two_1.from_ctx()
    feed[5][0].forward(0, feed[5][1])
    feed[4][0].relay(PAIR)
    spread_two_1.from_both()
    own_feed[3]()
    feed[3][0].finish()
    own_feed[1]()
    feed[1][0].finish()
    feed[4][0].hop(0)
    feed[5][0].pass_on(PAIR)
    spread_two_0.from_both()
    spread_two_1.finish()
    feed[4][0].hop(PAIR)
    feed[5][0].relay(0)
    spread_two_0.finish()
    moves.store(rows_two, normed_two)
    gate_part(piece_a)
    feed[5][0].relay(PAIR)
    gate_part(piece_b)
    up_part(piece_a)
    feed[5][0].hop(0)
    own_feed[4]()
    feed[4][0].finish()
    feed[5][0].hop(PAIR)
    up_part(piece_b)
    send_early(0)
    send_early(1)
    normed_stored()
    down_part(piece_a, False)
    own_feed[5]()
    feed[5][0].finish()
    back_part(piece_a)
    back_part(piece_b)
    down_part(piece_b, True)
    grad_part(piece_a, False)
    grad_part(piece_b, True)
    moves.store(mixed_t, mixed_out)
    moves.store(grad_gate, grad_gate_out)
    moves.store(grad_up, grad_up_out)
    for wait in early_waits:
        wait()
    moves.close()


def norm_back(grad, x, gain, gain_grad):
    unit, scale = unit_and_scale(x)
    gain_grad[...] += jnp.sum((grad * unit).reshape(-1, 8, grad.shape[-1]), axis=0)
    e = grad * gain
    return scale * (e - unit * jnp.mean(e * unit, axis=-1, keepdims=True))


def turn_kernel(
    bits, partial, mid, cot, gain, grad_mid, gain_grad, out,
    own, held, first, ctx_in, pair_in, sending, send, recv, local,
):
    place = Place(bits)
    moves = Moves(send, recv, local)
    place.greet()
    collect = Collect(
        moves, place, lambda j, t: partial.at[place.rows_of[j] + t], held, first, ctx_in, pair_in, sending, True
    )
    collect.to_ctx()
    collect.to_pair()
    collect.finish()
    gain_grad[...] = jnp.zeros_like(gain_grad)

    def back(at):
        g = cot[at].astype(F32) + norm_back(collect.total(at), mid[at], gain[...], gain_grad)
        grad_mid[at] = g
        own[at] = g.astype(BF16)

    row_loop(mid.shape[0], back)
    spread = Spread(moves, place, own, out)
    spread.from_pair()
    spread.from_ctx()
    spread.from_both()
    spread.finish()
    moves.close()


def last_kernel(
    bits, partial, hidden, grad_mid, gain, grad_in, gain_grad,
    held, first, ctx_in, pair_in, sending, send, recv, local,
):
    place = Place(bits)
    moves = Moves(send, recv, local)
    place.greet()
    collect = Collect(
        moves, place, lambda j, t: partial.at[place.rows_of[j] + t], held, first, ctx_in, pair_in, sending, True
    )
    collect.to_ctx()
    collect.to_pair()
    collect.finish()
    gain_grad[...] = jnp.zeros_like(gain_grad)

    def back(at):
        grad_in[at] = grad_mid[at] + norm_back(
            collect.total(at), hidden[at].astype(F32), gain[...], gain_grad
        )

    row_loop(hidden.shape[0], back)
    moves.close()


class Scatter:
    def __init__(self, moves, place, product, out0, in0, out1, in1, acc, acc_pair, spare):
        self.moves, self.place, self.product, self.spare = moves, place, product, spare
        self.out0, self.in0, self.out1, self.in1, self.acc, self.acc_pair = out0, in0, out1, in1, acc, acc_pair
        self.low, self.high = place.bits[1], place.bits[0]
        self.order = [self.high, self.high | PAIR, 0, PAIR]
        self.first, self.second, self.leaving = {}, {}, {}

    def send(self, i):
        slot = i % 2
        for wait in self.leaving.pop(slot, []):
            wait()

        def emit(at, value):
            self.out0[(slot, *at)] = value.astype(BF16)

        self.product(self.order[i] | self.low, emit)
        self.leaving[slot] = []
        self.first[i] = self.moves.swap(
            self.out0.at[slot], self.in0.at[i], self.in0.at[i], self.place.along(self.low), self.leaving[slot]
        )

    def take(self, i):
        self.first[i]()

        def emit(at, value):
            value = value + self.in0[(i, *at)].astype(F32)
            if i < 2:
                self.out1[(i, *at)] = value.astype(BF16)
            elif i == 2:
                self.acc[at] = value
            else:
                self.acc_pair[at] = value.astype(BF16)

        self.product(self.order[i], emit)
        if i < 2:
            to = self.in1.at[i]
            self.second[i] = Cross(
                self.moves, self.place, self.out1.at[i], to, self.spare.at[2 * i], to, self.spare.at[2 * i + 1], to
            )

    def relay(self, i):
        self.second[i].relay()

    def take_high(self, i):
        self.second[i].arrive()
        total = self.acc_pair if i else self.acc
        step = 64

        @pl.loop(0, total.shape[0] // step)
        def _(k):
            at = pl.ds(pl.multiple_of(k * step, step), step)
            total[at] = (total[at].astype(F32) + self.in1[i, at].astype(F32)).astype(total.dtype)

    def close(self):
        for waits in self.leaving.values():
            for wait in waits:
                wait()


class Blocks:
    def __init__(self, moves, place, slots, order):
        self.moves, self.place, self.slots, self.order = moves, place, slots, order
        self.next, self.waits = 0, {}
        self.start(0)

    def start(self, k):
        if k < len(self.order):
            ref, mask = self.order[k]
            size = self.slots.shape[2]
            at = pl.ds(pl.multiple_of(self.place.block(mask) * size, size), size)
            self.waits[k] = self.moves.load(ref.at[:, at], self.slots.at[k % 2])

    def get(self, ref, mask):
        k = self.next
        assert self.order[k][0] is ref and self.order[k][1] == mask
        self.next += 1
        self.waits.pop(k)()
        self.start(k + 1)
        return self.slots[k % 2]


def backward_kernel(
    bits, groups,
    cot, gain_attn, gain_mlp, starts, cos, sin, gain_q, gain_k,
    mid, hidden, part_two, part_hidden, normed_one, normed_two, cot_rows, qkv_in, att_in, qkv_weight, out_weight, grad_gate, grad_up,
    mixed_t, early_in,
    grad_in, hidden_out, gains, feed_own, feed_other, down_own, down_other, qkv_own, qkv_other, out_own, out_other,
    spare_feed, spare_down, spare_qkv, spare_out,
    own, rows_mid, feed, mixed, lhs, lhs_t, part, w_qkv, w_out, qkv, att, datt, dqkv,
    first, ctx_in, pair_in, sending, first_h, ctx_h, pair_h, sending_h, gain_a, gain_m, gain_h, tree, tree_in,
    f_out0, f_in0, f_out1, f_in1, f_acc, f_pair, d_out0, d_in0, d_out1, d_in1, d_acc, d_pair,
    q_out0, q_in0, q_out1, q_in1, q_acc, q_pair, o_out0, o_in0, o_out1, o_in1, o_acc, o_pair,
    send, recv, local,
):
    place = Place(bits)
    moves = Moves(send, recv, local)
    rows, width = cot.shape
    cols = mixed.shape[0]
    tile = lhs.shape[2]
    half = tile // 2
    high, low = bits
    place.greet()

    def lanes(start, size):
        return pl.ds(pl.multiple_of(start, size), size)

    ready_mid = moves.load(mid, hidden_out)
    ready_feed = [
        moves.load(grad_gate, feed.at[:, pl.ds(0, cols)]),
        moves.load(grad_up, feed.at[:, pl.ds(cols, cols)]),
    ]
    masks = [high, high | PAIR, 0, PAIR]
    sends = [m | low for m in masks]
    a, b, c, e = range(4)
    order = [
        (cot_rows, masks[b]), (cot_rows, sends[e]), (cot_rows, masks[a]), (normed_two, sends[a]),
        (cot_rows, masks[e]), (normed_two, sends[b]), (normed_two, masks[a]), (normed_two, sends[e]),
        (normed_two, masks[b]), (normed_two, masks[e]), (normed_one, sends[a]), (normed_one, sends[b]),
        (normed_one, masks[a]), (normed_two, sends[c]), (normed_one, sends[e]), (normed_one, masks[b]),
        (normed_two, masks[c]), (normed_one, sends[c]), (normed_one, masks[e]), (cot_rows, sends[c]),
        (normed_one, masks[c]), (cot_rows, masks[c]),
    ]
    blocks = Blocks(moves, place, lhs, order)
    ready_mixed = moves.load(mixed_t, mixed)
    ready_early = [moves.load(early_in.at[i], d_in0.at[i]) for i in range(2)]
    ready_late = [
        moves.load(out_weight, w_out),
        moves.load(att_in, att),
        moves.load(qkv_in, qkv),
        moves.load(qkv_weight, w_qkv),
    ]

    def by_rows(source, right):
        def product(mask, emit):
            lhs_t[...] = blocks.get(source, mask).T
            step = min(512, right.shape[1])

            @pl.loop(0, right.shape[1] // step)
            def _(i):
                at = lanes(i * step, step)
                emit((slice(None), at), dot(lhs_t[...], right[:, at]))

        return product

    def down_product(mask, emit):
        block = blocks.get(cot_rows, mask)
        step = min(256, cols)

        @pl.loop(0, cols // step)
        def _(i):
            at = lanes(i * step, step)
            emit((at, slice(None)), dot(mixed[at], block))

    def out_product(mask, emit):
        at = lanes(place.block(mask) * tile, tile)
        emit((slice(None), slice(None)), dot_rows(att[...], rows_mid[:, at]))

    feed_s = Scatter(moves, place, by_rows(normed_two, feed), f_out0, f_in0, f_out1, f_in1, f_acc, f_pair, spare_feed)
    down_s = Scatter(moves, place, down_product, d_out0, d_in0, d_out1, d_in1, d_acc, d_pair, spare_down)
    down_s.first = dict(enumerate(ready_early))
    qkv_s = Scatter(moves, place, by_rows(normed_one, dqkv), q_out0, q_in0, q_out1, q_in1, q_acc, q_pair, spare_qkv)
    out_s = Scatter(moves, place, out_product, o_out0, o_in0, o_out1, o_in1, o_acc, o_pair, spare_out)

    d = gain_q.shape[1]
    gain_m[...] = jnp.zeros_like(gain_m)
    gain_a[...] = jnp.zeros_like(gain_a)
    gain_h[...] = jnp.zeros_like(gain_h)

    twos = [None, None]

    def collect_part(h):
        at = pl.ds(h * rows // 2, rows // 2)
        return Collect(
            moves, place, lambda j, t: part_two.at[place.rows_of[j] + t, at], part.at[:, at], first.at[:, at],
            ctx_in.at[:, at], pair_in.at[at], sending.at[:, at], True,
        )

    def back_two(h):
        def body(there, at):
            x = hidden_out[at]
            g = cot[at].astype(F32) + norm_back(twos[h].total(there), x, gain_mlp[...], gain_m)
            hidden_out[at] = x + collect_hidden.two(0, at)
            grad_in[at] = g
            own[at] = g.astype(BF16)

        return body

    def back_one(at):
        grad_in[at] += norm_back(collect_one.total(at), own[at].astype(F32), gain_attn[...], gain_a)

    def end_hidden(at):
        hidden_out[at] += ctx_h[1, at].astype(F32) + pair_h[at].astype(F32)

    tree_waits = []

    def climb():
        k = len(tree_waits)
        if k == 1:
            tree_waits[0]()
            tree[1] = tree[0] + tree_in[0]
        if k > 1:
            for wait in tree_waits[-1]:
                wait()
            at = 1 + 4 * (k - 2)
            tree[k] = (tree_in[at] + tree_in[at + 1]) + (tree_in[at + 2] + tree_in[at + 3])
        if k == 0:
            tree_waits.append(moves.swap(tree.at[0], tree_in.at[0], tree_in.at[0], place.sibling))
        elif k < 3:
            mine, others = team(k)
            slots = 1 + 4 * (k - 1)
            tree_in[slots + mine] = tree[k]
            tree_waits.append(
                [
                    moves.swap(tree.at[k], tree_in.at[slots + mine], tree_in.at[slots + index], device)
                    for index, device in others
                ]
            )

    def team(k):
        if k == 1:
            return place.rows_of[0] // 2, [(place.rows_of[j] // 2, place.chips[j]) for j in (3, 2, 1)]

        def index(mask):
            f = place.block(mask)
            return (f // high) % 2 * 2 + f % 2

        return index(0), [(index(m), place.along(m)) for m in (high | low, high, low)]

    finals = []

    def pair_final(scatter, other):
        scatter.take_high(1)
        finals.append(moves.swap(scatter.acc_pair, other, other, place.chips[2]))

    def own_final(scatter, mine):
        scatter.take_high(0)
        moves.store(scatter.acc, mine)

    def mates_final(scatter, slot, piece, spare, other):
        scatter.take_high(slot)
        for j in (3, 2) if slot else (1,):
            out = spare(j)
            out[...] = piece(slot, place.at[j][1]).astype(BF16)
            finals.append(moves.swap(out, other.at[j - 1], other.at[j - 1], place.chips[j]))

    def qkv_piece(slot, c):
        return (q_pair if slot else q_acc)[lanes(c * half, half)]

    def out_piece(slot, c):
        return (o_pair if slot else o_acc)[:, lanes(c * half, half)]

    def qkv_spare(j):
        return q_in0.at[j, pl.ds(0, half)]

    def out_spare(j):
        return o_in0.at[j, :, pl.ds(0, half)]

    ready_mixed()
    down_s.take(b)
    twos[0] = collect_part(0)
    down_s.send(e)
    for wait in ready_feed:
        wait()
    twos[0].to_ctx()
    collect_hidden = Collect(
        moves, place, lambda j, t: part_hidden.at[place.rows_of[j] + t], part.at[pl.ds(4, 4)],
        first_h, ctx_h, pair_h, sending_h, True,
    )
    twos[1] = collect_part(1)
    down_s.take(a)
    down_s.relay(b)
    feed_s.send(a)
    collect_hidden.fold()
    down_s.take(e)
    twos[1].to_ctx()
    twos[0].to_pair()
    feed_s.send(b)
    twos[1].to_pair()
    twos[0].finish()
    ready_mid()
    half_loop(0, rows // 2, back_two(0))
    spread_0 = Spread(moves, place, own.at[pl.ds(0 * rows // 2, rows // 2)], rows_mid, 0, 2)
    down_s.relay(a)
    twos[1].finish()
    half_loop(1, rows // 2, back_two(1))
    spread_1 = Spread(moves, place, own.at[pl.ds(1 * rows // 2, rows // 2)], rows_mid, 1, 2)
    feed_s.take(a)
    spread_0.from_pair()
    spread_0.from_ctx()
    for wait in ready_late:
        wait()
    spread_1.from_ctx()
    spread_1.from_pair()
    pair_final(down_s, down_other)
    spread_0.from_both()
    feed_s.send(e)
    spread_1.from_both()
    feed_s.take(b)
    collect_hidden.post_ctx()
    spread_1.finish()
    spread_0.finish()
    ready_hidden = moves.load(hidden, own)
    out_s.send(a)
    @pl.loop(0, 4)
    def _(i):
        at = lanes(i * 2 * rows, 2 * rows)
        datt[at] = dot_cols(rows_mid[at], w_out[...]).astype(BF16)

    out_s.send(b)
    feed_s.relay(a)
    @pl.loop(0, 2)
    def _(s):
        attend_back_one(groups, s, qkv, att, datt, starts, cos, sin, gain_q, gain_k, dqkv, gain_h)

    @pl.loop(0, width // tile)
    def _(i):
        at = lanes(i * tile, tile)
        part[:, :, at] = dot_cols(dqkv[...], w_qkv[at]).astype(BF16).reshape(8, rows, tile)

    feed_s.take(e)
    collect_hidden.post_pair()
    collect_one = Collect(
        moves, place, lambda j, t: part.at[place.rows_of[j] + t], None, first, ctx_in, pair_in, sending, False
    )
    qkv_s.send(a)
    collect_one.to_ctx()
    out_s.send(e)
    out_s.send(c)
    out_s.take(b)
    qkv_s.send(b)
    feed_s.relay(b)
    out_s.take(c)
    qkv_s.take(a)
    feed_s.send(c)
    out_s.relay(b)
    out_s.take(a)
    collect_one.to_pair()
    qkv_s.relay(a)
    qkv_s.send(e)
    collect_hidden.came()
    row_loop(rows, end_hidden)
    out_s.take(e)
    qkv_s.take(b)
    feed_s.take(c)
    own_final(feed_s, feed_own)
    pair_final(feed_s, feed_other)
    collect_one.finish()
    qkv_s.send(c)
    qkv_s.take(e)
    down_s.send(c)
    ready_hidden()
    row_loop(rows, back_one)
    tree[0, :, 0:width] = jnp.sum(gain_a[...], axis=0, keepdims=True)
    tree[0, :, width : 2 * width] = jnp.sum(gain_m[...], axis=0, keepdims=True)
    tree[0, :, 2 * width : 2 * width + d] = jnp.sum(gain_h[0], axis=0, keepdims=True)
    tree[0, :, 2 * width + d : 2 * width + 2 * d] = jnp.sum(gain_h[1], axis=0, keepdims=True)
    climb()
    climb()
    qkv_s.relay(b)
    qkv_s.take(c)
    mates_final(qkv_s, 0, qkv_piece, qkv_spare, qkv_other)
    qkv_own[...] = qkv_piece(0, place.c)
    mates_final(out_s, 1, out_piece, out_spare, out_other)
    climb()
    out_s.relay(a)
    mates_final(qkv_s, 1, qkv_piece, qkv_spare, qkv_other)
    mates_final(out_s, 0, out_piece, out_spare, out_other)
    out_own[...] = out_piece(0, place.c)
    down_s.take(c)
    own_final(down_s, down_own)
    climb()
    gains[...] = tree[3]
    for scatter in (feed_s, down_s, qkv_s, out_s):
        scatter.close()
    for wait in finals:
        wait()
    moves.close()


def join_kernel(
    feed_own, feed_other, down_own, down_other, qkv_own, qkv_other, out_own, out_other, grad_in, hidden, gains,
    g_query, g_key, g_value, g_out, g_gate, g_up, g_down, g_in, h_out, gain_a, gain_m, gain_q, gain_k,
):
    c = lax.axis_index("ctx")
    pair = (lax.axis_index("fsdp") // PAIR) % 2
    cols, n_q = down_own.shape[0], out_own.shape[0]
    n_kv = (qkv_own.shape[1] - n_q) // 2

    def lanes(start, size):
        return pl.ds(pl.multiple_of(start, size), size)

    mine, theirs = lanes(pair * cols, cols), lanes((1 - pair) * cols, cols)
    g_gate[:, mine] = feed_own[:, :cols]
    g_up[:, mine] = feed_own[:, cols:]
    g_down[mine] = down_own[...]
    g_gate[:, theirs] = feed_other[:, :cols].astype(F32)
    g_up[:, theirs] = feed_other[:, cols:].astype(F32)
    g_down[theirs] = down_other[...].astype(F32)
    chunks = [c * 2 + pair, (1 - c) * 2 + pair, c * 2 + 1 - pair, (1 - c) * 2 + 1 - pair]
    for j, chunk in enumerate(chunks):
        qkv = qkv_own[...] if j == 0 else qkv_other[j - 1].astype(F32)
        g_query[:, lanes(chunk * n_q, n_q)] = qkv[:, :n_q]
        g_key[:, lanes(chunk * n_kv, n_kv)] = qkv[:, n_q : n_q + n_kv]
        g_value[:, lanes(chunk * n_kv, n_kv)] = qkv[:, n_q + n_kv :]
        g_out[lanes(chunk * n_q, n_q)] = out_own[...] if j == 0 else out_other[j - 1].astype(F32)
    g_in[...] = grad_in[...]
    h_out[...] = hidden[...]
    width, d = gain_a.shape[1], gain_q.shape[1]
    gain_a[...] = gains[:, :width]
    gain_m[...] = gains[:, width : 2 * width]
    gain_q[...] = gains[:, 2 * width : 2 * width + d]
    gain_k[...] = gains[:, 2 * width + d :]


VMEM_SPEC = pl.BlockSpec(memory_space=pltpu.VMEM)
ANY_SPEC = pl.BlockSpec(memory_space=pl.ANY)


def comm_call(kernel, bits, collective_id, operands, in_specs, outs, out_specs, scratch, nbytes, copies, *more):
    return pl.pallas_call(
        functools.partial(kernel, bits, *more),
        out_shape=outs,
        in_specs=in_specs,
        out_specs=out_specs,
        scratch_shapes=[
            *scratch,
            pltpu.SemaphoreType.DMA((copies,)),
            pltpu.SemaphoreType.DMA((copies,)),
            pltpu.SemaphoreType.DMA((96,)),
        ],
        compiler_params=pltpu.CompilerParams(
            collective_id=collective_id, has_side_effects=True, vmem_limit_bytes=61 << 20
        ),
        cost_estimate=pl.CostEstimate(flops=nbytes * 20, bytes_accessed=nbytes, transcendentals=0),
        name=kernel.__name__,
    )(*operands)


def build(mesh):
    n = mesh.size
    n_f = mesh.shape["fsdp"]
    spread_bits = [b for b in (1 << i for i in range(n_f.bit_length() - 2, -1, -1)) if b != PAIR]
    all_bits = sorted([*spread_bits, PAIR], reverse=True)

    def swap(v, bit):
        return lax.ppermute(v, AXES, [(i, i ^ bit) for i in range(n)])

    def bit_of(f, b):
        return (f // b) % 2

    def in_order(bit, own, other, axis):
        low = jnp.where(bit == 0, own, other)
        high = jnp.where(bit == 0, other, own)
        return jnp.stack([low, high], axis=axis)

    def pick(v, index, axis):
        return lax.dynamic_index_in_dim(v, index, axis, keepdims=False)

    def scatter(keep, got, f, width):
        v = keep + got.astype(F32)
        have = [b for b in all_bits if b != 1]
        v = v.reshape(*([2] * len(have)), width, v.shape[-1])
        for b in [b for b in reversed(spread_bits) if b != 1]:
            axis = have.index(b)
            bit = bit_of(f, b)
            v = pick(v, bit, axis) + swap(pick(v, 1 - bit, axis).astype(BF16), b * 4).astype(F32)
            have.remove(b)
        return v

    def body(
        hidden_in,
        cotangent,
        segments,
        w_query,
        key_projection_weight,
        value_projection_weight,
        w_out,
        w_gate,
        w_up,
        w_down,
        gain_attn,
        gain_mlp,
        gain_query,
        key_norm_gain,
    ):
        rows, width = hidden_in.shape
        d = gain_query.shape[0]
        length = segments.shape[0]
        f, c = lax.axis_index("fsdp"), lax.axis_index("ctx")
        pair = bit_of(f, PAIR)
        at_rows = w_query.shape[0]
        ff_rows = w_gate.shape[0]
        ff_cols = w_gate.shape[1] // 2
        q_cols, kv_cols = w_query.shape[1] // 4, key_projection_weight.shape[1] // 4
        groups = q_cols // kv_cols

        freqs = THETA ** (-2.0 * jnp.arange(d // 2, dtype=F32) / d)
        angles = jnp.arange(length, dtype=jnp.int32).astype(F32)[:, None] * freqs
        table_cos, table_sin = jnp.cos(angles), jnp.sin(angles)
        table = jnp.concatenate([table_cos, table_cos, -table_sin, table_sin], axis=-1)

        n_rows = 8 * rows
        all_rows = jax.ShapeDtypeStruct((n_rows, width), BF16)
        own_rows = jax.ShapeDtypeStruct((rows, width), F32)
        gain_rows = jax.ShapeDtypeStruct((8, width), F32)
        block = pltpu.VMEM((rows, width), BF16)
        nbytes = rows * width * 16
        qkv_cols = q_cols + 2 * kv_cols

        def shape(*dims):
            return jax.ShapeDtypeStruct(dims, BF16)

        copies = 160 + 10 * n_f
        natural = at_rows % 128 == 0 and ff_rows % 128 == 0
        out_dims = (q_cols, width) if natural else (width, q_cols)
        down_dims = (ff_cols, width) if natural else (width, ff_cols)
        out_part = (q_cols, 2 * at_rows) if natural else (2 * at_rows, q_cols)
        down_part_dims = (ff_cols, ff_rows) if natural else (ff_rows, ff_cols)
        border = ff_cols - 256 if ff_cols % 256 == 0 and ff_cols > 256 else ff_cols // 2
        feed_spares = []
        for piece in (border, ff_cols - border):
            feed_spares += [shape(4, ff_rows, piece)] * 2
            feed_spares.append(shape(4, piece, ff_rows) if natural else shape(4, ff_rows, piece))
        n_seq = 2 * length
        all_tables = jax.ShapeDtypeStruct((n_seq, d), F32)

        def v(*dims, dtype=BF16):
            return pltpu.VMEM(dims, dtype)

        (
            residual_mid, normed_one, normed_two, grad_rows, qkv, attended, full_qkv, full_out, starts, cos, sin,
            grad_gate, grad_up, mixed_t, norm_two_part, down_part, *_, early_in,
        ) = comm_call(
            forward_kernel, spread_bits, 0,
            (hidden_in, cotangent, gain_attn[None], gain_mlp[None], segments[None], table, gain_query[None],
             key_norm_gain[None], w_query, key_projection_weight, value_projection_weight,
             w_out if natural else w_out.T, w_gate, w_up, w_down if natural else w_down.T),
            [VMEM_SPEC] * 8 + [ANY_SPEC] * 7,
            (own_rows, all_rows, all_rows, all_rows, shape(n_rows, qkv_cols), shape(n_rows, q_cols),
             shape(width, qkv_cols), shape(*out_dims), jax.ShapeDtypeStruct((n_seq, 128), F32), all_tables, all_tables,
             shape(n_rows, ff_cols), shape(n_rows, ff_cols), shape(ff_cols, n_rows), shape(8, rows, width), all_rows,
             shape(4, 2 * at_rows, qkv_cols), shape(4, *out_part), *feed_spares,
             shape(2, *down_part_dims)),
            (VMEM_SPEC, *[ANY_SPEC] * 24),
            [block, block, v(n_rows, width), v(n_rows, width), v(n_rows, width), v(width, qkv_cols), v(*out_dims),
             v(width, ff_cols), v(width, ff_cols), v(*down_dims), v(n_rows, qkv_cols), v(n_rows, q_cols),
             v(8, rows, width), v(n_rows, ff_cols, dtype=F32), v(n_rows, ff_cols, dtype=F32), v(n_rows, ff_cols),
             v(n_rows, ff_cols), v(n_rows, ff_cols), v(ff_cols, n_rows), v(n_seq, 128, dtype=F32),
             v(n_seq, d, dtype=F32), v(n_seq, d, dtype=F32), v(1, length, dtype=jnp.int32), v(2, *down_part_dims),
             *collect_buffers(rows, width)],
            16 * nbytes, copies, groups, natural,
        )
        common = (starts, cos, sin, gain_query[None], key_norm_gain[None])
        backward = one_kernel if natural and len(spread_bits) == 2 else by_steps
        return backward(
            hidden_in, cotangent, residual_mid, gain_attn, gain_mlp, common, norm_two_part, down_part, normed_one,
            normed_two, grad_rows, qkv, attended, full_qkv, full_out, grad_gate, grad_up, mixed_t, early_in,
            (at_rows, ff_rows),
        )

    def one_kernel(
        hidden_in, cotangent, residual_mid, gain_attn, gain_mlp, common, norm_two_part, down_part, normed_one,
        normed_two, grad_rows, qkv, attended, full_qkv, full_out, grad_gate, grad_up, mixed_t, early_in, sizes,
    ):
        rows, width = hidden_in.shape
        cols, n_rows = mixed_t.shape
        (at_rows, ff_rows), q_cols, qkv_cols = sizes, attended.shape[1], qkv.shape[1]
        d = common[-1].shape[1]
        kv_cols = (qkv_cols - q_cols) // 2
        groups = q_cols // kv_cols

        def out(dtype, *dims):
            return jax.ShapeDtypeStruct(dims, dtype)

        def v(*dims, dtype=BF16):
            return pltpu.VMEM(dims, dtype)

        def scatter(*block):
            return [v(2, *block), v(4, *block), v(2, *block), v(2, *block), v(*block, dtype=F32), v(*block)]

        n_gain = 2 * width + 2 * d
        nbytes = n_rows * width * 20
        (
            grad_input, hidden_out, gains, feed_own, feed_other, down_own, down_other, qkv_own, qkv_other, out_own,
            out_other, *_,
        ) = comm_call(
            backward_kernel, spread_bits, 2,
            (cotangent, gain_attn[None], gain_mlp[None], *common, residual_mid, hidden_in, norm_two_part,
             down_part.reshape(8, rows, width), normed_one, normed_two, grad_rows, qkv, attended, full_qkv, full_out,
             grad_gate, grad_up, mixed_t, early_in),
            [VMEM_SPEC] * 8 + [ANY_SPEC] * 15,
            (out(F32, rows, width), out(F32, rows, width), out(F32, 1, n_gain), out(F32, ff_rows, 2 * cols),
             out(BF16, ff_rows, 2 * cols), out(F32, cols, ff_rows), out(BF16, cols, ff_rows),
             out(F32, at_rows, qkv_cols), out(BF16, 3, at_rows, qkv_cols), out(F32, q_cols, at_rows),
             out(BF16, 3, q_cols, at_rows), out(BF16, 4, ff_rows, 2 * cols), out(BF16, 4, cols, ff_rows),
             out(BF16, 4, ff_rows, qkv_cols), out(BF16, 4, q_cols, ff_rows)),
            (VMEM_SPEC, VMEM_SPEC, VMEM_SPEC, ANY_SPEC, ANY_SPEC, ANY_SPEC, ANY_SPEC, VMEM_SPEC, ANY_SPEC, VMEM_SPEC,
             *[ANY_SPEC] * 5),
            [v(rows, width), v(n_rows, width), v(n_rows, 2 * cols), v(cols, n_rows), v(2, n_rows, ff_rows),
             v(ff_rows, n_rows), v(8, rows, width), v(width, qkv_cols), v(q_cols, width), v(n_rows, qkv_cols),
             v(n_rows, q_cols), v(n_rows, q_cols), v(n_rows, qkv_cols),
             *collect_buffers(rows, width), *collect_buffers(rows, width), v(8, width, dtype=F32), v(8, width, dtype=F32), v(2, 8, d, dtype=F32),
             v(4, 1, n_gain, dtype=F32), v(9, 1, n_gain, dtype=F32),
             *scatter(ff_rows, 2 * cols), *scatter(cols, ff_rows), *scatter(ff_rows, qkv_cols),
             *scatter(q_cols, ff_rows)],
            nbytes, 110, groups,
        )
        own_rows = out(F32, rows, width)
        made = (
            out(F32, at_rows, 4 * q_cols), out(F32, at_rows, 4 * kv_cols), out(F32, at_rows, 4 * kv_cols),
            out(F32, 4 * q_cols, at_rows), out(F32, ff_rows, 2 * cols), out(F32, ff_rows, 2 * cols),
            out(F32, 2 * cols, ff_rows), own_rows, own_rows, out(F32, 1, width), out(F32, 1, width), out(F32, 1, d),
            out(F32, 1, d),
        )
        pieces = pl.pallas_call(
            join_kernel,
            out_shape=made,
            compiler_params=pltpu.CompilerParams(vmem_limit_bytes=61 << 20),
            name="join_kernel",
        )(feed_own, feed_other, down_own, down_other, qkv_own, qkv_other, out_own, out_other, grad_input, hidden_out, gains)
        grads, (grad_input, hidden_out), gains = pieces[:7], pieces[7:9], pieces[9:]
        return hidden_out, grad_input, *grads, *(g[0] for g in gains)

    def by_steps(
        hidden_in, cotangent, residual_mid, gain_attn, gain_mlp, common, norm_two_part, down_part, normed_one,
        normed_two, grad_rows, qkv, attended, full_qkv, full_out, grad_gate, grad_up, mixed_t, early_in, sizes,
    ):
        rows, width = hidden_in.shape
        (at_rows, ff_rows), ff_cols, q_cols = sizes, mixed_t.shape[0], attended.shape[1]
        d = common[-1].shape[1]
        kv_cols = (qkv.shape[1] - q_cols) // 2
        groups = q_cols // kv_cols
        natural = full_out.shape[0] != width
        times_t = dot_cols if natural else dot
        f, c = lax.axis_index("fsdp"), lax.axis_index("ctx")
        pair = bit_of(f, PAIR)
        all_rows = jax.ShapeDtypeStruct((8 * rows, width), BF16)
        own_rows = jax.ShapeDtypeStruct((rows, width), F32)
        gain_rows = jax.ShapeDtypeStruct((8, width), F32)
        block = pltpu.VMEM((rows, width), BF16)
        nbytes = rows * width * 16
        grad_mid, gain_mlp_part, grad_mid_rows = comm_call(
            turn_kernel, spread_bits, 2, (norm_two_part.reshape(8, rows, width), residual_mid, cotangent, gain_mlp[None]),
            [ANY_SPEC, VMEM_SPEC, VMEM_SPEC, VMEM_SPEC], (own_rows, gain_rows, all_rows),
            (VMEM_SPEC, VMEM_SPEC, ANY_SPEC),
            [block, pltpu.VMEM((4, rows, width), BF16), *collect_buffers(rows, width)], 2 * nbytes, 40,
        )

        low = bit_of(f, 1)

        def weight_grad(acts, grads):
            split = acts.reshape(acts.shape[0], n_f // 2, 2, width // n_f)
            mine = pick(split, low, 2).reshape(acts.shape[0], -1)
            theirs = pick(split, 1 - low, 2).reshape(acts.shape[0], -1)
            got = swap(dot_rows(theirs, grads).astype(BF16), 4)
            return scatter(dot_rows(mine, grads), got, f, width // n_f)

        def ff_grad(acts, grads):
            v = weight_grad(acts, grads)
            other = swap(pick(v, 1 - pair, 0).astype(BF16), PAIR_BIT).astype(F32)
            return in_order(pair, pick(v, pair, 0), other, 1).reshape(ff_rows, 2 * ff_cols)

        grad_w_gate = ff_grad(normed_two, grad_gate)
        grad_w_up = ff_grad(normed_two, grad_up)
        grad_w_down = ff_grad(grad_rows, mixed_t.T).T

        def attn_grad(acts, grads):
            v = weight_grad(acts, grads)
            v = v.reshape(2, 2, at_rows, v.shape[-1])
            mine = pick(pick(v, pair, 0), c, 0)
            by_ctx = swap(pick(pick(v, pair, 0), 1 - c, 0).astype(BF16), CTX_BIT).astype(F32)
            by_pair = swap(pick(pick(v, 1 - pair, 0), c, 0).astype(BF16), PAIR_BIT).astype(F32)
            by_both = swap(pick(pick(v, 1 - pair, 0), 1 - c, 0).astype(BF16), CTX_BIT | PAIR_BIT).astype(F32)
            near = in_order(pair, mine, by_pair, 1)
            far = in_order(pair, by_ctx, by_both, 1)
            return in_order(c, near, far, 1)

        grad_w_out = attn_grad(grad_mid_rows, attended).reshape(at_rows, 4 * q_cols).T

        datt = times_t(grad_mid_rows, full_out).astype(BF16)
        grad_qkv, head_gains = attend_back(groups, qkv, attended, datt, common)
        norm_one_part = dot_cols(grad_qkv, full_qkv).astype(BF16)
        grad_input, gain_attn_part = comm_call(
            last_kernel, spread_bits, 3, (norm_one_part.reshape(8, rows, width), hidden_in, grad_mid, gain_attn[None]),
            [ANY_SPEC, VMEM_SPEC, VMEM_SPEC, VMEM_SPEC], (own_rows, gain_rows), (VMEM_SPEC, VMEM_SPEC),
            [pltpu.VMEM((4, rows, width), BF16), *collect_buffers(rows, width)], nbytes, 40,
        )
        grad_qkv_w = attn_grad(normed_one, grad_qkv)
        grad_w_query = grad_qkv_w[..., :q_cols].reshape(at_rows, -1)
        grad_w_key = grad_qkv_w[..., q_cols : q_cols + kv_cols].reshape(at_rows, -1)
        grad_w_value = grad_qkv_w[..., q_cols + kv_cols :].reshape(at_rows, -1)

        head_gains = jnp.sum(head_gains, axis=1)
        gains = jnp.concatenate(
            [jnp.sum(gain_attn_part, axis=0), jnp.sum(gain_mlp_part, axis=0), head_gains[0], head_gains[1]]
        ).reshape(-1, d)
        for i in range(n.bit_length() - 1):
            gains = gains + swap(gains, 1 << i)
        gains = gains.reshape(-1)
        teams = sorted(
            sorted(i ^ b ^ p for b in range(4) for p in (0, PAIR_BIT))
            for i in range(0, n, 4)
            if not i & PAIR_BIT
        )
        hidden_out = residual_mid + lax.psum_scatter(
            down_part, AXES, scatter_dimension=0, axis_index_groups=teams, tiled=True
        ).astype(F32)
        return (
            hidden_out,
            grad_input,
            grad_w_query,
            grad_w_key,
            grad_w_value,
            grad_w_out,
            grad_w_gate,
            grad_w_up,
            grad_w_down,
            gains[:width],
            gains[width : 2 * width],
            gains[2 * width : 2 * width + d],
            gains[2 * width + d :],
        )

    return body


def solution(mesh):
    everyone = P(("fsdp", "ctx", "tp"), None)
    attn = P(("fsdp", "ctx"), "tp")
    attn_out = P("tp", ("fsdp", "ctx"))
    ff_in = P("fsdp", ("ctx", "tp"))
    ff_out = P(("ctx", "tp"), "fsdp")
    same = P()
    return jax.shard_map(
        build(mesh),
        mesh=mesh,
        in_specs=(
            everyone, everyone, P("fsdp"), attn, attn, attn, attn_out, ff_in, ff_in, ff_out,
            same, same, same, same,
        ),
        out_specs=(
            everyone, everyone, attn, attn, attn, attn_out, ff_in, ff_in, ff_out,
            same, same, same, same,
        ),
        check_vma=False,
    )
```

```python
import functools

import jax
import jax.numpy as jnp
from jax import lax
from jax.experimental import pallas as pl
from jax.experimental.pallas import tpu as pltpu
from jax.sharding import PartitionSpec as P

EPS = 1e-06
THETA = 1000000.0
AXES = ("fsdp", "ctx", "tp")
MESH = pl.DeviceIdType.MESH
BF16 = jnp.bfloat16
F32 = jnp.float32
TP_BIT, CTX_BIT = 1, 2
PAIR = 2
PAIR_BIT = PAIR * 4


def dot_rows(left, right):
    return lax.dot_general(left, right, (((0,), (0,)), ((), ())), preferred_element_type=F32)


def dot_cols(left, right):
    return lax.dot_general(left, right, (((1,), (1,)), ((), ())), preferred_element_type=F32)


def dot(left, right):
    return lax.dot_general(left, right, (((1,), (0,)), ((), ())), preferred_element_type=F32)


def remote(src, dst, send, recv, device):
    return pltpu.make_async_remote_copy(
        src_ref=src, dst_ref=dst, send_sem=send, recv_sem=recv, device_id=device, device_id_type=MESH
    )


class Moves:
    def __init__(self, send, recv, local):
        self.send, self.recv, self.local = send, recv, local
        self.sent, self.loads = 0, 0
        self.open = []

    def swap(self, src, there, here, device, open_=None):
        k = self.sent
        self.sent += 1
        copy = remote(src, there, self.send.at[k], self.recv.at[k], device)
        copy.start()
        (self.open if open_ is None else open_).append(copy.wait_send)
        return remote(src, here, self.send.at[k], self.recv.at[k], device).wait_recv

    def load(self, src, dst):
        k = self.loads
        self.loads += 1
        copy = pltpu.make_async_copy(src, dst, self.local.at[k])
        copy.start()
        return copy.wait

    def store(self, src, dst):
        self.open.append(self.load(src, dst))

    def close(self):
        for wait in self.open:
            wait()


class Place:
    def __init__(self, bits):
        self.bits = bits
        f, c, t = lax.axis_index("fsdp"), lax.axis_index("ctx"), lax.axis_index("tp")
        self.f, self.c, self.t = f, c, t
        self.pair = (f // PAIR) % 2
        far_f = self.block(PAIR)
        fs, cs = [f, f, far_f, far_f], [c, 1 - c, c, 1 - c]
        pairs = [self.pair, self.pair, 1 - self.pair, 1 - self.pair]
        self.at = [(fs[j], cs[j], pairs[j]) for j in range(4)]
        self.rows_of = [pairs[j] * 4 + cs[j] * 2 for j in range(4)]
        self.chunk_of = [cs[j] * 2 + pairs[j] for j in range(4)]
        self.relay = len(bits) == 2
        self.across_mask = bits[0] | PAIR
        self.inner = (f // bits[0]) % 2 != self.pair
        self.chips = [None, {"ctx": 1 - c}, {"fsdp": far_f}, {"fsdp": far_f, "ctx": 1 - c}]
        self.sibling = {"tp": 1 - t}

    def block(self, mask):
        out = self.f
        for i in range(mask.bit_length()):
            b = 1 << i
            if mask & b:
                out = out + b - 2 * b * ((self.f // b) % 2)
        return out

    def along(self, bit):
        return {"fsdp": self.block(bit)}

    def greet(self):
        barrier = pltpu.get_barrier_semaphore()
        devices = [*self.chips[1:], self.sibling, *[self.along(b) for b in self.bits]]
        if self.relay:
            devices += [self.along(self.across_mask), self.along(self.bits[0] | self.bits[1])]
        for device in devices:
            pl.semaphore_signal(barrier, inc=1, device_id=device, device_id_type=MESH)
        pl.semaphore_wait(barrier, len(devices))


class Cross:
    def __init__(self, moves, place, src, here, came_in, across_to, came_out, pair_to, held=None):
        self.place, self.here, self.held = place, here, held
        self.came_in, self.came_out = came_in, came_out
        k = moves.sent
        moves.sent += 4
        pair, across = place.chips[2], place.along(place.across_mask)

        def copy(i, source, to, device):
            return remote(source, to, moves.send.at[k + i], moves.recv.at[k + i], device)

        self.hand = copy(0, src, came_in, pair)
        self.own = copy(1, src, came_out, across)
        self.on = copy(2, came_in if held is None else held, across_to, across)
        self.back = copy(3, came_out, pair_to, pair)
        self.came = [copy(0, came_in, came_in, pair), copy(1, came_out, came_out, across)]
        self.landed = [copy(2, here, here, across), copy(3, here, here, pair)]
        moves.open.append(self.left)

        @pl.when(place.inner)
        def _():
            self.own.start()
            if held is not None:
                self.on.start()

        @pl.when(jnp.logical_not(place.inner))
        def _():
            if held is None:
                self.hand.start()

    def relay(self):
        @pl.when(self.place.inner)
        def _():
            if self.held is None:
                self.came[0].wait_recv()
                self.on.start()
            self.came[1].wait_recv()
            self.back.start()

    def arrive(self):
        @pl.when(self.place.inner)
        def _():
            self.landed[0].wait_recv()

        @pl.when(jnp.logical_not(self.place.inner))
        def _():
            self.landed[1].wait_recv()

    def left(self):
        @pl.when(self.place.inner)
        def _():
            self.own.wait_send()
            self.on.wait_send()
            self.back.wait_send()

        @pl.when(jnp.logical_not(self.place.inner))
        def _():
            if self.held is None:
                self.hand.wait_send()


class Spread:
    def __init__(self, moves, place, own, out, part=0, parts=1):
        self.moves, self.place, self.out = moves, place, out
        self.rows = own.shape[0]
        self.stride, self.offset = self.rows * parts, self.rows * part
        self.open = []
        mine = self.at(0, place.t)
        self.here = moves.load(own, mine)
        self.pair = moves.swap(own, mine, self.at(2, place.t), place.chips[2], self.open)
        self.ctx = moves.swap(own, mine, self.at(1, place.t), place.chips[1], self.open)
        self.beside = [moves.swap(own, mine, self.at(0, 1 - place.t), place.sibling, self.open)]

    def at(self, j, t):
        start = (self.place.rows_of[j] + t) * self.stride + self.offset
        return self.out.at[pl.ds(pl.multiple_of(start, self.rows), self.rows)]

    def hand(self, j):
        block = self.at(j, self.place.t)
        self.beside.append(
            self.moves.swap(block, block, self.at(j, 1 - self.place.t), self.place.sibling, self.open)
        )

    def from_pair(self):
        self.pair()
        block = self.at(2, self.place.t)
        self.both = self.moves.swap(block, block, self.at(3, self.place.t), self.place.chips[1], self.open)
        self.hand(2)

    def from_ctx(self):
        self.ctx()
        self.hand(1)

    def from_both(self):
        self.both()
        self.hand(3)

    def finish(self):
        self.here()
        for wait in (*self.beside, *self.open):
            wait()


class Collect:
    def __init__(self, moves, place, part, held, first, ctx_in, pair_in, sending, load):
        self.moves, self.place = moves, place
        self.first, self.ctx_in, self.pair_in, self.sending = first, ctx_in, pair_in, sending
        t = place.t
        self.hands, self.loads, self.open = {}, {}, []
        for j in (3, 1, 2, 0):
            self.hands[j] = moves.swap(part(j, 1 - t), first.at[j], first.at[j], place.sibling, self.open)
            if load:
                self.loads[j] = moves.load(part(j, t), held.at[j])
        self.held = (lambda j: held.at[j]) if load else (lambda j: part(j, t))

    def two(self, j, at):
        return self.held(j)[at].astype(F32) + self.first[j, at].astype(F32)

    def ready(self, j):
        self.hands[j]()
        if j in self.loads:
            self.loads[j]()

    def to_ctx(self):
        self.waits = {}
        for j, slot in ((3, 0), (1, 1)):
            self.ready(j)

            def body(at):
                self.sending[slot, at] = self.two(j, at).astype(BF16)

            row_loop(self.sending.shape[1], body)
            self.waits[j] = self.moves.swap(
                self.sending.at[slot], self.ctx_in.at[slot], self.ctx_in.at[slot], self.place.chips[1], self.open
            )

    def to_pair(self):
        self.ready(2)
        self.waits[3]()

        def body(at):
            self.sending[2, at] = (self.two(2, at) + self.ctx_in[0, at].astype(F32)).astype(BF16)

        row_loop(self.sending.shape[1], body)
        self.waits[2] = self.moves.swap(
            self.sending.at[2], self.pair_in, self.pair_in, self.place.chips[2], self.open
        )

    def fold(self):
        for j, slot in ((3, 0), (1, 1), (2, 2)):
            self.ready(j)

            def body(at):
                self.sending[slot, at] = self.two(j, at).astype(BF16)

            row_loop(self.sending.shape[1], body)
        self.ready(0)

    def post_ctx(self):
        self.waits = {}
        for j, slot in ((3, 0), (1, 1)):
            self.waits[j] = self.moves.swap(
                self.sending.at[slot], self.ctx_in.at[slot], self.ctx_in.at[slot], self.place.chips[1], self.open
            )

    def post_pair(self):
        self.waits[3]()

        def body(at):
            self.sending[2, at] = (self.sending[2, at].astype(F32) + self.ctx_in[0, at].astype(F32)).astype(BF16)

        row_loop(self.sending.shape[1], body)
        self.waits[2] = self.moves.swap(
            self.sending.at[2], self.pair_in, self.pair_in, self.place.chips[2], self.open
        )

    def came(self):
        for wait in (self.waits[1], self.waits[2], *self.open):
            wait()

    def finish(self):
        self.ready(0)
        self.waits[1]()
        self.waits[2]()
        for wait in self.open:
            wait()

    def total(self, at):
        return self.two(0, at) + (self.ctx_in[1, at].astype(F32) + self.pair_in[at].astype(F32))


def collect_buffers(rows, width):
    return [
        pltpu.VMEM((4, rows, width), BF16),
        pltpu.VMEM((2, rows, width), BF16),
        pltpu.VMEM((rows, width), BF16),
        pltpu.VMEM((3, rows, width), BF16),
    ]


def row_loop(rows, body):
    step = 16

    @pl.loop(0, rows // step)
    def _(i):
        body(pl.ds(pl.multiple_of(i * step, step), step))


def half_loop(part, rows, body):
    step = 16

    @pl.loop(0, rows // step)
    def _(i):
        body(
            pl.ds(pl.multiple_of(i * step, step), step),
            pl.ds(pl.multiple_of(part * rows + i * step, step), step),
        )


def unit_and_scale(x):
    scale = lax.rsqrt(jnp.mean(x * x, axis=-1, keepdims=True) + EPS)
    return x * scale, scale


class Gather:
    def __init__(self, moves, place, block, spare):
        self.moves, self.place, self.block, self.spare = moves, place, block, spare
        self.waits, self.crosses = {}, {}

    def forward(self, mask, src=None, held=None):
        done = [i for i, b in enumerate(self.place.bits) if mask & b]
        here = self.block(self.place.block(mask))
        for b in self.place.bits[max(done, default=-1) + 1 :]:
            if self.place.relay and b == self.place.bits[0]:
                far = self.place.across_mask
                slot = 0 if mask == 0 else 2
                self.crosses[mask] = Cross(
                    self.moves, self.place, here if src is None else src, self.block(self.place.block(mask | b)),
                    self.spare.at[slot], self.block(self.place.block(mask ^ PAIR)),
                    self.spare.at[slot + 1], self.block(self.place.block(mask ^ far)), held,
                )
                self.waits[mask | b] = self.crosses[mask].arrive
                continue
            self.waits[mask | b] = self.moves.swap(
                here if src is None else src, here, self.block(self.place.block(mask | b)), self.place.along(b)
            )

    def masks(self, stage):
        out = [0, PAIR]
        for b in self.place.bits[:stage]:
            out += [m | b for m in out]
        return [m | self.place.bits[stage] for m in out]

    def relay(self, m):
        if self.place.relay:
            self.crosses[m].relay()

    def hop(self, m):
        if self.place.relay:
            self.pass_on(m | self.place.bits[0])
        elif m == PAIR:
            self.middle()

    def pass_on(self, m, held=None):
        self.waits.pop(m)()
        self.forward(m, None, held)

    def middle(self):
        for stage in range(len(self.place.bits) - 1):
            for m in self.masks(stage):
                if m in self.waits:
                    self.pass_on(m)

    def finish(self):
        for wait in self.waits.values():
            wait()


def head_unit(x):
    scale = lax.rsqrt(jnp.mean(x * x, axis=-1, keepdims=True) + EPS)
    return x * scale, scale


def rot(a, cos, sin):
    return a * cos + pltpu.roll(a, a.shape[-1] // 2, 1) * sin


def rot_back(b, cos, sin):
    return b * cos - pltpu.roll(b, b.shape[-1] // 2, 1) * sin


def allowed_keys(start):
    length = start.shape[0]
    row = lax.broadcasted_iota(jnp.int32, (length, length), 0)
    col = lax.broadcasted_iota(jnp.int32, (length, length), 1)
    return (col.astype(F32) >= start) & (row >= col)


def soft_of(scores):
    peak = jnp.max(scores, axis=-1, keepdims=True)
    lse = peak + jnp.log(jnp.sum(jnp.exp(scores - peak), axis=-1, keepdims=True))
    return jnp.exp(scores - lse)


def attend_one(groups, s, qkv, starts, cos_ref, sin_ref, gain_q, gain_k, out):
    d = gain_q.shape[-1]
    length = cos_ref.shape[0] // 2
    rows = pl.ds(pl.multiple_of(s * length, length), length)
    cos, sin = cos_ref[rows], sin_ref[rows]
    allowed = allowed_keys(starts[rows, 0:1])
    unit_k, _ = head_unit(qkv[rows, groups * d : (groups + 1) * d].astype(F32))
    key = rot(unit_k * gain_k[...], cos, sin).astype(BF16)
    value = qkv[rows, (groups + 1) * d : (groups + 2) * d]
    for g in range(groups):
        unit_q, _ = head_unit(qkv[rows, g * d : (g + 1) * d].astype(F32))
        query = rot(unit_q * gain_q[...], cos, sin).astype(BF16)
        scores = jnp.where(allowed, dot_cols(query, key) * d**-0.5, -jnp.inf)
        soft = soft_of(scores).astype(BF16)
        out[rows, g * d : (g + 1) * d] = dot(soft, value).astype(BF16)


def through_norm(b, unit, scale, gain):
    e = b * gain
    return scale * (e - unit * jnp.mean(e * unit, axis=-1, keepdims=True))


def attend_back_one(
    groups, s, qkv, att, datt, starts, cos_ref, sin_ref, gain_q, gain_k, grad, gains
):
    d = gain_q.shape[-1]
    length = cos_ref.shape[0] // 2
    rows = pl.ds(pl.multiple_of(s * length, length), length)
    cos, sin = cos_ref[rows], sin_ref[rows]
    scale = d**-0.5
    allowed = allowed_keys(starts[rows, 0:1])
    at_k, at_v = slice(groups * d, (groups + 1) * d), slice((groups + 1) * d, (groups + 2) * d)
    unit_k, scale_k = head_unit(qkv[rows, at_k].astype(F32))
    key = rot(unit_k * gain_k[...], cos, sin).astype(BF16)
    value = qkv[rows, at_v]
    key_grad = jnp.zeros(unit_k.shape, F32)
    value_grad = jnp.zeros(unit_k.shape, F32)
    for g in range(groups):
        at = slice(g * d, (g + 1) * d)
        unit_q, scale_q = head_unit(qkv[rows, at].astype(F32))
        query = rot(unit_q * gain_q[...], cos, sin).astype(BF16)
        scores = jnp.where(allowed, dot_cols(query, key) * scale, -jnp.inf)
        soft = soft_of(scores)
        up = datt[rows, at]
        delta = jnp.sum(up.astype(F32) * att[rows, at].astype(F32), axis=-1, keepdims=True)
        ds = (soft * (dot_cols(up, value) - delta) * scale).astype(BF16)
        value_grad += dot_rows(soft.astype(BF16), up)
        key_grad += dot_rows(ds, query)
        b = rot_back(dot(ds, key), cos, sin)
        gains[0] += jnp.sum((b * unit_q).reshape(-1, 8, d), axis=0)
        grad[rows, at] = through_norm(b, unit_q, scale_q, gain_q[...]).astype(BF16)
    b = rot_back(key_grad, cos, sin)
    gains[1] += jnp.sum((b * unit_k).reshape(-1, 8, d), axis=0)
    grad[rows, at_k] = through_norm(b, unit_k, scale_k, gain_k[...]).astype(BF16)
    grad[rows, at_v] = value_grad.astype(BF16)


def attend_back_kernel(
    groups, qkv, att, datt, starts, cos, sin, gain_q, gain_k, grad, gains
):
    gains[...] = jnp.zeros_like(gains)

    @pl.loop(0, 2)
    def _(s):
        attend_back_one(groups, s, qkv, att, datt, starts, cos, sin, gain_q, gain_k, grad, gains)


def attend_back(groups, qkv, att, datt, common):
    n_rows, width = qkv.shape
    d = width // (groups + 2)
    length = n_rows // 2
    return pl.pallas_call(
        functools.partial(attend_back_kernel, groups),
        out_shape=(jax.ShapeDtypeStruct(qkv.shape, BF16), jax.ShapeDtypeStruct((2, 8, d), F32)),
        compiler_params=pltpu.CompilerParams(vmem_limit_bytes=40 << 20),
        cost_estimate=pl.CostEstimate(
            flops=n_rows * groups * length * (10 * d + 30),
            bytes_accessed=n_rows * width * 8,
            transcendentals=n_rows * groups * length * 2,
        ),
        name="attend_back",
    )(qkv, att, datt, *common)


def forward_kernel(
    bits, groups, natural,
    hidden, cot, gain_attn, gain_mlp, seg, table, gain_q, gain_k, wq, wk, wv, wo, wg, wu, wd,
    mid, normed_one, normed_two, cot_out, qkv_out, att_out, qkv_weight, out_weight, starts_out, cos_out, sin_out,
    grad_gate_out, grad_up_out, mixed_out, part_out, down_out, spare_qkv, spare_out,
    spare_gate_a, spare_up_a, spare_down_a, spare_gate_b, spare_up_b, spare_down_b, early_in,
    own_one, own_two, rows_one, rows_two, rows_cot, w_qkv, w_out, w_gate, w_up, w_down, qkv, att, part,
    gate, up, grad_gate, grad_up, mixed, mixed_t, starts, cos, sin, seg_in, early, first, ctx_in, pair_in, sending,
    send, recv, local,
):
    place = Place(bits)
    moves = Moves(send, recv, local)
    rows, width = hidden.shape
    at_rows, ff_rows, ff_cols = wq.shape[0], wg.shape[0], wg.shape[1] // 2
    q_cols, kv_cols = wq.shape[1] // 4, wk.shape[1] // 4
    n_rows, length = rows_one.shape[0], seg.shape[1]

    def lanes(start, size):
        return pl.ds(pl.multiple_of(start, size), size)

    def qkv_rows(f, c=None):
        if c is None:
            return lanes(f * 2 * at_rows, 2 * at_rows)
        return lanes((f * 2 + c) * at_rows, at_rows)

    place.greet()

    def out_block(f, c=None):
        return w_out.at[:, qkv_rows(f, c)] if natural else w_out.at[qkv_rows(f, c)]

    def out_chunk(j):
        at = lanes(place.chunk_of[j] * q_cols, q_cols)
        return wo.at[at] if natural else wo.at[:, at]

    pieces = (
        (wq, q_cols, pl.ds(0, q_cols)),
        (wk, kv_cols, pl.ds(q_cols, kv_cols)),
        (wv, kv_cols, pl.ds(q_cols + kv_cols, kv_cols)),
    )
    f0, c0, _ = place.at[0]
    qkv_in, out_in = {}, {}

    border = ff_cols - 256 if ff_cols % 256 == 0 and ff_cols > 256 else ff_cols // 2
    piece_a, piece_b = pl.ds(0, border), pl.ds(border, ff_cols - border)

    def feed_weight(weight, piece, source, spare, by_rows):
        start, size = (0, border) if piece is piece_a else (border, ff_cols - border)

        def block(f):
            at = lanes(f * ff_rows, ff_rows)
            return weight.at[at, piece] if by_rows else weight.at[piece, at]

        def half(which):
            at = pl.ds(pl.multiple_of(which * ff_cols + start, 128), size)
            return source.at[:, at] if by_rows else source.at[at]

        return Gather(moves, place, block, spare), half(place.pair), half(1 - place.pair)

    feed = []
    for piece, spares in ((piece_a, (spare_gate_a, spare_up_a, spare_down_a)), (piece_b, (spare_gate_b, spare_up_b, spare_down_b))):
        feed.append(feed_weight(w_gate, piece, wg, spares[0], True))
        feed.append(feed_weight(w_up, piece, wu, spares[1], True))
        feed.append(feed_weight(w_down, piece, wd, spares[2], not natural))
    own_feed = [moves.load(own, gather.block(place.f)) for gather, own, _ in feed]

    def swap_pair(i):
        gather, _, other = feed[i]
        gather.waits[PAIR] = moves.swap(
            other, gather.block(place.f), gather.block(place.block(PAIR)), place.along(PAIR)
        )

    early_waits = []

    def send_early(i):
        if place.relay:
            high, low = bits
            mask = (high, high | PAIR)[i] | low
            at = lanes(place.block(mask) * ff_rows, ff_rows)
            early[i] = dot(mixed_t[...], rows_cot[:, at]).astype(BF16)
            early_waits.append(moves.swap(early.at[i], early_in.at[i], early_in.at[i], place.along(low)))

    step = 2 * rows
    wide = min(256, w_qkv.shape[1])
    qkv_gather = Gather(moves, place, lambda f: w_qkv.at[qkv_rows(f)], spare_qkv)
    out_gather = Gather(moves, place, out_block, spare_out)

    def norm_one(at):
        unit, _ = unit_and_scale(hidden[at].astype(F32))
        own_one[at] = (unit * gain_attn[...]).astype(BF16)

    collects = [None, None]

    def collect_part(h):
        at = pl.ds(h * rows // 2, rows // 2)
        return Collect(
            moves, place, lambda j, t: part.at[place.rows_of[j] + t, at], None, first.at[:, at], ctx_in.at[:, at],
            pair_in.at[at], sending.at[:, at], False,
        )

    def norm_two(h):
        def body(there, at):
            x = hidden[at].astype(F32) + collects[h].total(there)
            mid[at] = x
            unit, _ = unit_and_scale(x)
            own_two[at] = (unit * gain_mlp[...]).astype(BF16)

        return body

    def columns_of(weight, at):
        return (dot, weight[:, at]) if natural else (dot_cols, weight[at])

    def gate_part(piece):
        @pl.loop(0, n_rows // step)
        def _(i):
            at = lanes(i * step, step)
            gate[at, piece] = dot(rows_two[at], w_gate[:, piece])

    def up_part(piece):
        @pl.loop(0, n_rows // step)
        def _(i):
            at = lanes(i * step, step)
            u = dot(rows_two[at], w_up[:, piece])
            up[at, piece] = u
            g = gate[at, piece]
            mix = g * jax.nn.sigmoid(g) * u
            mixed[at, piece] = mix.astype(BF16)
            mixed_t[piece, at] = mix.T.astype(BF16)

    def back_part(piece):
        @pl.loop(0, n_rows // step)
        def _(i):
            at = lanes(i * step, step)
            m = dot_cols(rows_cot[at], w_down[piece]) if natural else dot(rows_cot[at], w_down[:, piece])
            g = gate[at, piece]
            s = jax.nn.sigmoid(g)
            grad_gate[at, piece] = (m * up[at, piece] * s * (1.0 + g * (1.0 - s))).astype(BF16)
            grad_up[at, piece] = (m * (g * s)).astype(BF16)

    def grad_part(piece, last):
        for half in range(2):

            @pl.loop(0, width // 512)
            def _(i):
                at = lanes(half * (width // 2) + i * 256, 256)
                both = dot_cols(grad_gate[:, piece], w_gate[at, piece]) + dot_cols(grad_up[:, piece], w_up[at, piece])
                both = both.reshape(8, rows, 256)
                if last:
                    both = both + part[:, :, at].astype(F32)
                part[:, :, at] = both.astype(BF16)

            if last:
                at = pl.ds(half * (width // 2), width // 2)
                moves.store(part.at[:, :, at], part_out.at[:, :, at])

    def down_part(piece, last):
        @pl.loop(0, width // 256)
        def _(i):
            at = lanes(i * 256, 256)
            if natural:
                term = dot(mixed[:, piece], w_down[piece, at])
            else:
                term = dot_cols(mixed[:, piece], w_down[at, piece])
            if last:
                term = term + rows_one[:, at].astype(F32)
            rows_one[:, at] = term.astype(BF16)

        if last:
            moves.store(rows_one, down_out)

    for j in (3, 2, 1):
        fj, cj, _ = place.at[j]
        out_in[j] = moves.swap(out_chunk(j), out_block(f0, c0), out_block(fj, cj), place.chips[j])
    out_in[0] = moves.load(out_chunk(0), out_block(f0, c0))
    feed[1][0].forward(0, feed[1][1])
    for j in (1, 3, 2):
        fj, cj, _ = place.at[j]
        qkv_in[j] = [
            moves.swap(
                w.at[:, lanes(place.chunk_of[j] * size, size)],
                w_qkv.at[qkv_rows(f0, c0), to],
                w_qkv.at[qkv_rows(fj, cj), to],
                place.chips[j],
            )
            for w, size, to in pieces
        ]
    qkv_in[0] = [
        moves.load(w.at[:, lanes(place.chunk_of[0] * size, size)], w_qkv.at[qkv_rows(f0, c0), to])
        for w, size, to in pieces
    ]
    row_loop(rows, norm_one)
    spread_one = Spread(moves, place, own_one, rows_one)
    for wait in (*qkv_in[0], *qkv_in[1]):
        wait()
    qkv_gather.forward(0)
    feed[1][0].relay(0)
    for wait in (*qkv_in[2], *qkv_in[3]):
        wait()
    qkv_gather.forward(PAIR)
    out_in[2]()
    out_in[3]()
    out_gather.forward(PAIR)
    out_in[0]()
    out_in[1]()
    out_gather.forward(0)
    feed[0][0].forward(0, feed[0][1])
    seg_wait = moves.swap(seg, seg_in, seg_in, place.chips[2])
    swap_pair(0)
    spread_one.from_pair()
    swap_pair(1)
    qkv_gather.relay(0)
    qkv_gather.relay(PAIR)
    qkv_gather.hop(0)
    spread_one.from_both()
    out_gather.relay(0)
    out_gather.relay(PAIR)
    qkv_gather.hop(PAIR)
    feed[0][0].relay(0)
    spread_cot = Spread(moves, place, cot, rows_cot)
    swap_pair(5)
    out_gather.hop(0)
    spread_one.from_ctx()
    seg_wait()
    pair_first = place.pair == 0
    own_seg, far_seg = seg[...].astype(F32), seg_in[...].astype(F32)
    for i in range(2):
        here = pair_first if i == 0 else jnp.logical_not(pair_first)
        flags = jnp.where(here, own_seg, far_seg)
        both = jnp.broadcast_to(flags, (128, length)).T[:, 0:1]
        start = jnp.sum((flags < both).astype(F32), axis=1, keepdims=True)
        row = lax.broadcasted_iota(jnp.int32, (length, length), 0).astype(F32)
        col = lax.broadcasted_iota(jnp.int32, (length, length), 1).astype(F32)
        chosen = (row - start == col).astype(F32)
        at = pl.ds(i * length, length)
        both_tables = lax.dot_general(
            chosen, table[...], (((1,), (0,)), ((), ())),
            precision=lax.Precision.HIGHEST, preferred_element_type=F32,
        )
        d = gain_q.shape[1]
        starts[at] = jnp.broadcast_to(start, (length, 128))
        cos[at] = both_tables[:, :d]
        sin[at] = both_tables[:, d:]
    moves.store(starts, starts_out)
    moves.store(cos, cos_out)
    moves.store(sin, sin_out)
    spread_one.finish()
    normed_stored = moves.load(rows_one, normed_one)
    out_gather.hop(PAIR)
    feed[0][0].pass_on(PAIR, feed[0][2])
    feed[3][0].forward(0, feed[3][1])
    qkv_gather.finish()
    moves.store(w_qkv, qkv_weight)
    @pl.loop(0, w_qkv.shape[1] // wide)
    def _(i):
        at = lanes(i * wide, wide)
        qkv[:, at] = dot(rows_one[...], w_qkv[:, at]).astype(BF16)

    moves.store(qkv, qkv_out)
    @pl.loop(0, 2)
    def _(s):
        attend_one(groups, s, qkv, starts, cos, sin, gain_q, gain_k, att)

    moves.store(att, att_out)
    feed[1][0].pass_on(PAIR, feed[1][2])
    out_gather.finish()
    moves.store(w_out, out_weight)
    feed[1][0].hop(0)
    feed[0][0].relay(PAIR)
    @pl.loop(0, width // 256)
    def _(i):
        at = lanes(i * 256, 256)
        times, block = columns_of(w_out, at)
        part[:, :, at] = times(att[...], block).astype(BF16).reshape(8, rows, 256)

    swap_pair(4)
    collects[0] = collect_part(0)
    collects[1] = collect_part(1)
    collects[0].to_ctx()
    swap_pair(2)
    feed[4][0].forward(0, feed[4][1])
    collects[1].to_ctx()
    swap_pair(3)
    collects[0].to_pair()
    feed[2][0].forward(0, feed[2][1])
    feed[4][0].pass_on(PAIR, feed[4][2])
    feed[1][0].relay(PAIR)
    feed[0][0].hop(0)
    collects[1].to_pair()
    feed[4][0].relay(0)
    collects[0].finish()
    feed[4][0].relay(PAIR)
    feed[3][0].relay(0)
    half_loop(0, rows // 2, norm_two(0))
    feed[2][0].pass_on(PAIR, feed[2][2])
    spread_two_0 = Spread(moves, place, own_two.at[pl.ds(0 * rows // 2, rows // 2)], rows_two, 0, 2)
    feed[1][0].hop(PAIR)
    feed[3][0].pass_on(PAIR, feed[3][2])
    spread_cot.from_pair()
    collects[1].finish()
    half_loop(1, rows // 2, norm_two(1))
    feed[5][0].forward(0, feed[5][1])
    spread_two_1 = Spread(moves, place, own_two.at[pl.ds(1 * rows // 2, rows // 2)], rows_two, 1, 2)
    feed[0][0].hop(PAIR)
    feed[4][0].hop(0)
    feed[2][0].relay(0)
    feed[3][0].relay(PAIR)
    spread_cot.from_ctx()
    spread_cot.from_both()
    feed[3][0].hop(0)
    spread_two_0.from_ctx()
    spread_two_0.from_pair()
    spread_cot.finish()
    moves.store(rows_cot, cot_out)
    feed[2][0].relay(PAIR)
    spread_two_1.from_ctx()
    feed[5][0].pass_on(PAIR, feed[5][2])
    feed[4][0].hop(PAIR)
    feed[5][0].relay(0)
    own_feed[0]()
    feed[0][0].finish()
    spread_two_1.from_pair()
    spread_two_0.from_both()
    feed[2][0].hop(0)
    spread_two_1.from_both()
    own_feed[4]()
    feed[4][0].finish()
    spread_two_0.finish()
    own_feed[1]()
    feed[1][0].finish()
    feed[5][0].relay(PAIR)
    feed[3][0].hop(PAIR)
    spread_two_1.finish()
    moves.store(rows_two, normed_two)
    gate_part(piece_a)
    feed[2][0].hop(PAIR)
    up_part(piece_a)
    own_feed[3]()
    feed[3][0].finish()
    feed[5][0].hop(0)
    gate_part(piece_b)
    up_part(piece_b)
    send_early(0)
    moves.store(mixed_t, mixed_out)
    feed[5][0].hop(PAIR)
    own_feed[2]()
    feed[2][0].finish()
    normed_stored()
    down_part(piece_a, False)
    back_part(piece_a)
    send_early(1)
    grad_part(piece_a, False)
    own_feed[5]()
    feed[5][0].finish()
    back_part(piece_b)
    moves.store(grad_gate, grad_gate_out)
    moves.store(grad_up, grad_up_out)
    grad_part(piece_b, True)
    down_part(piece_b, True)
    for wait in early_waits:
        wait()
    moves.close()


def norm_back(grad, x, gain, gain_grad):
    unit, scale = unit_and_scale(x)
    gain_grad[...] += jnp.sum((grad * unit).reshape(-1, 8, grad.shape[-1]), axis=0)
    e = grad * gain
    return scale * (e - unit * jnp.mean(e * unit, axis=-1, keepdims=True))


def turn_kernel(
    bits, partial, mid, cot, gain, grad_mid, gain_grad, out,
    own, held, first, ctx_in, pair_in, sending, send, recv, local,
):
    place = Place(bits)
    moves = Moves(send, recv, local)
    place.greet()
    collect = Collect(
        moves, place, lambda j, t: partial.at[place.rows_of[j] + t], held, first, ctx_in, pair_in, sending, True
    )
    collect.to_ctx()
    collect.to_pair()
    collect.finish()
    gain_grad[...] = jnp.zeros_like(gain_grad)

    def back(at):
        g = cot[at].astype(F32) + norm_back(collect.total(at), mid[at], gain[...], gain_grad)
        grad_mid[at] = g
        own[at] = g.astype(BF16)

    row_loop(mid.shape[0], back)
    spread = Spread(moves, place, own, out)
    spread.from_pair()
    spread.from_ctx()
    spread.from_both()
    spread.finish()
    moves.close()


def last_kernel(
    bits, partial, hidden, grad_mid, gain, grad_in, gain_grad,
    held, first, ctx_in, pair_in, sending, send, recv, local,
):
    place = Place(bits)
    moves = Moves(send, recv, local)
    place.greet()
    collect = Collect(
        moves, place, lambda j, t: partial.at[place.rows_of[j] + t], held, first, ctx_in, pair_in, sending, True
    )
    collect.to_ctx()
    collect.to_pair()
    collect.finish()
    gain_grad[...] = jnp.zeros_like(gain_grad)

    def back(at):
        grad_in[at] = grad_mid[at] + norm_back(
            collect.total(at), hidden[at].astype(F32), gain[...], gain_grad
        )

    row_loop(hidden.shape[0], back)
    moves.close()


class Scatter:
    def __init__(self, moves, place, product, out0, in0, out1, in1, acc, acc_pair, spare):
        self.moves, self.place, self.product, self.spare = moves, place, product, spare
        self.out0, self.in0, self.out1, self.in1, self.acc, self.acc_pair = out0, in0, out1, in1, acc, acc_pair
        self.low, self.high = place.bits[1], place.bits[0]
        self.order = [self.high, self.high | PAIR, 0, PAIR]
        self.first, self.second, self.leaving = {}, {}, {}

    def send(self, i):
        slot = i % 2
        for wait in self.leaving.pop(slot, []):
            wait()

        def emit(at, value):
            self.out0[(slot, *at)] = value.astype(BF16)

        self.product(self.order[i] | self.low, emit)
        self.leaving[slot] = []
        self.first[i] = self.moves.swap(
            self.out0.at[slot], self.in0.at[i], self.in0.at[i], self.place.along(self.low), self.leaving[slot]
        )

    def take(self, i):
        self.first[i]()

        def emit(at, value):
            value = value + self.in0[(i, *at)].astype(F32)
            if i < 2:
                self.out1[(i, *at)] = value.astype(BF16)
            elif i == 2:
                self.acc[at] = value
            else:
                self.acc_pair[at] = value.astype(BF16)

        self.product(self.order[i], emit)
        if i < 2:
            to = self.in1.at[i]
            self.second[i] = Cross(
                self.moves, self.place, self.out1.at[i], to, self.spare.at[2 * i], to, self.spare.at[2 * i + 1], to
            )

    def relay(self, i):
        self.second[i].relay()

    def take_high(self, i):
        self.second[i].arrive()
        total = self.acc_pair if i else self.acc
        step = 64

        @pl.loop(0, total.shape[0] // step)
        def _(k):
            at = pl.ds(pl.multiple_of(k * step, step), step)
            total[at] = (total[at].astype(F32) + self.in1[i, at].astype(F32)).astype(total.dtype)

    def close(self):
        for waits in self.leaving.values():
            for wait in waits:
                wait()


class Blocks:
    def __init__(self, moves, place, slots, order):
        self.moves, self.place, self.slots, self.order = moves, place, slots, order
        self.next, self.waits = 0, {}
        self.start(0)

    def start(self, k):
        if k < len(self.order):
            ref, mask = self.order[k]
            size = self.slots.shape[2]
            at = pl.ds(pl.multiple_of(self.place.block(mask) * size, size), size)
            self.waits[k] = self.moves.load(ref.at[:, at], self.slots.at[k % 2])

    def get(self, ref, mask):
        k = self.next
        assert self.order[k][0] is ref and self.order[k][1] == mask
        self.next += 1
        self.waits.pop(k)()
        self.start(k + 1)
        return self.slots[k % 2]


def backward_kernel(
    bits, groups,
    cot, gain_attn, gain_mlp, starts, cos, sin, gain_q, gain_k,
    mid, hidden, part_two, part_hidden, normed_one, normed_two, cot_rows, qkv_in, att_in, qkv_weight, out_weight, grad_gate, grad_up,
    mixed_t, early_in,
    grad_in, hidden_out, gains, feed_own, feed_other, down_own, down_other, qkv_own, qkv_other, out_own, out_other,
    spare_feed, spare_down, spare_qkv, spare_out,
    own, rows_mid, feed, mixed, lhs, lhs_t, part, w_qkv, w_out, qkv, att, datt, dqkv,
    first, ctx_in, pair_in, sending, first_h, ctx_h, pair_h, sending_h, gain_a, gain_m, gain_h, tree, tree_in,
    f_out0, f_in0, f_out1, f_in1, f_acc, f_pair, d_out0, d_in0, d_out1, d_in1, d_acc, d_pair,
    q_out0, q_in0, q_out1, q_in1, q_acc, q_pair, o_out0, o_in0, o_out1, o_in1, o_acc, o_pair,
    send, recv, local,
):
    place = Place(bits)
    moves = Moves(send, recv, local)
    rows, width = cot.shape
    cols = mixed.shape[0]
    tile = lhs.shape[2]
    half = tile // 2
    high, low = bits
    place.greet()

    def lanes(start, size):
        return pl.ds(pl.multiple_of(start, size), size)

    ready_mid = moves.load(mid, hidden_out)
    ready_feed = [
        moves.load(grad_gate, feed.at[:, pl.ds(0, cols)]),
        moves.load(grad_up, feed.at[:, pl.ds(cols, cols)]),
    ]
    masks = [high, high | PAIR, 0, PAIR]
    sends = [m | low for m in masks]
    a, b, c, e = range(4)
    order = [
        (cot_rows, masks[b]), (cot_rows, sends[e]), (cot_rows, masks[a]), (normed_two, sends[a]),
        (cot_rows, masks[e]), (normed_two, sends[b]), (normed_two, masks[a]), (normed_two, sends[e]),
        (normed_two, masks[b]), (normed_two, masks[e]), (normed_one, sends[a]), (normed_one, sends[b]),
        (normed_one, masks[a]), (normed_two, sends[c]), (normed_one, sends[e]), (normed_one, masks[b]),
        (normed_two, masks[c]), (normed_one, sends[c]), (normed_one, masks[e]), (cot_rows, sends[c]),
        (normed_one, masks[c]), (cot_rows, masks[c]),
    ]
    blocks = Blocks(moves, place, lhs, order)
    ready_mixed = moves.load(mixed_t, mixed)
    ready_early = [moves.load(early_in.at[i], d_in0.at[i]) for i in range(2)]
    ready_late = [
        moves.load(out_weight, w_out),
        moves.load(att_in, att),
        moves.load(qkv_in, qkv),
        moves.load(qkv_weight, w_qkv),
    ]

    def by_rows(source, right):
        def product(mask, emit):
            lhs_t[...] = blocks.get(source, mask).T
            step = min(512, right.shape[1])

            @pl.loop(0, right.shape[1] // step)
            def _(i):
                at = lanes(i * step, step)
                emit((slice(None), at), dot(lhs_t[...], right[:, at]))

        return product

    def down_product(mask, emit):
        block = blocks.get(cot_rows, mask)
        step = min(256, cols)

        @pl.loop(0, cols // step)
        def _(i):
            at = lanes(i * step, step)
            emit((at, slice(None)), dot(mixed[at], block))

    def out_product(mask, emit):
        at = lanes(place.block(mask) * tile, tile)
        emit((slice(None), slice(None)), dot_rows(att[...], rows_mid[:, at]))

    feed_s = Scatter(moves, place, by_rows(normed_two, feed), f_out0, f_in0, f_out1, f_in1, f_acc, f_pair, spare_feed)
    down_s = Scatter(moves, place, down_product, d_out0, d_in0, d_out1, d_in1, d_acc, d_pair, spare_down)
    down_s.first = dict(enumerate(ready_early))
    qkv_s = Scatter(moves, place, by_rows(normed_one, dqkv), q_out0, q_in0, q_out1, q_in1, q_acc, q_pair, spare_qkv)
    out_s = Scatter(moves, place, out_product, o_out0, o_in0, o_out1, o_in1, o_acc, o_pair, spare_out)

    d = gain_q.shape[1]
    gain_m[...] = jnp.zeros_like(gain_m)
    gain_a[...] = jnp.zeros_like(gain_a)
    gain_h[...] = jnp.zeros_like(gain_h)

    twos = [None, None]

    def collect_part(h):
        at = pl.ds(h * rows // 2, rows // 2)
        return Collect(
            moves, place, lambda j, t: part_two.at[place.rows_of[j] + t, at], part.at[:, at], first.at[:, at],
            ctx_in.at[:, at], pair_in.at[at], sending.at[:, at], True,
        )

    def back_two(h):
        def body(there, at):
            x = hidden_out[at]
            g = cot[at].astype(F32) + norm_back(twos[h].total(there), x, gain_mlp[...], gain_m)
            hidden_out[at] = x + collect_hidden.two(0, at)
            grad_in[at] = g
            own[at] = g.astype(BF16)

        return body

    def back_one(at):
        grad_in[at] += norm_back(collect_one.total(at), own[at].astype(F32), gain_attn[...], gain_a)

    def end_hidden(at):
        hidden_out[at] += ctx_h[1, at].astype(F32) + pair_h[at].astype(F32)

    tree_waits = []

    def climb():
        k = len(tree_waits)
        if k == 1:
            tree_waits[0]()
            tree[1] = tree[0] + tree_in[0]
        if k > 1:
            for wait in tree_waits[-1]:
                wait()
            at = 1 + 4 * (k - 2)
            tree[k] = (tree_in[at] + tree_in[at + 1]) + (tree_in[at + 2] + tree_in[at + 3])
        if k == 0:
            tree_waits.append(moves.swap(tree.at[0], tree_in.at[0], tree_in.at[0], place.sibling))
        elif k < 3:
            mine, others = team(k)
            slots = 1 + 4 * (k - 1)
            tree_in[slots + mine] = tree[k]
            tree_waits.append(
                [
                    moves.swap(tree.at[k], tree_in.at[slots + mine], tree_in.at[slots + index], device)
                    for index, device in others
                ]
            )

    def team(k):
        if k == 1:
            return place.rows_of[0] // 2, [(place.rows_of[j] // 2, place.chips[j]) for j in (3, 2, 1)]

        def index(mask):
            f = place.block(mask)
            return (f // high) % 2 * 2 + f % 2

        return index(0), [(index(m), place.along(m)) for m in (high | low, high, low)]

    finals = []

    def pair_final(scatter, other):
        scatter.take_high(1)
        finals.append(moves.swap(scatter.acc_pair, other, other, place.chips[2]))

    def own_final(scatter, mine):
        scatter.take_high(0)
        moves.store(scatter.acc, mine)

    def mates_final(scatter, slot, piece, spare, other):
        scatter.take_high(slot)
        for j in (3, 2) if slot else (1,):
            out = spare(j)
            out[...] = piece(slot, place.at[j][1]).astype(BF16)
            finals.append(moves.swap(out, other.at[j - 1], other.at[j - 1], place.chips[j]))

    def qkv_piece(slot, c):
        return (q_pair if slot else q_acc)[lanes(c * half, half)]

    def out_piece(slot, c):
        return (o_pair if slot else o_acc)[:, lanes(c * half, half)]

    def qkv_spare(j):
        return q_in0.at[j, pl.ds(0, half)]

    def out_spare(j):
        return o_in0.at[j, :, pl.ds(0, half)]

    ready_mixed()
    down_s.take(b)
    twos[0] = collect_part(0)
    down_s.send(e)
    for wait in ready_feed:
        wait()
    twos[0].to_ctx()
    collect_hidden = Collect(
        moves, place, lambda j, t: part_hidden.at[place.rows_of[j] + t], part.at[pl.ds(4, 4)],
        first_h, ctx_h, pair_h, sending_h, True,
    )
    twos[1] = collect_part(1)
    down_s.take(a)
    down_s.relay(b)
    feed_s.send(a)
    collect_hidden.fold()
    down_s.take(e)
    twos[1].to_ctx()
    twos[0].to_pair()
    feed_s.send(b)
    twos[1].to_pair()
    twos[0].finish()
    ready_mid()
    half_loop(0, rows // 2, back_two(0))
    spread_0 = Spread(moves, place, own.at[pl.ds(0 * rows // 2, rows // 2)], rows_mid, 0, 2)
    down_s.relay(a)
    twos[1].finish()
    half_loop(1, rows // 2, back_two(1))
    spread_1 = Spread(moves, place, own.at[pl.ds(1 * rows // 2, rows // 2)], rows_mid, 1, 2)
    feed_s.take(a)
    spread_0.from_pair()
    spread_0.from_ctx()
    for wait in ready_late:
        wait()
    spread_1.from_ctx()
    spread_1.from_pair()
    pair_final(down_s, down_other)
    spread_0.from_both()
    feed_s.send(e)
    spread_1.from_both()
    feed_s.take(b)
    collect_hidden.post_ctx()
    spread_1.finish()
    spread_0.finish()
    ready_hidden = moves.load(hidden, own)
    out_s.send(a)
    @pl.loop(0, 4)
    def _(i):
        at = lanes(i * 2 * rows, 2 * rows)
        datt[at] = dot_cols(rows_mid[at], w_out[...]).astype(BF16)

    out_s.send(b)
    feed_s.relay(a)
    @pl.loop(0, 2)
    def _(s):
        attend_back_one(groups, s, qkv, att, datt, starts, cos, sin, gain_q, gain_k, dqkv, gain_h)

    @pl.loop(0, width // tile)
    def _(i):
        at = lanes(i * tile, tile)
        part[:, :, at] = dot_cols(dqkv[...], w_qkv[at]).astype(BF16).reshape(8, rows, tile)

    feed_s.take(e)
    collect_hidden.post_pair()
    collect_one = Collect(
        moves, place, lambda j, t: part.at[place.rows_of[j] + t], None, first, ctx_in, pair_in, sending, False
    )
    qkv_s.send(a)
    collect_one.to_ctx()
    out_s.send(e)
    out_s.send(c)
    out_s.take(b)
    qkv_s.send(b)
    feed_s.relay(b)
    out_s.take(c)
    qkv_s.take(a)
    feed_s.send(c)
    out_s.relay(b)
    out_s.take(a)
    collect_one.to_pair()
    qkv_s.relay(a)
    qkv_s.send(e)
    collect_hidden.came()
    row_loop(rows, end_hidden)
    out_s.take(e)
    qkv_s.take(b)
    feed_s.take(c)
    own_final(feed_s, feed_own)
    pair_final(feed_s, feed_other)
    collect_one.finish()
    qkv_s.send(c)
    qkv_s.take(e)
    down_s.send(c)
    ready_hidden()
    row_loop(rows, back_one)
    tree[0, :, 0:width] = jnp.sum(gain_a[...], axis=0, keepdims=True)
    tree[0, :, width : 2 * width] = jnp.sum(gain_m[...], axis=0, keepdims=True)
    tree[0, :, 2 * width : 2 * width + d] = jnp.sum(gain_h[0], axis=0, keepdims=True)
    tree[0, :, 2 * width + d : 2 * width + 2 * d] = jnp.sum(gain_h[1], axis=0, keepdims=True)
    climb()
    climb()
    qkv_s.relay(b)
    qkv_s.take(c)
    mates_final(qkv_s, 0, qkv_piece, qkv_spare, qkv_other)
    qkv_own[...] = qkv_piece(0, place.c)
    mates_final(out_s, 1, out_piece, out_spare, out_other)
    climb()
    out_s.relay(a)
    mates_final(qkv_s, 1, qkv_piece, qkv_spare, qkv_other)
    mates_final(out_s, 0, out_piece, out_spare, out_other)
    out_own[...] = out_piece(0, place.c)
    down_s.take(c)
    own_final(down_s, down_own)
    climb()
    gains[...] = tree[3]
    for scatter in (feed_s, down_s, qkv_s, out_s):
        scatter.close()
    for wait in finals:
        wait()
    moves.close()


def join_kernel(
    feed_own, feed_other, down_own, down_other, qkv_own, qkv_other, out_own, out_other, grad_in, hidden, gains,
    g_query, g_key, g_value, g_out, g_gate, g_up, g_down, g_in, h_out, gain_a, gain_m, gain_q, gain_k,
):
    c = lax.axis_index("ctx")
    pair = (lax.axis_index("fsdp") // PAIR) % 2
    cols, n_q = down_own.shape[0], out_own.shape[0]
    n_kv = (qkv_own.shape[1] - n_q) // 2

    def lanes(start, size):
        return pl.ds(pl.multiple_of(start, size), size)

    mine, theirs = lanes(pair * cols, cols), lanes((1 - pair) * cols, cols)
    g_gate[:, mine] = feed_own[:, :cols]
    g_up[:, mine] = feed_own[:, cols:]
    g_down[mine] = down_own[...]
    g_gate[:, theirs] = feed_other[:, :cols].astype(F32)
    g_up[:, theirs] = feed_other[:, cols:].astype(F32)
    g_down[theirs] = down_other[...].astype(F32)
    chunks = [c * 2 + pair, (1 - c) * 2 + pair, c * 2 + 1 - pair, (1 - c) * 2 + 1 - pair]
    for j, chunk in enumerate(chunks):
        qkv = qkv_own[...] if j == 0 else qkv_other[j - 1].astype(F32)
        g_query[:, lanes(chunk * n_q, n_q)] = qkv[:, :n_q]
        g_key[:, lanes(chunk * n_kv, n_kv)] = qkv[:, n_q : n_q + n_kv]
        g_value[:, lanes(chunk * n_kv, n_kv)] = qkv[:, n_q + n_kv :]
        g_out[lanes(chunk * n_q, n_q)] = out_own[...] if j == 0 else out_other[j - 1].astype(F32)
    g_in[...] = grad_in[...]
    h_out[...] = hidden[...]
    width, d = gain_a.shape[1], gain_q.shape[1]
    gain_a[...] = gains[:, :width]
    gain_m[...] = gains[:, width : 2 * width]
    gain_q[...] = gains[:, 2 * width : 2 * width + d]
    gain_k[...] = gains[:, 2 * width + d :]


VMEM_SPEC = pl.BlockSpec(memory_space=pltpu.VMEM)
ANY_SPEC = pl.BlockSpec(memory_space=pl.ANY)


def comm_call(kernel, bits, collective_id, operands, in_specs, outs, out_specs, scratch, nbytes, copies, *more):
    return pl.pallas_call(
        functools.partial(kernel, bits, *more),
        out_shape=outs,
        in_specs=in_specs,
        out_specs=out_specs,
        scratch_shapes=[
            *scratch,
            pltpu.SemaphoreType.DMA((copies,)),
            pltpu.SemaphoreType.DMA((copies,)),
            pltpu.SemaphoreType.DMA((96,)),
        ],
        compiler_params=pltpu.CompilerParams(
            collective_id=collective_id, has_side_effects=True, vmem_limit_bytes=61 << 20
        ),
        cost_estimate=pl.CostEstimate(flops=nbytes * 20, bytes_accessed=nbytes, transcendentals=0),
        name=kernel.__name__,
    )(*operands)


def build(mesh):
    n = mesh.size
    n_f = mesh.shape["fsdp"]
    spread_bits = [b for b in (1 << i for i in range(n_f.bit_length() - 2, -1, -1)) if b != PAIR]
    all_bits = sorted([*spread_bits, PAIR], reverse=True)

    def swap(v, bit):
        return lax.ppermute(v, AXES, [(i, i ^ bit) for i in range(n)])

    def bit_of(f, b):
        return (f // b) % 2

    def in_order(bit, own, other, axis):
        low = jnp.where(bit == 0, own, other)
        high = jnp.where(bit == 0, other, own)
        return jnp.stack([low, high], axis=axis)

    def pick(v, index, axis):
        return lax.dynamic_index_in_dim(v, index, axis, keepdims=False)

    def scatter(keep, got, f, width):
        v = keep + got.astype(F32)
        have = [b for b in all_bits if b != 1]
        v = v.reshape(*([2] * len(have)), width, v.shape[-1])
        for b in [b for b in reversed(spread_bits) if b != 1]:
            axis = have.index(b)
            bit = bit_of(f, b)
            v = pick(v, bit, axis) + swap(pick(v, 1 - bit, axis).astype(BF16), b * 4).astype(F32)
            have.remove(b)
        return v

    def body(
        hidden_in,
        cotangent,
        segments,
        w_query,
        key_projection_weight,
        value_projection_weight,
        w_out,
        w_gate,
        w_up,
        w_down,
        gain_attn,
        gain_mlp,
        gain_query,
        key_norm_gain,
    ):
        rows, width = hidden_in.shape
        d = gain_query.shape[0]
        length = segments.shape[0]
        f, c = lax.axis_index("fsdp"), lax.axis_index("ctx")
        pair = bit_of(f, PAIR)
        at_rows = w_query.shape[0]
        ff_rows = w_gate.shape[0]
        ff_cols = w_gate.shape[1] // 2
        q_cols, kv_cols = w_query.shape[1] // 4, key_projection_weight.shape[1] // 4
        groups = q_cols // kv_cols

        freqs = THETA ** (-2.0 * jnp.arange(d // 2, dtype=F32) / d)
        angles = jnp.arange(length, dtype=jnp.int32).astype(F32)[:, None] * freqs
        table_cos, table_sin = jnp.cos(angles), jnp.sin(angles)
        table = jnp.concatenate([table_cos, table_cos, -table_sin, table_sin], axis=-1)

        n_rows = 8 * rows
        all_rows = jax.ShapeDtypeStruct((n_rows, width), BF16)
        own_rows = jax.ShapeDtypeStruct((rows, width), F32)
        gain_rows = jax.ShapeDtypeStruct((8, width), F32)
        block = pltpu.VMEM((rows, width), BF16)
        nbytes = rows * width * 16
        qkv_cols = q_cols + 2 * kv_cols

        def shape(*dims):
            return jax.ShapeDtypeStruct(dims, BF16)

        copies = 160 + 10 * n_f
        natural = at_rows % 128 == 0 and ff_rows % 128 == 0
        out_dims = (q_cols, width) if natural else (width, q_cols)
        down_dims = (ff_cols, width) if natural else (width, ff_cols)
        out_part = (q_cols, 2 * at_rows) if natural else (2 * at_rows, q_cols)
        down_part_dims = (ff_cols, ff_rows) if natural else (ff_rows, ff_cols)
        border = ff_cols - 256 if ff_cols % 256 == 0 and ff_cols > 256 else ff_cols // 2
        feed_spares = []
        for piece in (border, ff_cols - border):
            feed_spares += [shape(4, ff_rows, piece)] * 2
            feed_spares.append(shape(4, piece, ff_rows) if natural else shape(4, ff_rows, piece))
        n_seq = 2 * length
        all_tables = jax.ShapeDtypeStruct((n_seq, d), F32)

        def v(*dims, dtype=BF16):
            return pltpu.VMEM(dims, dtype)

        (
            residual_mid, normed_one, normed_two, grad_rows, qkv, attended, full_qkv, full_out, starts, cos, sin,
            grad_gate, grad_up, mixed_t, norm_two_part, down_part, *_, early_in,
        ) = comm_call(
            forward_kernel, spread_bits, 0,
            (hidden_in, cotangent, gain_attn[None], gain_mlp[None], segments[None], table, gain_query[None],
             key_norm_gain[None], w_query, key_projection_weight, value_projection_weight,
             w_out if natural else w_out.T, w_gate, w_up, w_down if natural else w_down.T),
            [VMEM_SPEC] * 8 + [ANY_SPEC] * 7,
            (own_rows, all_rows, all_rows, all_rows, shape(n_rows, qkv_cols), shape(n_rows, q_cols),
             shape(width, qkv_cols), shape(*out_dims), jax.ShapeDtypeStruct((n_seq, 128), F32), all_tables, all_tables,
             shape(n_rows, ff_cols), shape(n_rows, ff_cols), shape(ff_cols, n_rows), shape(8, rows, width), all_rows,
             shape(4, 2 * at_rows, qkv_cols), shape(4, *out_part), *feed_spares,
             shape(2, *down_part_dims)),
            (VMEM_SPEC, *[ANY_SPEC] * 24),
            [block, block, v(n_rows, width), v(n_rows, width), v(n_rows, width), v(width, qkv_cols), v(*out_dims),
             v(width, ff_cols), v(width, ff_cols), v(*down_dims), v(n_rows, qkv_cols), v(n_rows, q_cols),
             v(8, rows, width), v(n_rows, ff_cols, dtype=F32), v(n_rows, ff_cols, dtype=F32), v(n_rows, ff_cols),
             v(n_rows, ff_cols), v(n_rows, ff_cols), v(ff_cols, n_rows), v(n_seq, 128, dtype=F32),
             v(n_seq, d, dtype=F32), v(n_seq, d, dtype=F32), v(1, length, dtype=jnp.int32), v(2, *down_part_dims),
             *collect_buffers(rows, width)],
            16 * nbytes, copies, groups, natural,
        )
        common = (starts, cos, sin, gain_query[None], key_norm_gain[None])
        backward = one_kernel if natural and len(spread_bits) == 2 else by_steps
        return backward(
            hidden_in, cotangent, residual_mid, gain_attn, gain_mlp, common, norm_two_part, down_part, normed_one,
            normed_two, grad_rows, qkv, attended, full_qkv, full_out, grad_gate, grad_up, mixed_t, early_in,
            (at_rows, ff_rows),
        )

    def one_kernel(
        hidden_in, cotangent, residual_mid, gain_attn, gain_mlp, common, norm_two_part, down_part, normed_one,
        normed_two, grad_rows, qkv, attended, full_qkv, full_out, grad_gate, grad_up, mixed_t, early_in, sizes,
    ):
        rows, width = hidden_in.shape
        cols, n_rows = mixed_t.shape
        (at_rows, ff_rows), q_cols, qkv_cols = sizes, attended.shape[1], qkv.shape[1]
        d = common[-1].shape[1]
        kv_cols = (qkv_cols - q_cols) // 2
        groups = q_cols // kv_cols

        def out(dtype, *dims):
            return jax.ShapeDtypeStruct(dims, dtype)

        def v(*dims, dtype=BF16):
            return pltpu.VMEM(dims, dtype)

        def scatter(*block):
            return [v(2, *block), v(4, *block), v(2, *block), v(2, *block), v(*block, dtype=F32), v(*block)]

        n_gain = 2 * width + 2 * d
        nbytes = n_rows * width * 20
        (
            grad_input, hidden_out, gains, feed_own, feed_other, down_own, down_other, qkv_own, qkv_other, out_own,
            out_other, *_,
        ) = comm_call(
            backward_kernel, spread_bits, 2,
            (cotangent, gain_attn[None], gain_mlp[None], *common, residual_mid, hidden_in, norm_two_part,
             down_part.reshape(8, rows, width), normed_one, normed_two, grad_rows, qkv, attended, full_qkv, full_out,
             grad_gate, grad_up, mixed_t, early_in),
            [VMEM_SPEC] * 8 + [ANY_SPEC] * 15,
            (out(F32, rows, width), out(F32, rows, width), out(F32, 1, n_gain), out(F32, ff_rows, 2 * cols),
             out(BF16, ff_rows, 2 * cols), out(F32, cols, ff_rows), out(BF16, cols, ff_rows),
             out(F32, at_rows, qkv_cols), out(BF16, 3, at_rows, qkv_cols), out(F32, q_cols, at_rows),
             out(BF16, 3, q_cols, at_rows), out(BF16, 4, ff_rows, 2 * cols), out(BF16, 4, cols, ff_rows),
             out(BF16, 4, ff_rows, qkv_cols), out(BF16, 4, q_cols, ff_rows)),
            (VMEM_SPEC, VMEM_SPEC, VMEM_SPEC, ANY_SPEC, ANY_SPEC, ANY_SPEC, ANY_SPEC, VMEM_SPEC, ANY_SPEC, VMEM_SPEC,
             *[ANY_SPEC] * 5),
            [v(rows, width), v(n_rows, width), v(n_rows, 2 * cols), v(cols, n_rows), v(2, n_rows, ff_rows),
             v(ff_rows, n_rows), v(8, rows, width), v(width, qkv_cols), v(q_cols, width), v(n_rows, qkv_cols),
             v(n_rows, q_cols), v(n_rows, q_cols), v(n_rows, qkv_cols),
             *collect_buffers(rows, width), *collect_buffers(rows, width), v(8, width, dtype=F32), v(8, width, dtype=F32), v(2, 8, d, dtype=F32),
             v(4, 1, n_gain, dtype=F32), v(9, 1, n_gain, dtype=F32),
             *scatter(ff_rows, 2 * cols), *scatter(cols, ff_rows), *scatter(ff_rows, qkv_cols),
             *scatter(q_cols, ff_rows)],
            nbytes, 110, groups,
        )
        own_rows = out(F32, rows, width)
        made = (
            out(F32, at_rows, 4 * q_cols), out(F32, at_rows, 4 * kv_cols), out(F32, at_rows, 4 * kv_cols),
            out(F32, 4 * q_cols, at_rows), out(F32, ff_rows, 2 * cols), out(F32, ff_rows, 2 * cols),
            out(F32, 2 * cols, ff_rows), own_rows, own_rows, out(F32, 1, width), out(F32, 1, width), out(F32, 1, d),
            out(F32, 1, d),
        )
        pieces = pl.pallas_call(
            join_kernel,
            out_shape=made,
            compiler_params=pltpu.CompilerParams(vmem_limit_bytes=61 << 20),
            name="join_kernel",
        )(feed_own, feed_other, down_own, down_other, qkv_own, qkv_other, out_own, out_other, grad_input, hidden_out, gains)
        grads, (grad_input, hidden_out), gains = pieces[:7], pieces[7:9], pieces[9:]
        return hidden_out, grad_input, *grads, *(g[0] for g in gains)

    def by_steps(
        hidden_in, cotangent, residual_mid, gain_attn, gain_mlp, common, norm_two_part, down_part, normed_one,
        normed_two, grad_rows, qkv, attended, full_qkv, full_out, grad_gate, grad_up, mixed_t, early_in, sizes,
    ):
        rows, width = hidden_in.shape
        (at_rows, ff_rows), ff_cols, q_cols = sizes, mixed_t.shape[0], attended.shape[1]
        d = common[-1].shape[1]
        kv_cols = (qkv.shape[1] - q_cols) // 2
        groups = q_cols // kv_cols
        natural = full_out.shape[0] != width
        times_t = dot_cols if natural else dot
        f, c = lax.axis_index("fsdp"), lax.axis_index("ctx")
        pair = bit_of(f, PAIR)
        all_rows = jax.ShapeDtypeStruct((8 * rows, width), BF16)
        own_rows = jax.ShapeDtypeStruct((rows, width), F32)
        gain_rows = jax.ShapeDtypeStruct((8, width), F32)
        block = pltpu.VMEM((rows, width), BF16)
        nbytes = rows * width * 16
        grad_mid, gain_mlp_part, grad_mid_rows = comm_call(
            turn_kernel, spread_bits, 2, (norm_two_part.reshape(8, rows, width), residual_mid, cotangent, gain_mlp[None]),
            [ANY_SPEC, VMEM_SPEC, VMEM_SPEC, VMEM_SPEC], (own_rows, gain_rows, all_rows),
            (VMEM_SPEC, VMEM_SPEC, ANY_SPEC),
            [block, pltpu.VMEM((4, rows, width), BF16), *collect_buffers(rows, width)], 2 * nbytes, 40,
        )

        low = bit_of(f, 1)

        def weight_grad(acts, grads):
            split = acts.reshape(acts.shape[0], n_f // 2, 2, width // n_f)
            mine = pick(split, low, 2).reshape(acts.shape[0], -1)
            theirs = pick(split, 1 - low, 2).reshape(acts.shape[0], -1)
            got = swap(dot_rows(theirs, grads).astype(BF16), 4)
            return scatter(dot_rows(mine, grads), got, f, width // n_f)

        def ff_grad(acts, grads):
            v = weight_grad(acts, grads)
            other = swap(pick(v, 1 - pair, 0).astype(BF16), PAIR_BIT).astype(F32)
            return in_order(pair, pick(v, pair, 0), other, 1).reshape(ff_rows, 2 * ff_cols)

        grad_w_gate = ff_grad(normed_two, grad_gate)
        grad_w_up = ff_grad(normed_two, grad_up)
        grad_w_down = ff_grad(grad_rows, mixed_t.T).T

        def attn_grad(acts, grads):
            v = weight_grad(acts, grads)
            v = v.reshape(2, 2, at_rows, v.shape[-1])
            mine = pick(pick(v, pair, 0), c, 0)
            by_ctx = swap(pick(pick(v, pair, 0), 1 - c, 0).astype(BF16), CTX_BIT).astype(F32)
            by_pair = swap(pick(pick(v, 1 - pair, 0), c, 0).astype(BF16), PAIR_BIT).astype(F32)
            by_both = swap(pick(pick(v, 1 - pair, 0), 1 - c, 0).astype(BF16), CTX_BIT | PAIR_BIT).astype(F32)
            near = in_order(pair, mine, by_pair, 1)
            far = in_order(pair, by_ctx, by_both, 1)
            return in_order(c, near, far, 1)

        grad_w_out = attn_grad(grad_mid_rows, attended).reshape(at_rows, 4 * q_cols).T

        datt = times_t(grad_mid_rows, full_out).astype(BF16)
        grad_qkv, head_gains = attend_back(groups, qkv, attended, datt, common)
        norm_one_part = dot_cols(grad_qkv, full_qkv).astype(BF16)
        grad_input, gain_attn_part = comm_call(
            last_kernel, spread_bits, 3, (norm_one_part.reshape(8, rows, width), hidden_in, grad_mid, gain_attn[None]),
            [ANY_SPEC, VMEM_SPEC, VMEM_SPEC, VMEM_SPEC], (own_rows, gain_rows), (VMEM_SPEC, VMEM_SPEC),
            [pltpu.VMEM((4, rows, width), BF16), *collect_buffers(rows, width)], nbytes, 40,
        )
        grad_qkv_w = attn_grad(normed_one, grad_qkv)
        grad_w_query = grad_qkv_w[..., :q_cols].reshape(at_rows, -1)
        grad_w_key = grad_qkv_w[..., q_cols : q_cols + kv_cols].reshape(at_rows, -1)
        grad_w_value = grad_qkv_w[..., q_cols + kv_cols :].reshape(at_rows, -1)

        head_gains = jnp.sum(head_gains, axis=1)
        gains = jnp.concatenate(
            [jnp.sum(gain_attn_part, axis=0), jnp.sum(gain_mlp_part, axis=0), head_gains[0], head_gains[1]]
        ).reshape(-1, d)
        for i in range(n.bit_length() - 1):
            gains = gains + swap(gains, 1 << i)
        gains = gains.reshape(-1)
        teams = sorted(
            sorted(i ^ b ^ p for b in range(4) for p in (0, PAIR_BIT))
            for i in range(0, n, 4)
            if not i & PAIR_BIT
        )
        hidden_out = residual_mid + lax.psum_scatter(
            down_part, AXES, scatter_dimension=0, axis_index_groups=teams, tiled=True
        ).astype(F32)
        return (
            hidden_out,
            grad_input,
            grad_w_query,
            grad_w_key,
            grad_w_value,
            grad_w_out,
            grad_w_gate,
            grad_w_up,
            grad_w_down,
            gains[:width],
            gains[width : 2 * width],
            gains[2 * width : 2 * width + d],
            gains[2 * width + d :],
        )

    return body


def solution(mesh):
    everyone = P(("fsdp", "ctx", "tp"), None)
    attn = P(("fsdp", "ctx"), "tp")
    attn_out = P("tp", ("fsdp", "ctx"))
    ff_in = P("fsdp", ("ctx", "tp"))
    ff_out = P(("ctx", "tp"), "fsdp")
    same = P()
    return jax.shard_map(
        build(mesh),
        mesh=mesh,
        in_specs=(
            everyone, everyone, P("fsdp"), attn, attn, attn, attn_out, ff_in, ff_in, ff_out,
            same, same, same, same,
        ),
        out_specs=(
            everyone, everyone, attn, attn, attn, attn_out, ff_in, ff_in, ff_out,
            same, same, same, same,
        ),
        check_vma=False,
    )
```

```python
import functools

import jax
import jax.numpy as jnp
import numpy as np
from jax import lax
from jax.experimental import pallas as pl
from jax.experimental.pallas import tpu as pltpu
from jax.sharding import PartitionSpec as P

EPS = 1e-06
THETA = 1000000.0
AXES = ("fsdp", "ctx", "tp")
MESH = pl.DeviceIdType.MESH
BF16 = jnp.bfloat16
F32 = jnp.float32
TP_BIT, CTX_BIT = 1, 2
PAIR = 2
PAIR_BIT = PAIR * 4


def dot_rows(left, right):
    return lax.dot_general(left, right, (((0,), (0,)), ((), ())), preferred_element_type=F32)


def dot_cols(left, right):
    return lax.dot_general(left, right, (((1,), (1,)), ((), ())), preferred_element_type=F32)


def dot(left, right):
    return lax.dot_general(left, right, (((1,), (0,)), ((), ())), preferred_element_type=F32)


def remote(src, dst, send, recv, device):
    return pltpu.make_async_remote_copy(
        src_ref=src, dst_ref=dst, send_sem=send, recv_sem=recv, device_id=device, device_id_type=MESH
    )


class Moves:
    def __init__(self, send, recv, local):
        self.send, self.recv, self.local = send, recv, local
        self.sent, self.loads = 0, 0
        self.open = []

    def swap(self, src, there, here, device, open_=None):
        k = self.sent
        self.sent += 1
        copy = remote(src, there, self.send.at[k], self.recv.at[k], device)
        copy.start()
        (self.open if open_ is None else open_).append(copy.wait_send)
        return remote(src, here, self.send.at[k], self.recv.at[k], device).wait_recv

    def load(self, src, dst):
        k = self.loads
        self.loads += 1
        copy = pltpu.make_async_copy(src, dst, self.local.at[k])
        copy.start()
        return copy.wait

    def store(self, src, dst):
        self.open.append(self.load(src, dst))

    def close(self):
        for wait in self.open:
            wait()


class Place:
    def __init__(self, bits):
        self.bits = bits
        f, c, t = lax.axis_index("fsdp"), lax.axis_index("ctx"), lax.axis_index("tp")
        self.f, self.c, self.t = f, c, t
        self.pair = (f // PAIR) % 2
        far_f = self.block(PAIR)
        fs, cs = [f, f, far_f, far_f], [c, 1 - c, c, 1 - c]
        pairs = [self.pair, self.pair, 1 - self.pair, 1 - self.pair]
        self.at = [(fs[j], cs[j], pairs[j]) for j in range(4)]
        self.rows_of = [pairs[j] * 4 + cs[j] * 2 for j in range(4)]
        self.chunk_of = [cs[j] * 2 + pairs[j] for j in range(4)]
        self.relay = len(bits) == 2
        self.across_mask = bits[0] | PAIR
        self.inner = (f // bits[0]) % 2 != self.pair
        self.chips = [None, {"ctx": 1 - c}, {"fsdp": far_f}, {"fsdp": far_f, "ctx": 1 - c}]
        self.sibling = {"tp": 1 - t}

    def block(self, mask):
        out = self.f
        for i in range(mask.bit_length()):
            b = 1 << i
            if mask & b:
                out = out + b - 2 * b * ((self.f // b) % 2)
        return out

    def along(self, bit):
        return {"fsdp": self.block(bit)}

    def greet(self):
        barrier = pltpu.get_barrier_semaphore()
        devices = [*self.chips[1:], self.sibling, *[self.along(b) for b in self.bits]]
        if self.relay:
            devices += [self.along(self.across_mask), self.along(self.bits[0] | self.bits[1])]
        for device in devices:
            pl.semaphore_signal(barrier, inc=1, device_id=device, device_id_type=MESH)
        pl.semaphore_wait(barrier, len(devices))


class Cross:
    def __init__(self, moves, place, src, here, came_in, across_to, came_out, pair_to, held=None):
        self.place, self.here, self.held = place, here, held
        self.came_in, self.came_out = came_in, came_out
        k = moves.sent
        moves.sent += 4
        pair, across = place.chips[2], place.along(place.across_mask)

        def copy(i, source, to, device):
            return remote(source, to, moves.send.at[k + i], moves.recv.at[k + i], device)

        self.hand = copy(0, src, came_in, pair)
        self.own = copy(1, src, came_out, across)
        self.on = copy(2, came_in if held is None else held, across_to, across)
        self.back = copy(3, came_out, pair_to, pair)
        self.came = [copy(0, came_in, came_in, pair), copy(1, came_out, came_out, across)]
        self.landed = [copy(2, here, here, across), copy(3, here, here, pair)]
        moves.open.append(self.left)

        @pl.when(place.inner)
        def _():
            self.own.start()
            if held is not None:
                self.on.start()

        @pl.when(jnp.logical_not(place.inner))
        def _():
            if held is None:
                self.hand.start()

    def relay(self):
        @pl.when(self.place.inner)
        def _():
            if self.held is None:
                self.came[0].wait_recv()
                self.on.start()
            self.came[1].wait_recv()
            self.back.start()

    def arrive(self):
        @pl.when(self.place.inner)
        def _():
            self.landed[0].wait_recv()

        @pl.when(jnp.logical_not(self.place.inner))
        def _():
            self.landed[1].wait_recv()

    def left(self):
        @pl.when(self.place.inner)
        def _():
            self.own.wait_send()
            self.on.wait_send()
            self.back.wait_send()

        @pl.when(jnp.logical_not(self.place.inner))
        def _():
            if self.held is None:
                self.hand.wait_send()


class Spread:
    def __init__(self, moves, place, own, out, part=0, parts=1):
        self.moves, self.place, self.out = moves, place, out
        self.rows = own.shape[0]
        self.stride, self.offset = self.rows * parts, self.rows * part
        self.open = []
        mine = self.at(0, place.t)
        self.here = moves.load(own, mine)
        self.pair = moves.swap(own, mine, self.at(2, place.t), place.chips[2], self.open)
        self.ctx = moves.swap(own, mine, self.at(1, place.t), place.chips[1], self.open)
        self.beside = [moves.swap(own, mine, self.at(0, 1 - place.t), place.sibling, self.open)]

    def at(self, j, t):
        start = (self.place.rows_of[j] + t) * self.stride + self.offset
        return self.out.at[pl.ds(pl.multiple_of(start, self.rows), self.rows)]

    def hand(self, j):
        block = self.at(j, self.place.t)
        self.beside.append(
            self.moves.swap(block, block, self.at(j, 1 - self.place.t), self.place.sibling, self.open)
        )

    def from_pair(self):
        self.pair()
        block = self.at(2, self.place.t)
        self.both = self.moves.swap(block, block, self.at(3, self.place.t), self.place.chips[1], self.open)
        self.hand(2)

    def from_ctx(self):
        self.ctx()
        self.hand(1)

    def from_both(self):
        self.both()
        self.hand(3)

    def finish(self):
        self.here()
        for wait in (*self.beside, *self.open):
            wait()


class Collect:
    def __init__(self, moves, place, part, held, first, ctx_in, pair_in, sending, load):
        self.moves, self.place = moves, place
        self.first, self.ctx_in, self.pair_in, self.sending = first, ctx_in, pair_in, sending
        t = place.t
        self.hands, self.loads, self.open = {}, {}, []
        for j in (3, 1, 2, 0):
            self.hands[j] = moves.swap(part(j, 1 - t), first.at[j], first.at[j], place.sibling, self.open)
            if load:
                self.loads[j] = moves.load(part(j, t), held.at[j])
        self.held = (lambda j: held.at[j]) if load else (lambda j: part(j, t))

    def two(self, j, at):
        return self.held(j)[at].astype(F32) + self.first[j, at].astype(F32)

    def ready(self, j):
        self.hands[j]()
        if j in self.loads:
            self.loads[j]()

    def to_ctx(self):
        self.waits = {}
        for j, slot in ((3, 0), (1, 1)):
            self.ready(j)

            def body(at):
                self.sending[slot, at] = self.two(j, at).astype(BF16)

            row_loop(self.sending.shape[1], body)
            self.waits[j] = self.moves.swap(
                self.sending.at[slot], self.ctx_in.at[slot], self.ctx_in.at[slot], self.place.chips[1], self.open
            )

    def to_pair(self):
        self.ready(2)
        self.waits[3]()

        def body(at):
            self.sending[2, at] = (self.two(2, at) + self.ctx_in[0, at].astype(F32)).astype(BF16)

        row_loop(self.sending.shape[1], body)
        self.waits[2] = self.moves.swap(
            self.sending.at[2], self.pair_in, self.pair_in, self.place.chips[2], self.open
        )

    def fold(self):
        for j, slot in ((3, 0), (1, 1), (2, 2)):
            self.ready(j)

            def body(at):
                self.sending[slot, at] = self.two(j, at).astype(BF16)

            row_loop(self.sending.shape[1], body)
        self.ready(0)

    def post_ctx(self):
        self.waits = {}
        for j, slot in ((3, 0), (1, 1)):
            self.waits[j] = self.moves.swap(
                self.sending.at[slot], self.ctx_in.at[slot], self.ctx_in.at[slot], self.place.chips[1], self.open
            )

    def post_pair(self):
        self.waits[3]()

        def body(at):
            self.sending[2, at] = (self.sending[2, at].astype(F32) + self.ctx_in[0, at].astype(F32)).astype(BF16)

        row_loop(self.sending.shape[1], body)
        self.waits[2] = self.moves.swap(
            self.sending.at[2], self.pair_in, self.pair_in, self.place.chips[2], self.open
        )

    def came(self):
        for wait in (self.waits[1], self.waits[2], *self.open):
            wait()

    def finish(self):
        self.ready(0)
        self.waits[1]()
        self.waits[2]()
        for wait in self.open:
            wait()

    def total(self, at):
        return self.two(0, at) + (self.ctx_in[1, at].astype(F32) + self.pair_in[at].astype(F32))


def collect_buffers(rows, width):
    return [
        pltpu.VMEM((4, rows, width), BF16),
        pltpu.VMEM((2, rows, width), BF16),
        pltpu.VMEM((rows, width), BF16),
        pltpu.VMEM((3, rows, width), BF16),
    ]


def row_loop(rows, body):
    step = 16

    @pl.loop(0, rows // step)
    def _(i):
        body(pl.ds(pl.multiple_of(i * step, step), step))


def half_loop(part, rows, body):
    step = 16

    @pl.loop(0, rows // step)
    def _(i):
        body(
            pl.ds(pl.multiple_of(i * step, step), step),
            pl.ds(pl.multiple_of(part * rows + i * step, step), step),
        )


def unit_and_scale(x):
    scale = lax.rsqrt(jnp.mean(x * x, axis=-1, keepdims=True) + EPS)
    return x * scale, scale


class Gather:
    def __init__(self, moves, place, block, spare):
        self.moves, self.place, self.block, self.spare = moves, place, block, spare
        self.waits, self.crosses = {}, {}

    def forward(self, mask, src=None, held=None):
        done = [i for i, b in enumerate(self.place.bits) if mask & b]
        here = self.block(self.place.block(mask))
        for b in self.place.bits[max(done, default=-1) + 1 :]:
            if self.place.relay and b == self.place.bits[0]:
                far = self.place.across_mask
                slot = 0 if mask == 0 else 2
                self.crosses[mask] = Cross(
                    self.moves, self.place, here if src is None else src, self.block(self.place.block(mask | b)),
                    self.spare.at[slot], self.block(self.place.block(mask ^ PAIR)),
                    self.spare.at[slot + 1], self.block(self.place.block(mask ^ far)), held,
                )
                self.waits[mask | b] = self.crosses[mask].arrive
                continue
            self.waits[mask | b] = self.moves.swap(
                here if src is None else src, here, self.block(self.place.block(mask | b)), self.place.along(b)
            )

    def masks(self, stage):
        out = [0, PAIR]
        for b in self.place.bits[:stage]:
            out += [m | b for m in out]
        return [m | self.place.bits[stage] for m in out]

    def relay(self, m):
        if self.place.relay:
            self.crosses[m].relay()

    def hop(self, m):
        if self.place.relay:
            self.pass_on(m | self.place.bits[0])
        elif m == PAIR:
            self.middle()

    def pass_on(self, m, held=None):
        self.waits.pop(m)()
        self.forward(m, None, held)

    def middle(self):
        for stage in range(len(self.place.bits) - 1):
            for m in self.masks(stage):
                if m in self.waits:
                    self.pass_on(m)

    def finish(self):
        for wait in self.waits.values():
            wait()


def head_unit(x):
    scale = lax.rsqrt(jnp.mean(x * x, axis=-1, keepdims=True) + EPS)
    return x * scale, scale


def rot(a, cos, sin):
    return a * cos + pltpu.roll(a, a.shape[-1] // 2, 1) * sin


def rot_back(b, cos, sin):
    return b * cos - pltpu.roll(b, b.shape[-1] // 2, 1) * sin


def allowed_keys(start):
    length = start.shape[0]
    row = lax.broadcasted_iota(jnp.int32, (length, length), 0)
    col = lax.broadcasted_iota(jnp.int32, (length, length), 1)
    return (col.astype(F32) >= start) & (row >= col)


def soft_of(scores):
    peak = jnp.max(scores, axis=-1, keepdims=True)
    lse = peak + jnp.log(jnp.sum(jnp.exp(scores - peak), axis=-1, keepdims=True))
    return jnp.exp(scores - lse)


def attend_one(groups, s, qkv, starts, cos_ref, sin_ref, gain_q, gain_k, out):
    d = gain_q.shape[-1]
    length = cos_ref.shape[0] // 2
    rows = pl.ds(pl.multiple_of(s * length, length), length)
    cos, sin = cos_ref[rows], sin_ref[rows]
    allowed = allowed_keys(starts[rows, 0:1])
    unit_k, _ = head_unit(qkv[rows, groups * d : (groups + 1) * d].astype(F32))
    key = rot(unit_k * gain_k[...], cos, sin).astype(BF16)
    value = qkv[rows, (groups + 1) * d : (groups + 2) * d]
    for g in range(groups):
        unit_q, _ = head_unit(qkv[rows, g * d : (g + 1) * d].astype(F32))
        query = rot(unit_q * gain_q[...], cos, sin).astype(BF16)
        scores = jnp.where(allowed, dot_cols(query, key) * d**-0.5, -jnp.inf)
        soft = soft_of(scores).astype(BF16)
        out[rows, g * d : (g + 1) * d] = dot(soft, value).astype(BF16)


def through_norm(b, unit, scale, gain):
    e = b * gain
    return scale * (e - unit * jnp.mean(e * unit, axis=-1, keepdims=True))


def attend_back_one(
    groups, s, qkv, att, datt, starts, cos_ref, sin_ref, gain_q, gain_k, grad, gains
):
    d = gain_q.shape[-1]
    length = cos_ref.shape[0] // 2
    rows = pl.ds(pl.multiple_of(s * length, length), length)
    cos, sin = cos_ref[rows], sin_ref[rows]
    scale = d**-0.5
    allowed = allowed_keys(starts[rows, 0:1])
    at_k, at_v = slice(groups * d, (groups + 1) * d), slice((groups + 1) * d, (groups + 2) * d)
    unit_k, scale_k = head_unit(qkv[rows, at_k].astype(F32))
    key = rot(unit_k * gain_k[...], cos, sin).astype(BF16)
    value = qkv[rows, at_v]
    key_grad = jnp.zeros(unit_k.shape, F32)
    value_grad = jnp.zeros(unit_k.shape, F32)
    for g in range(groups):
        at = slice(g * d, (g + 1) * d)
        unit_q, scale_q = head_unit(qkv[rows, at].astype(F32))
        query = rot(unit_q * gain_q[...], cos, sin).astype(BF16)
        scores = jnp.where(allowed, dot_cols(query, key) * scale, -jnp.inf)
        soft = soft_of(scores)
        up = datt[rows, at]
        delta = jnp.sum(up.astype(F32) * att[rows, at].astype(F32), axis=-1, keepdims=True)
        ds = (soft * (dot_cols(up, value) - delta) * scale).astype(BF16)
        value_grad += dot_rows(soft.astype(BF16), up)
        key_grad += dot_rows(ds, query)
        b = rot_back(dot(ds, key), cos, sin)
        gains[0] += jnp.sum((b * unit_q).reshape(-1, 8, d), axis=0)
        grad[rows, at] = through_norm(b, unit_q, scale_q, gain_q[...]).astype(BF16)
    b = rot_back(key_grad, cos, sin)
    gains[1] += jnp.sum((b * unit_k).reshape(-1, 8, d), axis=0)
    grad[rows, at_k] = through_norm(b, unit_k, scale_k, gain_k[...]).astype(BF16)
    grad[rows, at_v] = value_grad.astype(BF16)


def attend_back_kernel(
    groups, qkv, att, datt, starts, cos, sin, gain_q, gain_k, grad, gains
):
    gains[...] = jnp.zeros_like(gains)

    @pl.loop(0, 2)
    def _(s):
        attend_back_one(groups, s, qkv, att, datt, starts, cos, sin, gain_q, gain_k, grad, gains)


def attend_back(groups, qkv, att, datt, common):
    n_rows, width = qkv.shape
    d = width // (groups + 2)
    length = n_rows // 2
    return pl.pallas_call(
        functools.partial(attend_back_kernel, groups),
        out_shape=(jax.ShapeDtypeStruct(qkv.shape, BF16), jax.ShapeDtypeStruct((2, 8, d), F32)),
        compiler_params=pltpu.CompilerParams(vmem_limit_bytes=40 << 20),
        cost_estimate=pl.CostEstimate(
            flops=n_rows * groups * length * (10 * d + 30),
            bytes_accessed=n_rows * width * 8,
            transcendentals=n_rows * groups * length * 2,
        ),
        name="attend_back",
    )(qkv, att, datt, *common)


def forward_kernel(
    bits, groups, natural,
    hidden, cot, gain_attn, gain_mlp, seg, table, gain_q, gain_k, wq, wk, wv, wo, wg, wu, wd,
    mid, normed_one, normed_two, cot_out, qkv_out, att_out, qkv_weight, out_weight, starts_out, cos_out, sin_out,
    grad_gate_out, grad_up_out, mixed_out, part_out, down_out, spare_qkv, spare_out,
    spare_gate_a, spare_up_a, spare_down_a, spare_gate_b, spare_up_b, spare_down_b, early_in,
    own_one, own_two, rows_one, rows_two, rows_cot, w_qkv, w_out, w_gate, w_up, w_down, qkv, att, part,
    gate, up, grad_gate, grad_up, mixed, mixed_t, starts, cos, sin, seg_in, early, first, ctx_in, pair_in, sending,
    send, recv, local,
):
    place = Place(bits)
    moves = Moves(send, recv, local)
    rows, width = hidden.shape
    at_rows, ff_rows, ff_cols = wq.shape[0], wg.shape[0], wg.shape[1] // 2
    q_cols, kv_cols = wq.shape[1] // 4, wk.shape[1] // 4
    n_rows, length = rows_one.shape[0], seg.shape[1]

    def lanes(start, size):
        return pl.ds(pl.multiple_of(start, size), size)

    def qkv_rows(f, c=None):
        if c is None:
            return lanes(f * 2 * at_rows, 2 * at_rows)
        return lanes((f * 2 + c) * at_rows, at_rows)

    place.greet()

    def out_block(f, c=None):
        return w_out.at[:, qkv_rows(f, c)] if natural else w_out.at[qkv_rows(f, c)]

    def out_chunk(j):
        at = lanes(place.chunk_of[j] * q_cols, q_cols)
        return wo.at[at] if natural else wo.at[:, at]

    pieces = (
        (wq, q_cols, pl.ds(0, q_cols)),
        (wk, kv_cols, pl.ds(q_cols, kv_cols)),
        (wv, kv_cols, pl.ds(q_cols + kv_cols, kv_cols)),
    )
    f0, c0, _ = place.at[0]
    qkv_in, out_in = {}, {}

    border = ff_cols - 256 if ff_cols % 256 == 0 and ff_cols > 256 else ff_cols // 2
    piece_a, piece_b = pl.ds(0, border), pl.ds(border, ff_cols - border)

    def feed_weight(weight, piece, source, spare, by_rows):
        start, size = (0, border) if piece is piece_a else (border, ff_cols - border)

        def block(f):
            at = lanes(f * ff_rows, ff_rows)
            return weight.at[at, piece] if by_rows else weight.at[piece, at]

        def half(which):
            at = pl.ds(pl.multiple_of(which * ff_cols + start, 128), size)
            return source.at[:, at] if by_rows else source.at[at]

        return Gather(moves, place, block, spare), half(place.pair), half(1 - place.pair)

    feed = []
    for piece, spares in ((piece_a, (spare_gate_a, spare_up_a, spare_down_a)), (piece_b, (spare_gate_b, spare_up_b, spare_down_b))):
        feed.append(feed_weight(w_gate, piece, wg, spares[0], True))
        feed.append(feed_weight(w_up, piece, wu, spares[1], True))
        feed.append(feed_weight(w_down, piece, wd, spares[2], not natural))
    own_feed = [moves.load(own, gather.block(place.f)) for gather, own, _ in feed]

    def swap_pair(i):
        gather, _, other = feed[i]
        gather.waits[PAIR] = moves.swap(
            other, gather.block(place.f), gather.block(place.block(PAIR)), place.along(PAIR)
        )

    early_waits = []

    def send_early(i):
        if place.relay:
            high, low = bits
            mask = (high, high | PAIR)[i] | low
            at = lanes(place.block(mask) * ff_rows, ff_rows)
            early[i] = dot(mixed_t[...], rows_cot[:, at]).astype(BF16)
            early_waits.append(moves.swap(early.at[i], early_in.at[i], early_in.at[i], place.along(low)))

    step = 2 * rows
    wide = min(256, w_qkv.shape[1])
    qkv_gather = Gather(moves, place, lambda f: w_qkv.at[qkv_rows(f)], spare_qkv)
    out_gather = Gather(moves, place, out_block, spare_out)

    def norm_one(at):
        unit, _ = unit_and_scale(hidden[at].astype(F32))
        own_one[at] = (unit * gain_attn[...]).astype(BF16)

    collects = [None, None]

    def collect_part(h):
        at = pl.ds(h * rows // 2, rows // 2)
        return Collect(
            moves, place, lambda j, t: part.at[place.rows_of[j] + t, at], None, first.at[:, at], ctx_in.at[:, at],
            pair_in.at[at], sending.at[:, at], False,
        )

    def norm_two(h):
        def body(there, at):
            x = hidden[at].astype(F32) + collects[h].total(there)
            mid[at] = x
            unit, _ = unit_and_scale(x)
            own_two[at] = (unit * gain_mlp[...]).astype(BF16)

        return body

    def columns_of(weight, at):
        return (dot, weight[:, at]) if natural else (dot_cols, weight[at])

    def gate_part(piece):
        @pl.loop(0, n_rows // step)
        def _(i):
            at = lanes(i * step, step)
            gate[at, piece] = dot(rows_two[at], w_gate[:, piece])

    def up_part(piece):
        @pl.loop(0, n_rows // step)
        def _(i):
            at = lanes(i * step, step)
            u = dot(rows_two[at], w_up[:, piece])
            up[at, piece] = u
            g = gate[at, piece]
            mix = g * jax.nn.sigmoid(g) * u
            mixed[at, piece] = mix.astype(BF16)
            mixed_t[piece, at] = mix.T.astype(BF16)

    def back_part(piece):
        @pl.loop(0, n_rows // step)
        def _(i):
            at = lanes(i * step, step)
            m = dot_cols(rows_cot[at], w_down[piece]) if natural else dot(rows_cot[at], w_down[:, piece])
            g = gate[at, piece]
            s = jax.nn.sigmoid(g)
            grad_gate[at, piece] = (m * up[at, piece] * s * (1.0 + g * (1.0 - s))).astype(BF16)
            grad_up[at, piece] = (m * (g * s)).astype(BF16)

    def grad_part(piece, last):
        for half in range(2):

            @pl.loop(0, width // 512)
            def _(i):
                at = lanes(half * (width // 2) + i * 256, 256)
                both = dot_cols(grad_gate[:, piece], w_gate[at, piece]) + dot_cols(grad_up[:, piece], w_up[at, piece])
                both = both.reshape(8, rows, 256)
                if last:
                    both = both + part[:, :, at].astype(F32)
                part[:, :, at] = both.astype(BF16)

            if last:
                at = pl.ds(half * (width // 2), width // 2)
                moves.store(part.at[:, :, at], part_out.at[:, :, at])

    def down_part(piece, last):
        @pl.loop(0, width // 256)
        def _(i):
            at = lanes(i * 256, 256)
            if natural:
                term = dot(mixed[:, piece], w_down[piece, at])
            else:
                term = dot_cols(mixed[:, piece], w_down[at, piece])
            if last:
                term = term + rows_one[:, at].astype(F32)
            rows_one[:, at] = term.astype(BF16)

        if last:
            moves.store(rows_one, down_out)

    for j in (3, 2, 1):
        fj, cj, _ = place.at[j]
        out_in[j] = moves.swap(out_chunk(j), out_block(f0, c0), out_block(fj, cj), place.chips[j])
    out_in[0] = moves.load(out_chunk(0), out_block(f0, c0))
    feed[1][0].forward(0, feed[1][1])
    for j in (1, 3, 2):
        fj, cj, _ = place.at[j]
        qkv_in[j] = [
            moves.swap(
                w.at[:, lanes(place.chunk_of[j] * size, size)],
                w_qkv.at[qkv_rows(f0, c0), to],
                w_qkv.at[qkv_rows(fj, cj), to],
                place.chips[j],
            )
            for w, size, to in pieces
        ]
    qkv_in[0] = [
        moves.load(w.at[:, lanes(place.chunk_of[0] * size, size)], w_qkv.at[qkv_rows(f0, c0), to])
        for w, size, to in pieces
    ]
    row_loop(rows, norm_one)
    spread_one = Spread(moves, place, own_one, rows_one)
    for wait in (*qkv_in[0], *qkv_in[1]):
        wait()
    qkv_gather.forward(0)
    feed[1][0].relay(0)
    for wait in (*qkv_in[2], *qkv_in[3]):
        wait()
    qkv_gather.forward(PAIR)
    out_in[2]()
    out_in[3]()
    out_gather.forward(PAIR)
    out_in[0]()
    out_in[1]()
    out_gather.forward(0)
    feed[0][0].forward(0, feed[0][1])
    seg_wait = moves.swap(seg, seg_in, seg_in, place.chips[2])
    swap_pair(0)
    spread_one.from_pair()
    swap_pair(1)
    qkv_gather.relay(0)
    qkv_gather.relay(PAIR)
    qkv_gather.hop(0)
    spread_one.from_both()
    out_gather.relay(0)
    out_gather.relay(PAIR)
    qkv_gather.hop(PAIR)
    feed[0][0].relay(0)
    spread_cot = Spread(moves, place, cot, rows_cot)
    swap_pair(5)
    out_gather.hop(0)
    spread_one.from_ctx()
    seg_wait()
    pair_first = place.pair == 0
    own_seg, far_seg = seg[...].astype(F32), seg_in[...].astype(F32)
    for i in range(2):
        here = pair_first if i == 0 else jnp.logical_not(pair_first)
        flags = jnp.where(here, own_seg, far_seg)
        both = jnp.broadcast_to(flags, (128, length)).T[:, 0:1]
        start = jnp.sum((flags < both).astype(F32), axis=1, keepdims=True)
        row = lax.broadcasted_iota(jnp.int32, (length, length), 0).astype(F32)
        col = lax.broadcasted_iota(jnp.int32, (length, length), 1).astype(F32)
        chosen = (row - start == col).astype(F32)
        at = pl.ds(i * length, length)
        both_tables = lax.dot_general(
            chosen, table[...], (((1,), (0,)), ((), ())),
            precision=lax.Precision.HIGHEST, preferred_element_type=F32,
        )
        d = gain_q.shape[1]
        starts[at] = jnp.broadcast_to(start, (length, 128))
        cos[at] = both_tables[:, :d]
        sin[at] = both_tables[:, d:]
    moves.store(starts, starts_out)
    moves.store(cos, cos_out)
    moves.store(sin, sin_out)
    spread_one.finish()
    normed_stored = moves.load(rows_one, normed_one)
    out_gather.hop(PAIR)
    feed[0][0].pass_on(PAIR, feed[0][2])
    feed[3][0].forward(0, feed[3][1])
    qkv_gather.finish()
    moves.store(w_qkv, qkv_weight)
    @pl.loop(0, w_qkv.shape[1] // wide)
    def _(i):
        at = lanes(i * wide, wide)
        qkv[:, at] = dot(rows_one[...], w_qkv[:, at]).astype(BF16)

    moves.store(qkv, qkv_out)
    @pl.loop(0, 2)
    def _(s):
        attend_one(groups, s, qkv, starts, cos, sin, gain_q, gain_k, att)

    moves.store(att, att_out)
    feed[1][0].pass_on(PAIR, feed[1][2])
    out_gather.finish()
    moves.store(w_out, out_weight)
    feed[1][0].hop(0)
    feed[0][0].relay(PAIR)
    @pl.loop(0, width // 256)
    def _(i):
        at = lanes(i * 256, 256)
        times, block = columns_of(w_out, at)
        part[:, :, at] = times(att[...], block).astype(BF16).reshape(8, rows, 256)

    swap_pair(4)
    collects[0] = collect_part(0)
    collects[1] = collect_part(1)
    collects[0].to_ctx()
    swap_pair(2)
    feed[4][0].forward(0, feed[4][1])
    collects[1].to_ctx()
    swap_pair(3)
    collects[0].to_pair()
    feed[2][0].forward(0, feed[2][1])
    feed[4][0].pass_on(PAIR, feed[4][2])
    feed[1][0].relay(PAIR)
    feed[0][0].hop(0)
    collects[1].to_pair()
    feed[4][0].relay(0)
    collects[0].finish()
    feed[4][0].relay(PAIR)
    feed[3][0].relay(0)
    half_loop(0, rows // 2, norm_two(0))
    feed[2][0].pass_on(PAIR, feed[2][2])
    spread_two_0 = Spread(moves, place, own_two.at[pl.ds(0 * rows // 2, rows // 2)], rows_two, 0, 2)
    feed[1][0].hop(PAIR)
    feed[3][0].pass_on(PAIR, feed[3][2])
    spread_cot.from_pair()
    collects[1].finish()
    half_loop(1, rows // 2, norm_two(1))
    feed[5][0].forward(0, feed[5][1])
    spread_two_1 = Spread(moves, place, own_two.at[pl.ds(1 * rows // 2, rows // 2)], rows_two, 1, 2)
    feed[0][0].hop(PAIR)
    feed[4][0].hop(0)
    feed[2][0].relay(0)
    feed[3][0].relay(PAIR)
    spread_cot.from_ctx()
    spread_cot.from_both()
    feed[3][0].hop(0)
    spread_two_0.from_ctx()
    spread_two_0.from_pair()
    spread_cot.finish()
    moves.store(rows_cot, cot_out)
    feed[2][0].relay(PAIR)
    spread_two_1.from_ctx()
    feed[5][0].pass_on(PAIR, feed[5][2])
    feed[4][0].hop(PAIR)
    feed[5][0].relay(0)
    own_feed[0]()
    feed[0][0].finish()
    spread_two_1.from_pair()
    spread_two_0.from_both()
    feed[2][0].hop(0)
    spread_two_1.from_both()
    own_feed[4]()
    feed[4][0].finish()
    spread_two_0.finish()
    own_feed[1]()
    feed[1][0].finish()
    feed[5][0].relay(PAIR)
    feed[3][0].hop(PAIR)
    spread_two_1.finish()
    moves.store(rows_two, normed_two)
    gate_part(piece_a)
    feed[2][0].hop(PAIR)
    up_part(piece_a)
    own_feed[3]()
    feed[3][0].finish()
    feed[5][0].hop(0)
    gate_part(piece_b)
    up_part(piece_b)
    send_early(0)
    moves.store(mixed_t, mixed_out)
    feed[5][0].hop(PAIR)
    own_feed[2]()
    feed[2][0].finish()
    normed_stored()
    down_part(piece_a, False)
    back_part(piece_a)
    send_early(1)
    grad_part(piece_a, False)
    own_feed[5]()
    feed[5][0].finish()
    back_part(piece_b)
    moves.store(grad_gate, grad_gate_out)
    moves.store(grad_up, grad_up_out)
    grad_part(piece_b, True)
    down_part(piece_b, True)
    for wait in early_waits:
        wait()
    moves.close()


def norm_back(grad, x, gain, gain_grad):
    unit, scale = unit_and_scale(x)
    gain_grad[...] += jnp.sum((grad * unit).reshape(-1, 8, grad.shape[-1]), axis=0)
    e = grad * gain
    return scale * (e - unit * jnp.mean(e * unit, axis=-1, keepdims=True))


def turn_kernel(
    bits, partial, mid, cot, gain, grad_mid, gain_grad, out,
    own, held, first, ctx_in, pair_in, sending, send, recv, local,
):
    place = Place(bits)
    moves = Moves(send, recv, local)
    place.greet()
    collect = Collect(
        moves, place, lambda j, t: partial.at[place.rows_of[j] + t], held, first, ctx_in, pair_in, sending, True
    )
    collect.to_ctx()
    collect.to_pair()
    collect.finish()
    gain_grad[...] = jnp.zeros_like(gain_grad)

    def back(at):
        g = cot[at].astype(F32) + norm_back(collect.total(at), mid[at], gain[...], gain_grad)
        grad_mid[at] = g
        own[at] = g.astype(BF16)

    row_loop(mid.shape[0], back)
    spread = Spread(moves, place, own, out)
    spread.from_pair()
    spread.from_ctx()
    spread.from_both()
    spread.finish()
    moves.close()


def last_kernel(
    bits, partial, hidden, grad_mid, gain, grad_in, gain_grad,
    held, first, ctx_in, pair_in, sending, send, recv, local,
):
    place = Place(bits)
    moves = Moves(send, recv, local)
    place.greet()
    collect = Collect(
        moves, place, lambda j, t: partial.at[place.rows_of[j] + t], held, first, ctx_in, pair_in, sending, True
    )
    collect.to_ctx()
    collect.to_pair()
    collect.finish()
    gain_grad[...] = jnp.zeros_like(gain_grad)

    def back(at):
        grad_in[at] = grad_mid[at] + norm_back(
            collect.total(at), hidden[at].astype(F32), gain[...], gain_grad
        )

    row_loop(hidden.shape[0], back)
    moves.close()


class Scatter:
    def __init__(self, moves, place, product, out0, in0, out1, in1, acc, acc_pair, spare):
        self.moves, self.place, self.product, self.spare = moves, place, product, spare
        self.out0, self.in0, self.out1, self.in1, self.acc, self.acc_pair = out0, in0, out1, in1, acc, acc_pair
        self.low, self.high = place.bits[1], place.bits[0]
        self.order = [self.high, self.high | PAIR, 0, PAIR]
        self.first, self.second, self.leaving = {}, {}, {}

    def send(self, i):
        slot = i % 2
        for wait in self.leaving.pop(slot, []):
            wait()

        def emit(at, value):
            self.out0[(slot, *at)] = value.astype(BF16)

        self.product(self.order[i] | self.low, emit)
        self.leaving[slot] = []
        self.first[i] = self.moves.swap(
            self.out0.at[slot], self.in0.at[i], self.in0.at[i], self.place.along(self.low), self.leaving[slot]
        )

    def take(self, i):
        self.first[i]()

        def emit(at, value):
            value = value + self.in0[(i, *at)].astype(F32)
            if i < 2:
                self.out1[(i, *at)] = value.astype(BF16)
            elif i == 2:
                self.acc[at] = value
            else:
                self.acc_pair[at] = value.astype(BF16)

        self.product(self.order[i], emit)
        if i < 2:
            to = self.in1.at[i]
            self.second[i] = Cross(
                self.moves, self.place, self.out1.at[i], to, self.spare.at[2 * i], to, self.spare.at[2 * i + 1], to
            )

    def relay(self, i):
        self.second[i].relay()

    def take_high(self, i):
        self.second[i].arrive()
        total = self.acc_pair if i else self.acc
        step = 64

        @pl.loop(0, total.shape[0] // step)
        def _(k):
            at = pl.ds(pl.multiple_of(k * step, step), step)
            total[at] = (total[at].astype(F32) + self.in1[i, at].astype(F32)).astype(total.dtype)

    def close(self):
        for waits in self.leaving.values():
            for wait in waits:
                wait()


class Blocks:
    def __init__(self, moves, place, slots, order):
        self.moves, self.place, self.slots, self.order = moves, place, slots, order
        self.next, self.waits = 0, {}
        self.start(0)

    def start(self, k):
        if k < len(self.order):
            ref, mask = self.order[k]
            size = self.slots.shape[2]
            at = pl.ds(pl.multiple_of(self.place.block(mask) * size, size), size)
            self.waits[k] = self.moves.load(ref.at[:, at], self.slots.at[k % 2])

    def get(self, ref, mask):
        k = self.next
        assert self.order[k][0] is ref and self.order[k][1] == mask
        self.next += 1
        self.waits.pop(k)()
        self.start(k + 1)
        return self.slots[k % 2]


def backward_kernel(
    bits, groups,
    cot, gain_attn, gain_mlp, starts, cos, sin, gain_q, gain_k,
    mid, hidden, part_two, part_hidden, normed_one, normed_two, cot_rows, qkv_in, att_in, qkv_weight, out_weight, grad_gate, grad_up,
    mixed_t, early_in,
    grad_in, hidden_out, gains, feed_own, feed_other, down_own, down_other, qkv_own, qkv_other, out_own, out_other,
    spare_feed, spare_down, spare_qkv, spare_out,
    own, rows_mid, feed, mixed, lhs, lhs_t, part, w_qkv, w_out, qkv, att, datt, dqkv,
    first, ctx_in, pair_in, sending, first_h, ctx_h, pair_h, sending_h, gain_a, gain_m, gain_h, tree, tree_in,
    f_out0, f_in0, f_out1, f_in1, f_acc, f_pair, d_out0, d_in0, d_out1, d_in1, d_acc, d_pair,
    q_out0, q_in0, q_out1, q_in1, q_acc, q_pair, o_out0, o_in0, o_out1, o_in1, o_acc, o_pair,
    send, recv, local,
):
    place = Place(bits)
    moves = Moves(send, recv, local)
    rows, width = cot.shape
    cols = mixed.shape[0]
    tile = lhs.shape[2]
    half = tile // 2
    high, low = bits
    place.greet()

    def lanes(start, size):
        return pl.ds(pl.multiple_of(start, size), size)

    ready_mid = moves.load(mid, hidden_out)
    ready_feed = [
        moves.load(grad_gate, feed.at[:, pl.ds(0, cols)]),
        moves.load(grad_up, feed.at[:, pl.ds(cols, cols)]),
    ]
    masks = [high, high | PAIR, 0, PAIR]
    sends = [m | low for m in masks]
    a, b, c, e = range(4)
    order = [
        (cot_rows, masks[b]), (cot_rows, sends[e]), (cot_rows, masks[a]), (normed_two, sends[a]),
        (cot_rows, masks[e]), (normed_two, sends[b]), (normed_two, masks[a]), (normed_two, sends[e]),
        (normed_two, masks[b]), (normed_two, masks[e]), (normed_one, sends[a]), (normed_one, sends[b]),
        (normed_one, masks[a]), (normed_two, sends[c]), (normed_one, sends[e]), (normed_one, masks[b]),
        (normed_two, masks[c]), (normed_one, sends[c]), (normed_one, masks[e]), (cot_rows, sends[c]),
        (normed_one, masks[c]), (cot_rows, masks[c]),
    ]
    blocks = Blocks(moves, place, lhs, order)
    ready_mixed = moves.load(mixed_t, mixed)
    ready_early = [moves.load(early_in.at[i], d_in0.at[i]) for i in range(2)]
    ready_late = [
        moves.load(out_weight, w_out),
        moves.load(att_in, att),
        moves.load(qkv_in, qkv),
        moves.load(qkv_weight, w_qkv),
    ]

    def by_rows(source, right):
        def product(mask, emit):
            lhs_t[...] = blocks.get(source, mask).T
            step = min(512, right.shape[1])

            @pl.loop(0, right.shape[1] // step)
            def _(i):
                at = lanes(i * step, step)
                emit((slice(None), at), dot(lhs_t[...], right[:, at]))

        return product

    def down_product(mask, emit):
        block = blocks.get(cot_rows, mask)
        step = min(256, cols)

        @pl.loop(0, cols // step)
        def _(i):
            at = lanes(i * step, step)
            emit((at, slice(None)), dot(mixed[at], block))

    def out_product(mask, emit):
        at = lanes(place.block(mask) * tile, tile)
        emit((slice(None), slice(None)), dot_rows(att[...], rows_mid[:, at]))

    feed_s = Scatter(moves, place, by_rows(normed_two, feed), f_out0, f_in0, f_out1, f_in1, f_acc, f_pair, spare_feed)
    down_s = Scatter(moves, place, down_product, d_out0, d_in0, d_out1, d_in1, d_acc, d_pair, spare_down)
    down_s.first = dict(enumerate(ready_early))
    qkv_s = Scatter(moves, place, by_rows(normed_one, dqkv), q_out0, q_in0, q_out1, q_in1, q_acc, q_pair, spare_qkv)
    out_s = Scatter(moves, place, out_product, o_out0, o_in0, o_out1, o_in1, o_acc, o_pair, spare_out)

    d = gain_q.shape[1]
    gain_m[...] = jnp.zeros_like(gain_m)
    gain_a[...] = jnp.zeros_like(gain_a)
    gain_h[...] = jnp.zeros_like(gain_h)

    twos = [None, None]

    def collect_part(h):
        at = pl.ds(h * rows // 2, rows // 2)
        return Collect(
            moves, place, lambda j, t: part_two.at[place.rows_of[j] + t, at], part.at[:, at], first.at[:, at],
            ctx_in.at[:, at], pair_in.at[at], sending.at[:, at], True,
        )

    def back_two(h):
        def body(there, at):
            x = hidden_out[at]
            g = cot[at].astype(F32) + norm_back(twos[h].total(there), x, gain_mlp[...], gain_m)
            hidden_out[at] = x + collect_hidden.two(0, at)
            grad_in[at] = g
            own[at] = g.astype(BF16)

        return body

    def back_one(at):
        grad_in[at] += norm_back(collect_one.total(at), own[at].astype(F32), gain_attn[...], gain_a)

    def end_hidden(at):
        hidden_out[at] += ctx_h[1, at].astype(F32) + pair_h[at].astype(F32)

    tree_waits = []

    def climb():
        k = len(tree_waits)
        if k == 1:
            tree_waits[0]()
            tree[1] = tree[0] + tree_in[0]
        if k > 1:
            for wait in tree_waits[-1]:
                wait()
            at = 1 + 4 * (k - 2)
            tree[k] = (tree_in[at] + tree_in[at + 1]) + (tree_in[at + 2] + tree_in[at + 3])
        if k == 0:
            tree_waits.append(moves.swap(tree.at[0], tree_in.at[0], tree_in.at[0], place.sibling))
        elif k < 3:
            mine, others = team(k)
            slots = 1 + 4 * (k - 1)
            tree_in[slots + mine] = tree[k]
            tree_waits.append(
                [
                    moves.swap(tree.at[k], tree_in.at[slots + mine], tree_in.at[slots + index], device)
                    for index, device in others
                ]
            )

    def team(k):
        if k == 1:
            return place.rows_of[0] // 2, [(place.rows_of[j] // 2, place.chips[j]) for j in (3, 2, 1)]

        def index(mask):
            f = place.block(mask)
            return (f // high) % 2 * 2 + f % 2

        return index(0), [(index(m), place.along(m)) for m in (high | low, high, low)]

    finals = []

    def pair_final(scatter, other):
        scatter.take_high(1)
        finals.append(moves.swap(scatter.acc_pair, other, other, place.chips[2]))

    def own_final(scatter, mine):
        scatter.take_high(0)
        moves.store(scatter.acc, mine)

    def mates_final(scatter, slot, piece, spare, other):
        scatter.take_high(slot)
        for j in (3, 2) if slot else (1,):
            out = spare(j)
            out[...] = piece(slot, place.at[j][1]).astype(BF16)
            finals.append(moves.swap(out, other.at[j - 1], other.at[j - 1], place.chips[j]))

    def qkv_piece(slot, c):
        return (q_pair if slot else q_acc)[lanes(c * half, half)]

    def out_piece(slot, c):
        return (o_pair if slot else o_acc)[:, lanes(c * half, half)]

    def qkv_spare(j):
        return q_in0.at[j, pl.ds(0, half)]

    def out_spare(j):
        return o_in0.at[j, :, pl.ds(0, half)]

    ready_mixed()
    down_s.take(b)
    twos[0] = collect_part(0)
    down_s.send(e)
    for wait in ready_feed:
        wait()
    twos[0].to_ctx()
    collect_hidden = Collect(
        moves, place, lambda j, t: part_hidden.at[place.rows_of[j] + t], part.at[pl.ds(4, 4)],
        first_h, ctx_h, pair_h, sending_h, True,
    )
    twos[1] = collect_part(1)
    down_s.take(a)
    down_s.relay(b)
    feed_s.send(a)
    collect_hidden.fold()
    down_s.take(e)
    twos[1].to_ctx()
    twos[0].to_pair()
    feed_s.send(b)
    twos[1].to_pair()
    twos[0].finish()
    ready_mid()
    half_loop(0, rows // 2, back_two(0))
    spread_0 = Spread(moves, place, own.at[pl.ds(0 * rows // 2, rows // 2)], rows_mid, 0, 2)
    down_s.relay(a)
    twos[1].finish()
    half_loop(1, rows // 2, back_two(1))
    spread_1 = Spread(moves, place, own.at[pl.ds(1 * rows // 2, rows // 2)], rows_mid, 1, 2)
    feed_s.take(a)
    spread_0.from_pair()
    spread_0.from_ctx()
    for wait in ready_late:
        wait()
    spread_1.from_ctx()
    spread_1.from_pair()
    pair_final(down_s, down_other)
    spread_0.from_both()
    feed_s.send(e)
    spread_1.from_both()
    feed_s.take(b)
    collect_hidden.post_ctx()
    spread_1.finish()
    spread_0.finish()
    ready_hidden = moves.load(hidden, own)
    out_s.send(a)
    @pl.loop(0, 4)
    def _(i):
        at = lanes(i * 2 * rows, 2 * rows)
        datt[at] = dot_cols(rows_mid[at], w_out[...]).astype(BF16)

    out_s.send(b)
    feed_s.relay(a)
    @pl.loop(0, 2)
    def _(s):
        attend_back_one(groups, s, qkv, att, datt, starts, cos, sin, gain_q, gain_k, dqkv, gain_h)

    @pl.loop(0, width // tile)
    def _(i):
        at = lanes(i * tile, tile)
        part[:, :, at] = dot_cols(dqkv[...], w_qkv[at]).astype(BF16).reshape(8, rows, tile)

    feed_s.take(e)
    collect_hidden.post_pair()
    collect_one = Collect(
        moves, place, lambda j, t: part.at[place.rows_of[j] + t], None, first, ctx_in, pair_in, sending, False
    )
    qkv_s.send(a)
    collect_one.to_ctx()
    out_s.send(e)
    out_s.send(c)
    out_s.take(b)
    qkv_s.send(b)
    feed_s.relay(b)
    out_s.take(c)
    qkv_s.take(a)
    feed_s.send(c)
    out_s.relay(b)
    out_s.take(a)
    collect_one.to_pair()
    qkv_s.relay(a)
    qkv_s.send(e)
    collect_hidden.came()
    row_loop(rows, end_hidden)
    out_s.take(e)
    qkv_s.take(b)
    feed_s.take(c)
    own_final(feed_s, feed_own)
    pair_final(feed_s, feed_other)
    collect_one.finish()
    qkv_s.send(c)
    qkv_s.take(e)
    down_s.send(c)
    ready_hidden()
    row_loop(rows, back_one)
    tree[0, :, 0:width] = jnp.sum(gain_a[...], axis=0, keepdims=True)
    tree[0, :, width : 2 * width] = jnp.sum(gain_m[...], axis=0, keepdims=True)
    tree[0, :, 2 * width : 2 * width + d] = jnp.sum(gain_h[0], axis=0, keepdims=True)
    tree[0, :, 2 * width + d : 2 * width + 2 * d] = jnp.sum(gain_h[1], axis=0, keepdims=True)
    climb()
    climb()
    qkv_s.relay(b)
    qkv_s.take(c)
    mates_final(qkv_s, 0, qkv_piece, qkv_spare, qkv_other)
    qkv_own[...] = qkv_piece(0, place.c)
    mates_final(out_s, 1, out_piece, out_spare, out_other)
    climb()
    out_s.relay(a)
    mates_final(qkv_s, 1, qkv_piece, qkv_spare, qkv_other)
    mates_final(out_s, 0, out_piece, out_spare, out_other)
    out_own[...] = out_piece(0, place.c)
    down_s.take(c)
    own_final(down_s, down_own)
    climb()
    gains[...] = tree[3]
    for scatter in (feed_s, down_s, qkv_s, out_s):
        scatter.close()
    for wait in finals:
        wait()
    moves.close()


def join_kernel(
    feed_own, feed_other, down_own, down_other, qkv_own, qkv_other, out_own, out_other, grad_in, hidden, gains,
    g_query, g_key, g_value, g_out, g_gate, g_up, g_down, g_in, h_out, gain_a, gain_m, gain_q, gain_k,
):
    c = lax.axis_index("ctx")
    pair = (lax.axis_index("fsdp") // PAIR) % 2
    cols, n_q = down_own.shape[0], out_own.shape[0]
    n_kv = (qkv_own.shape[1] - n_q) // 2

    def lanes(start, size):
        return pl.ds(pl.multiple_of(start, size), size)

    mine, theirs = lanes(pair * cols, cols), lanes((1 - pair) * cols, cols)
    g_gate[:, mine] = feed_own[:, :cols]
    g_up[:, mine] = feed_own[:, cols:]
    g_down[mine] = down_own[...]
    g_gate[:, theirs] = feed_other[:, :cols].astype(F32)
    g_up[:, theirs] = feed_other[:, cols:].astype(F32)
    g_down[theirs] = down_other[...].astype(F32)
    chunks = [c * 2 + pair, (1 - c) * 2 + pair, c * 2 + 1 - pair, (1 - c) * 2 + 1 - pair]
    for j, chunk in enumerate(chunks):
        qkv = qkv_own[...] if j == 0 else qkv_other[j - 1].astype(F32)
        g_query[:, lanes(chunk * n_q, n_q)] = qkv[:, :n_q]
        g_key[:, lanes(chunk * n_kv, n_kv)] = qkv[:, n_q : n_q + n_kv]
        g_value[:, lanes(chunk * n_kv, n_kv)] = qkv[:, n_q + n_kv :]
        g_out[lanes(chunk * n_q, n_q)] = out_own[...] if j == 0 else out_other[j - 1].astype(F32)
    g_in[...] = grad_in[...]
    h_out[...] = hidden[...]
    width, d = gain_a.shape[1], gain_q.shape[1]
    gain_a[...] = gains[:, :width]
    gain_m[...] = gains[:, width : 2 * width]
    gain_q[...] = gains[:, 2 * width : 2 * width + d]
    gain_k[...] = gains[:, 2 * width + d :]


VMEM_SPEC = pl.BlockSpec(memory_space=pltpu.VMEM)
ANY_SPEC = pl.BlockSpec(memory_space=pl.ANY)


def comm_call(kernel, bits, collective_id, operands, in_specs, outs, out_specs, scratch, nbytes, copies, *more):
    return pl.pallas_call(
        functools.partial(kernel, bits, *more),
        out_shape=outs,
        in_specs=in_specs,
        out_specs=out_specs,
        scratch_shapes=[
            *scratch,
            pltpu.SemaphoreType.DMA((copies,)),
            pltpu.SemaphoreType.DMA((copies,)),
            pltpu.SemaphoreType.DMA((96,)),
        ],
        compiler_params=pltpu.CompilerParams(
            collective_id=collective_id, has_side_effects=True, vmem_limit_bytes=61 << 20
        ),
        cost_estimate=pl.CostEstimate(flops=nbytes * 20, bytes_accessed=nbytes, transcendentals=0),
        name=kernel.__name__,
    )(*operands)


def build(mesh):
    n = mesh.size
    n_f = mesh.shape["fsdp"]
    spread_bits = [b for b in (1 << i for i in range(n_f.bit_length() - 2, -1, -1)) if b != PAIR]
    all_bits = sorted([*spread_bits, PAIR], reverse=True)

    def swap(v, bit):
        return lax.ppermute(v, AXES, [(i, i ^ bit) for i in range(n)])

    def bit_of(f, b):
        return (f // b) % 2

    def in_order(bit, own, other, axis):
        low = jnp.where(bit == 0, own, other)
        high = jnp.where(bit == 0, other, own)
        return jnp.stack([low, high], axis=axis)

    def pick(v, index, axis):
        return lax.dynamic_index_in_dim(v, index, axis, keepdims=False)

    def scatter(keep, got, f, width):
        v = keep + got.astype(F32)
        have = [b for b in all_bits if b != 1]
        v = v.reshape(*([2] * len(have)), width, v.shape[-1])
        for b in [b for b in reversed(spread_bits) if b != 1]:
            axis = have.index(b)
            bit = bit_of(f, b)
            v = pick(v, bit, axis) + swap(pick(v, 1 - bit, axis).astype(BF16), b * 4).astype(F32)
            have.remove(b)
        return v

    def body(
        hidden_in,
        cotangent,
        segments,
        w_query,
        key_projection_weight,
        value_projection_weight,
        w_out,
        w_gate,
        w_up,
        w_down,
        gain_attn,
        gain_mlp,
        gain_query,
        key_norm_gain,
    ):
        rows, width = hidden_in.shape
        d = gain_query.shape[0]
        length = segments.shape[0]
        f, c = lax.axis_index("fsdp"), lax.axis_index("ctx")
        pair = bit_of(f, PAIR)
        at_rows = w_query.shape[0]
        ff_rows = w_gate.shape[0]
        ff_cols = w_gate.shape[1] // 2
        q_cols, kv_cols = w_query.shape[1] // 4, key_projection_weight.shape[1] // 4
        groups = q_cols // kv_cols

        freqs = (THETA ** (-2.0 * np.arange(d // 2, dtype=np.float32) / d)).astype(np.float32)
        angles = (np.arange(length, dtype=np.float32)[:, None] * freqs).astype(np.float64)
        table_cos, table_sin = np.cos(angles), np.sin(angles)
        table = jnp.asarray(np.concatenate([table_cos, table_cos, -table_sin, table_sin], axis=-1), F32)

        n_rows = 8 * rows
        all_rows = jax.ShapeDtypeStruct((n_rows, width), BF16)
        own_rows = jax.ShapeDtypeStruct((rows, width), F32)
        gain_rows = jax.ShapeDtypeStruct((8, width), F32)
        block = pltpu.VMEM((rows, width), BF16)
        nbytes = rows * width * 16
        qkv_cols = q_cols + 2 * kv_cols

        def shape(*dims):
            return jax.ShapeDtypeStruct(dims, BF16)

        copies = 160 + 10 * n_f
        natural = at_rows % 128 == 0 and ff_rows % 128 == 0
        out_dims = (q_cols, width) if natural else (width, q_cols)
        down_dims = (ff_cols, width) if natural else (width, ff_cols)
        out_part = (q_cols, 2 * at_rows) if natural else (2 * at_rows, q_cols)
        down_part_dims = (ff_cols, ff_rows) if natural else (ff_rows, ff_cols)
        border = ff_cols - 256 if ff_cols % 256 == 0 and ff_cols > 256 else ff_cols // 2
        feed_spares = []
        for piece in (border, ff_cols - border):
            feed_spares += [shape(4, ff_rows, piece)] * 2
            feed_spares.append(shape(4, piece, ff_rows) if natural else shape(4, ff_rows, piece))
        n_seq = 2 * length
        all_tables = jax.ShapeDtypeStruct((n_seq, d), F32)

        def v(*dims, dtype=BF16):
            return pltpu.VMEM(dims, dtype)

        (
            residual_mid, normed_one, normed_two, grad_rows, qkv, attended, full_qkv, full_out, starts, cos, sin,
            grad_gate, grad_up, mixed_t, norm_two_part, down_part, *_, early_in,
        ) = comm_call(
            forward_kernel, spread_bits, 0,
            (hidden_in, cotangent, gain_attn[None], gain_mlp[None], segments[None], table, gain_query[None],
             key_norm_gain[None], w_query, key_projection_weight, value_projection_weight,
             w_out if natural else w_out.T, w_gate, w_up, w_down if natural else w_down.T),
            [VMEM_SPEC] * 8 + [ANY_SPEC] * 7,
            (own_rows, all_rows, all_rows, all_rows, shape(n_rows, qkv_cols), shape(n_rows, q_cols),
             shape(width, qkv_cols), shape(*out_dims), jax.ShapeDtypeStruct((n_seq, 128), F32), all_tables, all_tables,
             shape(n_rows, ff_cols), shape(n_rows, ff_cols), shape(ff_cols, n_rows), shape(8, rows, width), all_rows,
             shape(4, 2 * at_rows, qkv_cols), shape(4, *out_part), *feed_spares,
             shape(2, *down_part_dims)),
            (VMEM_SPEC, *[ANY_SPEC] * 24),
            [block, block, v(n_rows, width), v(n_rows, width), v(n_rows, width), v(width, qkv_cols), v(*out_dims),
             v(width, ff_cols), v(width, ff_cols), v(*down_dims), v(n_rows, qkv_cols), v(n_rows, q_cols),
             v(8, rows, width), v(n_rows, ff_cols, dtype=F32), v(n_rows, ff_cols, dtype=F32), v(n_rows, ff_cols),
             v(n_rows, ff_cols), v(n_rows, ff_cols), v(ff_cols, n_rows), v(n_seq, 128, dtype=F32),
             v(n_seq, d, dtype=F32), v(n_seq, d, dtype=F32), v(1, length, dtype=jnp.int32), v(2, *down_part_dims),
             *collect_buffers(rows, width)],
            16 * nbytes, copies, groups, natural,
        )
        common = (starts, cos, sin, gain_query[None], key_norm_gain[None])
        backward = one_kernel if natural and len(spread_bits) == 2 else by_steps
        return backward(
            hidden_in, cotangent, residual_mid, gain_attn, gain_mlp, common, norm_two_part, down_part, normed_one,
            normed_two, grad_rows, qkv, attended, full_qkv, full_out, grad_gate, grad_up, mixed_t, early_in,
            (at_rows, ff_rows),
        )

    def one_kernel(
        hidden_in, cotangent, residual_mid, gain_attn, gain_mlp, common, norm_two_part, down_part, normed_one,
        normed_two, grad_rows, qkv, attended, full_qkv, full_out, grad_gate, grad_up, mixed_t, early_in, sizes,
    ):
        rows, width = hidden_in.shape
        cols, n_rows = mixed_t.shape
        (at_rows, ff_rows), q_cols, qkv_cols = sizes, attended.shape[1], qkv.shape[1]
        d = common[-1].shape[1]
        kv_cols = (qkv_cols - q_cols) // 2
        groups = q_cols // kv_cols

        def out(dtype, *dims):
            return jax.ShapeDtypeStruct(dims, dtype)

        def v(*dims, dtype=BF16):
            return pltpu.VMEM(dims, dtype)

        def scatter(*block):
            return [v(2, *block), v(4, *block), v(2, *block), v(2, *block), v(*block, dtype=F32), v(*block)]

        n_gain = 2 * width + 2 * d
        nbytes = n_rows * width * 20
        (
            grad_input, hidden_out, gains, feed_own, feed_other, down_own, down_other, qkv_own, qkv_other, out_own,
            out_other, *_,
        ) = comm_call(
            backward_kernel, spread_bits, 2,
            (cotangent, gain_attn[None], gain_mlp[None], *common, residual_mid, hidden_in, norm_two_part,
             down_part.reshape(8, rows, width), normed_one, normed_two, grad_rows, qkv, attended, full_qkv, full_out,
             grad_gate, grad_up, mixed_t, early_in),
            [VMEM_SPEC] * 8 + [ANY_SPEC] * 15,
            (out(F32, rows, width), out(F32, rows, width), out(F32, 1, n_gain), out(F32, ff_rows, 2 * cols),
             out(BF16, ff_rows, 2 * cols), out(F32, cols, ff_rows), out(BF16, cols, ff_rows),
             out(F32, at_rows, qkv_cols), out(BF16, 3, at_rows, qkv_cols), out(F32, q_cols, at_rows),
             out(BF16, 3, q_cols, at_rows), out(BF16, 4, ff_rows, 2 * cols), out(BF16, 4, cols, ff_rows),
             out(BF16, 4, ff_rows, qkv_cols), out(BF16, 4, q_cols, ff_rows)),
            (VMEM_SPEC, VMEM_SPEC, VMEM_SPEC, ANY_SPEC, ANY_SPEC, ANY_SPEC, ANY_SPEC, VMEM_SPEC, ANY_SPEC, VMEM_SPEC,
             *[ANY_SPEC] * 5),
            [v(rows, width), v(n_rows, width), v(n_rows, 2 * cols), v(cols, n_rows), v(2, n_rows, ff_rows),
             v(ff_rows, n_rows), v(8, rows, width), v(width, qkv_cols), v(q_cols, width), v(n_rows, qkv_cols),
             v(n_rows, q_cols), v(n_rows, q_cols), v(n_rows, qkv_cols),
             *collect_buffers(rows, width), *collect_buffers(rows, width), v(8, width, dtype=F32), v(8, width, dtype=F32), v(2, 8, d, dtype=F32),
             v(4, 1, n_gain, dtype=F32), v(9, 1, n_gain, dtype=F32),
             *scatter(ff_rows, 2 * cols), *scatter(cols, ff_rows), *scatter(ff_rows, qkv_cols),
             *scatter(q_cols, ff_rows)],
            nbytes, 110, groups,
        )
        own_rows = out(F32, rows, width)
        made = (
            out(F32, at_rows, 4 * q_cols), out(F32, at_rows, 4 * kv_cols), out(F32, at_rows, 4 * kv_cols),
            out(F32, 4 * q_cols, at_rows), out(F32, ff_rows, 2 * cols), out(F32, ff_rows, 2 * cols),
            out(F32, 2 * cols, ff_rows), own_rows, own_rows, out(F32, 1, width), out(F32, 1, width), out(F32, 1, d),
            out(F32, 1, d),
        )
        pieces = pl.pallas_call(
            join_kernel,
            out_shape=made,
            compiler_params=pltpu.CompilerParams(vmem_limit_bytes=61 << 20),
            name="join_kernel",
        )(feed_own, feed_other, down_own, down_other, qkv_own, qkv_other, out_own, out_other, grad_input, hidden_out, gains)
        grads, (grad_input, hidden_out), gains = pieces[:7], pieces[7:9], pieces[9:]
        return hidden_out, grad_input, *grads, *(g[0] for g in gains)

    def by_steps(
        hidden_in, cotangent, residual_mid, gain_attn, gain_mlp, common, norm_two_part, down_part, normed_one,
        normed_two, grad_rows, qkv, attended, full_qkv, full_out, grad_gate, grad_up, mixed_t, early_in, sizes,
    ):
        rows, width = hidden_in.shape
        (at_rows, ff_rows), ff_cols, q_cols = sizes, mixed_t.shape[0], attended.shape[1]
        d = common[-1].shape[1]
        kv_cols = (qkv.shape[1] - q_cols) // 2
        groups = q_cols // kv_cols
        natural = full_out.shape[0] != width
        times_t = dot_cols if natural else dot
        f, c = lax.axis_index("fsdp"), lax.axis_index("ctx")
        pair = bit_of(f, PAIR)
        all_rows = jax.ShapeDtypeStruct((8 * rows, width), BF16)
        own_rows = jax.ShapeDtypeStruct((rows, width), F32)
        gain_rows = jax.ShapeDtypeStruct((8, width), F32)
        block = pltpu.VMEM((rows, width), BF16)
        nbytes = rows * width * 16
        grad_mid, gain_mlp_part, grad_mid_rows = comm_call(
            turn_kernel, spread_bits, 2, (norm_two_part.reshape(8, rows, width), residual_mid, cotangent, gain_mlp[None]),
            [ANY_SPEC, VMEM_SPEC, VMEM_SPEC, VMEM_SPEC], (own_rows, gain_rows, all_rows),
            (VMEM_SPEC, VMEM_SPEC, ANY_SPEC),
            [block, pltpu.VMEM((4, rows, width), BF16), *collect_buffers(rows, width)], 2 * nbytes, 40,
        )

        low = bit_of(f, 1)

        def weight_grad(acts, grads):
            split = acts.reshape(acts.shape[0], n_f // 2, 2, width // n_f)
            mine = pick(split, low, 2).reshape(acts.shape[0], -1)
            theirs = pick(split, 1 - low, 2).reshape(acts.shape[0], -1)
            got = swap(dot_rows(theirs, grads).astype(BF16), 4)
            return scatter(dot_rows(mine, grads), got, f, width // n_f)

        def ff_grad(acts, grads):
            v = weight_grad(acts, grads)
            other = swap(pick(v, 1 - pair, 0).astype(BF16), PAIR_BIT).astype(F32)
            return in_order(pair, pick(v, pair, 0), other, 1).reshape(ff_rows, 2 * ff_cols)

        grad_w_gate = ff_grad(normed_two, grad_gate)
        grad_w_up = ff_grad(normed_two, grad_up)
        grad_w_down = ff_grad(grad_rows, mixed_t.T).T

        def attn_grad(acts, grads):
            v = weight_grad(acts, grads)
            v = v.reshape(2, 2, at_rows, v.shape[-1])
            mine = pick(pick(v, pair, 0), c, 0)
            by_ctx = swap(pick(pick(v, pair, 0), 1 - c, 0).astype(BF16), CTX_BIT).astype(F32)
            by_pair = swap(pick(pick(v, 1 - pair, 0), c, 0).astype(BF16), PAIR_BIT).astype(F32)
            by_both = swap(pick(pick(v, 1 - pair, 0), 1 - c, 0).astype(BF16), CTX_BIT | PAIR_BIT).astype(F32)
            near = in_order(pair, mine, by_pair, 1)
            far = in_order(pair, by_ctx, by_both, 1)
            return in_order(c, near, far, 1)

        grad_w_out = attn_grad(grad_mid_rows, attended).reshape(at_rows, 4 * q_cols).T

        datt = times_t(grad_mid_rows, full_out).astype(BF16)
        grad_qkv, head_gains = attend_back(groups, qkv, attended, datt, common)
        norm_one_part = dot_cols(grad_qkv, full_qkv).astype(BF16)
        grad_input, gain_attn_part = comm_call(
            last_kernel, spread_bits, 3, (norm_one_part.reshape(8, rows, width), hidden_in, grad_mid, gain_attn[None]),
            [ANY_SPEC, VMEM_SPEC, VMEM_SPEC, VMEM_SPEC], (own_rows, gain_rows), (VMEM_SPEC, VMEM_SPEC),
            [pltpu.VMEM((4, rows, width), BF16), *collect_buffers(rows, width)], nbytes, 40,
        )
        grad_qkv_w = attn_grad(normed_one, grad_qkv)
        grad_w_query = grad_qkv_w[..., :q_cols].reshape(at_rows, -1)
        grad_w_key = grad_qkv_w[..., q_cols : q_cols + kv_cols].reshape(at_rows, -1)
        grad_w_value = grad_qkv_w[..., q_cols + kv_cols :].reshape(at_rows, -1)

        head_gains = jnp.sum(head_gains, axis=1)
        gains = jnp.concatenate(
            [jnp.sum(gain_attn_part, axis=0), jnp.sum(gain_mlp_part, axis=0), head_gains[0], head_gains[1]]
        ).reshape(-1, d)
        for i in range(n.bit_length() - 1):
            gains = gains + swap(gains, 1 << i)
        gains = gains.reshape(-1)
        teams = sorted(
            sorted(i ^ b ^ p for b in range(4) for p in (0, PAIR_BIT))
            for i in range(0, n, 4)
            if not i & PAIR_BIT
        )
        hidden_out = residual_mid + lax.psum_scatter(
            down_part, AXES, scatter_dimension=0, axis_index_groups=teams, tiled=True
        ).astype(F32)
        return (
            hidden_out,
            grad_input,
            grad_w_query,
            grad_w_key,
            grad_w_value,
            grad_w_out,
            grad_w_gate,
            grad_w_up,
            grad_w_down,
            gains[:width],
            gains[width : 2 * width],
            gains[2 * width : 2 * width + d],
            gains[2 * width + d :],
        )

    return body


def solution(mesh):
    everyone = P(("fsdp", "ctx", "tp"), None)
    attn = P(("fsdp", "ctx"), "tp")
    attn_out = P("tp", ("fsdp", "ctx"))
    ff_in = P("fsdp", ("ctx", "tp"))
    ff_out = P(("ctx", "tp"), "fsdp")
    same = P()
    return jax.shard_map(
        build(mesh),
        mesh=mesh,
        in_specs=(
            everyone, everyone, P("fsdp"), attn, attn, attn, attn_out, ff_in, ff_in, ff_out,
            same, same, same, same,
        ),
        out_specs=(
            everyone, everyone, attn, attn, attn, attn_out, ff_in, ff_in, ff_out,
            same, same, same, same,
        ),
        check_vma=False,
    )
```
